32 devices in a mesh: seq: 8 (over y, x, core), mp: 4 (over z).
Axes of the slice: x: 2, y: 2, z: 4, core: 2. Of those that a mesh axis runs over, the one named last changes fastest.
Arguments:
- tokens: bfloat16 [16384, 768], P('seq'), may hold values from -6 to 6
- cotangent: bfloat16 [16384, 768], P('seq'), may hold values from -6 to 6
- past_state: bfloat16 [16, 512, 768], P('seq', None, 'mp'), may hold values from -6 to 6
- positions: int32 [16, 128], P('seq'), may hold values from 0 to 511, as said below
- counts: int32 [16], P('seq'), may hold values from 16 to 128, as said below
- ln1_gain: bfloat16 [768], P('seq'), may hold values from 0.5 to 1.5
- ln1_bias: bfloat16 [768], P('seq'), may hold values from -1 to 1
- w_qkv: bfloat16 [3, 768, 768], P(None, 'seq', 'mp'), may hold values from -0.21875 to 0.21875
- b_qv: bfloat16 [2, 12, 64], P(None, 'mp', 'seq'), may hold values from -1.5 to 1.5
- w_out: bfloat16 [768, 768], P('mp', 'seq'), may hold values from -3 to 3
- b_out: bfloat16 [768], P('seq'), may hold values from -1.5 to 1.5
- ln2_gain: bfloat16 [768], P('seq'), may hold values from 0.5 to 1.5
- ln2_bias: bfloat16 [768], P('seq'), may hold values from -1 to 1
- w_up: bfloat16 [768, 3072], P('seq', 'mp'), may hold values from -0.25 to 0.25
- b_up: bfloat16 [48, 64], P('mp', 'seq'), may hold values from -2.5 to 2.5
- w_down: bfloat16 [3072, 768], P('mp', 'seq'), may hold values from -0.109375 to 0.109375
- b_down: bfloat16 [768], P('seq'), may hold values from -1.5 to 1.5
Outputs:
- out: bfloat16 [16384, 768], P('seq')
- tokens_grad: bfloat16 [16384, 768], P('seq')
- past_grad: float32 [16, 512, 768], P('seq', None, 'mp')
- ln1_gain_grad: float32 [768], P('seq')
- ln1_bias_grad: float32 [768], P('seq')
- w_qkv_grad: float32 [3, 768, 768], P(None, 'seq', 'mp')
- b_qv_grad: float32 [2, 12, 64], P(None, 'mp', 'seq')
- w_out_grad: float32 [768, 768], P('mp', 'seq')
- b_out_grad: float32 [768], P('seq')
- ln2_gain_grad: float32 [768], P('seq')
- ln2_bias_grad: float32 [768], P('seq')
- w_up_grad: float32 [768, 3072], P('seq', 'mp')
- b_up_grad: float32 [48, 64], P('mp', 'seq')
- w_down_grad: float32 [3072, 768], P('mp', 'seq')
- b_down_grad: float32 [768], P('seq')
The draws below stay inside these ranges and needn't reach their ends.
Inputs may be any that keep to these rules, and one draw needn't show every extreme that they name: The 128 positions of one old segment are distinct. Slots 0 to counts[i] - 1 of old segment i are used; some old segment uses all 128.
All inputs are finite; a program needn't handle non-finite values.
Results may differ from the reference program's by a relative error of at most 0.03.
Values may be sent and summed in bfloat16 or wider, within the bound.
A program may use at most 192 MiB of HBM per device.

```python
import math
import jax
import jax.numpy as jnp
from jax import lax

D = 768
HEADS = 12
DH = 64
FF = 3072
NB = 256
SEG = 512
S_MAX = 128
TOKENS = 16384
ITEMS = 16


def draw_positions(key, part):
    subkeys = jax.random.split(key, ITEMS)
    picked = jax.vmap(lambda subkey: jax.random.permutation(subkey, SEG)[:S_MAX])(subkeys)
    return picked.astype(jnp.int32)


def draw_counts(key, part):
    lengths = jax.random.randint(key, (ITEMS,), S_MAX // 8, S_MAX + 1)
    fullest = jax.random.randint(jax.random.fold_in(key, 7), (), 0, ITEMS)
    return lengths.at[fullest].set(S_MAX).astype(jnp.int32)


def draw_w_up(key, part):
    noise = jax.random.normal(key, (D, FF), jnp.float32)
    values = 0.05 + noise * D ** (-0.5)
    return jnp.clip(values, -0.25, 0.25).astype(jnp.bfloat16)


def shard_levels(rng, extent, shards, least, high):
    level, own = 1.0, jax.random.fold_in(rng, 6)
    for axis_at, shards_of in shards:
        heights = jnp.exp(jax.random.uniform(jax.random.fold_in(own, axis_at), (shards_of,), jnp.float32, least / len(shards), high / len(shards)))
        level = level * jnp.repeat(heights, extent[axis_at] // shards_of).reshape([-1 if axis == axis_at else 1 for axis in range(len(extent))])
    return level


def scatter_about(stream_key, shape, scale, bound, shards=(), held_as=jnp.bfloat16):
    factor_of = shard_levels(stream_key, shape, shards, -0.22, 0.18) if shards else 1.0
    values = jax.random.normal(stream_key, shape, jnp.float32) * scale * factor_of
    return jnp.minimum(jnp.maximum(values, -bound), bound).astype(held_as)


def setup_inputs(seed: int = 0) -> dict:
    key_of = jax.random.split(jax.random.key(seed), 18)
    tokens = scatter_about(key_of[0], (TOKENS, D), 1.0, 6.0, ((0, 8),))
    cotangent = scatter_about(key_of[1], (TOKENS, D), 1.0, 6.0, ((0, 8),))
    past_state = scatter_about(key_of[2], (ITEMS, SEG, D), 1.0, 6.0, ((0, 8), (2, 4)))
    positions = draw_positions(jax.random.fold_in(key_of[17], 71), 0)
    counts = draw_counts(jax.random.fold_in(key_of[17], 71), 0)
    ln1_gain = jnp.clip(1.0 + 0.1 * jax.random.normal(key_of[5], (D,), jnp.float32), 0.5, 1.5).astype(jnp.bfloat16)
    ln1_bias = scatter_about(key_of[6], (D,), 0.2, 1.0, ((0, 8),))
    w_qkv = scatter_about(key_of[7], (3, D, D), D ** -0.5, 0.21875, ((1, 8), (2, 4)))
    b_qv = scatter_about(key_of[8], (2, HEADS, DH), 0.3, 1.5, ((1, 4), (2, 8)))
    w_out = scatter_about(key_of[9], (D, D), 4 ** -0.5, 3.0, ((0, 4), (1, 8)))
    b_out = scatter_about(key_of[10], (D,), 0.3, 1.5, ((0, 8),))
    ln2_gain = jnp.clip(1.0 + 0.1 * jax.random.normal(key_of[11], (D,), jnp.float32), 0.5, 1.5).astype(jnp.bfloat16)
    ln2_bias = scatter_about(key_of[12], (D,), 0.2, 1.0, ((0, 8),))
    w_up = draw_w_up(jax.random.fold_in(key_of[17], 71), 0)
    b_up = scatter_about(key_of[14], (FF // DH, DH), 0.5, 2.5, ((0, 4), (1, 8)))
    w_down = scatter_about(key_of[15], (FF, D), FF ** -0.5, 0.109375, ((0, 4), (1, 8)))
    b_down = scatter_about(key_of[16], (D,), 0.3, 1.5, ((0, 8),))
    return {"tokens": tokens, "cotangent": cotangent, "past_state": past_state, "positions": positions, "counts": counts, "ln1_gain": ln1_gain, "ln1_bias": ln1_bias, "w_qkv": w_qkv, "b_qv": b_qv, "w_out": w_out, "b_out": b_out, "ln2_gain": ln2_gain, "ln2_bias": ln2_bias, "w_up": w_up, "b_up": b_up, "w_down": w_down, "b_down": b_down}


NORM_EPSILON = 1e-05
RIDGE_WEIGHT = 1.0
NARROW_WIDTH = 0.01
BROAD_WIDTH = 0.05
GELU_SCALE = 0.7978845608028654
GELU_CUBIC = 0.044715

@jax.custom_vjp
def low(v):
    return lax.optimization_barrier(v.astype(jnp.bfloat16)).astype(jnp.float32)

@jax.custom_vjp
def low_back(v):
    return v

def low_keep(v):
    return (low(v), None)

def low_pass(kept, grad):
    return (grad,)

def back_keep(v):
    return (v, None)

def back_low(kept, grad):
    return (low(grad),)
low.defvjp(low_keep, low_pass)
low_back.defvjp(back_keep, back_low)

def matmul(left, right):
    return jnp.dot(left, right, precision=lax.Precision.HIGHEST)

def norm_rows(values, gain, bias):
    centered = values - lax.optimization_barrier(jnp.mean(values, axis=-1, keepdims=True))
    inverse = lax.rsqrt(lax.optimization_barrier(jnp.mean(centered * centered, axis=-1, keepdims=True)) + NORM_EPSILON)
    return centered * inverse * gain + bias

def gelu_tanh(inputs):
    return 0.5 * inputs * (1.0 + jnp.tanh(GELU_SCALE * (inputs + GELU_CUBIC * inputs * inputs * inputs)))

def attend_group(queries, key_rows, values, memory_keys, memory_values):
    scaling = 1.0 / math.sqrt(queries.shape[-1])
    highest = lax.Precision.HIGHEST
    recall = jnp.einsum('glhe,nhe->ghln', queries, memory_keys, precision=highest) * scaling
    window = jnp.einsum('glhe,gmhe->ghlm', queries, key_rows, precision=highest) * scaling
    scores = low_back(jnp.concatenate([recall, window], axis=-1))
    length = queries.shape[1]
    slots = memory_keys.shape[0]
    causal = jnp.concatenate([jnp.ones((length, slots), dtype=bool), jnp.arange(length)[:, None] >= jnp.arange(length)[None, :]], axis=1)
    scores = jnp.where(causal, scores, -1e+30)
    probs = low(jax.nn.softmax(scores, axis=-1))
    output = jnp.einsum('ghln,nhe->glhe', probs[..., :slots], memory_values, precision=highest)
    return output + jnp.einsum('ghlm,gmhe->glhe', probs[..., slots:], values, precision=highest)

def forward(tokens, past_rows, gain_one, bias_one, w_qkv, b_qv, w_out, b_out, gain_two, bias_two, w_up, b_up, w_down, b_down, positions, counts):
    items, seg_len, width = past_rows.shape
    slots = positions.shape[1]
    places = (jnp.arange(items, dtype=jnp.float32)[:, None] + (positions.astype(jnp.float32) + 0.5) / seg_len) / items
    centers = (jnp.arange(NB, dtype=jnp.float32) + 0.5) / NB
    widths = jnp.where(jnp.arange(NB) % 2 == 0, NARROW_WIDTH, BROAD_WIDTH).astype(jnp.float32)
    slot_used = (jnp.arange(slots)[None, :] < counts[:, None]).astype(jnp.float32)
    basis_rows = jnp.exp(-0.5 * jnp.square((places[:, :, None] - centers) / widths)) * slot_used[:, :, None]
    basis_rows = basis_rows.reshape(items * slots, NB)
    sampled = jnp.take_along_axis(past_rows, positions[:, :, None], axis=1).reshape(items * slots, width)
    gram_mat = matmul(basis_rows.T, basis_rows) + RIDGE_WEIGHT * jnp.eye(NB, dtype=jnp.float32)
    coefficients = jnp.linalg.solve(gram_mat, matmul(basis_rows.T, sampled))
    memory = low(norm_rows(coefficients, gain_one, bias_one))
    head_count = b_qv.shape[1]
    head_size = b_qv.shape[2]
    bias_query = b_qv[0].reshape(-1)
    bias_value = b_qv[1].reshape(-1)
    memory_keys = low(matmul(memory, w_qkv[1])).reshape(NB, head_count, head_size)
    memory_values = low(matmul(memory, w_qkv[2]) + bias_value).reshape(NB, head_count, head_size)
    hidden_one = low(norm_rows(tokens, gain_one, bias_one))
    queries = low_back(low(matmul(hidden_one, w_qkv[0]) + bias_query))
    key_rows = low_back(low(matmul(hidden_one, w_qkv[1])))
    values = low_back(low(matmul(hidden_one, w_qkv[2]) + bias_value))
    token_count = tokens.shape[0]
    segments = token_count // SEG
    group = math.gcd(segments, 4)
    block_shape = (segments // group, group, SEG, head_count, head_size)
    checked = jax.checkpoint(attend_group)
    attended = lax.map(lambda blocks: checked(blocks[0], blocks[1], blocks[2], memory_keys, memory_values), (queries.reshape(block_shape), key_rows.reshape(block_shape), values.reshape(block_shape)))
    attended = low_back(low(attended.reshape(token_count, head_count * head_size)))
    residual = tokens + low_back(matmul(attended, w_out) + b_out)
    hidden_two = low(norm_rows(residual, gain_two, bias_two))
    pre_act = low_back(matmul(hidden_two, w_up) + b_up.reshape(-1))
    activation = low(gelu_tanh(pre_act))
    return residual + low_back(matmul(activation, w_down) + b_down)

def reference(tokens, cotangent, past_state, positions, counts, ln1_gain, ln1_bias, w_qkv, b_qv, w_out, b_out, ln2_gain, ln2_bias, w_up, b_up, w_down, b_down):
    floats = tuple((array.astype(jnp.float32) for array in (tokens, past_state, ln1_gain, ln1_bias, w_qkv, b_qv, w_out, b_out, ln2_gain, ln2_bias, w_up, b_up, w_down, b_down)))

    def mapping(*inputs):
        return forward(*inputs, positions, counts)
    result, pullback = jax.vjp(mapping, *floats)
    grads = pullback(cotangent.astype(jnp.float32))
    return (result.astype(jnp.bfloat16), grads[0].astype(jnp.bfloat16), grads[1], grads[2], grads[3], grads[4], grads[5], grads[6], grads[7], grads[8], grads[9], grads[10], grads[11], grads[12], grads[13])
```

```python
import functools
import math

import jax
import jax.numpy as jnp
from jax import lax
from jax.experimental import pallas as pl
from jax.experimental.pallas import tpu as pltpu
from jax.sharding import PartitionSpec as P

NB = 256
NORM_EPSILON = 1e-05
RIDGE_WEIGHT = 1.0
NARROW_WIDTH = 0.01
BROAD_WIDTH = 0.05
GELU_SCALE = 0.7978845608028654
GELU_CUBIC = 0.044715

BF = jnp.bfloat16
F32 = jnp.float32
HIGHEST = lax.Precision.HIGHEST
BIG_VMEM = 60 * 1024 * 1024


def dot(a, b):
    return jnp.dot(a, b, preferred_element_type=F32)


def dot_nt(a, b):
    return lax.dot_general(a, b, (((1,), (1,)), ((), ())), preferred_element_type=F32)


def dot_tn(a, b, precision=None):
    return lax.dot_general(
        a, b, (((0,), (0,)), ((), ())), preferred_element_type=F32, precision=precision
    )


def norm_parts(values):
    centered = values - jnp.mean(values, axis=-1, keepdims=True)
    inverse = lax.rsqrt(jnp.mean(centered * centered, axis=-1, keepdims=True) + NORM_EPSILON)
    return centered * inverse, inverse


def norm_back(upstream, normed, inverse, gain):
    scaled = upstream * gain
    inner = scaled - jnp.mean(scaled, axis=-1, keepdims=True)
    inner = inner - normed * jnp.mean(scaled * normed, axis=-1, keepdims=True)
    return inner * inverse


def col_sum(values):
    return jnp.sum(values, axis=0, keepdims=True)


def basis_of(places, used):
    column = lax.broadcasted_iota(jnp.int32, (places.shape[0], NB), 1)
    centers = (column.astype(F32) + 0.5) / NB
    widths = jnp.where(column % 2 == 0, NARROW_WIDTH, BROAD_WIDTH).astype(F32)
    scaled = (places - centers) / widths
    return jnp.exp(-0.5 * (scaled * scaled)) * used


def slot_parts(positions, counts, item, total, seg_len):
    places = (item + (positions.astype(F32) + 0.5) / seg_len) / total
    slot = lax.broadcasted_iota(jnp.int32, positions.shape, 0)
    return places, (slot < counts).astype(F32)


def sample_kernel(past_ref, pos_ref, out_ref):
    slots = pos_ref.shape[1]
    seg_len = past_ref.shape[1]
    at = lax.broadcasted_iota(jnp.int32, (slots, seg_len), 1)
    pick = (at == pos_ref[0]).astype(F32).astype(BF)
    out_ref[0] = dot(pick, past_ref[0]).astype(BF)


def sample_rows(past, pos):
    items, seg_len, width = past.shape
    slots = pos.shape[1]
    return pl.pallas_call(
        sample_kernel,
        grid=(items,),
        in_specs=[
            pl.BlockSpec((1, seg_len, width), lambda i: (i, 0, 0)),
            pl.BlockSpec((1, slots, 1), lambda i: (i, 0, 0)),
        ],
        out_specs=pl.BlockSpec((1, slots, width), lambda i: (i, 0, 0)),
        out_shape=jax.ShapeDtypeStruct((items, slots, width), BF),
        name="sample_rows",
    )(past, pos)


def invert_in_place(mat_ref):
    block = 32
    row = lax.broadcasted_iota(jnp.int32, (NB, NB), 0)
    col = lax.broadcasted_iota(jnp.int32, (NB, NB), 1)
    lane = lax.broadcasted_iota(jnp.int32, (block, NB), 1)
    line = lax.broadcasted_iota(jnp.int32, (block, NB), 0)

    def step(_, carry):
        panel = mat_ref[0:block, :]
        for k in range(block):
            pivot_row = panel[k : k + 1, :]
            factor = 1.0 / pivot_row[:, k : k + 1]
            here = lane[0:1] == k
            scaled = jnp.where(here, factor, pivot_row * factor)
            column = panel[:, k : k + 1]
            rest = jnp.where(lane == k, 0.0, panel) - column * scaled
            panel = jnp.where(line == k, scaled, rest)
        mat_ref[0:block, :] = panel
        mat = mat_ref[...]
        inside_row = row < block
        inside_col = col < block
        left = jnp.where(inside_col & ~inside_row, mat, 0.0)
        right = jnp.where(inside_row, mat, 0.0)
        update = jnp.dot(left, right, preferred_element_type=F32, precision=HIGHEST)
        mat = jnp.where(inside_row, mat, jnp.where(inside_col, 0.0, mat) - update)
        mat = pltpu.roll(mat, NB - block, 1)
        mat_ref[0 : NB - block, :] = mat[block:, :]
        mat_ref[NB - block :, :] = mat[:block, :]
        return carry

    lax.fori_loop(0, NB // block, step, 0)


def solve_kernel(sampled_ref, pos_ref, count_ref, coef_ref, inv_ref, mat_ref, mom_ref, *, seg_len):
    total = pos_ref.shape[0]
    slots = pos_ref.shape[1]
    mat_ref[...] = jnp.zeros_like(mat_ref)
    mom_ref[...] = jnp.zeros_like(mom_ref)

    def item(i, carry):
        places, used = slot_parts(pos_ref[i], count_ref[i], i.astype(F32), total, seg_len)
        rows = basis_of(places, used)
        mat_ref[...] += dot_tn(rows, rows, HIGHEST)
        mom_ref[...] += dot_tn(rows, sampled_ref[i].astype(F32), HIGHEST)
        return carry

    lax.fori_loop(0, total, item, 0)
    row = lax.broadcasted_iota(jnp.int32, (NB, NB), 0)
    col = lax.broadcasted_iota(jnp.int32, (NB, NB), 1)
    mat_ref[...] += jnp.where(row == col, RIDGE_WEIGHT, 0.0)
    invert_in_place(mat_ref)
    inverse = mat_ref[...]
    inv_ref[...] = inverse
    coef_ref[...] = jnp.dot(
        inverse, mom_ref[...], preferred_element_type=F32, precision=HIGHEST
    ).astype(BF)


def solve_memory(sampled, pos, counts, seg_len):
    width = sampled.shape[-1]
    return pl.pallas_call(
        functools.partial(solve_kernel, seg_len=seg_len),
        out_shape=(
            jax.ShapeDtypeStruct((NB, width), BF),
            jax.ShapeDtypeStruct((NB, NB), F32),
        ),
        scratch_shapes=[pltpu.VMEM((NB, NB), F32), pltpu.VMEM((NB, width), F32)],
        compiler_params=pltpu.CompilerParams(vmem_limit_bytes=BIG_VMEM),
        name="solve_memory",
    )(sampled, pos, counts)


def past_kernel(
    gmem_ref, coef_ref, vec_ref, inv_ref, pos_ref, count_ref, out_ref, gv_ref, *, total
):
    item_count, slots = pos_ref.shape[0], pos_ref.shape[1]
    seg_len, width = out_ref.shape[1], out_ref.shape[2]
    normed, inverse = norm_parts(coef_ref[...].astype(F32))
    gmem = gmem_ref[...]
    gain = vec_ref[0:1, :]
    coef_grad = norm_back(gmem, normed, inverse, gain)
    gv_ref[...] = jnp.zeros_like(gv_ref)
    gv_ref[0:1, :] = col_sum(gmem * normed)
    gv_ref[1:2, :] = col_sum(gmem)
    features = coef_grad.shape[1]
    part = lax.axis_index("mp")
    row = lax.broadcasted_iota(jnp.int32, (features, width), 0)
    col = lax.broadcasted_iota(jnp.int32, (features, width), 1)
    pick = (row == col + part * width).astype(F32)
    mine = jnp.dot(coef_grad, pick, preferred_element_type=F32, precision=HIGHEST)
    moment = jnp.dot(inv_ref[...], mine, preferred_element_type=F32, precision=HIGHEST)
    first = (lax.axis_index("seq") * item_count).astype(F32)
    at = lax.broadcasted_iota(jnp.int32, (slots, seg_len), 1)
    for i in range(item_count):
        places, used = slot_parts(pos_ref[i], count_ref[i], first + i, total, seg_len)
        rows = basis_of(places, used)
        sampled = jnp.dot(rows, moment, preferred_element_type=F32, precision=HIGHEST)
        spread = (at == pos_ref[i]).astype(F32)
        out_ref[i] = dot_tn(spread, sampled, HIGHEST)


def past_grads(gmem, coef, vec, inv, pos, counts, total, seg_len, width):
    return pl.pallas_call(
        functools.partial(past_kernel, total=total),
        out_shape=(
            jax.ShapeDtypeStruct((pos.shape[0], seg_len, width), F32),
            jax.ShapeDtypeStruct((8, coef.shape[1]), F32),
        ),
        compiler_params=pltpu.CompilerParams(vmem_limit_bytes=BIG_VMEM),
        name="past_grads",
    )(gmem, coef, vec, inv, pos, counts)


def forward_kernel(
    tok_ref,
    coef_ref,
    vec_ref,
    gvec_ref,
    wa_ref,
    wu_ref,
    wd_ref,
    out_ref,
    res_ref,
    hm_ref,
    h2_ref,
    prob_ref,
    key_ref,
    val_ref,
    query_ref,
    att_ref,
    act_ref,
    slope_ref,
    acc_ref,
    *,
    groups,
    head,
):
    step = pl.program_id(0)
    rows, width = tok_ref.shape
    local = query_ref.shape[2]
    half = rows // 2

    @pl.when(step == 0)
    def _():
        gain, bias = vec_ref[0:1, :], vec_ref[1:2, :]
        normed, _ = norm_parts(coef_ref[...].astype(F32))
        hm_ref[0:NB, :] = (normed * gain + bias).astype(BF)
        normed, _ = norm_parts(tok_ref[...].astype(F32))
        hm_ref[NB:, :] = (normed * gain + bias).astype(BF)
        acc_ref[...] = jnp.zeros_like(acc_ref)

    @pl.when(step < groups)
    def _():
        weights = wa_ref[0, 0]
        projected = dot(hm_ref[...], weights[:, : 3 * local]) + gvec_ref[0, 0:1, : 3 * local]
        query = projected[NB:, :local].astype(BF)
        keys = projected[:, local : 2 * local].astype(BF)
        values = projected[:, 2 * local :].astype(BF)
        query_ref[0] = query
        key_ref[0] = keys
        val_ref[0] = values
        query_t = query.T * BF(1.0 / math.sqrt(head))
        value_t = values.T
        line = lax.broadcasted_iota(jnp.int32, (local, rows), 0)
        for h in range(local // head):
            own = (line >= h * head) & (line < (h + 1) * head)
            masked = jnp.where(own, query_t, BF(0.0))
            value_h = value_t[h * head : (h + 1) * head, :]
            for b in range(2):
                span = NB + (b + 1) * half
                scores = dot(keys[:span, :], masked[:, b * half : (b + 1) * half])
                key_at = lax.broadcasted_iota(jnp.int32, (half, half), 0)
                row_at = lax.broadcasted_iota(jnp.int32, (half, half), 1)
                edge = jnp.where(key_at <= row_at, scores[span - half :, :], -1e30)
                scores = jnp.concatenate([scores[: span - half, :], edge], axis=0)
                scores = jnp.exp(scores - jnp.max(scores, axis=0, keepdims=True))
                probs = (scores * (1.0 / jnp.sum(scores, axis=0, keepdims=True))).astype(BF)
                prob_ref[0, h, 0:span, b * half : (b + 1) * half] = probs
                att_ref[0, h * head : (h + 1) * head, b * half : (b + 1) * half] = dot(
                    value_h[:, :span], probs
                ).astype(BF)
        attended = att_ref[0].T
        acc_ref[...] += dot_nt(attended, weights[:, 3 * local :])

    @pl.when(step == groups)
    def _():
        residual = tok_ref[...].astype(F32) + acc_ref[...] + vec_ref[4:5, :]
        res_ref[...] = residual
        normed, _ = norm_parts(residual)
        h2_ref[...] = (normed * vec_ref[2:3, :] + vec_ref[3:4, :]).astype(BF)
        acc_ref[...] = jnp.zeros_like(acc_ref)

    @pl.when(step >= groups)
    def _():
        pre = dot(h2_ref[...], wu_ref[0, 0]) + gvec_ref[0, 1:2, :]
        square = pre * pre
        inner = jnp.tanh(GELU_SCALE * (pre + GELU_CUBIC * pre * square))
        half_up = 0.5 * (1.0 + inner)
        act = (pre * half_up).astype(BF)
        act_ref[0] = act
        slope = GELU_SCALE * (1.0 + 3.0 * GELU_CUBIC * square)
        slope_ref[0] = (half_up + 0.5 * pre * (1.0 - inner * inner) * slope).astype(BF)
        acc_ref[...] += dot_nt(act, wd_ref[0, 0])

    @pl.when(step == 2 * groups - 1)
    def _():
        out_ref[...] = (res_ref[...] + acc_ref[...] + vec_ref[5:6, :]).astype(BF)


def forward_pass(tok, coef, vec, gvec, wide, head):
    rows, width = tok.shape
    groups = wide.shape[0]
    local = width // groups
    hidden = wide.shape[3]
    heads = local // head
    keyed = NB + rows
    first = lambda i: jnp.minimum(i, groups - 1)
    second = lambda i: jnp.maximum(i - groups, 0)
    whole = lambda shape: pl.BlockSpec(shape, lambda i: (0,) * len(shape))
    return pl.pallas_call(
        functools.partial(forward_kernel, groups=groups, head=head),
        grid=(2 * groups,),
        in_specs=[
            whole((rows, width)),
            whole((NB, width)),
            whole((8, width)),
            pl.BlockSpec((1, 8, width), lambda i: (i % groups, 0, 0)),
            pl.BlockSpec((1, 1, width, width), lambda i: (first(i), 0, 0, 0)),
            pl.BlockSpec((1, 1, width, hidden), lambda i: (second(i), 1, 0, 0)),
            pl.BlockSpec((1, 1, width, hidden), lambda i: (second(i), 2, 0, 0)),
        ],
        out_specs=[
            whole((rows, width)),
            whole((rows, width)),
            whole((keyed, width)),
            whole((rows, width)),
            pl.BlockSpec((1, heads, keyed, rows), lambda i: (first(i), 0, 0, 0)),
            pl.BlockSpec((1, keyed, local), lambda i: (first(i), 0, 0)),
            pl.BlockSpec((1, keyed, local), lambda i: (first(i), 0, 0)),
            pl.BlockSpec((1, rows, local), lambda i: (first(i), 0, 0)),
            pl.BlockSpec((1, local, rows), lambda i: (first(i), 0, 0)),
            pl.BlockSpec((1, rows, hidden), lambda i: (second(i), 0, 0)),
            pl.BlockSpec((1, rows, hidden), lambda i: (second(i), 0, 0)),
        ],
        out_shape=[
            jax.ShapeDtypeStruct((rows, width), BF),
            jax.ShapeDtypeStruct((rows, width), F32),
            jax.ShapeDtypeStruct((keyed, width), BF),
            jax.ShapeDtypeStruct((rows, width), BF),
            jax.ShapeDtypeStruct((groups, heads, keyed, rows), BF),
            jax.ShapeDtypeStruct((groups, keyed, local), BF),
            jax.ShapeDtypeStruct((groups, keyed, local), BF),
            jax.ShapeDtypeStruct((groups, rows, local), BF),
            jax.ShapeDtypeStruct((groups, local, rows), BF),
            jax.ShapeDtypeStruct((groups, rows, hidden), BF),
            jax.ShapeDtypeStruct((groups, rows, hidden), BF),
        ],
        scratch_shapes=[pltpu.VMEM((rows, width), F32)],
        compiler_params=pltpu.CompilerParams(vmem_limit_bytes=BIG_VMEM),
        name="forward_pass",
    )(tok, coef, vec, gvec, wide, wide, wide)


def backward_kernel(
    tok_ref,
    cot_ref,
    res_ref,
    vec_ref,
    hm_ref,
    h2_ref,
    prob_ref,
    key_ref,
    val_ref,
    query_ref,
    att_ref,
    act_ref,
    slope_ref,
    wa_ref,
    wu_ref,
    wd_ref,
    tg_ref,
    gmem_ref,
    gmlp_ref,
    gatt_ref,
    gv_ref,
    ggv_ref,
    acc_ref,
    hmt_ref,
    h2t_ref,
    cott_ref,
    gres_ref,
    proj_ref,
    *,
    groups,
    head,
):
    step = pl.program_id(0)
    rows, width = tok_ref.shape
    local = query_ref.shape[2]
    half = rows // 2

    @pl.when(step == 0)
    def _():
        acc_ref[...] = jnp.zeros_like(acc_ref)
        h2t_ref[...] = h2_ref[...].T
        cott_ref[...] = cot_ref[...].T
        gv_ref[...] = jnp.zeros_like(gv_ref)

    @pl.when(step < groups)
    def _():
        upstream = cot_ref[...]
        grad = (dot(upstream, wd_ref[0, 0]) * slope_ref[0].astype(F32)).astype(BF)
        gmlp_ref[0, 1] = dot(cott_ref[...], act_ref[0]).astype(BF)
        gmlp_ref[0, 0] = dot(h2t_ref[...], grad).astype(BF)
        ggv_ref[0] = jnp.zeros_like(ggv_ref[0])
        ggv_ref[0, 0:1, :] = col_sum(grad.astype(F32))
        acc_ref[NB:, :] += dot_nt(grad, wu_ref[0, 0])

    @pl.when(step == groups)
    def _():
        upstream = cot_ref[...].astype(F32)
        normed, inverse = norm_parts(res_ref[...])
        grad = acc_ref[NB:, :]
        g_res = upstream + norm_back(grad, normed, inverse, vec_ref[2:3, :])
        gres_ref[...] = g_res
        g_attn = g_res.astype(BF)
        gv_ref[2:3, :] = col_sum(grad * normed)
        gv_ref[3:4, :] = col_sum(grad)
        gv_ref[4:5, :] = col_sum(g_attn.astype(F32))
        gv_ref[5:6, :] = col_sum(upstream)
        cott_ref[...] = g_attn.T
        h2t_ref[...] = h2t_ref[...]
        hmt_ref[...] = hm_ref[...].T
        acc_ref[...] = jnp.zeros_like(acc_ref)
        proj_ref[0:NB, :] = jnp.zeros((NB, proj_ref.shape[1]), BF)

    @pl.when(step >= groups)
    def _():
        weights = wa_ref[0, 0]
        g_attn = gres_ref[...].astype(BF)
        g_att = dot(g_attn, weights[:, 3 * local :]).astype(BF)
        g_att_t = g_att.T
        att_t = att_ref[0]
        product = g_att_t.astype(F32) * att_t.astype(F32)
        keys, values, query = key_ref[0], val_ref[0], query_ref[0]
        key_t = keys.T
        scale = 1.0 / math.sqrt(head)
        line = lax.broadcasted_iota(jnp.int32, (local, rows), 0)
        lane = lax.broadcasted_iota(jnp.int32, (rows, local), 1)
        key_grad = [jnp.zeros((NB + rows - half, local), F32), jnp.zeros((half, local), F32)]
        val_grad = [jnp.zeros((NB + rows - half, local), F32), jnp.zeros((half, local), F32)]
        query_grads = []
        for h in range(local // head):
            own_t = (line >= h * head) & (line < (h + 1) * head)
            own = (lane >= h * head) & (lane < (h + 1) * head)
            grad_t = jnp.where(own_t, g_att_t, BF(0.0))
            grad_h = jnp.where(own, g_att, BF(0.0))
            query_h = jnp.where(own, query, BF(0.0))
            inner = jnp.sum(product[h * head : (h + 1) * head, :], axis=0, keepdims=True)
            key_h = key_t[h * head : (h + 1) * head, :]
            parts = []
            for b in range(2):
                span = NB + (b + 1) * half
                cols = slice(b * half, (b + 1) * half)
                probs = prob_ref[0, h, 0:span, cols]
                dprob = dot(values[:span, :], grad_t[:, cols])
                dscore = (probs.astype(F32) * (dprob - inner[:, cols])).astype(BF)
                parts.append(dot(key_h[:, :span], dscore))
                val_part = dot(probs, grad_h[cols, :])
                key_part = dot(dscore, query_h[cols, :])
                low = NB + rows - half
                val_grad[0] = val_grad[0] + val_part[:low, :]
                key_grad[0] = key_grad[0] + key_part[:low, :]
                if b == 1:
                    val_grad[1] = val_grad[1] + val_part[low:, :]
                    key_grad[1] = key_grad[1] + key_part[low:, :]
            query_grads.append(jnp.concatenate(parts, axis=1))
        query_grad = (jnp.concatenate(query_grads, axis=0) * scale).astype(BF).T
        key_grad = (jnp.concatenate(key_grad, axis=0) * scale).astype(BF)
        val_sum = jnp.concatenate(val_grad, axis=0)
        val_grad = val_sum.astype(BF)
        proj_ref[NB:, 0:local] = query_grad
        proj_ref[:, local : 2 * local] = key_grad
        proj_ref[:, 2 * local :] = val_grad
        proj = proj_ref[...]
        ggv_ref[0] = jnp.zeros_like(ggv_ref[0])
        ggv_ref[0, 0:1, 0 : 3 * local] = col_sum(proj.astype(F32))
        gatt_ref[0, :, 0 : 3 * local] = dot(hmt_ref[...], proj).astype(BF)
        gatt_ref[0, :, 3 * local :] = dot_nt(cott_ref[...], att_t).astype(BF)
        acc_ref[...] += dot_nt(proj, weights[:, : 3 * local])

    @pl.when(step == 2 * groups - 1)
    def _():
        gmem_ref[...] = acc_ref[0:NB, :]
        grad = acc_ref[NB:, :]
        normed, inverse = norm_parts(tok_ref[...].astype(F32))
        part = norm_back(grad, normed, inverse, vec_ref[0:1, :])
        tg_ref[...] = (gres_ref[...] + part).astype(BF)
        gv_ref[0:1, :] = col_sum(grad * normed)
        gv_ref[1:2, :] = col_sum(grad)


def backward_pass(tok, cot, vec, saved, wide, head):
    res, hm, h2, prob, keys, vals, query, att, act, slope = saved
    rows, width = tok.shape
    groups = wide.shape[0]
    local = width // groups
    hidden = wide.shape[3]
    heads = local // head
    keyed = NB + rows
    first = lambda i: jnp.minimum(i, groups - 1)
    second = lambda i: jnp.maximum(i - groups, 0)
    whole = lambda shape: pl.BlockSpec(shape, lambda i: (0,) * len(shape))
    return pl.pallas_call(
        functools.partial(backward_kernel, groups=groups, head=head),
        grid=(2 * groups,),
        in_specs=[
            whole((rows, width)),
            whole((rows, width)),
            whole((rows, width)),
            whole((8, width)),
            whole((keyed, width)),
            whole((rows, width)),
            pl.BlockSpec((1, heads, keyed, rows), lambda i: (second(i), 0, 0, 0)),
            pl.BlockSpec((1, keyed, local), lambda i: (second(i), 0, 0)),
            pl.BlockSpec((1, keyed, local), lambda i: (second(i), 0, 0)),
            pl.BlockSpec((1, rows, local), lambda i: (second(i), 0, 0)),
            pl.BlockSpec((1, local, rows), lambda i: (second(i), 0, 0)),
            pl.BlockSpec((1, rows, hidden), lambda i: (first(i), 0, 0)),
            pl.BlockSpec((1, rows, hidden), lambda i: (first(i), 0, 0)),
            pl.BlockSpec((1, 1, width, width), lambda i: (second(i), 0, 0, 0)),
            pl.BlockSpec((1, 1, width, hidden), lambda i: (first(i), 1, 0, 0)),
            pl.BlockSpec((1, 1, width, hidden), lambda i: (first(i), 2, 0, 0)),
        ],
        out_specs=[
            whole((rows, width)),
            whole((NB, width)),
            pl.BlockSpec((1, 2, width, hidden), lambda i: (first(i), 0, 0, 0)),
            pl.BlockSpec((1, width, width), lambda i: (second(i), 0, 0)),
            whole((8, width)),
            pl.BlockSpec((1, 8, hidden), lambda i: (i, 0, 0)),
        ],
        out_shape=[
            jax.ShapeDtypeStruct((rows, width), BF),
            jax.ShapeDtypeStruct((NB, width), F32),
            jax.ShapeDtypeStruct((groups, 2, width, hidden), BF),
            jax.ShapeDtypeStruct((groups, width, width), BF),
            jax.ShapeDtypeStruct((8, width), F32),
            jax.ShapeDtypeStruct((2 * groups, 8, hidden), F32),
        ],
        scratch_shapes=[
            pltpu.VMEM((keyed, width), F32),
            pltpu.VMEM((width, keyed), BF),
            pltpu.VMEM((width, rows), BF),
            pltpu.VMEM((width, rows), BF),
            pltpu.VMEM((rows, width), F32),
            pltpu.VMEM((keyed, 3 * local), BF),
        ],
        compiler_params=pltpu.CompilerParams(vmem_limit_bytes=BIG_VMEM),
        name="backward_pass",
    )(
        tok, cot, res, vec, hm, h2, prob, keys, vals, query, att, act, slope, wide, wide, wide
    )


def local(
    tokens,
    cotangent,
    past_state,
    positions,
    counts,
    ln1_gain,
    ln1_bias,
    w_qkv,
    b_qv,
    w_out,
    b_out,
    ln2_gain,
    ln2_bias,
    w_up,
    b_up,
    w_down,
    b_down,
):
    seq, mp = lax.axis_size("seq"), lax.axis_size("mp")
    mp_index = lax.axis_index("mp")
    both = ("seq", "mp")
    item_count, seg_len, local_width = past_state.shape
    slots = positions.shape[1]
    total = item_count * seq
    width = tokens.shape[1]
    part = width // seq
    heads_local = b_qv.shape[1]
    piece = b_qv.shape[2]
    head = piece * seq
    hidden = w_up.shape[1]
    rows = tokens.shape[0] // mp

    pos3 = positions.reshape(item_count, slots, 1)
    counts3 = counts.reshape(item_count, 1, 1)
    sampled = sample_rows(past_state, pos3)
    all_sampled = lax.all_gather(sampled, "seq", axis=0, tiled=True)
    all_pos = lax.all_gather(positions, "seq", axis=0, tiled=True).reshape(total, slots, 1)
    all_counts = lax.all_gather(counts, "seq", axis=0, tiled=True).reshape(total, 1, 1)
    coef_part, inverse = solve_memory(all_sampled, all_pos, all_counts, seg_len)
    coef = lax.all_gather(coef_part, "mp", axis=1, tiled=True)

    shard = jnp.stack(
        [jnp.concatenate([w_qkv[0], w_qkv[1], w_qkv[2], w_out.T], axis=1), w_up, w_down.T]
    )
    wide = lax.all_gather(lax.all_gather(shard, "seq", axis=1, tiled=True), "mp", axis=0)
    small = jnp.concatenate(
        [ln1_gain, ln1_bias, ln2_gain, ln2_bias, b_out, b_down, b_qv.reshape(-1), b_up.reshape(-1)]
    )
    small = lax.all_gather(lax.all_gather(small, "seq", axis=0), "mp", axis=0)
    vec = small[0, :, : 6 * part].reshape(seq, 6, part).transpose(1, 0, 2).reshape(6, width)
    vec = jnp.concatenate([vec, jnp.zeros((2, width), BF)]).astype(F32)
    at = 6 * part
    size = 2 * heads_local * piece
    bias_qv = small[:, :, at : at + size].reshape(mp, seq, 2, heads_local, piece)
    bias_qv = bias_qv.transpose(0, 2, 3, 1, 4).reshape(mp, 2, local_width)
    bias_up = small[:, :, at + size :].reshape(mp, seq, -1, piece)
    bias_up = bias_up.transpose(0, 2, 1, 3).reshape(mp, hidden)
    zero = jnp.zeros((mp, local_width), BF)
    first = jnp.concatenate([bias_qv[:, 0], zero, bias_qv[:, 1], zero], axis=1)
    gvec = jnp.concatenate(
        [first[:, None], bias_up[:, None], jnp.zeros((mp, 6, width), BF)], axis=1
    ).astype(F32)

    tok = lax.dynamic_slice_in_dim(tokens, mp_index * rows, rows, 0)
    cot = lax.dynamic_slice_in_dim(cotangent, mp_index * rows, rows, 0)
    forward = forward_pass(tok, coef, vec, gvec, wide, head)
    block_out = lax.all_gather(forward[0], "mp", axis=0, tiled=True)
    tok_grad, gmem, g_mlp, g_att, gv, ggv = backward_pass(tok, cot, vec, forward[1:], wide, head)
    block_grad = lax.all_gather(tok_grad, "mp", axis=0, tiled=True)

    gmem, gv, ggv = lax.psum((gmem, gv, ggv), both)
    past_grad, gv_mem = past_grads(
        gmem, coef, vec, inverse, pos3, counts3, total, seg_len, local_width
    )
    gv = gv + gv_mem

    grads = jnp.concatenate([g_att[:, None], g_mlp], axis=1)
    grads = lax.psum_scatter(grads, "mp", scatter_dimension=0, tiled=False)
    grads = lax.psum_scatter(grads, "seq", scatter_dimension=1, tiled=True).astype(F32)
    attn = grads[0]
    qkv_grad = jnp.stack([attn[:, i * local_width : (i + 1) * local_width] for i in range(3)])
    out_grad = attn[:, 3 * local_width :].T
    seq_index = lax.axis_index("seq")
    vec_own = lax.dynamic_slice_in_dim(gv, seq_index * part, part, 1)
    qv = lax.dynamic_slice_in_dim(ggv, mp + mp_index, 1, 0)[0, 0]
    qv = jnp.stack([qv[:local_width], qv[2 * local_width : 3 * local_width]])
    qv = qv.reshape(2, heads_local, head)
    qv = lax.dynamic_slice_in_dim(qv, seq_index * piece, piece, 2)
    up = lax.dynamic_slice_in_dim(ggv, mp_index, 1, 0)[0, 0].reshape(-1, head)
    up = lax.dynamic_slice_in_dim(up, seq_index * piece, piece, 1)
    return (
        block_out,
        block_grad,
        past_grad,
        vec_own[0],
        vec_own[1],
        qkv_grad,
        qv,
        out_grad,
        vec_own[4],
        vec_own[2],
        vec_own[3],
        grads[1],
        up,
        grads[2].T,
        vec_own[5],
    )


def solution(mesh):
    row = P("seq", None)
    placed = (
        row,
        row,
        P("seq", None, "mp"),
        row,
        P("seq"),
        P("seq"),
        P("seq"),
        P(None, "seq", "mp"),
        P(None, "mp", "seq"),
        P("mp", "seq"),
        P("seq"),
        P("seq"),
        P("seq"),
        P("seq", "mp"),
        P("mp", "seq"),
        P("mp", "seq"),
        P("seq"),
    )
    return jax.shard_map(
        local,
        mesh=mesh,
        in_specs=placed,
        out_specs=(row, row, placed[2]) + placed[5:],
        check_vma=False,
    )
```

```python
import functools
import math

import jax
import jax.numpy as jnp
from jax import lax
from jax.experimental import pallas as pl
from jax.experimental.pallas import tpu as pltpu
from jax.sharding import PartitionSpec as P

NB = 256
NORM_EPSILON = 1e-05
RIDGE_WEIGHT = 1.0
NARROW_WIDTH = 0.01
BROAD_WIDTH = 0.05
GELU_SCALE = 0.7978845608028654
GELU_CUBIC = 0.044715

BF = jnp.bfloat16
F32 = jnp.float32
HIGHEST = lax.Precision.HIGHEST
BIG_VMEM = 60 * 1024 * 1024


def dot(a, b):
    return jnp.dot(a, b, preferred_element_type=F32)


def dot_nt(a, b):
    return lax.dot_general(a, b, (((1,), (1,)), ((), ())), preferred_element_type=F32)


def dot_tn(a, b, precision=None):
    return lax.dot_general(
        a, b, (((0,), (0,)), ((), ())), preferred_element_type=F32, precision=precision
    )


def norm_parts(values):
    centered = values - jnp.mean(values, axis=-1, keepdims=True)
    inverse = lax.rsqrt(jnp.mean(centered * centered, axis=-1, keepdims=True) + NORM_EPSILON)
    return centered * inverse, inverse


def norm_back(upstream, normed, inverse, gain):
    scaled = upstream * gain
    inner = scaled - jnp.mean(scaled, axis=-1, keepdims=True)
    inner = inner - normed * jnp.mean(scaled * normed, axis=-1, keepdims=True)
    return inner * inverse


def col_sum(values):
    return jnp.sum(values, axis=0, keepdims=True)


def basis_of(places, used):
    column = lax.broadcasted_iota(jnp.int32, (places.shape[0], NB), 1)
    centers = (column.astype(F32) + 0.5) / NB
    widths = jnp.where(column % 2 == 0, NARROW_WIDTH, BROAD_WIDTH).astype(F32)
    scaled = (places - centers) / widths
    return jnp.exp(-0.5 * (scaled * scaled)) * used


def sample_kernel(past_ref, pos_ref, out_ref):
    slots = pos_ref.shape[1]
    seg_len = past_ref.shape[1]
    at = lax.broadcasted_iota(jnp.int32, (slots, seg_len), 1)
    pick = (at == pos_ref[0]).astype(F32).astype(BF)
    out_ref[0] = dot(pick, past_ref[0]).astype(BF)


def sample_rows(past, pos):
    items, seg_len, width = past.shape
    slots = pos.shape[1]
    return pl.pallas_call(
        sample_kernel,
        grid=(items,),
        in_specs=[
            pl.BlockSpec((1, seg_len, width), lambda i: (i, 0, 0)),
            pl.BlockSpec((1, slots, 1), lambda i: (i, 0, 0)),
        ],
        out_specs=pl.BlockSpec((1, slots, width), lambda i: (i, 0, 0)),
        out_shape=jax.ShapeDtypeStruct((items, slots, width), BF),
        name="sample_rows",
    )(past, pos)


def invert_in_place(mat_ref):
    block = 32
    row = lax.broadcasted_iota(jnp.int32, (NB, NB), 0)
    col = lax.broadcasted_iota(jnp.int32, (NB, NB), 1)
    lane = lax.broadcasted_iota(jnp.int32, (block, NB), 1)
    line = lax.broadcasted_iota(jnp.int32, (block, NB), 0)

    def step(_, carry):
        panel = mat_ref[0:block, :]
        for k in range(block):
            pivot_row = panel[k : k + 1, :]
            factor = 1.0 / pivot_row[:, k : k + 1]
            here = lane[0:1] == k
            scaled = jnp.where(here, factor, pivot_row * factor)
            column = panel[:, k : k + 1]
            rest = jnp.where(lane == k, 0.0, panel) - column * scaled
            panel = jnp.where(line == k, scaled, rest)
        mat_ref[0:block, :] = panel
        mat = mat_ref[...]
        inside_row = row < block
        inside_col = col < block
        left = jnp.where(inside_col & ~inside_row, mat, 0.0)
        right = jnp.where(inside_row, mat, 0.0)
        update = jnp.dot(left, right, preferred_element_type=F32, precision=HIGHEST)
        mat = jnp.where(inside_row, mat, jnp.where(inside_col, 0.0, mat) - update)
        mat = pltpu.roll(mat, NB - block, 1)
        mat_ref[0 : NB - block, :] = mat[block:, :]
        mat_ref[NB - block :, :] = mat[:block, :]
        return carry

    lax.fori_loop(0, NB // block, step, 0)


def solve_kernel(sampled_ref, meta_ref, coef_ref, inv_ref, mat_ref, mom_ref, *, items):
    slots = meta_ref.shape[2]
    mat_ref[...] = jnp.zeros_like(mat_ref)
    mom_ref[...] = jnp.zeros_like(mom_ref)

    def owner(s, carry):
        column = meta_ref[s].T
        for i in range(items):
            rows = basis_of(column[:, i : i + 1], column[:, items + i : items + i + 1])
            mat_ref[...] += dot_tn(rows, rows, HIGHEST)
            sampled = sampled_ref[s, i * slots : (i + 1) * slots, :]
            mom_ref[...] += dot_tn(rows, sampled.astype(F32), HIGHEST)
        return carry

    lax.fori_loop(0, meta_ref.shape[0], owner, 0)
    row = lax.broadcasted_iota(jnp.int32, (NB, NB), 0)
    col = lax.broadcasted_iota(jnp.int32, (NB, NB), 1)
    mat_ref[...] += jnp.where(row == col, RIDGE_WEIGHT, 0.0)
    invert_in_place(mat_ref)
    inverse = mat_ref[...]
    inv_ref[...] = inverse
    coef_ref[...] = jnp.dot(
        inverse, mom_ref[...], preferred_element_type=F32, precision=HIGHEST
    ).astype(BF)


def solve_memory(sampled, meta, items):
    width = sampled.shape[-1]
    return pl.pallas_call(
        functools.partial(solve_kernel, items=items),
        out_shape=(
            jax.ShapeDtypeStruct((NB, width), BF),
            jax.ShapeDtypeStruct((NB, NB), F32),
        ),
        scratch_shapes=[pltpu.VMEM((NB, NB), F32), pltpu.VMEM((NB, width), F32)],
        compiler_params=pltpu.CompilerParams(vmem_limit_bytes=BIG_VMEM),
        name="solve_memory",
    )(sampled, meta)


def past_kernel(gmem_ref, coef_ref, vec_ref, inv_ref, meta_ref, pos_ref, out_ref, gv_ref):
    item_count, slots = pos_ref.shape[0], pos_ref.shape[1]
    seg_len, width = out_ref.shape[1], out_ref.shape[2]
    normed, inverse = norm_parts(coef_ref[...].astype(F32))
    gmem = gmem_ref[...]
    coef_grad = norm_back(gmem, normed, inverse, vec_ref[0:1, :])
    gv_ref[...] = jnp.zeros_like(gv_ref)
    gv_ref[0:1, :] = col_sum(gmem * normed)
    gv_ref[1:2, :] = col_sum(gmem)
    features = coef_grad.shape[1]
    part = lax.axis_index("mp")
    row = lax.broadcasted_iota(jnp.int32, (features, width), 0)
    col = lax.broadcasted_iota(jnp.int32, (features, width), 1)
    pick = (row == col + part * width).astype(F32)
    mine = jnp.dot(coef_grad, pick, preferred_element_type=F32, precision=HIGHEST)
    moment = jnp.dot(inv_ref[...], mine, preferred_element_type=F32, precision=HIGHEST)
    at = lax.broadcasted_iota(jnp.int32, (slots, seg_len), 1)
    column = meta_ref[...].T
    for i in range(item_count):
        rows = basis_of(column[:, i : i + 1], column[:, item_count + i : item_count + i + 1])
        sampled = jnp.dot(rows, moment, preferred_element_type=F32, precision=HIGHEST)
        spread = (at == pos_ref[i]).astype(F32)
        out_ref[i] = dot_tn(spread, sampled, HIGHEST)


def past_grads(gmem, coef, vec, inv, meta, pos, seg_len, width):
    return pl.pallas_call(
        past_kernel,
        out_shape=(
            jax.ShapeDtypeStruct((pos.shape[0], seg_len, width), F32),
            jax.ShapeDtypeStruct((8, coef.shape[1]), F32),
        ),
        compiler_params=pltpu.CompilerParams(vmem_limit_bytes=BIG_VMEM),
        name="past_grads",
    )(gmem, coef, vec, inv, meta, pos)


def forward_kernel(
    tok_ref,
    coef_ref,
    vec_ref,
    gvec_ref,
    wa_ref,
    wu_ref,
    wd_ref,
    out_ref,
    res_ref,
    hm_ref,
    h2_ref,
    prob_ref,
    key_ref,
    val_ref,
    query_ref,
    att_ref,
    act_ref,
    slope_ref,
    acc_ref,
    *,
    groups,
    head,
):
    step = pl.program_id(0)
    rows, width = tok_ref.shape
    local = query_ref.shape[2]
    half = rows // 2

    @pl.when(step == 0)
    def _():
        gain, bias = vec_ref[0:1, :], vec_ref[1:2, :]
        normed, _ = norm_parts(coef_ref[...].astype(F32))
        hm_ref[0:NB, :] = (normed * gain + bias).astype(BF)
        normed, _ = norm_parts(tok_ref[...].astype(F32))
        hm_ref[NB:, :] = (normed * gain + bias).astype(BF)
        acc_ref[...] = jnp.zeros_like(acc_ref)

    @pl.when(step < groups)
    def _():
        weights = wa_ref[0]
        projected = dot(hm_ref[...], weights[:, : 3 * local]) + gvec_ref[0, 0:1, : 3 * local]
        query = projected[NB:, :local].astype(BF)
        keys = projected[:, local : 2 * local].astype(BF)
        values = projected[:, 2 * local :].astype(BF)
        query_ref[0] = query
        key_ref[0] = keys
        val_ref[0] = values
        query_t = query.T * BF(1.0 / math.sqrt(head))
        value_t = values.T
        line = lax.broadcasted_iota(jnp.int32, (local, rows), 0)
        for h in range(local // head):
            own = (line >= h * head) & (line < (h + 1) * head)
            masked = jnp.where(own, query_t, BF(0.0))
            value_h = value_t[h * head : (h + 1) * head, :]
            for b in range(2):
                span = NB + (b + 1) * half
                scores = dot(keys[:span, :], masked[:, b * half : (b + 1) * half])
                key_at = lax.broadcasted_iota(jnp.int32, (half, half), 0)
                row_at = lax.broadcasted_iota(jnp.int32, (half, half), 1)
                edge = jnp.where(key_at <= row_at, scores[span - half :, :], -1e30)
                scores = jnp.concatenate([scores[: span - half, :], edge], axis=0)
                scores = jnp.exp(scores - jnp.max(scores, axis=0, keepdims=True))
                probs = (scores * (1.0 / jnp.sum(scores, axis=0, keepdims=True))).astype(BF)
                prob_ref[0, h, 0:span, b * half : (b + 1) * half] = probs
                att_ref[0, h * head : (h + 1) * head, b * half : (b + 1) * half] = dot(
                    value_h[:, :span], probs
                ).astype(BF)
        attended = att_ref[0].T
        acc_ref[...] += dot_nt(attended, weights[:, 3 * local :])

    @pl.when(step == groups)
    def _():
        residual = tok_ref[...].astype(F32) + acc_ref[...] + vec_ref[4:5, :]
        res_ref[...] = residual
        normed, _ = norm_parts(residual)
        h2_ref[...] = (normed * vec_ref[2:3, :] + vec_ref[3:4, :]).astype(BF)
        acc_ref[...] = jnp.zeros_like(acc_ref)

    @pl.when(step >= groups)
    def _():
        pre = dot(h2_ref[...], wu_ref[0]) + gvec_ref[0, 1:2, :]
        square = pre * pre
        inner = jnp.tanh(GELU_SCALE * (pre + GELU_CUBIC * pre * square))
        half_up = 0.5 * (1.0 + inner)
        act = (pre * half_up).astype(BF)
        act_ref[0] = act
        slope = GELU_SCALE * (1.0 + 3.0 * GELU_CUBIC * square)
        slope_ref[0] = (half_up + 0.5 * pre * (1.0 - inner * inner) * slope).astype(BF)
        acc_ref[...] += dot_nt(act, wd_ref[0])

    @pl.when(step == 2 * groups - 1)
    def _():
        out_ref[...] = (res_ref[...] + acc_ref[...] + vec_ref[5:6, :]).astype(BF)


def forward_pass(tok, coef, vec, gvec, wide, head):
    rows, width = tok.shape
    groups = wide[0].shape[0]
    local = width // groups
    hidden = wide[1].shape[2]
    heads = local // head
    keyed = NB + rows
    first = lambda i: jnp.minimum(i, groups - 1)
    second = lambda i: jnp.maximum(i - groups, 0)
    whole = lambda shape: pl.BlockSpec(shape, lambda i: (0,) * len(shape))
    return pl.pallas_call(
        functools.partial(forward_kernel, groups=groups, head=head),
        grid=(2 * groups,),
        in_specs=[
            whole((rows, width)),
            whole((NB, width)),
            whole((8, width)),
            pl.BlockSpec((1, 8, width), lambda i: (i % groups, 0, 0)),
            pl.BlockSpec((1, width, width), lambda i: (first(i), 0, 0)),
            pl.BlockSpec((1, width, hidden), lambda i: (second(i), 0, 0)),
            pl.BlockSpec((1, width, hidden), lambda i: (second(i), 0, 0)),
        ],
        out_specs=[
            whole((rows, width)),
            whole((rows, width)),
            whole((keyed, width)),
            whole((rows, width)),
            pl.BlockSpec((1, heads, keyed, rows), lambda i: (first(i), 0, 0, 0)),
            pl.BlockSpec((1, keyed, local), lambda i: (first(i), 0, 0)),
            pl.BlockSpec((1, keyed, local), lambda i: (first(i), 0, 0)),
            pl.BlockSpec((1, rows, local), lambda i: (first(i), 0, 0)),
            pl.BlockSpec((1, local, rows), lambda i: (first(i), 0, 0)),
            pl.BlockSpec((1, rows, hidden), lambda i: (second(i), 0, 0)),
            pl.BlockSpec((1, rows, hidden), lambda i: (second(i), 0, 0)),
        ],
        out_shape=[
            jax.ShapeDtypeStruct((rows, width), BF),
            jax.ShapeDtypeStruct((rows, width), F32),
            jax.ShapeDtypeStruct((keyed, width), BF),
            jax.ShapeDtypeStruct((rows, width), BF),
            jax.ShapeDtypeStruct((groups, heads, keyed, rows), BF),
            jax.ShapeDtypeStruct((groups, keyed, local), BF),
            jax.ShapeDtypeStruct((groups, keyed, local), BF),
            jax.ShapeDtypeStruct((groups, rows, local), BF),
            jax.ShapeDtypeStruct((groups, local, rows), BF),
            jax.ShapeDtypeStruct((groups, rows, hidden), BF),
            jax.ShapeDtypeStruct((groups, rows, hidden), BF),
        ],
        scratch_shapes=[pltpu.VMEM((rows, width), F32)],
        compiler_params=pltpu.CompilerParams(vmem_limit_bytes=BIG_VMEM),
        name="forward_pass",
    )(tok, coef, vec, gvec, *wide)


def backward_kernel(
    tok_ref,
    cot_ref,
    res_ref,
    vec_ref,
    hm_ref,
    h2_ref,
    prob_ref,
    key_ref,
    val_ref,
    query_ref,
    att_ref,
    act_ref,
    slope_ref,
    wa_ref,
    wu_ref,
    wd_ref,
    tg_ref,
    gmem_ref,
    gup_ref,
    gdown_ref,
    gatt_ref,
    gv_ref,
    ggv_ref,
    acc_ref,
    hmt_ref,
    h2t_ref,
    cott_ref,
    gres_ref,
    proj_ref,
    *,
    groups,
    head,
):
    step = pl.program_id(0)
    rows, width = tok_ref.shape
    local = query_ref.shape[2]
    half = rows // 2

    @pl.when(step == 0)
    def _():
        acc_ref[...] = jnp.zeros_like(acc_ref)
        h2t_ref[...] = h2_ref[...].T
        cott_ref[...] = cot_ref[...].T
        gv_ref[...] = jnp.zeros_like(gv_ref)

    @pl.when(step < groups)
    def _():
        upstream = cot_ref[...]
        grad = (dot(upstream, wd_ref[0]) * slope_ref[0].astype(F32)).astype(BF)
        gdown_ref[0] = dot(cott_ref[...], act_ref[0]).astype(BF)
        gup_ref[0] = dot(h2t_ref[...], grad).astype(BF)
        ggv_ref[0] = jnp.zeros_like(ggv_ref[0])
        ggv_ref[0, 0:1, :] = col_sum(grad.astype(F32))
        acc_ref[NB:, :] += dot_nt(grad, wu_ref[0])

    @pl.when(step == groups)
    def _():
        upstream = cot_ref[...].astype(F32)
        normed, inverse = norm_parts(res_ref[...])
        grad = acc_ref[NB:, :]
        g_res = upstream + norm_back(grad, normed, inverse, vec_ref[2:3, :])
        gres_ref[...] = g_res
        g_attn = g_res.astype(BF)
        gv_ref[2:3, :] = col_sum(grad * normed)
        gv_ref[3:4, :] = col_sum(grad)
        gv_ref[4:5, :] = col_sum(g_attn.astype(F32))
        gv_ref[5:6, :] = col_sum(upstream)
        cott_ref[...] = g_attn.T
        hmt_ref[...] = hm_ref[...].T
        acc_ref[...] = jnp.zeros_like(acc_ref)
        proj_ref[0:NB, :] = jnp.zeros((NB, proj_ref.shape[1]), BF)

    @pl.when(step >= groups)
    def _():
        weights = wa_ref[0]
        g_attn = gres_ref[...].astype(BF)
        g_att = dot(g_attn, weights[:, 3 * local :]).astype(BF)
        g_att_t = g_att.T
        att_t = att_ref[0]
        product = g_att_t.astype(F32) * att_t.astype(F32)
        keys, values, query = key_ref[0], val_ref[0], query_ref[0]
        key_t = keys.T
        scale = 1.0 / math.sqrt(head)
        line = lax.broadcasted_iota(jnp.int32, (local, rows), 0)
        lane = lax.broadcasted_iota(jnp.int32, (rows, local), 1)
        key_grad = [jnp.zeros((NB + rows - half, local), F32), jnp.zeros((half, local), F32)]
        val_grad = [jnp.zeros((NB + rows - half, local), F32), jnp.zeros((half, local), F32)]
        query_grads = []
        for h in range(local // head):
            own_t = (line >= h * head) & (line < (h + 1) * head)
            own = (lane >= h * head) & (lane < (h + 1) * head)
            grad_t = jnp.where(own_t, g_att_t, BF(0.0))
            grad_h = jnp.where(own, g_att, BF(0.0))
            query_h = jnp.where(own, query, BF(0.0))
            inner = jnp.sum(product[h * head : (h + 1) * head, :], axis=0, keepdims=True)
            key_h = key_t[h * head : (h + 1) * head, :]
            parts = []
            for b in range(2):
                span = NB + (b + 1) * half
                cols = slice(b * half, (b + 1) * half)
                probs = prob_ref[0, h, 0:span, cols]
                dprob = dot(values[:span, :], grad_t[:, cols])
                dscore = (probs.astype(F32) * (dprob - inner[:, cols])).astype(BF)
                parts.append(dot(key_h[:, :span], dscore))
                val_part = dot(probs, grad_h[cols, :])
                key_part = dot(dscore, query_h[cols, :])
                low = NB + rows - half
                val_grad[0] = val_grad[0] + val_part[:low, :]
                key_grad[0] = key_grad[0] + key_part[:low, :]
                if b == 1:
                    val_grad[1] = val_grad[1] + val_part[low:, :]
                    key_grad[1] = key_grad[1] + key_part[low:, :]
            query_grads.append(jnp.concatenate(parts, axis=1))
        query_grad = (jnp.concatenate(query_grads, axis=0) * scale).astype(BF).T
        key_grad = (jnp.concatenate(key_grad, axis=0) * scale).astype(BF)
        val_sum = jnp.concatenate(val_grad, axis=0)
        val_grad = val_sum.astype(BF)
        proj_ref[NB:, 0:local] = query_grad
        proj_ref[:, local : 2 * local] = key_grad
        proj_ref[:, 2 * local :] = val_grad
        proj = proj_ref[...]
        ggv_ref[0] = jnp.zeros_like(ggv_ref[0])
        ggv_ref[0, 0:1, 0 : 3 * local] = col_sum(proj.astype(F32))
        gatt_ref[0, :, 0 : 3 * local] = dot(hmt_ref[...], proj).astype(BF)
        gatt_ref[0, :, 3 * local :] = dot_nt(cott_ref[...], att_t).astype(BF)
        acc_ref[...] += dot_nt(proj, weights[:, : 3 * local])

    @pl.when(step == 2 * groups - 1)
    def _():
        gmem_ref[...] = acc_ref[0:NB, :]
        grad = acc_ref[NB:, :]
        normed, inverse = norm_parts(tok_ref[...].astype(F32))
        part = norm_back(grad, normed, inverse, vec_ref[0:1, :])
        tg_ref[...] = (gres_ref[...] + part).astype(BF)
        gv_ref[0:1, :] = col_sum(grad * normed)
        gv_ref[1:2, :] = col_sum(grad)


def backward_pass(tok, cot, vec, saved, wide, head):
    res, hm, h2, prob, keys, vals, query, att, act, slope = saved
    rows, width = tok.shape
    groups = wide[0].shape[0]
    local = width // groups
    hidden = wide[1].shape[2]
    heads = local // head
    keyed = NB + rows
    first = lambda i: jnp.minimum(i, groups - 1)
    second = lambda i: jnp.maximum(i - groups, 0)
    whole = lambda shape: pl.BlockSpec(shape, lambda i: (0,) * len(shape))
    return pl.pallas_call(
        functools.partial(backward_kernel, groups=groups, head=head),
        grid=(2 * groups,),
        in_specs=[
            whole((rows, width)),
            whole((rows, width)),
            whole((rows, width)),
            whole((8, width)),
            whole((keyed, width)),
            whole((rows, width)),
            pl.BlockSpec((1, heads, keyed, rows), lambda i: (second(i), 0, 0, 0)),
            pl.BlockSpec((1, keyed, local), lambda i: (second(i), 0, 0)),
            pl.BlockSpec((1, keyed, local), lambda i: (second(i), 0, 0)),
            pl.BlockSpec((1, rows, local), lambda i: (second(i), 0, 0)),
            pl.BlockSpec((1, local, rows), lambda i: (second(i), 0, 0)),
            pl.BlockSpec((1, rows, hidden), lambda i: (first(i), 0, 0)),
            pl.BlockSpec((1, rows, hidden), lambda i: (first(i), 0, 0)),
            pl.BlockSpec((1, width, width), lambda i: (second(i), 0, 0)),
            pl.BlockSpec((1, width, hidden), lambda i: (first(i), 0, 0)),
            pl.BlockSpec((1, width, hidden), lambda i: (first(i), 0, 0)),
        ],
        out_specs=[
            whole((rows, width)),
            whole((NB, width)),
            pl.BlockSpec((1, width, hidden), lambda i: (first(i), 0, 0)),
            pl.BlockSpec((1, width, hidden), lambda i: (first(i), 0, 0)),
            pl.BlockSpec((1, width, width), lambda i: (second(i), 0, 0)),
            whole((8, width)),
            pl.BlockSpec((1, 8, hidden), lambda i: (i, 0, 0)),
        ],
        out_shape=[
            jax.ShapeDtypeStruct((rows, width), BF),
            jax.ShapeDtypeStruct((NB, width), F32),
            jax.ShapeDtypeStruct((groups, width, hidden), BF),
            jax.ShapeDtypeStruct((groups, width, hidden), BF),
            jax.ShapeDtypeStruct((groups, width, width), BF),
            jax.ShapeDtypeStruct((8, width), F32),
            jax.ShapeDtypeStruct((2 * groups, 8, hidden), F32),
        ],
        scratch_shapes=[
            pltpu.VMEM((keyed, width), F32),
            pltpu.VMEM((width, keyed), BF),
            pltpu.VMEM((width, rows), BF),
            pltpu.VMEM((width, rows), BF),
            pltpu.VMEM((rows, width), F32),
            pltpu.VMEM((keyed, 3 * local), BF),
        ],
        compiler_params=pltpu.CompilerParams(vmem_limit_bytes=BIG_VMEM),
        name="backward_pass",
    )(
        tok, cot, res, vec, hm, h2, prob, keys, vals, query, att, act, slope, *wide
    )


MESH = pl.DeviceIdType.MESH
LINE = 4
PLANE = 8
NEAR = (0, -1, 1, -2, 2, -3, 3)
FAR = (-3, 3, -2, 2, -1, 1, 0)


class Place:
    def __init__(self):
        self.s = lax.axis_index("seq")
        self.z = lax.axis_index("mp")
        core = lax.rem(self.s, 2)
        x = lax.rem(self.s // 2, 2)
        y = self.s // 4
        self.turn = 1 - 2 * core
        self.partner = self.s + self.turn
        self.sx = self.s + 2 - 4 * x
        self.sy = self.s + 4 - 8 * y
        self.sd = self.sx + 4 - 8 * y
        self.low = self.z > 0
        self.high = self.z < LINE - 1


def valid(m):
    return (m >= 0) & (m < LINE)


def when(condition, act):
    if condition is None:
        act()
    else:
        pl.when(condition)(act)


def greet(place, line=True, plane=True):
    barrier = pltpu.get_barrier_semaphore()

    def signal(seq, z):
        pl.semaphore_signal(barrier, inc=1, device_id=(seq, z), device_id_type=MESH)

    if plane:
        for seq in (place.partner, place.sx, place.sy):
            signal(seq, place.z)
    if line:
        pl.when(place.low)(lambda: signal(place.s, place.z - 1))
        pl.when(place.high)(lambda: signal(place.s, place.z + 1))
    peers = 3 if plane else 0
    if line:
        peers = peers + (place.z + LINE - 1) // LINE + (2 * LINE - 2 - place.z) // LINE
    pl.semaphore_wait(barrier, peers)


UP, DOWN, ACROSS_X, ACROSS_Y, PARTNER = range(5)


class Spread:
    def __init__(self, place, src, dst, send, recv, local, line=True):
        self.p, self.src, self.dst = place, src, dst
        self.send, self.recv, self.line = send, recv, line
        self.rows = src.shape[0]
        self.sent = []
        self.own = pltpu.make_async_copy(src, self.at(self.mine(), place.s), local)

    def mine(self):
        return self.p.z if self.line else 0

    def at(self, m, s):
        return self.dst.at[m, pl.ds(s * self.rows, self.rows), :]

    def copy(self, direction, m, s, own=False):
        p = self.p
        device = (
            (p.s, p.z + 1),
            (p.s, p.z - 1),
            (p.sx, p.z),
            (p.sy, p.z),
            (p.partner, p.z),
        )[direction]
        return pltpu.make_async_remote_copy(
            src_ref=self.src if own else self.at(m, s),
            dst_ref=self.at(m, s),
            send_sem=self.send.at[direction, m * 4 + s // 2],
            recv_sem=self.recv.at[m * PLANE + s],
            device_id=device,
            device_id_type=MESH,
        )

    def start(self, condition, *what, **how):
        when(condition, lambda: self.copy(*what, **how).start())
        self.sent.append((condition, what, how))

    def arrived(self, m, s):
        self.copy(PARTNER, m, s).wait_recv()

    def around(self):
        if not self.line:
            return [(0, None, 0)]
        return [(d, valid(self.p.z + d), self.p.z + d) for d in NEAR]

    def first(self):
        p, m = self.p, self.mine()
        self.own.start()
        if self.line:
            self.start(p.high, UP, m, p.s, own=True)
            self.start(p.low, DOWN, m, p.s, own=True)
        for direction in (ACROSS_X, ACROSS_Y, PARTNER):
            self.start(None, direction, m, p.s, own=True)

    def along(self):
        p = self.p
        for d, ok, m in self.around()[1:]:
            when(ok, lambda: self.arrived(m, p.s))
            if d < 0:
                self.start(ok & p.high, UP, m, p.s)
            else:
                self.start(ok & p.low, DOWN, m, p.s)
            for direction in (ACROSS_X, ACROSS_Y, PARTNER):
                self.start(ok, direction, m, p.s)

    def across(self):
        p = self.p
        for d, ok, m in self.around():
            odd = lax.rem(m, 2) == 1 if self.line else None
            when(ok, lambda: self.arrived(m, p.sx))
            if self.line:
                self.start(ok & odd, ACROSS_Y, m, p.sx)
            self.start(ok, PARTNER, m, p.sx)
            when(ok, lambda: self.arrived(m, p.sy))
            self.start(ok & ~odd if self.line else None, ACROSS_X, m, p.sy)
            self.start(ok, PARTNER, m, p.sy)

    def corner(self):
        p = self.p
        for d, ok, m in self.around():
            when(ok, lambda: self.arrived(m, p.sd))
            self.start(ok, PARTNER, m, p.sd)

    def finish(self):
        p = self.p

        @pl.loop(0, LINE if self.line else 1)
        def _(m):
            for s in (p.s, p.sx, p.sy, p.sd):
                self.arrived(m, s + p.turn)

        for condition, what, how in self.sent:
            when(condition, lambda: self.copy(*what, **how).wait_send())
        self.own.wait()


def spread_kernel(*refs, count, line):
    place = Place()
    srcs, dsts = refs[:count], refs[count : 2 * count]
    send, recv, local = refs[2 * count :]
    greet(place, line)
    parts = [
        Spread(place, srcs[i], dsts[i], send.at[i], recv.at[i], local.at[i], line)
        for i in range(count)
    ]
    for turn in range(count + 3):
        for i in range(count):
            stage = turn - i
            if stage == 0:
                parts[i].first()
            elif stage == 1:
                parts[i].along()
            elif stage == 2:
                parts[i].across()
            elif stage == 3:
                parts[i].corner()
    for part in parts:
        part.finish()


def spread(blocks, collective_id, name, line=True):
    count = len(blocks)
    depth = LINE if line else 1
    dma = pltpu.SemaphoreType.DMA
    return pl.pallas_call(
        functools.partial(spread_kernel, count=count, line=line),
        out_shape=[
            jax.ShapeDtypeStruct((depth, b.shape[0] * PLANE, b.shape[1]), b.dtype) for b in blocks
        ],
        in_specs=[pl.BlockSpec(memory_space=pl.ANY)] * count,
        out_specs=[pl.BlockSpec(memory_space=pl.ANY)] * count,
        scratch_shapes=[
            dma((count, 5, depth * 4)),
            dma((count, depth * PLANE)),
            dma((count,)),
        ],
        compiler_params=pltpu.CompilerParams(collective_id=collective_id, has_side_effects=True),
        name=name,
    )(*blocks)


class Line:
    def __init__(self, place, src, dst, send, recv, local):
        self.p, self.src, self.dst = place, src, dst
        self.send, self.recv = send, recv
        self.sent = []
        self.own = pltpu.make_async_copy(src, dst.at[place.z], local)

    def copy(self, up, m, own=False):
        p = self.p
        return pltpu.make_async_remote_copy(
            src_ref=self.src if own else self.dst.at[m],
            dst_ref=self.dst.at[m],
            send_sem=self.send.at[1 if up else 0, m],
            recv_sem=self.recv.at[m],
            device_id=(p.s, p.z + 1 if up else p.z - 1),
            device_id_type=MESH,
        )

    def start(self, condition, *what, **how):
        when(condition, lambda: self.copy(*what, **how).start())
        self.sent.append((condition, what, how))

    def first(self):
        p = self.p
        self.own.start()
        self.start(p.high, True, p.z, own=True)
        self.start(p.low, False, p.z, own=True)

    def step(self, distance):
        p = self.p
        for d in (-distance, distance):
            m = p.z + d
            ok = valid(m)
            when(ok, lambda: self.copy(True, m).wait_recv())
            if d < 0:
                self.start(ok & p.high, True, m)
            else:
                self.start(ok & p.low, False, m)

    def finish(self):
        for condition, what, how in self.sent:
            when(condition, lambda: self.copy(*what, **how).wait_send())
        self.own.wait()


def line_kernel(src, dst, send, recv, local):
    place = Place()
    greet(place, plane=False)
    line = Line(place, src, dst, send, recv, local)
    line.first()
    for distance in range(1, LINE):
        line.step(distance)
    line.finish()


def line_gather(block, collective_id, name):
    dma = pltpu.SemaphoreType.DMA
    return pl.pallas_call(
        line_kernel,
        out_shape=jax.ShapeDtypeStruct((LINE,) + block.shape, block.dtype),
        in_specs=[pl.BlockSpec(memory_space=pl.ANY)],
        out_specs=pl.BlockSpec(memory_space=pl.ANY),
        scratch_shapes=[dma((2, LINE)), dma((LINE,)), dma(())],
        compiler_params=pltpu.CompilerParams(collective_id=collective_id, has_side_effects=True),
        name=name,
    )(block)


class Collect:
    OWN, SIDE_X, SIDE_Y, CORNER = range(4)

    def __init__(self, place, grads, out, buffers, sems):
        self.p, self.grads, self.out = place, grads, out
        self.mine, self.pin, self.din, self.xin, self.yin, self.uin, self.win = buffers
        self.block_sems, self.sems = sems
        self.rows = out.shape[0]
        self.columns = (place.s, place.sx, place.sy, place.sd)

    def unit(self, c, m, turn=0):
        s = self.columns[c] + turn
        return self.grads.at[m, pl.ds(s * self.rows, self.rows), :]

    def load(self, c, m):
        return pltpu.make_async_copy(
            self.unit(c, m), self.mine.at[c, m], self.block_sems.at[0, c, m]
        )

    def remote(self, src, dst, send, recv, device):
        return pltpu.make_async_remote_copy(
            src_ref=src,
            dst_ref=dst,
            send_sem=send,
            recv_sem=recv,
            device_id=device,
            device_id_type=MESH,
        )

    def swap(self, c, m):
        p = self.p
        return self.remote(
            self.unit(c, m, p.turn),
            self.pin.at[c, m],
            self.block_sems.at[1, c, m],
            self.block_sems.at[2, c, m],
            (p.partner, p.z),
        )

    def hop(self, kind, m, by_x=True):
        p = self.p
        src, dst, device = (
            (self.CORNER, self.din, (p.sx if by_x else p.sy, p.z)),
            (self.SIDE_X, self.xin, (p.sx, p.z)),
            (self.SIDE_Y, self.yin, (p.sy, p.z)),
        )[kind]
        return self.remote(
            self.mine.at[src, m],
            dst.at[m],
            self.sems.at[kind, m],
            self.sems.at[4 + kind, m],
            device,
        )

    def climb(self, m, up):
        p = self.p
        return self.remote(
            self.mine.at[self.OWN, m],
            (self.uin if up else self.win).at[m],
            self.sems.at[3, m],
            self.sems.at[7 if up else 8, m],
            (p.s, p.z + 1 if up else p.z - 1),
        )

    def add(self, c, m, *others):
        total = self.mine[c, m].astype(F32)
        for other in others:
            total = total + other[m].astype(F32)
        self.mine[c, m] = total.astype(BF)

    def ring(self, body):
        for d in FAR:
            m = self.p.z + d
            pl.when(valid(m))(functools.partial(body, d, m))

    def begin(self):
        for c in (self.CORNER, self.SIDE_X, self.SIDE_Y, self.OWN):

            @pl.loop(0, LINE)
            def _(m):
                self.load(c, m).start()
                self.swap(c, m).start()

    def join(self, c, m):
        self.load(c, m).wait()
        self.swap(c, m).wait_recv()
        self.add(c, m, self.pin.at[c])

    def corner(self):
        def body(d, m):
            self.join(self.CORNER, m)
            even = lax.rem(m, 2) == 0
            pl.when(even)(lambda: self.hop(0, m, True).start())
            pl.when(~even)(lambda: self.hop(0, m, False).start())

        self.ring(body)

    def sides(self):
        def body(d, m):
            even = lax.rem(m, 2) == 0
            self.join(self.SIDE_X, m)
            self.join(self.SIDE_Y, m)
            pl.when(even)(lambda: self.hop(1, m).start())
            pl.when(~even)(lambda: self.hop(2, m).start())

        self.ring(body)

    def relay(self):
        def body(d, m):
            even = lax.rem(m, 2) == 0
            self.hop(0, m).wait_recv()

            @pl.when(even)
            def _():
                self.add(self.SIDE_Y, m, self.din)
                self.hop(2, m).start()

            @pl.when(~even)
            def _():
                self.add(self.SIDE_X, m, self.din)
                self.hop(1, m).start()

        self.ring(body)

    def line(self):
        p = self.p

        def body(d, m):
            self.join(self.OWN, m)
            self.hop(1, m).wait_recv()
            self.hop(2, m).wait_recv()
            self.add(self.OWN, m, self.xin, self.yin)
            if d > 0:

                @pl.when(p.low)
                def _():
                    self.climb(m, True).wait_recv()
                    self.add(self.OWN, m, self.uin)

                self.climb(m, True).start()
            elif d < 0:

                @pl.when(p.high)
                def _():
                    self.climb(m, False).wait_recv()
                    self.add(self.OWN, m, self.win)

                self.climb(m, False).start()

        self.ring(body)

    def result(self):
        p = self.p
        self.out[...] = self.mine[self.OWN, p.z].astype(F32)

        @pl.when(p.low)
        def _():
            self.climb(p.z, True).wait_recv()
            self.out[...] += self.uin[p.z].astype(F32)

        @pl.when(p.high)
        def _():
            self.climb(p.z, False).wait_recv()
            self.out[...] += self.win[p.z].astype(F32)

    def finish(self):
        for c in range(4):

            @pl.loop(0, LINE)
            def _(m):
                self.swap(c, m).wait_send()

        @pl.loop(0, LINE)
        def _(m):
            for kind in range(3):
                self.hop(kind, m).wait_send()
            pl.when(m != self.p.z)(lambda: self.climb(m, True).wait_send())


BUFFERS = ((4, LINE), (4, LINE), (LINE,), (LINE,), (LINE,), (LINE,), (LINE,))


def collect_kernel(*refs, count):
    place = Place()
    grads, rows = refs[:count], refs[count]
    outs, all_rows = refs[count + 1 : 2 * count + 1], refs[2 * count + 1]
    rest = refs[2 * count + 2 :]
    buffers, (block_sems, sems, line_send, line_recv, line_own) = rest[:-5], rest[-5:]
    greet(place)
    parts = [
        Collect(
            place, grads[i], outs[i], buffers[i :: count], (block_sems.at[i], sems.at[i])
        )
        for i in range(count)
    ]
    line = Line(place, rows, all_rows, line_send, line_recv, line_own)
    for part in parts:
        part.begin()
    for turn in range(count + 4):
        if turn == 1:
            line.first()
        elif turn == 2:
            line.step(1)
        elif turn == 4:
            line.step(2)
        elif turn == 5:
            line.step(3)
        for i in range(count):
            stage = turn - i
            if stage == 0:
                parts[i].corner()
            elif stage == 1:
                parts[i].sides()
            elif stage == 2:
                parts[i].relay()
            elif stage == 3:
                parts[i].line()
            elif stage == 4:
                parts[i].result()
    for part in parts:
        part.finish()
    line.finish()


def collect(grads, rows, collective_id):
    count = len(grads)
    dma = pltpu.SemaphoreType.DMA
    anywhere = pl.BlockSpec(memory_space=pl.ANY)
    blocks = [(g.shape[1] // PLANE, g.shape[2]) for g in grads]
    return pl.pallas_call(
        functools.partial(collect_kernel, count=count),
        out_shape=[jax.ShapeDtypeStruct(b, F32) for b in blocks]
        + [jax.ShapeDtypeStruct((LINE,) + rows.shape, rows.dtype)],
        in_specs=[anywhere] * (count + 1),
        out_specs=[pl.BlockSpec(memory_space=pltpu.VMEM)] * count + [anywhere],
        scratch_shapes=[pltpu.VMEM(lead + b, BF) for lead in BUFFERS for b in blocks]
        + [
            dma((count, 3, 4, LINE)),
            dma((count, 9, LINE)),
            dma((2, LINE)),
            dma((LINE,)),
            dma(()),
        ],
        compiler_params=pltpu.CompilerParams(
            collective_id=collective_id, has_side_effects=True, vmem_limit_bytes=BIG_VMEM
        ),
        name="collect_grads",
    )(*grads, rows)


def local(
    tokens,
    cotangent,
    past_state,
    positions,
    counts,
    ln1_gain,
    ln1_bias,
    w_qkv,
    b_qv,
    w_out,
    b_out,
    ln2_gain,
    ln2_bias,
    w_up,
    b_up,
    w_down,
    b_down,
):
    seq, mp = lax.axis_size("seq"), lax.axis_size("mp")
    seq_index, mp_index = lax.axis_index("seq"), lax.axis_index("mp")
    item_count, seg_len, local_width = past_state.shape
    slots = positions.shape[1]
    total = item_count * seq
    width = tokens.shape[1]
    part = width // seq
    heads_local, piece = b_qv.shape[1], b_qv.shape[2]
    head = piece * seq
    hidden = w_up.shape[1]
    rows = tokens.shape[0] // mp
    direct = seq == PLANE and mp == LINE and part % 16 == 0 and hidden == width
    mem_rows = NB // (seq * mp)

    items = (seq_index * item_count + jnp.arange(item_count)).astype(F32)
    places = (items[:, None] + (positions.astype(F32) + 0.5) / seg_len) / total
    used = (jnp.arange(slots)[None, :] < counts[:, None]).astype(F32)
    meta = jnp.concatenate([places, used, jnp.zeros((8 - 2 * item_count, slots), F32)])
    pos3 = positions.reshape(item_count, slots, 1)
    sampled = sample_rows(past_state, pos3).reshape(item_count * slots, local_width)
    if direct:
        all_sampled, all_meta = spread([sampled, meta], 1, "spread_samples", line=False)
    else:
        all_sampled = lax.all_gather(sampled, "seq", axis=0)
        all_meta = lax.all_gather(meta, "seq", axis=0)
    all_sampled = all_sampled.reshape(seq, item_count * slots, local_width)
    coef_part, inverse = solve_memory(all_sampled, all_meta.reshape(seq, 8, slots), item_count)
    if direct:
        coef = line_gather(coef_part, 2, "line_coef")
    else:
        coef = lax.all_gather(coef_part, "mp", axis=0)
    coef = coef.transpose(1, 0, 2).reshape(NB, width)

    attn = jnp.concatenate([w_qkv[0], w_qkv[1], w_qkv[2], w_out.T], axis=1)
    small = jnp.concatenate(
        [ln1_gain, ln1_bias, ln2_gain, ln2_bias, b_out, b_down, b_qv.reshape(-1), b_up.reshape(-1)]
    )
    if direct:
        room = jnp.zeros((16, width), BF).at[0, : small.shape[0]].set(small)
        room, *wide = spread([room, attn, w_up, w_down.T], 3, "spread_weights")
        small = room.reshape(mp, seq, 16, width)[:, :, 0]
    else:
        wide = [
            lax.all_gather(lax.all_gather(shard, "seq", axis=0, tiled=True), "mp", axis=0)
            for shard in (attn, w_up, w_down.T)
        ]
        small = lax.all_gather(lax.all_gather(small, "seq", axis=0), "mp", axis=0)
    vec = small[0, :, : 6 * part].reshape(seq, 6, part).transpose(1, 0, 2).reshape(6, width)
    vec = jnp.concatenate([vec, jnp.zeros((2, width), BF)]).astype(F32)
    at = 6 * part
    size = 2 * heads_local * piece
    up_size = hidden // seq
    bias_qv = small[:, :, at : at + size].reshape(mp, seq, 2, heads_local, piece)
    bias_qv = bias_qv.transpose(0, 2, 3, 1, 4).reshape(mp, 2, local_width)
    bias_up = small[:, :, at + size : at + size + up_size].reshape(mp, seq, -1, piece)
    bias_up = bias_up.transpose(0, 2, 1, 3).reshape(mp, hidden)
    zero = jnp.zeros((mp, local_width), BF)
    first = jnp.concatenate([bias_qv[:, 0], zero, bias_qv[:, 1], zero], axis=1)
    gvec = jnp.concatenate(
        [first[:, None], bias_up[:, None], jnp.zeros((mp, 6, width), BF)], axis=1
    ).astype(F32)

    tok = lax.dynamic_slice_in_dim(tokens, mp_index * rows, rows, 0)
    cot = lax.dynamic_slice_in_dim(cotangent, mp_index * rows, rows, 0)
    forward = forward_pass(tok, coef, vec, gvec, wide, head)
    block_out = lax.all_gather(forward[0], "mp", axis=0, tiled=True)
    tok_grad, gmem, g_up, g_down, g_attn, gv, ggv = backward_pass(
        tok, cot, vec, forward[1:], wide, head
    )

    tail = gv[:6].reshape(6, seq, part).transpose(1, 0, 2).reshape(1, seq, 6 * part)
    tail = jnp.broadcast_to(tail, (mp, seq, 6 * part))
    qv = ggv[mp:, 0]
    qv = jnp.stack([qv[:, :local_width], qv[:, 2 * local_width : 3 * local_width]], axis=1)
    qv = qv.reshape(mp, 2, heads_local, seq, piece).transpose(0, 3, 1, 2, 4).reshape(mp, seq, size)
    up = ggv[:mp, 0].reshape(mp, -1, seq, piece).transpose(0, 2, 1, 3).reshape(mp, seq, up_size)
    tail = jnp.concatenate([tail, qv, up], axis=2)
    if direct:
        tail = jnp.pad(tail, ((0, 0), (0, 0), (0, width - tail.shape[2])))[:, :, None]
        mem = gmem.reshape(mp, seq, mem_rows, width)
        pad = jnp.zeros((mp, seq, 15 - mem_rows, width), F32)
        side = jnp.concatenate([mem, tail, pad], axis=2).astype(BF).reshape(mp, seq * 16, width)
        side, attn, up_grad, down_grad, block_grad = collect(
            [side, g_attn, g_up, g_down], tok_grad, 4
        )
        block_grad = block_grad.reshape(mp * rows, width)
        (gmem,) = spread([side[:mem_rows]], 5, "spread_memory")
        gmem = gmem.reshape(NB, width)
        own = side[mem_rows]
    else:
        block_grad = lax.all_gather(tok_grad, "mp", axis=0, tiled=True)
        gmem, tail = lax.psum((gmem, tail), ("seq", "mp"))
        own = tail[mp_index, seq_index]
        attn, up_grad, down_grad = (
            lax.psum_scatter(
                lax.psum_scatter(g, "mp", scatter_dimension=0, tiled=False),
                "seq",
                scatter_dimension=0,
                tiled=True,
            ).astype(F32)
            for g in (g_attn, g_up, g_down)
        )
    past_grad, gv_mem = past_grads(gmem, coef, vec, inverse, meta, pos3, seg_len, local_width)
    gv_own = lax.dynamic_slice_in_dim(gv_mem, seq_index * part, part, 1)
    vec_own = own[: 6 * part].reshape(6, part)
    qkv_grad = jnp.stack([attn[:, i * local_width : (i + 1) * local_width] for i in range(3)])
    return (
        block_out,
        block_grad,
        past_grad,
        vec_own[0] + gv_own[0],
        vec_own[1] + gv_own[1],
        qkv_grad,
        own[at : at + size].reshape(2, heads_local, piece),
        attn[:, 3 * local_width :].T,
        vec_own[4],
        vec_own[2],
        vec_own[3],
        up_grad,
        own[at + size : at + size + up_size].reshape(-1, piece),
        down_grad.T,
        vec_own[5],
    )


def solution(mesh):
    row = P("seq", None)
    placed = (
        row,
        row,
        P("seq", None, "mp"),
        row,
        P("seq"),
        P("seq"),
        P("seq"),
        P(None, "seq", "mp"),
        P(None, "mp", "seq"),
        P("mp", "seq"),
        P("seq"),
        P("seq"),
        P("seq"),
        P("seq", "mp"),
        P("mp", "seq"),
        P("mp", "seq"),
        P("seq"),
    )
    return jax.shard_map(
        local,
        mesh=mesh,
        in_specs=placed,
        out_specs=(row, row, placed[2]) + placed[5:],
        check_vma=False,
    )
```

```python
import functools
import math

import jax
import jax.numpy as jnp
from jax import lax
from jax.experimental import pallas as pl
from jax.experimental.pallas import tpu as pltpu
from jax.sharding import PartitionSpec as P

NB = 256
PIVOTS = 32
NORM_EPSILON = 1e-05
RIDGE_WEIGHT = 1.0
NARROW_WIDTH = 0.01
BROAD_WIDTH = 0.05
GELU_SCALE = 0.7978845608028654
GELU_CUBIC = 0.044715

BF = jnp.bfloat16
F32 = jnp.float32
HIGHEST = lax.Precision.HIGHEST
BIG_VMEM = 60 * 1024 * 1024


def dot(a, b):
    return jnp.dot(a, b, preferred_element_type=F32)


def dot_nt(a, b):
    return lax.dot_general(a, b, (((1,), (1,)), ((), ())), preferred_element_type=F32)


def dot_tn(a, b, precision=None):
    return lax.dot_general(
        a, b, (((0,), (0,)), ((), ())), preferred_element_type=F32, precision=precision
    )


def norm_parts(values):
    centered = values - jnp.mean(values, axis=-1, keepdims=True)
    inverse = lax.rsqrt(jnp.mean(centered * centered, axis=-1, keepdims=True) + NORM_EPSILON)
    return centered * inverse, inverse


def norm_back(upstream, normed, inverse, gain):
    scaled = upstream * gain
    inner = scaled - jnp.mean(scaled, axis=-1, keepdims=True)
    inner = inner - normed * jnp.mean(scaled * normed, axis=-1, keepdims=True)
    return inner * inverse


def col_sum(values):
    return jnp.sum(values, axis=0, keepdims=True)


def basis_of(places, used):
    column = lax.broadcasted_iota(jnp.int32, (places.shape[0], NB), 1)
    centers = (column.astype(F32) + 0.5) / NB
    widths = jnp.where(column % 2 == 0, NARROW_WIDTH, BROAD_WIDTH).astype(F32)
    scaled = (places - centers) / widths
    return jnp.exp(-0.5 * (scaled * scaled)) * used


def position_of(column, i, items):
    return column[:, 2 * items + i : 2 * items + i + 1].astype(jnp.int32)


def invert_step(mat_ref):
    block = PIVOTS
    lane = lax.broadcasted_iota(jnp.int32, (block, NB), 1)
    line = lax.broadcasted_iota(jnp.int32, (block, NB), 0)
    panel = mat_ref[0:block, :]
    for k in range(block):
        pivot_row = panel[k : k + 1, :]
        factor = 1.0 / pivot_row[:, k : k + 1]
        scaled = jnp.where(lane[0:1] == k, factor, pivot_row * factor)
        column = panel[:, k : k + 1]
        rest = jnp.where(lane == k, 0.0, panel) - column * scaled
        panel = jnp.where(line == k, scaled, rest)
    mat_ref[0:block, :] = panel
    row = lax.broadcasted_iota(jnp.int32, (NB, NB), 0)
    col = lax.broadcasted_iota(jnp.int32, (NB, NB), 1)
    mat = mat_ref[...]
    inside_row = row < block
    inside_col = col < block
    left = jnp.where(inside_col & ~inside_row, mat, 0.0)
    right = jnp.where(inside_row, mat, 0.0)
    update = jnp.dot(left, right, preferred_element_type=F32, precision=HIGHEST)
    mat = jnp.where(inside_row, mat, jnp.where(inside_col, 0.0, mat) - update)
    mat = pltpu.roll(mat, NB - block, 1)
    mat_ref[0 : NB - block, :] = mat[block:, :]
    mat_ref[NB - block :, :] = mat[:block, :]


def gather_moments(samples, meta, mat_ref, mom_ref, items):
    slots = meta.shape[1]
    column = meta.T
    rows = [
        basis_of(column[:, i : i + 1], column[:, items + i : items + i + 1]) for i in range(items)
    ]
    rows = jnp.concatenate(rows, axis=0)
    mat_ref[...] += dot_tn(rows, rows, HIGHEST)
    mom_ref[...] += dot_tn(rows, samples.astype(F32), HIGHEST)


def clear_moments(mat_ref, mom_ref):
    row = lax.broadcasted_iota(jnp.int32, (NB, NB), 0)
    col = lax.broadcasted_iota(jnp.int32, (NB, NB), 1)
    mat_ref[...] = jnp.where(row == col, RIDGE_WEIGHT, 0.0)
    mom_ref[...] = jnp.zeros_like(mom_ref)


def coefficients(mat_ref, mom_ref):
    return jnp.dot(mat_ref[...], mom_ref[...], preferred_element_type=F32, precision=HIGHEST)


def pick_samples(past, meta, items):
    slots, seg_len = meta.shape[1], past.shape[1]
    column = meta.T
    at = lax.broadcasted_iota(jnp.int32, (slots, seg_len), 1)
    rows = []
    for i in range(items):
        pick = (at == position_of(column, i, items)).astype(F32).astype(BF)
        rows.append(dot(pick, past[i]).astype(BF))
    return jnp.concatenate(rows, axis=0)


def sample_kernel(past_ref, meta_ref, out_ref, *, items):
    out_ref[...] = pick_samples(past_ref[...], meta_ref[...], items)


def sample_rows(past, meta):
    items, seg_len, width = past.shape
    return pl.pallas_call(
        functools.partial(sample_kernel, items=items),
        out_shape=jax.ShapeDtypeStruct((items * meta.shape[1], width), BF),
        name="sample_rows",
    )(past, meta)


def solve_kernel(sampled_ref, meta_ref, coef_ref, inv_ref, mat_ref, mom_ref, *, items):
    clear_moments(mat_ref, mom_ref)

    def owner(s, carry):
        gather_moments(sampled_ref[s], meta_ref[s], mat_ref, mom_ref, items)
        return carry

    lax.fori_loop(0, meta_ref.shape[0], owner, 0)

    def step(s, carry):
        invert_step(mat_ref)
        return carry

    lax.fori_loop(0, NB // PIVOTS, step, 0)
    inv_ref[...] = mat_ref[...]
    coef_ref[...] = coefficients(mat_ref, mom_ref).astype(BF)


def solve_memory(sampled, meta, items):
    width = sampled.shape[-1]
    return pl.pallas_call(
        functools.partial(solve_kernel, items=items),
        out_shape=(
            jax.ShapeDtypeStruct((NB, width), BF),
            jax.ShapeDtypeStruct((NB, NB), F32),
        ),
        scratch_shapes=[pltpu.VMEM((NB, NB), F32), pltpu.VMEM((NB, width), F32)],
        compiler_params=pltpu.CompilerParams(vmem_limit_bytes=BIG_VMEM),
        name="solve_memory",
    )(sampled, meta)


def past_kernel(gmem_ref, coef_ref, vec_ref, inv_ref, meta_ref, out_ref, gv_ref):
    slots = meta_ref.shape[1]
    item_count, seg_len, width = out_ref.shape
    normed, inverse = norm_parts(coef_ref[...].astype(F32))
    gmem = gmem_ref[...]
    coef_grad = norm_back(gmem, normed, inverse, vec_ref[0:1, :])
    gv_ref[...] = jnp.zeros_like(gv_ref)
    gv_ref[0:1, :] = col_sum(gmem * normed)
    gv_ref[1:2, :] = col_sum(gmem)
    features = coef_grad.shape[1]
    part = lax.axis_index("mp")
    row = lax.broadcasted_iota(jnp.int32, (features, width), 0)
    col = lax.broadcasted_iota(jnp.int32, (features, width), 1)
    pick = (row == col + part * width).astype(F32)
    mine = jnp.dot(coef_grad, pick, preferred_element_type=F32, precision=HIGHEST)
    moment = jnp.dot(inv_ref[...], mine, preferred_element_type=F32, precision=HIGHEST)
    at = lax.broadcasted_iota(jnp.int32, (slots, seg_len), 1)
    column = meta_ref[...].T
    for i in range(item_count):
        rows = basis_of(column[:, i : i + 1], column[:, item_count + i : item_count + i + 1])
        sampled = jnp.dot(rows, moment, preferred_element_type=F32, precision=HIGHEST)
        spread = (at == position_of(column, i, item_count)).astype(F32)
        out_ref[i] = dot_tn(spread, sampled, HIGHEST)


def past_grads(gmem, coef, vec, inv, meta, items, seg_len, width):
    return pl.pallas_call(
        past_kernel,
        out_shape=(
            jax.ShapeDtypeStruct((items, seg_len, width), F32),
            jax.ShapeDtypeStruct((8, coef.shape[1]), F32),
        ),
        compiler_params=pltpu.CompilerParams(vmem_limit_bytes=BIG_VMEM),
        name="past_grads",
    )(gmem, coef, vec, inv, meta)


MESH = pl.DeviceIdType.MESH
LINE = 4
PLANE = 8
NEAR = (0, -1, 1, -2, 2, -3, 3)
FAR = (-3, 3, -2, 2, -1, 1, 0)


class Place:
    def __init__(self):
        self.s = lax.axis_index("seq")
        self.z = lax.axis_index("mp")
        core = lax.rem(self.s, 2)
        x = lax.rem(self.s // 2, 2)
        y = self.s // 4
        self.turn = 1 - 2 * core
        self.partner = self.s + self.turn
        self.sx = self.s + 2 - 4 * x
        self.sy = self.s + 4 - 8 * y
        self.sd = self.sx + 4 - 8 * y
        self.low = self.z > 0
        self.high = self.z < LINE - 1
        self.near = [
            (
                d,
                valid(self.z + d),
                self.z + d,
                lax.rem(self.z + d + LINE, 2) == 1,
                lax.rem(self.z + d + LINE, 2) == 0,
            )
            for d in NEAR
        ]


def valid(m):
    return (m >= 0) & (m < LINE)


def when(conditions, act):
    conditions = [c for c in conditions if c is not None]
    if conditions:
        pl.when(functools.reduce(lambda a, b: a & b, conditions))(act)
    else:
        act()


def greet(place, line=True, plane=True):
    barrier = pltpu.get_barrier_semaphore()

    def signal(seq, z):
        pl.semaphore_signal(barrier, inc=1, device_id=(seq, z), device_id_type=MESH)

    if plane:
        for seq in (place.partner, place.sx, place.sy):
            signal(seq, place.z)
    if line:
        pl.when(place.low)(lambda: signal(place.s, place.z - 1))
        pl.when(place.high)(lambda: signal(place.s, place.z + 1))
    peers = 3 if plane else 0
    if line:
        peers = peers + (place.z + LINE - 1) // LINE + (2 * LINE - 2 - place.z) // LINE
    pl.semaphore_wait(barrier, peers)


UP, DOWN, ACROSS_X, ACROSS_Y, PARTNER = range(5)


class Spread:
    def __init__(self, place, src, dst, send, recv, local, line=True):
        self.p, self.src, self.dst = place, src, dst
        self.send, self.recv, self.line = send, recv, line
        self.rows = src.shape[0]
        self.sent = []
        self.mine = place.z if line else 0
        self.around = place.near if line else [(0, None, 0, None, None)]
        self.own = pltpu.make_async_copy(src, self.at(self.mine, place.s), local)

    def at(self, m, s):
        return self.dst.at[m, pl.ds(s * self.rows, self.rows), :]

    def copy(self, direction, m, s, own=False):
        p = self.p
        device = (
            (p.s, p.z + 1),
            (p.s, p.z - 1),
            (p.sx, p.z),
            (p.sy, p.z),
            (p.partner, p.z),
        )[direction]
        return pltpu.make_async_remote_copy(
            src_ref=self.src if own else self.at(m, s),
            dst_ref=self.at(m, s),
            send_sem=self.send.at[direction, m * 4 + s // 2],
            recv_sem=self.recv.at[m * PLANE + s],
            device_id=device,
            device_id_type=MESH,
        )

    def start(self, conditions, *what, **how):
        when(conditions, lambda: self.copy(*what, **how).start())
        self.sent.append((conditions, what, how))

    def arrived(self, m, s):
        self.copy(PARTNER, m, s).wait_recv()

    def first(self):
        p, m = self.p, self.mine
        self.own.start()
        if self.line:
            self.start((p.high,), UP, m, p.s, own=True)
            self.start((p.low,), DOWN, m, p.s, own=True)
        for direction in (ACROSS_X, ACROSS_Y, PARTNER):
            self.start((), direction, m, p.s, own=True)

    def along(self, d, ok, m, odd, even):
        p = self.p
        when((ok,), lambda: self.arrived(m, p.s))
        if d < 0:
            self.start((ok, p.high), UP, m, p.s)
        else:
            self.start((ok, p.low), DOWN, m, p.s)
        for direction in (ACROSS_X, ACROSS_Y, PARTNER):
            self.start((ok,), direction, m, p.s)

    def across(self, d, ok, m, odd, even):
        p = self.p
        when((ok,), lambda: self.arrived(m, p.sx))
        if self.line:
            self.start((ok, odd), ACROSS_Y, m, p.sx)
        self.start((ok,), PARTNER, m, p.sx)
        when((ok,), lambda: self.arrived(m, p.sy))
        if self.line:
            self.start((ok, even), ACROSS_X, m, p.sy)
        else:
            self.start((), ACROSS_X, m, p.sy)
        self.start((ok,), PARTNER, m, p.sy)

    def corner(self, d, ok, m, odd, even):
        p = self.p
        when((ok,), lambda: self.arrived(m, p.sd))
        self.start((ok,), PARTNER, m, p.sd)

    def stages(self):
        part = functools.partial
        return (
            [self.first],
            [part(self.along, *one) for one in self.around[1:]],
            [part(self.across, *one) for one in self.around],
            [part(self.corner, *one) for one in self.around],
        )

    def close(self, m):
        p = self.p
        for s in (p.s, p.sx, p.sy, p.sd):
            self.arrived(m, s + p.turn)

    def settle(self):
        for conditions, what, how in self.sent:
            when(conditions, lambda: self.copy(*what, **how).wait_send())


def woven(parts):
    stages = [part.stages() for part in parts]
    steps = []
    for turn in range(len(parts) + 3):
        for i in range(len(parts)):
            if 0 <= turn - i < 4:
                steps += stages[i][turn - i]
    return steps


def spread_kernel(*refs, count, line):
    place = Place()
    srcs, dsts = refs[:count], refs[count : 2 * count]
    send, recv, local = refs[2 * count :]
    greet(place, line)
    parts = [
        Spread(place, srcs[i], dsts[i], send.at[i], recv.at[i], local.at[i], line)
        for i in range(count)
    ]
    for step in woven(parts):
        step()
    for part in parts:

        @pl.loop(0, LINE if line else 1)
        def _(m):
            part.close(m)

        part.settle()
        part.own.wait()


def spread(blocks, collective_id, name, line=True):
    count = len(blocks)
    depth = LINE if line else 1
    dma = pltpu.SemaphoreType.DMA
    return pl.pallas_call(
        functools.partial(spread_kernel, count=count, line=line),
        out_shape=[
            jax.ShapeDtypeStruct((depth, b.shape[0] * PLANE, b.shape[1]), b.dtype) for b in blocks
        ],
        in_specs=[pl.BlockSpec(memory_space=pl.ANY)] * count,
        out_specs=[pl.BlockSpec(memory_space=pl.ANY)] * count,
        scratch_shapes=[
            dma((count, 5, depth * 4)),
            dma((count, depth * PLANE)),
            dma((count,)),
        ],
        compiler_params=pltpu.CompilerParams(collective_id=collective_id, has_side_effects=True),
        name=name,
    )(*blocks)


class Line:
    def __init__(self, place, src, dst, send, recv, local):
        self.p, self.src, self.dst = place, src, dst
        self.send, self.recv = send, recv
        self.sent = []
        self.own = pltpu.make_async_copy(src, dst.at[place.z], local)

    def copy(self, up, m, own=False):
        p = self.p
        return pltpu.make_async_remote_copy(
            src_ref=self.src if own else self.dst.at[m],
            dst_ref=self.dst.at[m],
            send_sem=self.send.at[1 if up else 0, m],
            recv_sem=self.recv.at[m],
            device_id=(p.s, p.z + 1 if up else p.z - 1),
            device_id_type=MESH,
        )

    def start(self, conditions, *what, **how):
        when(conditions, lambda: self.copy(*what, **how).start())
        self.sent.append((conditions, what, how))

    def first(self):
        p = self.p
        self.own.start()
        self.start((p.high,), True, p.z, own=True)
        self.start((p.low,), False, p.z, own=True)

    def step(self, distance):
        p = self.p
        for d, ok, m, odd, even in p.near:
            if abs(d) != distance:
                continue
            when((ok,), lambda: self.copy(True, m).wait_recv())
            if d < 0:
                self.start((ok, p.high), True, m)
            else:
                self.start((ok, p.low), False, m)

    def finish_sends(self):
        for conditions, what, how in self.sent:
            when(conditions, lambda: self.copy(*what, **how).wait_send())

    def finish(self):
        self.finish_sends()
        self.own.wait()


class Collect:
    OWN, SIDE_X, SIDE_Y, CORNER = range(4)

    def __init__(self, place, grads, out, buffers, sems):
        self.p, self.grads, self.out = place, grads, out
        self.mine, self.pin, self.din, self.xin, self.yin, self.uin, self.win = buffers
        self.block_sems, self.sems = sems
        self.rows = out.shape[0]
        self.columns = (place.s, place.sx, place.sy, place.sd)

    def unit(self, c, m, turn=0):
        s = self.columns[c] + turn
        return self.grads.at[m, pl.ds(s * self.rows, self.rows), :]

    def load(self, c, m):
        return pltpu.make_async_copy(
            self.unit(c, m), self.mine.at[c, m], self.block_sems.at[0, c, m]
        )

    def remote(self, src, dst, send, recv, device):
        return pltpu.make_async_remote_copy(
            src_ref=src,
            dst_ref=dst,
            send_sem=send,
            recv_sem=recv,
            device_id=device,
            device_id_type=MESH,
        )

    def swap(self, c, m):
        p = self.p
        return self.remote(
            self.unit(c, m, p.turn),
            self.pin.at[c, m],
            self.block_sems.at[1, c, m],
            self.block_sems.at[2, c, m],
            (p.partner, p.z),
        )

    def hop(self, kind, m, by_x=True):
        p = self.p
        src, dst, device = (
            (self.CORNER, self.din, (p.sx if by_x else p.sy, p.z)),
            (self.SIDE_X, self.xin, (p.sx, p.z)),
            (self.SIDE_Y, self.yin, (p.sy, p.z)),
        )[kind]
        return self.remote(
            self.mine.at[src, m],
            dst.at[m],
            self.sems.at[kind, m],
            self.sems.at[4 + kind, m],
            device,
        )

    def climb(self, m, up):
        p = self.p
        return self.remote(
            self.mine.at[self.OWN, m],
            (self.uin if up else self.win).at[m],
            self.sems.at[3, m],
            self.sems.at[7 if up else 8, m],
            (p.s, p.z + 1 if up else p.z - 1),
        )

    def add(self, c, m, *others):
        total = self.mine[c, m].astype(F32)
        for other in others:
            total = total + other[m].astype(F32)
        self.mine[c, m] = total.astype(BF)

    def ring(self, body):
        for d in FAR:
            m = self.p.z + d
            pl.when(valid(m))(functools.partial(body, d, m))

    def begin(self):
        for c in (self.CORNER, self.SIDE_X, self.SIDE_Y, self.OWN):

            @pl.loop(0, LINE)
            def _(m):
                self.load(c, m).start()
                self.swap(c, m).start()

    def join(self, c, m):
        self.load(c, m).wait()
        self.swap(c, m).wait_recv()
        self.add(c, m, self.pin.at[c])

    def corner(self):
        def body(d, m):
            self.join(self.CORNER, m)
            even = lax.rem(m, 2) == 0
            pl.when(even)(lambda: self.hop(0, m, True).start())
            pl.when(~even)(lambda: self.hop(0, m, False).start())

        self.ring(body)

    def sides(self):
        def body(d, m):
            even = lax.rem(m, 2) == 0
            self.join(self.SIDE_X, m)
            self.join(self.SIDE_Y, m)
            pl.when(even)(lambda: self.hop(1, m).start())
            pl.when(~even)(lambda: self.hop(2, m).start())

        self.ring(body)

    def relay(self):
        def body(d, m):
            even = lax.rem(m, 2) == 0
            self.hop(0, m).wait_recv()

            @pl.when(even)
            def _():
                self.add(self.SIDE_Y, m, self.din)
                self.hop(2, m).start()

            @pl.when(~even)
            def _():
                self.add(self.SIDE_X, m, self.din)
                self.hop(1, m).start()

        self.ring(body)

    def line(self):
        p = self.p

        def body(d, m):
            self.join(self.OWN, m)
            self.hop(1, m).wait_recv()
            self.hop(2, m).wait_recv()
            self.add(self.OWN, m, self.xin, self.yin)
            if d > 0:

                @pl.when(p.low)
                def _():
                    self.climb(m, True).wait_recv()
                    self.add(self.OWN, m, self.uin)

                self.climb(m, True).start()
            elif d < 0:

                @pl.when(p.high)
                def _():
                    self.climb(m, False).wait_recv()
                    self.add(self.OWN, m, self.win)

                self.climb(m, False).start()

        self.ring(body)

    def result(self):
        p = self.p
        self.out[...] = self.mine[self.OWN, p.z].astype(F32)

        @pl.when(p.low)
        def _():
            self.climb(p.z, True).wait_recv()
            self.out[...] += self.uin[p.z].astype(F32)

        @pl.when(p.high)
        def _():
            self.climb(p.z, False).wait_recv()
            self.out[...] += self.win[p.z].astype(F32)

    def finish(self):
        for c in range(4):

            @pl.loop(0, LINE)
            def _(m):
                self.swap(c, m).wait_send()

        @pl.loop(0, LINE)
        def _(m):
            for kind in range(3):
                self.hop(kind, m).wait_send()
            pl.when(m != self.p.z)(lambda: self.climb(m, True).wait_send())


BUFFERS = ((4, LINE), (4, LINE), (LINE,), (LINE,), (LINE,), (LINE,), (LINE,))


def collect_kernel(*refs, count):
    place = Place()
    grads, rows = refs[:count], refs[count]
    outs, all_rows = refs[count + 1 : 2 * count + 1], refs[2 * count + 1]
    rest = refs[2 * count + 2 :]
    buffers, (block_sems, sems, line_send, line_recv, line_own) = rest[:-5], rest[-5:]
    greet(place)
    parts = [
        Collect(
            place, grads[i], outs[i], buffers[i :: count], (block_sems.at[i], sems.at[i])
        )
        for i in range(count)
    ]
    line = Line(place, rows, all_rows, line_send, line_recv, line_own)
    for part in parts:
        part.begin()
    for turn in range(count + 4):
        if turn == 1:
            line.first()
        elif turn == 2:
            line.step(1)
        elif turn == 4:
            line.step(2)
        elif turn == 5:
            line.step(3)
        for i in range(count):
            stage = turn - i
            if stage == 0:
                parts[i].corner()
            elif stage == 1:
                parts[i].sides()
            elif stage == 2:
                parts[i].relay()
            elif stage == 3:
                parts[i].line()
            elif stage == 4:
                parts[i].result()
    for part in parts:
        part.finish()
    line.finish()


def collect(grads, rows, collective_id):
    count = len(grads)
    dma = pltpu.SemaphoreType.DMA
    anywhere = pl.BlockSpec(memory_space=pl.ANY)
    blocks = [(g.shape[1] // PLANE, g.shape[2]) for g in grads]
    return pl.pallas_call(
        functools.partial(collect_kernel, count=count),
        out_shape=[jax.ShapeDtypeStruct(b, F32) for b in blocks]
        + [jax.ShapeDtypeStruct((LINE,) + rows.shape, rows.dtype)],
        in_specs=[anywhere] * (count + 1),
        out_specs=[pl.BlockSpec(memory_space=pltpu.VMEM)] * count + [anywhere],
        scratch_shapes=[pltpu.VMEM(lead + b, BF) for lead in BUFFERS for b in blocks]
        + [
            dma((count, 3, 4, LINE)),
            dma((count, 9, LINE)),
            dma((2, LINE)),
            dma((LINE,)),
            dma(()),
        ],
        compiler_params=pltpu.CompilerParams(
            collective_id=collective_id, has_side_effects=True, vmem_limit_bytes=BIG_VMEM
        ),
        name="collect_grads",
    )(*grads, rows)


def project(rows, weights, bias, local):
    return (dot(rows, weights[:, : 3 * local]) + bias[:, : 3 * local]).astype(BF)


def attend(query, keys, values, head, store, between):
    rows, local = query.shape
    half = rows // 2
    query_t = query.T * BF(1.0 / math.sqrt(head))
    value_t = values.T
    line = lax.broadcasted_iota(jnp.int32, (local, rows), 0)
    heads = []
    for h in range(local // head):
        own = (line >= h * head) & (line < (h + 1) * head)
        masked = jnp.where(own, query_t, BF(0.0))
        value_h = value_t[h * head : (h + 1) * head, :]
        parts = []
        for b in range(2):
            span = NB + (b + 1) * half
            scores = dot(keys[:span, :], masked[:, b * half : (b + 1) * half])
            key_at = lax.broadcasted_iota(jnp.int32, (half, half), 0)
            row_at = lax.broadcasted_iota(jnp.int32, (half, half), 1)
            edge = jnp.where(key_at <= row_at, scores[span - half :, :], -1e30)
            scores = jnp.concatenate([scores[: span - half, :], edge], axis=0)
            scores = jnp.exp(scores - jnp.max(scores, axis=0, keepdims=True))
            probs = (scores * (1.0 / jnp.sum(scores, axis=0, keepdims=True))).astype(BF)
            store(h, slice(0, span), slice(b * half, (b + 1) * half), probs)
            parts.append(dot(value_h[:, :span], probs))
        heads.append(jnp.concatenate(parts, axis=1).astype(BF))
        between(h)
    return jnp.concatenate(heads, axis=0)


def gelu_parts(pre):
    square = pre * pre
    inner = jnp.tanh(GELU_SCALE * (pre + GELU_CUBIC * pre * square))
    half_up = 0.5 * (1.0 + inner)
    slope = GELU_SCALE * (1.0 + 3.0 * GELU_CUBIC * square)
    return (pre * half_up).astype(BF), half_up + 0.5 * pre * (1.0 - inner * inner) * slope


def forward_kernel(
    tokens_ref,
    past_ref,
    meta_ref,
    room_ref,
    attn_ref,
    up_ref,
    down_ref,
    wa_ref,
    wu_ref,
    wd_ref,
    out_ref,
    res_ref,
    hm_ref,
    h2_ref,
    prob_ref,
    key_ref,
    val_ref,
    query_ref,
    att_ref,
    act_ref,
    slope_ref,
    vec_ref,
    inv_ref,
    coef_ref,
    tok_ref,
    acc_ref,
    mom_ref,
    sampled_ref,
    all_sampled_ref,
    all_meta_ref,
    all_room_ref,
    coef_part_ref,
    all_coef_ref,
    wide_ref,
    past_vmem,
    flat_send,
    flat_recv,
    flat_local,
    send,
    recv,
    own_sem,
    line_send,
    line_recv,
    line_own,
    load_sem,
    *,
    items,
    head,
):
    step = pl.program_id(0)
    rows, width = tok_ref.shape
    local = query_ref.shape[2]
    place = Place()
    flat = [
        Spread(
            place, src, dst, flat_send.at[i], flat_recv.at[i], flat_local.at[i], line=False
        )
        for i, (src, dst) in enumerate(
            ((sampled_ref, all_sampled_ref), (meta_ref, all_meta_ref))
        )
    ]
    wide = [
        Spread(place, src, dst, send.at[i], recv.at[i], own_sem.at[i])
        for i, (src, dst) in enumerate(
            ((room_ref, all_room_ref), (attn_ref, wa_ref), (up_ref, wu_ref), (down_ref, wd_ref))
        )
    ]
    room, attn, up, down = wide
    line = Line(place, coef_part_ref, all_coef_ref, line_send, line_recv, line_own)

    attn_at = SOLVE_STEPS
    mlp_at = attn_at + LINE
    last = mlp_at + LINE - 1
    steps = woven(wide)
    plan = {}
    done = 0
    for slot, upto in transfer_plan(len(steps)):
        plan[slot] = steps[done:upto]
        done = upto
    plan[(mlp_at, 0)] = steps[done:]

    def transfers(at, position):
        if plan.get((at, position)):

            @pl.when(step == at)
            def _():
                for one in plan[(at, position)]:
                    one()

    def load(ref, m, slot, which):
        return pltpu.make_async_copy(ref.at[m], wide_ref.at[slot, which], load_sem.at[slot, which])

    @pl.when(step == 0)
    def _():
        bring_tok = pltpu.make_async_copy(
            tokens_ref.at[pl.ds(place.z * rows, rows), :], tok_ref, load_sem.at[0, 0]
        )
        bring_past = pltpu.make_async_copy(past_ref, past_vmem, load_sem.at[0, 1])
        bring_tok.start()
        bring_past.start()
        greet(place)
        bring_past.wait()
        sampled_ref[...] = pick_samples(past_vmem[...], meta_ref[...], items)
        for part in flat:
            part.stages()[0][0]()
        bring_tok.wait()
        acc_ref[...] = jnp.zeros_like(acc_ref)
        clear_moments(inv_ref, mom_ref)

    transfers(0, 0)

    @pl.when(step == 1)
    def _():
        for stage in (2, 3):
            for part in flat:
                part.stages()[stage][0]()
        for part in flat:
            part.close(0)

    transfers(1, 0)

    @pl.when(step == 1)
    def _():
        for part in flat:
            part.own.wait()

        def owner(s, carry):
            count = sampled_ref.shape[0]
            samples = all_sampled_ref[0, pl.ds(s * count, count), :]
            gather_moments(
                samples, all_meta_ref[0, pl.ds(s * 8, 8), :], inv_ref, mom_ref, items
            )
            return carry

        lax.fori_loop(0, PLANE, owner, 0)

    transfers(1, 1)

    inverse_end = 2 + NB // PIVOTS

    @pl.when((step >= 2) & (step < inverse_end))
    def _():
        invert_step(inv_ref)

    for at in range(2, inverse_end):
        transfers(at, 0)

    @pl.when(step == inverse_end)
    def _():
        coef_part_ref[...] = coefficients(inv_ref, mom_ref).astype(BF)
        line.first()

    transfers(inverse_end, 0)

    @pl.when(step == inverse_end)
    def _():
        line.step(1)
        room.own.wait()
        for m in range(LINE):
            room.close(m)
            total = all_room_ref[m, 0:16, :].astype(F32)
            for s in range(1, PLANE):
                total = total + all_room_ref[m, s * 16 : (s + 1) * 16, :].astype(F32)
            vec_ref[m] = total
        gain, bias = vec_ref[0, 0:1, :], vec_ref[0, 1:2, :]
        normed, _ = norm_parts(tok_ref[...].astype(F32))
        hm_ref[NB:, :] = (normed * gain + bias).astype(BF)
        line.step(2)
        attn.own.wait()
        attn.close(0)
        load(wa_ref, 0, 0, 0).start()
        line.step(3)
        line.own.wait()
        for m in range(LINE):
            coef_ref[:, m * local : (m + 1) * local] = all_coef_ref[m]
        normed, _ = norm_parts(coef_ref[...].astype(F32))
        hm_ref[0:NB, :] = (normed * gain + bias).astype(BF)

    @pl.when((step >= attn_at) & (step < mlp_at))
    def _():
        m = step - attn_at
        slot = lax.rem(m, 2)
        load(wa_ref, m, slot, 0).wait()

        @pl.when(m < LINE - 1)
        def _():
            attn.close(m + 1)
            load(wa_ref, m + 1, 1 - slot, 0).start()

        weights = wide_ref[slot, 0]
        projected = project(hm_ref[...], weights, vec_ref[m, 6:7, :], local)
        query = projected[NB:, :local]
        keys = projected[:, local : 2 * local]
        values = projected[:, 2 * local :]
        query_ref[0] = query
        key_ref[0] = keys
        val_ref[0] = values

        def store(h, lines, columns, probs):
            prob_ref[0, h, lines, columns] = probs

        def between(h):
            for at in range(attn_at, mlp_at):
                transfers(at, h)

        attended = attend(query, keys, values, head, store, between)
        att_ref[0] = attended
        acc_ref[...] += dot_nt(attended.T, wide_ref[slot, 0, :, 3 * local :])

    transfers(mlp_at, 0)

    @pl.when(step == mlp_at)
    def _():
        for part in (up, down):
            part.own.wait()
            part.close(0)
        load(wu_ref, 0, 0, 0).start()
        load(wd_ref, 0, 0, 1).start()
        residual = tok_ref[...].astype(F32) + acc_ref[...] + vec_ref[0, 4:5, :]
        res_ref[...] = residual
        normed, _ = norm_parts(residual)
        h2_ref[...] = (normed * vec_ref[0, 2:3, :] + vec_ref[0, 3:4, :]).astype(BF)
        acc_ref[...] = jnp.zeros_like(acc_ref)

    @pl.when(step >= mlp_at)
    def _():
        m = step - mlp_at
        slot = lax.rem(m, 2)
        load(wu_ref, m, slot, 0).wait()
        load(wd_ref, m, slot, 1).wait()

        @pl.when(m < LINE - 1)
        def _():
            up.close(m + 1)
            down.close(m + 1)
            load(wu_ref, m + 1, 1 - slot, 0).start()
            load(wd_ref, m + 1, 1 - slot, 1).start()

        pre = dot(h2_ref[...], wide_ref[slot, 0]) + vec_ref[m, 7:8, :]
        act, slope = gelu_parts(pre)
        act_ref[0] = act
        slope_ref[0] = slope.astype(BF)
        acc_ref[...] += dot_nt(act, wide_ref[slot, 1])

    @pl.when(step == last)
    def _():
        out_ref[...] = (res_ref[...] + acc_ref[...] + vec_ref[0, 5:6, :]).astype(BF)
        for part in flat + wide:
            part.settle()
        line.finish_sends()


SOLVE_STEPS = 3 + NB // PIVOTS


def transfer_plan(count):
    attn_at = SOLVE_STEPS
    slots = [((0, 0), 0.06), ((1, 0), 0.16), ((1, 1), 0.26)]
    inverse_end = 2 + NB // PIVOTS
    for i in range(2, inverse_end):
        slots.append(((i, 0), 0.26 + 0.44 * (i - 1) / (inverse_end - 2)))
    slots.append(((inverse_end, 0), 0.76))
    for i in range(LINE):
        for h in range(3):
            slots.append(((attn_at + i, h), 0.76 + 0.24 * (3 * i + h + 1) / (3 * LINE)))
    return [(slot, round(count * share)) for slot, share in slots]


def forward_pass(tokens, past, meta, room, attn, up, down, head):
    width = tokens.shape[1]
    rows = tokens.shape[0] // LINE
    items = past.shape[0]
    local = width // LINE
    hidden = up.shape[1]
    heads = local // head
    keyed = NB + rows
    samples = items * meta.shape[1]
    attn_at = SOLVE_STEPS
    mlp_at = attn_at + LINE
    first = lambda i: jnp.clip(i - attn_at, 0, LINE - 1)
    second = lambda i: jnp.clip(i - mlp_at, 0, LINE - 1)
    whole = lambda shape: pl.BlockSpec(shape, lambda i: (0,) * len(shape))
    anywhere = pl.BlockSpec(memory_space=pl.ANY)
    vmem = pl.BlockSpec(memory_space=pltpu.VMEM)
    dma = pltpu.SemaphoreType.DMA
    shape = jax.ShapeDtypeStruct
    return pl.pallas_call(
        functools.partial(forward_kernel, items=items, head=head),
        grid=(mlp_at + LINE,),
        in_specs=[anywhere, anywhere, vmem, vmem, anywhere, anywhere, anywhere],
        out_specs=[
            anywhere,
            anywhere,
            anywhere,
            whole((rows, width)),
            whole((rows, width)),
            whole((keyed, width)),
            whole((rows, width)),
            pl.BlockSpec((1, heads, keyed, rows), lambda i: (first(i), 0, 0, 0)),
            pl.BlockSpec((1, keyed, local), lambda i: (first(i), 0, 0)),
            pl.BlockSpec((1, keyed, local), lambda i: (first(i), 0, 0)),
            pl.BlockSpec((1, rows, local), lambda i: (first(i), 0, 0)),
            pl.BlockSpec((1, local, rows), lambda i: (first(i), 0, 0)),
            pl.BlockSpec((1, rows, hidden), lambda i: (second(i), 0, 0)),
            pl.BlockSpec((1, rows, hidden), lambda i: (second(i), 0, 0)),
            whole((LINE, 16, width)),
            whole((NB, NB)),
            whole((NB, width)),
        ],
        out_shape=[
            shape((LINE, width, width), BF),
            shape((LINE, width, hidden), BF),
            shape((LINE, width, hidden), BF),
            shape((rows, width), BF),
            shape((rows, width), F32),
            shape((keyed, width), BF),
            shape((rows, width), BF),
            shape((LINE, heads, keyed, rows), BF),
            shape((LINE, keyed, local), BF),
            shape((LINE, keyed, local), BF),
            shape((LINE, rows, local), BF),
            shape((LINE, local, rows), BF),
            shape((LINE, rows, hidden), BF),
            shape((LINE, rows, hidden), BF),
            shape((LINE, 16, width), F32),
            shape((NB, NB), F32),
            shape((NB, width), BF),
        ],
        scratch_shapes=[
            pltpu.VMEM((rows, width), BF),
            pltpu.VMEM((rows, width), F32),
            pltpu.VMEM((NB, local), F32),
            pltpu.VMEM((samples, local), BF),
            pltpu.VMEM((1, PLANE * samples, local), BF),
            pltpu.VMEM((1, PLANE * 8, meta.shape[1]), F32),
            pltpu.VMEM((LINE, PLANE * 16, width), BF),
            pltpu.VMEM((NB, local), BF),
            pltpu.VMEM((LINE, NB, local), BF),
            pltpu.VMEM((2, 2, width, width), BF),
            pltpu.VMEM(past.shape, BF),
            dma((2, 5, 4)),
            dma((2, PLANE)),
            dma((2,)),
            dma((4, 5, LINE * 4)),
            dma((4, LINE * PLANE)),
            dma((4,)),
            dma((2, LINE)),
            dma((LINE,)),
            dma(()),
            dma((2, 2)),
        ],
        compiler_params=pltpu.CompilerParams(
            collective_id=1, has_side_effects=True, vmem_limit_bytes=BIG_VMEM
        ),
        name="forward_pass",
    )(tokens, past, meta, room, attn, up, down)


def plain_forward_kernel(
    tok_ref,
    coef_ref,
    vec_ref,
    wa_ref,
    wu_ref,
    wd_ref,
    out_ref,
    res_ref,
    hm_ref,
    h2_ref,
    prob_ref,
    key_ref,
    val_ref,
    query_ref,
    att_ref,
    act_ref,
    slope_ref,
    acc_ref,
    *,
    groups,
    head,
):
    step = pl.program_id(0)
    rows, width = tok_ref.shape
    local = query_ref.shape[2]

    @pl.when(step == 0)
    def _():
        gain, bias = vec_ref[0, 0:1, :], vec_ref[0, 1:2, :]
        normed, _ = norm_parts(coef_ref[...].astype(F32))
        hm_ref[0:NB, :] = (normed * gain + bias).astype(BF)
        normed, _ = norm_parts(tok_ref[...].astype(F32))
        hm_ref[NB:, :] = (normed * gain + bias).astype(BF)
        acc_ref[...] = jnp.zeros_like(acc_ref)

    @pl.when(step < groups)
    def _():
        weights = wa_ref[0]
        projected = project(hm_ref[...], weights, vec_ref[step, 6:7, :], local)
        query = projected[NB:, :local]
        keys = projected[:, local : 2 * local]
        values = projected[:, 2 * local :]
        query_ref[0] = query
        key_ref[0] = keys
        val_ref[0] = values

        def store(h, lines, columns, probs):
            prob_ref[0, h, lines, columns] = probs

        attended = attend(query, keys, values, head, store, lambda h: None)
        att_ref[0] = attended
        acc_ref[...] += dot_nt(attended.T, weights[:, 3 * local :])

    @pl.when(step == groups)
    def _():
        residual = tok_ref[...].astype(F32) + acc_ref[...] + vec_ref[0, 4:5, :]
        res_ref[...] = residual
        normed, _ = norm_parts(residual)
        h2_ref[...] = (normed * vec_ref[0, 2:3, :] + vec_ref[0, 3:4, :]).astype(BF)
        acc_ref[...] = jnp.zeros_like(acc_ref)

    @pl.when(step >= groups)
    def _():
        pre = dot(h2_ref[...], wu_ref[0]) + vec_ref[step - groups, 7:8, :]
        act, slope = gelu_parts(pre)
        act_ref[0] = act
        slope_ref[0] = slope.astype(BF)
        acc_ref[...] += dot_nt(act, wd_ref[0])

    @pl.when(step == 2 * groups - 1)
    def _():
        out_ref[...] = (res_ref[...] + acc_ref[...] + vec_ref[0, 5:6, :]).astype(BF)


def plain_forward(tok, coef, vec, wide, head):
    rows, width = tok.shape
    groups = wide[0].shape[0]
    local = width // groups
    hidden = wide[1].shape[2]
    heads = local // head
    keyed = NB + rows
    first = lambda i: jnp.minimum(i, groups - 1)
    second = lambda i: jnp.maximum(i - groups, 0)
    whole = lambda shape: pl.BlockSpec(shape, lambda i: (0,) * len(shape))
    shape = jax.ShapeDtypeStruct
    return pl.pallas_call(
        functools.partial(plain_forward_kernel, groups=groups, head=head),
        grid=(2 * groups,),
        in_specs=[
            whole((rows, width)),
            whole((NB, width)),
            whole((groups, 16, width)),
            pl.BlockSpec((1, width, width), lambda i: (first(i), 0, 0)),
            pl.BlockSpec((1, width, hidden), lambda i: (second(i), 0, 0)),
            pl.BlockSpec((1, width, hidden), lambda i: (second(i), 0, 0)),
        ],
        out_specs=[
            whole((rows, width)),
            whole((rows, width)),
            whole((keyed, width)),
            whole((rows, width)),
            pl.BlockSpec((1, heads, keyed, rows), lambda i: (first(i), 0, 0, 0)),
            pl.BlockSpec((1, keyed, local), lambda i: (first(i), 0, 0)),
            pl.BlockSpec((1, keyed, local), lambda i: (first(i), 0, 0)),
            pl.BlockSpec((1, rows, local), lambda i: (first(i), 0, 0)),
            pl.BlockSpec((1, local, rows), lambda i: (first(i), 0, 0)),
            pl.BlockSpec((1, rows, hidden), lambda i: (second(i), 0, 0)),
            pl.BlockSpec((1, rows, hidden), lambda i: (second(i), 0, 0)),
        ],
        out_shape=[
            shape((rows, width), BF),
            shape((rows, width), F32),
            shape((keyed, width), BF),
            shape((rows, width), BF),
            shape((groups, heads, keyed, rows), BF),
            shape((groups, keyed, local), BF),
            shape((groups, keyed, local), BF),
            shape((groups, rows, local), BF),
            shape((groups, local, rows), BF),
            shape((groups, rows, hidden), BF),
            shape((groups, rows, hidden), BF),
        ],
        scratch_shapes=[pltpu.VMEM((rows, width), F32)],
        compiler_params=pltpu.CompilerParams(vmem_limit_bytes=BIG_VMEM),
        name="plain_forward",
    )(tok, coef, vec, *wide)


def backward_kernel(
    tok_ref,
    cot_ref,
    res_ref,
    vec_ref,
    hm_ref,
    h2_ref,
    prob_ref,
    key_ref,
    val_ref,
    query_ref,
    att_ref,
    act_ref,
    slope_ref,
    wa_ref,
    wu_ref,
    wd_ref,
    tg_ref,
    gmem_ref,
    gup_ref,
    gdown_ref,
    gatt_ref,
    gv_ref,
    ggv_ref,
    acc_ref,
    hmt_ref,
    h2t_ref,
    cott_ref,
    gres_ref,
    proj_ref,
    *,
    groups,
    head,
):
    step = pl.program_id(0)
    rows, width = tok_ref.shape
    local = query_ref.shape[2]
    half = rows // 2

    @pl.when(step == 0)
    def _():
        acc_ref[...] = jnp.zeros_like(acc_ref)
        h2t_ref[...] = h2_ref[...].T
        cott_ref[...] = cot_ref[...].T
        gv_ref[...] = jnp.zeros_like(gv_ref)

    @pl.when(step < groups)
    def _():
        upstream = cot_ref[...]
        grad = (dot(upstream, wd_ref[0]) * slope_ref[0].astype(F32)).astype(BF)
        gdown_ref[0] = dot(cott_ref[...], act_ref[0]).astype(BF)
        gup_ref[0] = dot(h2t_ref[...], grad).astype(BF)
        ggv_ref[0] = jnp.zeros_like(ggv_ref[0])
        ggv_ref[0, 0:1, :] = col_sum(grad.astype(F32))
        acc_ref[NB:, :] += dot_nt(grad, wu_ref[0])

    @pl.when(step == groups)
    def _():
        upstream = cot_ref[...].astype(F32)
        normed, inverse = norm_parts(res_ref[...])
        grad = acc_ref[NB:, :]
        g_res = upstream + norm_back(grad, normed, inverse, vec_ref[2:3, :])
        gres_ref[...] = g_res
        g_attn = g_res.astype(BF)
        gv_ref[2:3, :] = col_sum(grad * normed)
        gv_ref[3:4, :] = col_sum(grad)
        gv_ref[4:5, :] = col_sum(g_attn.astype(F32))
        gv_ref[5:6, :] = col_sum(upstream)
        cott_ref[...] = g_attn.T
        hmt_ref[...] = hm_ref[...].T
        acc_ref[...] = jnp.zeros_like(acc_ref)
        proj_ref[0:NB, :] = jnp.zeros((NB, proj_ref.shape[1]), BF)

    @pl.when(step >= groups)
    def _():
        weights = wa_ref[0]
        g_attn = gres_ref[...].astype(BF)
        g_att = dot(g_attn, weights[:, 3 * local :]).astype(BF)
        g_att_t = g_att.T
        att_t = att_ref[0]
        product = g_att_t.astype(F32) * att_t.astype(F32)
        keys, values, query = key_ref[0], val_ref[0], query_ref[0]
        key_t = keys.T
        scale = 1.0 / math.sqrt(head)
        line = lax.broadcasted_iota(jnp.int32, (local, rows), 0)
        lane = lax.broadcasted_iota(jnp.int32, (rows, local), 1)
        key_grad = [jnp.zeros((NB + rows - half, local), F32), jnp.zeros((half, local), F32)]
        val_grad = [jnp.zeros((NB + rows - half, local), F32), jnp.zeros((half, local), F32)]
        query_grads = []
        for h in range(local // head):
            own_t = (line >= h * head) & (line < (h + 1) * head)
            own = (lane >= h * head) & (lane < (h + 1) * head)
            grad_t = jnp.where(own_t, g_att_t, BF(0.0))
            grad_h = jnp.where(own, g_att, BF(0.0))
            query_h = jnp.where(own, query, BF(0.0))
            inner = jnp.sum(product[h * head : (h + 1) * head, :], axis=0, keepdims=True)
            key_h = key_t[h * head : (h + 1) * head, :]
            parts = []
            for b in range(2):
                span = NB + (b + 1) * half
                cols = slice(b * half, (b + 1) * half)
                probs = prob_ref[0, h, 0:span, cols]
                dprob = dot(values[:span, :], grad_t[:, cols])
                dscore = (probs.astype(F32) * (dprob - inner[:, cols])).astype(BF)
                parts.append(dot(key_h[:, :span], dscore))
                val_part = dot(probs, grad_h[cols, :])
                key_part = dot(dscore, query_h[cols, :])
                low = NB + rows - half
                val_grad[0] = val_grad[0] + val_part[:low, :]
                key_grad[0] = key_grad[0] + key_part[:low, :]
                if b == 1:
                    val_grad[1] = val_grad[1] + val_part[low:, :]
                    key_grad[1] = key_grad[1] + key_part[low:, :]
            query_grads.append(jnp.concatenate(parts, axis=1))
        query_grad = (jnp.concatenate(query_grads, axis=0) * scale).astype(BF).T
        key_grad = (jnp.concatenate(key_grad, axis=0) * scale).astype(BF)
        val_sum = jnp.concatenate(val_grad, axis=0)
        val_grad = val_sum.astype(BF)
        proj_ref[NB:, 0:local] = query_grad
        proj_ref[:, local : 2 * local] = key_grad
        proj_ref[:, 2 * local :] = val_grad
        proj = proj_ref[...]
        ggv_ref[0] = jnp.zeros_like(ggv_ref[0])
        ggv_ref[0, 0:1, 0 : 3 * local] = col_sum(proj.astype(F32))
        gatt_ref[0, :, 0 : 3 * local] = dot(hmt_ref[...], proj).astype(BF)
        gatt_ref[0, :, 3 * local :] = dot_nt(cott_ref[...], att_t).astype(BF)
        acc_ref[...] += dot_nt(proj, weights[:, : 3 * local])

    @pl.when(step == 2 * groups - 1)
    def _():
        gmem_ref[...] = acc_ref[0:NB, :]
        grad = acc_ref[NB:, :]
        normed, inverse = norm_parts(tok_ref[...].astype(F32))
        part = norm_back(grad, normed, inverse, vec_ref[0:1, :])
        tg_ref[...] = (gres_ref[...] + part).astype(BF)
        gv_ref[0:1, :] = col_sum(grad * normed)
        gv_ref[1:2, :] = col_sum(grad)


def backward_pass(tok, cot, vec, saved, wide, head):
    res, hm, h2, prob, keys, vals, query, att, act, slope = saved
    rows, width = tok.shape
    groups = wide[0].shape[0]
    local = width // groups
    hidden = wide[1].shape[2]
    heads = local // head
    keyed = NB + rows
    first = lambda i: jnp.minimum(i, groups - 1)
    second = lambda i: jnp.maximum(i - groups, 0)
    whole = lambda shape: pl.BlockSpec(shape, lambda i: (0,) * len(shape))
    return pl.pallas_call(
        functools.partial(backward_kernel, groups=groups, head=head),
        grid=(2 * groups,),
        in_specs=[
            whole((rows, width)),
            whole((rows, width)),
            whole((rows, width)),
            whole((16, width)),
            whole((keyed, width)),
            whole((rows, width)),
            pl.BlockSpec((1, heads, keyed, rows), lambda i: (second(i), 0, 0, 0)),
            pl.BlockSpec((1, keyed, local), lambda i: (second(i), 0, 0)),
            pl.BlockSpec((1, keyed, local), lambda i: (second(i), 0, 0)),
            pl.BlockSpec((1, rows, local), lambda i: (second(i), 0, 0)),
            pl.BlockSpec((1, local, rows), lambda i: (second(i), 0, 0)),
            pl.BlockSpec((1, rows, hidden), lambda i: (first(i), 0, 0)),
            pl.BlockSpec((1, rows, hidden), lambda i: (first(i), 0, 0)),
            pl.BlockSpec((1, width, width), lambda i: (second(i), 0, 0)),
            pl.BlockSpec((1, width, hidden), lambda i: (first(i), 0, 0)),
            pl.BlockSpec((1, width, hidden), lambda i: (first(i), 0, 0)),
        ],
        out_specs=[
            whole((rows, width)),
            whole((NB, width)),
            pl.BlockSpec((1, width, hidden), lambda i: (first(i), 0, 0)),
            pl.BlockSpec((1, width, hidden), lambda i: (first(i), 0, 0)),
            pl.BlockSpec((1, width, width), lambda i: (second(i), 0, 0)),
            whole((8, width)),
            pl.BlockSpec((1, 8, hidden), lambda i: (i, 0, 0)),
        ],
        out_shape=[
            jax.ShapeDtypeStruct((rows, width), BF),
            jax.ShapeDtypeStruct((NB, width), F32),
            jax.ShapeDtypeStruct((groups, width, hidden), BF),
            jax.ShapeDtypeStruct((groups, width, hidden), BF),
            jax.ShapeDtypeStruct((groups, width, width), BF),
            jax.ShapeDtypeStruct((8, width), F32),
            jax.ShapeDtypeStruct((2 * groups, 8, hidden), F32),
        ],
        scratch_shapes=[
            pltpu.VMEM((keyed, width), F32),
            pltpu.VMEM((width, keyed), BF),
            pltpu.VMEM((width, rows), BF),
            pltpu.VMEM((width, rows), BF),
            pltpu.VMEM((rows, width), F32),
            pltpu.VMEM((keyed, 3 * local), BF),
        ],
        compiler_params=pltpu.CompilerParams(vmem_limit_bytes=BIG_VMEM),
        name="backward_pass",
    )(
        tok, cot, res, vec, hm, h2, prob, keys, vals, query, att, act, slope, *wide
    )


def local(
    tokens,
    cotangent,
    past_state,
    positions,
    counts,
    ln1_gain,
    ln1_bias,
    w_qkv,
    b_qv,
    w_out,
    b_out,
    ln2_gain,
    ln2_bias,
    w_up,
    b_up,
    w_down,
    b_down,
):
    seq, mp = lax.axis_size("seq"), lax.axis_size("mp")
    seq_index, mp_index = lax.axis_index("seq"), lax.axis_index("mp")
    item_count, seg_len, local_width = past_state.shape
    slots = positions.shape[1]
    total = item_count * seq
    width = tokens.shape[1]
    part = width // seq
    heads_local, piece = b_qv.shape[1], b_qv.shape[2]
    head = piece * seq
    hidden = w_up.shape[1]
    rows = tokens.shape[0] // mp
    direct = seq == PLANE and mp == LINE and part % 16 == 0 and hidden == width

    items = (seq_index * item_count + jnp.arange(item_count)).astype(F32)
    spots = positions.astype(F32)
    places = (items[:, None] + (spots + 0.5) / seg_len) / total
    used = (jnp.arange(slots)[None, :] < counts[:, None]).astype(F32)
    meta = jnp.concatenate([places, used, spots, jnp.zeros((8 - 3 * item_count, slots), F32)])

    here = (jnp.arange(seq) == seq_index).astype(BF)
    vectors = jnp.stack([ln1_gain, ln1_bias, ln2_gain, ln2_bias, b_out, b_down])
    vectors = (vectors[:, None, :] * here[None, :, None]).reshape(6, width)
    bias_qv = (b_qv[:, :, None, :] * here[None, None, :, None]).reshape(2, local_width)
    bias_qv = jnp.concatenate([bias_qv, jnp.zeros((2, local_width), BF)], axis=1)
    bias_up = (b_up[:, None, :] * here[None, :, None]).reshape(1, hidden)
    room = jnp.concatenate([vectors, bias_qv.reshape(1, width), bias_up, jnp.zeros((8, width), BF)])
    attn = jnp.concatenate([w_qkv[0], w_qkv[1], w_qkv[2], w_out.T], axis=1)

    tok = lax.dynamic_slice_in_dim(tokens, mp_index * rows, rows, 0)
    cot = lax.dynamic_slice_in_dim(cotangent, mp_index * rows, rows, 0)
    if direct:
        results = forward_pass(tokens, past_state, meta, room, attn, w_up, w_down.T, head)
        wide, forward, (vec, inverse, coef) = results[:3], results[3:14], results[14:]
    else:
        sampled = sample_rows(past_state, meta)
        all_sampled = lax.all_gather(sampled, "seq", axis=0)
        all_meta = lax.all_gather(meta, "seq", axis=0)
        coef_part, inverse = solve_memory(all_sampled, all_meta, item_count)
        coef = lax.all_gather(coef_part, "mp", axis=0).transpose(1, 0, 2).reshape(NB, width)
        wide = [
            lax.all_gather(lax.all_gather(shard, "seq", axis=0, tiled=True), "mp", axis=0)
            for shard in (attn, w_up, w_down.T)
        ]
        vec = lax.psum(room.astype(F32), "seq")
        vec = lax.all_gather(vec, "mp", axis=0)
        forward = plain_forward(tok, coef, vec, wide, head)
    block_out = lax.all_gather(forward[0], "mp", axis=0, tiled=True)
    tok_grad, gmem, g_up, g_down, g_attn, gv, ggv = backward_pass(
        tok, cot, vec[0], forward[1:], wide, head
    )

    tail = jnp.concatenate(
        [jnp.broadcast_to(gv[None, :6], (mp, 6, width)), ggv[mp:, :1], ggv[:mp, :1]], axis=1
    )
    if direct:
        mem = gmem.reshape(mp, seq, 8, width)
        side = jnp.concatenate([mem, jnp.broadcast_to(tail[:, None], mem.shape)], axis=2)
        side = side.astype(BF).reshape(mp, seq * 16, width)
        side, attn, up_grad, down_grad, block_grad = collect(
            [side, g_attn, g_up, g_down], tok_grad, 2
        )
        block_grad = block_grad.reshape(mp * rows, width)
        (gmem,) = spread([side[:8]], 3, "spread_memory")
        gmem = gmem.reshape(NB, width)
        own = side[8:]
    else:
        block_grad = lax.all_gather(tok_grad, "mp", axis=0, tiled=True)
        gmem, tail = lax.psum((gmem, tail), ("seq", "mp"))
        own = lax.dynamic_index_in_dim(tail, mp_index, 0, keepdims=False)
        attn, up_grad, down_grad = (
            lax.psum_scatter(
                lax.psum_scatter(g, "mp", scatter_dimension=0, tiled=False),
                "seq",
                scatter_dimension=0,
                tiled=True,
            ).astype(F32)
            for g in (g_attn, g_up, g_down)
        )
    past_grad, gv_mem = past_grads(
        gmem, coef, vec[0], inverse, meta, item_count, seg_len, local_width
    )
    own = own + jnp.concatenate([gv_mem[:2], jnp.zeros((6, width), F32)])
    vec_own = lax.dynamic_slice_in_dim(own[:6], seq_index * part, part, 1)
    qv = jnp.stack([own[6, :local_width], own[6, 2 * local_width : 3 * local_width]])
    qv = qv.reshape(2, heads_local, head)
    qv = lax.dynamic_slice_in_dim(qv, seq_index * piece, piece, 2)
    up = lax.dynamic_slice_in_dim(own[7].reshape(-1, head), seq_index * piece, piece, 1)
    qkv_grad = jnp.stack([attn[:, i * local_width : (i + 1) * local_width] for i in range(3)])
    return (
        block_out,
        block_grad,
        past_grad,
        vec_own[0],
        vec_own[1],
        qkv_grad,
        qv,
        attn[:, 3 * local_width :].T,
        vec_own[4],
        vec_own[2],
        vec_own[3],
        up_grad,
        up,
        down_grad.T,
        vec_own[5],
    )


def solution(mesh):
    row = P("seq", None)
    placed = (
        row,
        row,
        P("seq", None, "mp"),
        row,
        P("seq"),
        P("seq"),
        P("seq"),
        P(None, "seq", "mp"),
        P(None, "mp", "seq"),
        P("mp", "seq"),
        P("seq"),
        P("seq"),
        P("seq"),
        P("seq", "mp"),
        P("mp", "seq"),
        P("mp", "seq"),
        P("seq"),
    )
    return jax.shard_map(
        local,
        mesh=mesh,
        in_specs=placed,
        out_specs=(row, row, placed[2]) + placed[5:],
        check_vma=False,
    )
```

```python
import functools
import math

import jax
import jax.numpy as jnp
from jax import lax
from jax.experimental import pallas as pl
from jax.experimental.pallas import tpu as pltpu
from jax.sharding import PartitionSpec as P

NB = 256
PIVOTS = 32
NORM_EPSILON = 1e-05
RIDGE_WEIGHT = 1.0
NARROW_WIDTH = 0.01
BROAD_WIDTH = 0.05
GELU_SCALE = 0.7978845608028654
GELU_CUBIC = 0.044715

BF = jnp.bfloat16
F32 = jnp.float32
HIGHEST = lax.Precision.HIGHEST
BIG_VMEM = 60 * 1024 * 1024
MAX_VMEM = 67043328


def dot(a, b):
    return jnp.dot(a, b, preferred_element_type=F32)


def dot_nt(a, b):
    return lax.dot_general(a, b, (((1,), (1,)), ((), ())), preferred_element_type=F32)


def dot_tn(a, b, precision=None):
    return lax.dot_general(
        a, b, (((0,), (0,)), ((), ())), preferred_element_type=F32, precision=precision
    )


def norm_parts(values):
    centered = values - jnp.mean(values, axis=-1, keepdims=True)
    inverse = lax.rsqrt(jnp.mean(centered * centered, axis=-1, keepdims=True) + NORM_EPSILON)
    return centered * inverse, inverse


def norm_back(upstream, normed, inverse, gain):
    scaled = upstream * gain
    inner = scaled - jnp.mean(scaled, axis=-1, keepdims=True)
    inner = inner - normed * jnp.mean(scaled * normed, axis=-1, keepdims=True)
    return inner * inverse


def col_sum(values):
    return jnp.sum(values, axis=0, keepdims=True)


def basis_of(places, used):
    column = lax.broadcasted_iota(jnp.int32, (places.shape[0], NB), 1)
    centers = (column.astype(F32) + 0.5) / NB
    widths = jnp.where(column % 2 == 0, NARROW_WIDTH, BROAD_WIDTH).astype(F32)
    scaled = (places - centers) / widths
    return jnp.exp(-0.5 * (scaled * scaled)) * used


def position_of(column, i, items):
    return column[:, 2 * items + i : 2 * items + i + 1].astype(jnp.int32)


def invert_step(mat_ref):
    block = PIVOTS
    lane = lax.broadcasted_iota(jnp.int32, (block, NB), 1)
    line = lax.broadcasted_iota(jnp.int32, (block, NB), 0)
    panel = mat_ref[0:block, :]
    for k in range(block):
        pivot_row = panel[k : k + 1, :]
        factor = 1.0 / pivot_row[:, k : k + 1]
        scaled = jnp.where(lane[0:1] == k, factor, pivot_row * factor)
        column = panel[:, k : k + 1]
        rest = jnp.where(lane == k, 0.0, panel) - column * scaled
        panel = jnp.where(line == k, scaled, rest)
    mat_ref[0:block, :] = panel
    row = lax.broadcasted_iota(jnp.int32, (NB, NB), 0)
    col = lax.broadcasted_iota(jnp.int32, (NB, NB), 1)
    mat = mat_ref[...]
    inside_row = row < block
    inside_col = col < block
    left = jnp.where(inside_col & ~inside_row, mat, 0.0)
    right = jnp.where(inside_row, mat, 0.0)
    update = jnp.dot(left, right, preferred_element_type=F32, precision=HIGHEST)
    mat = jnp.where(inside_row, mat, jnp.where(inside_col, 0.0, mat) - update)
    mat = pltpu.roll(mat, NB - block, 1)
    mat_ref[0 : NB - block, :] = mat[block:, :]
    mat_ref[NB - block :, :] = mat[:block, :]


def gather_moments(samples, meta, mat_ref, mom_ref, items):
    slots = meta.shape[1]
    column = meta.T
    rows = [
        basis_of(column[:, i : i + 1], column[:, items + i : items + i + 1]) for i in range(items)
    ]
    rows = jnp.concatenate(rows, axis=0)
    mat_ref[...] += dot_tn(rows, rows, HIGHEST)
    mom_ref[...] += dot_tn(rows, samples.astype(F32), HIGHEST)


def clear_moments(mat_ref, mom_ref):
    row = lax.broadcasted_iota(jnp.int32, (NB, NB), 0)
    col = lax.broadcasted_iota(jnp.int32, (NB, NB), 1)
    mat_ref[...] = jnp.where(row == col, RIDGE_WEIGHT, 0.0)
    mom_ref[...] = jnp.zeros_like(mom_ref)


def coefficients(mat_ref, mom_ref):
    return jnp.dot(mat_ref[...], mom_ref[...], preferred_element_type=F32, precision=HIGHEST)


def pick_samples(past, meta, items):
    slots, seg_len = meta.shape[1], past.shape[1]
    column = meta.T
    at = lax.broadcasted_iota(jnp.int32, (slots, seg_len), 1)
    rows = []
    for i in range(items):
        pick = (at == position_of(column, i, items)).astype(F32).astype(BF)
        rows.append(dot(pick, past[i]).astype(BF))
    return jnp.concatenate(rows, axis=0)


def sample_kernel(past_ref, meta_ref, out_ref, *, items):
    out_ref[...] = pick_samples(past_ref[...], meta_ref[...], items)


def sample_rows(past, meta):
    items, seg_len, width = past.shape
    return pl.pallas_call(
        functools.partial(sample_kernel, items=items),
        out_shape=jax.ShapeDtypeStruct((items * meta.shape[1], width), BF),
        name="sample_rows",
    )(past, meta)


def solve_kernel(sampled_ref, meta_ref, coef_ref, inv_ref, mat_ref, mom_ref, *, items):
    clear_moments(mat_ref, mom_ref)

    def owner(s, carry):
        gather_moments(sampled_ref[s], meta_ref[s], mat_ref, mom_ref, items)
        return carry

    lax.fori_loop(0, meta_ref.shape[0], owner, 0)

    def step(s, carry):
        invert_step(mat_ref)
        return carry

    lax.fori_loop(0, NB // PIVOTS, step, 0)
    inv_ref[...] = mat_ref[...]
    coef_ref[...] = coefficients(mat_ref, mom_ref).astype(BF)


def solve_memory(sampled, meta, items):
    width = sampled.shape[-1]
    return pl.pallas_call(
        functools.partial(solve_kernel, items=items),
        out_shape=(
            jax.ShapeDtypeStruct((NB, width), BF),
            jax.ShapeDtypeStruct((NB, NB), F32),
        ),
        scratch_shapes=[pltpu.VMEM((NB, NB), F32), pltpu.VMEM((NB, width), F32)],
        compiler_params=pltpu.CompilerParams(vmem_limit_bytes=BIG_VMEM),
        name="solve_memory",
    )(sampled, meta)


def give_past(gmem, coef_ref, vec_ref, inv_ref, meta_ref, out_ref, gv_ref):
    slots = meta_ref.shape[1]
    item_count, seg_len, width = out_ref.shape
    normed, inverse = norm_parts(coef_ref[...].astype(F32))
    coef_grad = norm_back(gmem, normed, inverse, vec_ref[0, 0:1, :])
    gv_ref[...] = jnp.zeros_like(gv_ref)
    gv_ref[0:1, :] = col_sum(gmem * normed)
    gv_ref[1:2, :] = col_sum(gmem)
    features = coef_grad.shape[1]
    part = lax.axis_index("mp")
    row = lax.broadcasted_iota(jnp.int32, (features, width), 0)
    col = lax.broadcasted_iota(jnp.int32, (features, width), 1)
    pick = (row == col + part * width).astype(F32)
    mine = jnp.dot(coef_grad, pick, preferred_element_type=F32, precision=HIGHEST)
    moment = jnp.dot(inv_ref[...], mine, preferred_element_type=F32, precision=HIGHEST)
    at = lax.broadcasted_iota(jnp.int32, (slots, seg_len), 1)
    column = meta_ref[...].T
    for i in range(item_count):
        rows = basis_of(column[:, i : i + 1], column[:, item_count + i : item_count + i + 1])
        sampled = jnp.dot(rows, moment, preferred_element_type=F32, precision=HIGHEST)
        spread = (at == position_of(column, i, item_count)).astype(F32)
        out_ref[i] = dot_tn(spread, sampled, HIGHEST)


def past_kernel(gmem_ref, coef_ref, vec_ref, inv_ref, meta_ref, out_ref, gv_ref):
    give_past(gmem_ref[...], coef_ref, vec_ref, inv_ref, meta_ref, out_ref, gv_ref)


def past_grads(gmem, coef, vec, inv, meta, items, seg_len, width):
    return pl.pallas_call(
        past_kernel,
        out_shape=(
            jax.ShapeDtypeStruct((items, seg_len, width), F32),
            jax.ShapeDtypeStruct((8, coef.shape[1]), F32),
        ),
        compiler_params=pltpu.CompilerParams(vmem_limit_bytes=BIG_VMEM),
        name="past_grads",
    )(gmem, coef, vec, inv, meta)


MESH = pl.DeviceIdType.MESH
LINE = 4
PLANE = 8
NEAR = (0, -1, 1, -2, 2, -3, 3)


class Place:
    def __init__(self):
        self.s = lax.axis_index("seq")
        self.z = lax.axis_index("mp")
        core = lax.rem(self.s, 2)
        x = lax.rem(self.s // 2, 2)
        y = self.s // 4
        self.turn = 1 - 2 * core
        self.partner = self.s + self.turn
        self.sx = self.s + 2 - 4 * x
        self.sy = self.s + 4 - 8 * y
        self.sd = self.sx + 4 - 8 * y
        self.low = self.z > 0
        self.high = self.z < LINE - 1
        self.near = [
            (
                d,
                valid(self.z + d),
                self.z + d,
                lax.rem(self.z + d + LINE, 2) == 1,
                lax.rem(self.z + d + LINE, 2) == 0,
            )
            for d in NEAR
        ]


def valid(m):
    return (m >= 0) & (m < LINE)


def when(conditions, act):
    conditions = [c for c in conditions if c is not None]
    if conditions:
        pl.when(functools.reduce(lambda a, b: a & b, conditions))(act)
    else:
        act()


def greet(place, line=True, plane=True):
    barrier = pltpu.get_barrier_semaphore()

    def signal(seq, z):
        pl.semaphore_signal(barrier, inc=1, device_id=(seq, z), device_id_type=MESH)

    if plane:
        for seq in (place.partner, place.sx, place.sy):
            signal(seq, place.z)
    if line:
        pl.when(place.low)(lambda: signal(place.s, place.z - 1))
        pl.when(place.high)(lambda: signal(place.s, place.z + 1))
    peers = 3 if plane else 0
    if line:
        peers = peers + (place.z + LINE - 1) // LINE + (2 * LINE - 2 - place.z) // LINE
    pl.semaphore_wait(barrier, peers)


UP, DOWN, ACROSS_X, ACROSS_Y, PARTNER = range(5)


class Spread:
    def __init__(self, place, src, dst, send, recv, local, line=True):
        self.p, self.src, self.dst = place, src, dst
        self.send, self.recv, self.line = send, recv, line
        self.rows = src.shape[0]
        self.sent = []
        self.mine = place.z if line else 0
        self.around = place.near if line else [(0, None, 0, None, None)]
        self.own = pltpu.make_async_copy(src, self.at(self.mine, place.s), local)

    def at(self, m, s):
        return self.dst.at[m, pl.ds(s * self.rows, self.rows), :]

    def copy(self, direction, m, s, own=False):
        p = self.p
        device = (
            (p.s, p.z + 1),
            (p.s, p.z - 1),
            (p.sx, p.z),
            (p.sy, p.z),
            (p.partner, p.z),
        )[direction]
        return pltpu.make_async_remote_copy(
            src_ref=self.src if own else self.at(m, s),
            dst_ref=self.at(m, s),
            send_sem=self.send.at[direction, m * 4 + s // 2],
            recv_sem=self.recv.at[m * PLANE + s],
            device_id=device,
            device_id_type=MESH,
        )

    def start(self, conditions, *what, **how):
        when(conditions, lambda: self.copy(*what, **how).start())
        self.sent.append((conditions, what, how))

    def arrived(self, m, s):
        self.copy(PARTNER, m, s).wait_recv()

    def first(self):
        p, m = self.p, self.mine
        self.own.start()
        if self.line:
            self.start((p.high,), UP, m, p.s, own=True)
            self.start((p.low,), DOWN, m, p.s, own=True)
        for direction in (ACROSS_X, ACROSS_Y, PARTNER):
            self.start((), direction, m, p.s, own=True)

    def along(self, d, ok, m, odd, even):
        p = self.p
        when((ok,), lambda: self.arrived(m, p.s))
        if d < 0:
            self.start((ok, p.high), UP, m, p.s)
        else:
            self.start((ok, p.low), DOWN, m, p.s)
        for direction in (ACROSS_X, ACROSS_Y, PARTNER):
            self.start((ok,), direction, m, p.s)

    def across(self, d, ok, m, odd, even):
        p = self.p
        when((ok,), lambda: self.arrived(m, p.sx))
        if self.line:
            self.start((ok, odd), ACROSS_Y, m, p.sx)
        self.start((ok,), PARTNER, m, p.sx)
        when((ok,), lambda: self.arrived(m, p.sy))
        if self.line:
            self.start((ok, even), ACROSS_X, m, p.sy)
        else:
            self.start((), ACROSS_X, m, p.sy)
        self.start((ok,), PARTNER, m, p.sy)

    def corner(self, d, ok, m, odd, even):
        p = self.p
        when((ok,), lambda: self.arrived(m, p.sd))
        self.start((ok,), PARTNER, m, p.sd)

    def stages(self):
        part = functools.partial
        return (
            [self.first],
            [part(self.along, *one) for one in self.around[1:]],
            [part(self.across, *one) for one in self.around],
            [part(self.corner, *one) for one in self.around],
        )

    def close(self, m):
        p = self.p
        for s in (p.s, p.sx, p.sy, p.sd):
            self.arrived(m, s + p.turn)

    def settle(self):
        for conditions, what, how in self.sent:
            when(conditions, lambda: self.copy(*what, **how).wait_send())


def woven(parts):
    stages = [part.stages() for part in parts]
    steps = []
    for turn in range(len(parts) + 3):
        for i in range(len(parts)):
            if 0 <= turn - i < 4:
                steps += stages[i][turn - i]
    return steps


class Line:
    def __init__(self, place, src, dst, send, recv, local):
        self.p, self.src, self.dst = place, src, dst
        self.send, self.recv = send, recv
        self.sent = []
        self.own = pltpu.make_async_copy(src, dst.at[place.z], local)

    def copy(self, up, m, own=False):
        p = self.p
        return pltpu.make_async_remote_copy(
            src_ref=self.src if own else self.dst.at[m],
            dst_ref=self.dst.at[m],
            send_sem=self.send.at[1 if up else 0, m],
            recv_sem=self.recv.at[m],
            device_id=(p.s, p.z + 1 if up else p.z - 1),
            device_id_type=MESH,
        )

    def start(self, conditions, *what, **how):
        when(conditions, lambda: self.copy(*what, **how).start())
        self.sent.append((conditions, what, how))

    def first(self):
        p = self.p
        self.own.start()
        self.start((p.high,), True, p.z, own=True)
        self.start((p.low,), False, p.z, own=True)

    def step(self, distance):
        p = self.p
        for d, ok, m, odd, even in p.near:
            if abs(d) != distance:
                continue
            when((ok,), lambda: self.copy(True, m).wait_recv())
            if d < 0:
                self.start((ok, p.high), True, m)
            else:
                self.start((ok, p.low), False, m)

    def finish_sends(self):
        for conditions, what, how in self.sent:
            when(conditions, lambda: self.copy(*what, **how).wait_send())

    def finish(self):
        self.finish_sends()
        self.own.wait()


class Collect:
    OWN, SIDE_X, SIDE_Y, CORNER = range(4)

    def __init__(self, place, grads, out, buffers, sems):
        self.p, self.grads, self.out = place, grads, out
        self.pin, self.din, self.xin, self.yin, self.zin = buffers
        self.block_sems, self.sems = sems
        self.rows = out.shape[1]
        self.columns = (place.s, place.sx, place.sy, place.sd)

    def plane(self, i):
        upper = self.p.z // 2
        return (1 - upper) * (LINE - 1 - i) + upper * i

    def unit(self, c, m, turn=0):
        s = self.columns[c] + turn
        return self.grads.at[m, :, pl.ds(s * self.rows, self.rows), :]

    def remote(self, src, dst, send, recv, device):
        return pltpu.make_async_remote_copy(
            src_ref=src,
            dst_ref=dst,
            send_sem=send,
            recv_sem=recv,
            device_id=device,
            device_id_type=MESH,
        )

    def swap(self, c, m):
        p = self.p
        return self.remote(
            self.unit(c, m, p.turn),
            self.pin.at[c, m],
            self.block_sems.at[0, c, m],
            self.block_sems.at[1, c, m],
            (p.partner, p.z),
        )

    def hop(self, kind, m, by_x=True):
        p = self.p
        src, dst, device = (
            (self.CORNER, self.din, (p.sx if by_x else p.sy, p.z)),
            (self.SIDE_X, self.xin, (p.sx, p.z)),
            (self.SIDE_Y, self.yin, (p.sy, p.z)),
        )[kind]
        return self.remote(
            self.unit(src, m),
            dst.at[m],
            self.sems.at[kind, m],
            self.sems.at[4 + kind, m],
            device,
        )

    def slot(self, m, z):
        ends = 1 // (1 + z - m)
        return m + (LINE - m) * ends

    def climb(self, m, up):
        p = self.p
        return self.remote(
            self.unit(self.OWN, m),
            self.zin.at[m if up else self.slot(m, p.z - 1)],
            self.sems.at[3, m],
            self.sems.at[7 if up else 8, m],
            (p.s, p.z + 1 if up else p.z - 1),
        )

    def climbed(self, m, up):
        zin = self.zin.at[m if up else self.slot(m, self.p.z)]
        return self.remote(
            zin, zin, self.sems.at[3, m], self.sems.at[7 if up else 8, m], (self.p.partner, self.p.z)
        )

    def add(self, c, m, *others):
        mine = self.unit(c, m)
        total = mine[...].astype(F32)
        for other in others:
            total = total + other[m].astype(F32)
        mine[...] = total.astype(BF)

    def begin(self, m):
        for c in (self.CORNER, self.SIDE_X, self.SIDE_Y, self.OWN):
            self.swap(c, m).start()

    def join(self, c, m):
        self.swap(c, m).wait_recv()
        self.add(c, m, self.pin.at[c])

    def corner(self, i):
        m = self.plane(i)
        self.join(self.CORNER, m)
        even = lax.rem(m, 2) == 0
        pl.when(even)(lambda: self.hop(0, m, True).start())
        pl.when(~even)(lambda: self.hop(0, m, False).start())

    def sides(self, i):
        m = self.plane(i)
        even = lax.rem(m, 2) == 0
        self.join(self.SIDE_X, m)
        self.join(self.SIDE_Y, m)
        pl.when(even)(lambda: self.hop(1, m).start())
        pl.when(~even)(lambda: self.hop(2, m).start())

    def relay(self, i):
        m = self.plane(i)
        even = lax.rem(m, 2) == 0
        self.hop(0, m).wait_recv()

        @pl.when(even)
        def _():
            self.add(self.SIDE_Y, m, self.din)
            self.hop(2, m).start()

        @pl.when(~even)
        def _():
            self.add(self.SIDE_X, m, self.din)
            self.hop(1, m).start()

    def line(self, i):
        p = self.p
        m = self.plane(i)
        self.join(self.OWN, m)
        self.hop(1, m).wait_recv()
        self.hop(2, m).wait_recv()
        self.add(self.OWN, m, self.xin, self.yin)

        @pl.when(m > p.z)
        def _():
            @pl.when(p.low)
            def _():
                self.climbed(m, True).wait_recv()
                self.add(self.OWN, m, self.zin)

            self.climb(m, True).start()

        @pl.when(m < p.z)
        def _():
            @pl.when(p.high)
            def _():
                self.climbed(m, False).wait_recv()
                self.add(self.OWN, m, self.zin)

            self.climb(m, False).start()

    def result(self):
        p = self.p
        self.out[...] = self.unit(self.OWN, p.z)[...].astype(F32)

        @pl.when(p.low)
        def _():
            self.climbed(p.z, True).wait_recv()
            self.out[...] += self.zin[p.z].astype(F32)

        @pl.when(p.high)
        def _():
            self.climbed(p.z, False).wait_recv()
            self.out[...] += self.zin[LINE].astype(F32)

    def settle(self):
        @pl.loop(0, LINE)
        def _(m):
            for c in range(4):
                self.swap(c, m).wait_send()
            for kind in range(3):
                self.hop(kind, m).wait_send()
            pl.when(m != self.p.z)(lambda: self.climb(m, True).wait_send())


BUFFERS = ((4, LINE), (LINE,), (LINE,), (LINE,), (LINE + 1,))


def project(rows, weights, bias, local):
    return (dot(rows, weights[:, : 3 * local]) + bias[:, : 3 * local]).astype(BF)


def attend(query, keys, values, head, store, between):
    rows, local = query.shape
    half = rows // 2
    query_t = query.T * BF(1.0 / math.sqrt(head))
    value_t = values.T
    line = lax.broadcasted_iota(jnp.int32, (local, rows), 0)
    heads = []
    for h in range(local // head):
        own = (line >= h * head) & (line < (h + 1) * head)
        masked = jnp.where(own, query_t, BF(0.0))
        value_h = value_t[h * head : (h + 1) * head, :]
        parts = []
        for b in range(2):
            span = NB + (b + 1) * half
            scores = dot(keys[:span, :], masked[:, b * half : (b + 1) * half])
            key_at = lax.broadcasted_iota(jnp.int32, (half, half), 0)
            row_at = lax.broadcasted_iota(jnp.int32, (half, half), 1)
            edge = jnp.where(key_at <= row_at, scores[span - half :, :], -1e30)
            scores = jnp.concatenate([scores[: span - half, :], edge], axis=0)
            scores = jnp.exp(scores - jnp.max(scores, axis=0, keepdims=True))
            probs = (scores * (1.0 / jnp.sum(scores, axis=0, keepdims=True))).astype(BF)
            store(h, slice(0, span), slice(b * half, (b + 1) * half), probs)
            parts.append(dot(value_h[:, :span], probs))
        heads.append(jnp.concatenate(parts, axis=1).astype(BF))
        between(h)
    return jnp.concatenate(heads, axis=0)


def gelu_parts(pre):
    square = pre * pre
    inner = jnp.tanh(GELU_SCALE * (pre + GELU_CUBIC * pre * square))
    half_up = 0.5 * (1.0 + inner)
    slope = GELU_SCALE * (1.0 + 3.0 * GELU_CUBIC * square)
    return (pre * half_up).astype(BF), half_up + 0.5 * pre * (1.0 - inner * inner) * slope


def forward_kernel(
    tokens_ref,
    past_ref,
    meta_ref,
    room_ref,
    attn_ref,
    up_ref,
    down_ref,
    wa_ref,
    wu_ref,
    wd_ref,
    out_ref,
    res_ref,
    hmt_ref,
    h2t_ref,
    prob_ref,
    key_ref,
    val_ref,
    query_ref,
    att_ref,
    act_ref,
    slope_ref,
    vec_ref,
    inv_ref,
    coef_ref,
    hm_ref,
    h2_ref,
    tok_ref,
    acc_ref,
    mom_ref,
    sampled_ref,
    all_sampled_ref,
    all_meta_ref,
    all_room_ref,
    coef_part_ref,
    all_coef_ref,
    wide_ref,
    past_vmem,
    flat_send,
    flat_recv,
    flat_local,
    send,
    recv,
    own_sem,
    line_send,
    line_recv,
    line_own,
    load_sem,
    *,
    items,
    head,
):
    step = pl.program_id(0)
    rows, width = tok_ref.shape
    local = query_ref.shape[2]
    place = Place()
    flat = [
        Spread(
            place, src, dst, flat_send.at[i], flat_recv.at[i], flat_local.at[i], line=False
        )
        for i, (src, dst) in enumerate(
            ((sampled_ref, all_sampled_ref), (meta_ref, all_meta_ref))
        )
    ]
    wide = [
        Spread(place, src, dst, send.at[i], recv.at[i], own_sem.at[i])
        for i, (src, dst) in enumerate(
            ((room_ref, all_room_ref), (attn_ref, wa_ref), (up_ref, wu_ref), (down_ref, wd_ref))
        )
    ]
    room, attn, up, down = wide
    line = Line(place, coef_part_ref, all_coef_ref, line_send, line_recv, line_own)

    attn_at = SOLVE_STEPS
    mlp_at = attn_at + LINE
    last = mlp_at + LINE - 1
    steps = woven(wide)
    plan = {}
    done = 0
    for slot, upto in transfer_plan(len(steps)):
        plan[slot] = steps[done:upto]
        done = upto
    plan[(mlp_at, 0)] = steps[done:]

    def transfers(at, position):
        if plan.get((at, position)):

            @pl.when(step == at)
            def _():
                for one in plan[(at, position)]:
                    one()

    def load(ref, m, slot, which):
        return pltpu.make_async_copy(ref.at[m], wide_ref.at[slot, which], load_sem.at[slot, which])

    @pl.when(step == 0)
    def _():
        bring_tok = pltpu.make_async_copy(
            tokens_ref.at[pl.ds(place.z * rows, rows), :], tok_ref, load_sem.at[0, 0]
        )
        bring_past = pltpu.make_async_copy(past_ref, past_vmem, load_sem.at[0, 1])
        bring_tok.start()
        bring_past.start()
        greet(place)
        bring_past.wait()
        sampled_ref[...] = pick_samples(past_vmem[...], meta_ref[...], items)
        for part in flat:
            part.stages()[0][0]()
        bring_tok.wait()
        acc_ref[...] = jnp.zeros_like(acc_ref)
        clear_moments(inv_ref, mom_ref)

    transfers(0, 0)

    @pl.when(step == 1)
    def _():
        for stage in (2, 3):
            for part in flat:
                part.stages()[stage][0]()
        for part in flat:
            part.close(0)

    transfers(1, 0)

    @pl.when(step == 1)
    def _():
        for part in flat:
            part.own.wait()

        def owner(s, carry):
            count = sampled_ref.shape[0]
            samples = all_sampled_ref[0, pl.ds(s * count, count), :]
            gather_moments(
                samples, all_meta_ref[0, pl.ds(s * 8, 8), :], inv_ref, mom_ref, items
            )
            return carry

        lax.fori_loop(0, PLANE, owner, 0)

    transfers(1, 1)

    inverse_end = 2 + NB // PIVOTS

    @pl.when((step >= 2) & (step < inverse_end))
    def _():
        invert_step(inv_ref)

    for at in range(2, inverse_end):
        transfers(at, 0)

    @pl.when(step == inverse_end)
    def _():
        coef_part_ref[...] = coefficients(inv_ref, mom_ref).astype(BF)
        line.first()

    transfers(inverse_end, 0)

    @pl.when(step == inverse_end)
    def _():
        line.step(1)
        room.own.wait()
        for m in range(LINE):
            room.close(m)
            total = all_room_ref[m, 0:16, :].astype(F32)
            for s in range(1, PLANE):
                total = total + all_room_ref[m, s * 16 : (s + 1) * 16, :].astype(F32)
            vec_ref[m] = total
        gain, bias = vec_ref[0, 0:1, :], vec_ref[0, 1:2, :]
        normed, _ = norm_parts(tok_ref[...].astype(F32))
        hm_ref[NB:, :] = (normed * gain + bias).astype(BF)
        line.step(2)
        attn.own.wait()
        attn.close(0)
        load(wa_ref, 0, 0, 0).start()
        line.step(3)
        line.own.wait()
        for m in range(LINE):
            coef_ref[:, m * local : (m + 1) * local] = all_coef_ref[m]
        normed, _ = norm_parts(coef_ref[...].astype(F32))
        hm_ref[0:NB, :] = (normed * gain + bias).astype(BF)
        hmt_ref[...] = hm_ref[...].T

    @pl.when((step >= attn_at) & (step < mlp_at))
    def _():
        m = step - attn_at
        slot = lax.rem(m, 2)
        load(wa_ref, m, slot, 0).wait()

        @pl.when(m < LINE - 1)
        def _():
            attn.close(m + 1)
            load(wa_ref, m + 1, 1 - slot, 0).start()

        weights = wide_ref[slot, 0]
        projected = project(hm_ref[...], weights, vec_ref[m, 6:7, :], local)
        query = projected[NB:, :local]
        keys = projected[:, local : 2 * local]
        values = projected[:, 2 * local :]
        query_ref[0] = query
        key_ref[0] = keys
        val_ref[0] = values

        def store(h, lines, columns, probs):
            prob_ref[0, h, lines, columns] = probs

        def between(h):
            for at in range(attn_at, mlp_at):
                transfers(at, h)

        attended = attend(query, keys, values, head, store, between)
        att_ref[0] = attended
        acc_ref[...] += dot_nt(attended.T, wide_ref[slot, 0, :, 3 * local :])

    transfers(mlp_at, 0)

    @pl.when(step == mlp_at)
    def _():
        for part in (up, down):
            part.own.wait()
            part.close(0)
        load(wu_ref, 0, 0, 0).start()
        load(wd_ref, 0, 0, 1).start()
        residual = tok_ref[...].astype(F32) + acc_ref[...] + vec_ref[0, 4:5, :]
        res_ref[...] = residual
        normed, _ = norm_parts(residual)
        h2_ref[...] = (normed * vec_ref[0, 2:3, :] + vec_ref[0, 3:4, :]).astype(BF)
        h2t_ref[...] = h2_ref[...].T
        acc_ref[...] = jnp.zeros_like(acc_ref)

    @pl.when(step >= mlp_at)
    def _():
        m = step - mlp_at
        slot = lax.rem(m, 2)
        load(wu_ref, m, slot, 0).wait()
        load(wd_ref, m, slot, 1).wait()

        @pl.when(m < LINE - 1)
        def _():
            up.close(m + 1)
            down.close(m + 1)
            load(wu_ref, m + 1, 1 - slot, 0).start()
            load(wd_ref, m + 1, 1 - slot, 1).start()

        pre = dot(h2_ref[...], wide_ref[slot, 0]) + vec_ref[m, 7:8, :]
        act, slope = gelu_parts(pre)
        act_ref[0] = act
        slope_ref[0] = slope.astype(BF)
        acc_ref[...] += dot_nt(act, wide_ref[slot, 1])

    @pl.when(step == last)
    def _():
        out_ref[...] = (res_ref[...] + acc_ref[...] + vec_ref[0, 5:6, :]).astype(BF)
        for part in flat + wide:
            part.settle()
        line.finish_sends()


SOLVE_STEPS = 3 + NB // PIVOTS


def transfer_plan(count):
    attn_at = SOLVE_STEPS
    slots = [((0, 0), 0.06), ((1, 0), 0.16), ((1, 1), 0.26)]
    inverse_end = 2 + NB // PIVOTS
    for i in range(2, inverse_end):
        slots.append(((i, 0), 0.26 + 0.44 * (i - 1) / (inverse_end - 2)))
    slots.append(((inverse_end, 0), 0.76))
    for i in range(LINE):
        for h in range(3):
            slots.append(((attn_at + i, h), 0.76 + 0.24 * (3 * i + h + 1) / (3 * LINE)))
    return [(slot, round(count * share)) for slot, share in slots]


def forward_pass(tokens, past, meta, room, attn, up, down, head):
    width = tokens.shape[1]
    rows = tokens.shape[0] // LINE
    items = past.shape[0]
    local = width // LINE
    hidden = up.shape[1]
    heads = local // head
    keyed = NB + rows
    samples = items * meta.shape[1]
    attn_at = SOLVE_STEPS
    mlp_at = attn_at + LINE
    first = lambda i: jnp.clip(i - attn_at, 0, LINE - 1)
    second = lambda i: jnp.clip(i - mlp_at, 0, LINE - 1)
    whole = lambda shape: pl.BlockSpec(shape, lambda i: (0,) * len(shape))
    anywhere = pl.BlockSpec(memory_space=pl.ANY)
    vmem = pl.BlockSpec(memory_space=pltpu.VMEM)
    dma = pltpu.SemaphoreType.DMA
    shape = jax.ShapeDtypeStruct
    return pl.pallas_call(
        functools.partial(forward_kernel, items=items, head=head),
        grid=(mlp_at + LINE,),
        in_specs=[anywhere, anywhere, vmem, vmem, anywhere, anywhere, anywhere],
        out_specs=[
            anywhere,
            anywhere,
            anywhere,
            whole((rows, width)),
            whole((rows, width)),
            whole((width, keyed)),
            whole((width, rows)),
            pl.BlockSpec((1, heads, keyed, rows), lambda i: (first(i), 0, 0, 0)),
            pl.BlockSpec((1, keyed, local), lambda i: (first(i), 0, 0)),
            pl.BlockSpec((1, keyed, local), lambda i: (first(i), 0, 0)),
            pl.BlockSpec((1, rows, local), lambda i: (first(i), 0, 0)),
            pl.BlockSpec((1, local, rows), lambda i: (first(i), 0, 0)),
            pl.BlockSpec((1, rows, hidden), lambda i: (second(i), 0, 0)),
            pl.BlockSpec((1, rows, hidden), lambda i: (second(i), 0, 0)),
            whole((LINE, 16, width)),
            whole((NB, NB)),
            whole((NB, width)),
        ],
        out_shape=[
            shape((LINE, width, width), BF),
            shape((LINE, width, hidden), BF),
            shape((LINE, width, hidden), BF),
            shape((rows, width), BF),
            shape((rows, width), F32),
            shape((width, keyed), BF),
            shape((width, rows), BF),
            shape((LINE, heads, keyed, rows), BF),
            shape((LINE, keyed, local), BF),
            shape((LINE, keyed, local), BF),
            shape((LINE, rows, local), BF),
            shape((LINE, local, rows), BF),
            shape((LINE, rows, hidden), BF),
            shape((LINE, rows, hidden), BF),
            shape((LINE, 16, width), F32),
            shape((NB, NB), F32),
            shape((NB, width), BF),
        ],
        scratch_shapes=[
            pltpu.VMEM((keyed, width), BF),
            pltpu.VMEM((rows, width), BF),
            pltpu.VMEM((rows, width), BF),
            pltpu.VMEM((rows, width), F32),
            pltpu.VMEM((NB, local), F32),
            pltpu.VMEM((samples, local), BF),
            pltpu.VMEM((1, PLANE * samples, local), BF),
            pltpu.VMEM((1, PLANE * 8, meta.shape[1]), F32),
            pltpu.VMEM((LINE, PLANE * 16, width), BF),
            pltpu.VMEM((NB, local), BF),
            pltpu.VMEM((LINE, NB, local), BF),
            pltpu.VMEM((2, 2, width, width), BF),
            pltpu.VMEM(past.shape, BF),
            dma((2, 5, 4)),
            dma((2, PLANE)),
            dma((2,)),
            dma((4, 5, LINE * 4)),
            dma((4, LINE * PLANE)),
            dma((4,)),
            dma((2, LINE)),
            dma((LINE,)),
            dma(()),
            dma((2, 2)),
        ],
        compiler_params=pltpu.CompilerParams(
            collective_id=1, has_side_effects=True, vmem_limit_bytes=BIG_VMEM
        ),
        name="forward_pass",
    )(tokens, past, meta, room, attn, up, down)


def plain_forward_kernel(
    tok_ref,
    coef_ref,
    vec_ref,
    wa_ref,
    wu_ref,
    wd_ref,
    out_ref,
    res_ref,
    hm_ref,
    h2_ref,
    prob_ref,
    key_ref,
    val_ref,
    query_ref,
    att_ref,
    act_ref,
    slope_ref,
    acc_ref,
    *,
    groups,
    head,
):
    step = pl.program_id(0)
    rows, width = tok_ref.shape
    local = query_ref.shape[2]

    @pl.when(step == 0)
    def _():
        gain, bias = vec_ref[0, 0:1, :], vec_ref[0, 1:2, :]
        normed, _ = norm_parts(coef_ref[...].astype(F32))
        hm_ref[0:NB, :] = (normed * gain + bias).astype(BF)
        normed, _ = norm_parts(tok_ref[...].astype(F32))
        hm_ref[NB:, :] = (normed * gain + bias).astype(BF)
        acc_ref[...] = jnp.zeros_like(acc_ref)

    @pl.when(step < groups)
    def _():
        weights = wa_ref[0]
        projected = project(hm_ref[...], weights, vec_ref[step, 6:7, :], local)
        query = projected[NB:, :local]
        keys = projected[:, local : 2 * local]
        values = projected[:, 2 * local :]
        query_ref[0] = query
        key_ref[0] = keys
        val_ref[0] = values

        def store(h, lines, columns, probs):
            prob_ref[0, h, lines, columns] = probs

        attended = attend(query, keys, values, head, store, lambda h: None)
        att_ref[0] = attended
        acc_ref[...] += dot_nt(attended.T, weights[:, 3 * local :])

    @pl.when(step == groups)
    def _():
        residual = tok_ref[...].astype(F32) + acc_ref[...] + vec_ref[0, 4:5, :]
        res_ref[...] = residual
        normed, _ = norm_parts(residual)
        h2_ref[...] = (normed * vec_ref[0, 2:3, :] + vec_ref[0, 3:4, :]).astype(BF)
        acc_ref[...] = jnp.zeros_like(acc_ref)

    @pl.when(step >= groups)
    def _():
        pre = dot(h2_ref[...], wu_ref[0]) + vec_ref[step - groups, 7:8, :]
        act, slope = gelu_parts(pre)
        act_ref[0] = act
        slope_ref[0] = slope.astype(BF)
        acc_ref[...] += dot_nt(act, wd_ref[0])

    @pl.when(step == 2 * groups - 1)
    def _():
        out_ref[...] = (res_ref[...] + acc_ref[...] + vec_ref[0, 5:6, :]).astype(BF)


def plain_forward(tok, coef, vec, wide, head):
    rows, width = tok.shape
    groups = wide[0].shape[0]
    local = width // groups
    hidden = wide[1].shape[2]
    heads = local // head
    keyed = NB + rows
    first = lambda i: jnp.minimum(i, groups - 1)
    second = lambda i: jnp.maximum(i - groups, 0)
    whole = lambda shape: pl.BlockSpec(shape, lambda i: (0,) * len(shape))
    shape = jax.ShapeDtypeStruct
    return pl.pallas_call(
        functools.partial(plain_forward_kernel, groups=groups, head=head),
        grid=(2 * groups,),
        in_specs=[
            whole((rows, width)),
            whole((NB, width)),
            whole((groups, 16, width)),
            pl.BlockSpec((1, width, width), lambda i: (first(i), 0, 0)),
            pl.BlockSpec((1, width, hidden), lambda i: (second(i), 0, 0)),
            pl.BlockSpec((1, width, hidden), lambda i: (second(i), 0, 0)),
        ],
        out_specs=[
            whole((rows, width)),
            whole((rows, width)),
            whole((keyed, width)),
            whole((rows, width)),
            pl.BlockSpec((1, heads, keyed, rows), lambda i: (first(i), 0, 0, 0)),
            pl.BlockSpec((1, keyed, local), lambda i: (first(i), 0, 0)),
            pl.BlockSpec((1, keyed, local), lambda i: (first(i), 0, 0)),
            pl.BlockSpec((1, rows, local), lambda i: (first(i), 0, 0)),
            pl.BlockSpec((1, local, rows), lambda i: (first(i), 0, 0)),
            pl.BlockSpec((1, rows, hidden), lambda i: (second(i), 0, 0)),
            pl.BlockSpec((1, rows, hidden), lambda i: (second(i), 0, 0)),
        ],
        out_shape=[
            shape((rows, width), BF),
            shape((rows, width), F32),
            shape((keyed, width), BF),
            shape((rows, width), BF),
            shape((groups, heads, keyed, rows), BF),
            shape((groups, keyed, local), BF),
            shape((groups, keyed, local), BF),
            shape((groups, rows, local), BF),
            shape((groups, local, rows), BF),
            shape((groups, rows, hidden), BF),
            shape((groups, rows, hidden), BF),
        ],
        scratch_shapes=[pltpu.VMEM((rows, width), F32)],
        compiler_params=pltpu.CompilerParams(vmem_limit_bytes=BIG_VMEM),
        name="plain_forward",
    )(tok, coef, vec, *wide)


def attend_back(g_att, att_t, keys, values, query, probs_of, head, between):
    rows, local = g_att.shape
    half = rows // 2
    low = NB + rows - half
    g_att_t = g_att.T
    product = g_att_t.astype(F32) * att_t.astype(F32)
    key_t = keys.T
    scale = 1.0 / math.sqrt(head)
    line = lax.broadcasted_iota(jnp.int32, (local, rows), 0)
    lane = lax.broadcasted_iota(jnp.int32, (rows, local), 1)
    key_grad = [jnp.zeros((low, local), F32), jnp.zeros((half, local), F32)]
    val_grad = [jnp.zeros((low, local), F32), jnp.zeros((half, local), F32)]
    query_grads = []
    for h in range(local // head):
        own_t = (line >= h * head) & (line < (h + 1) * head)
        own = (lane >= h * head) & (lane < (h + 1) * head)
        grad_t = jnp.where(own_t, g_att_t, BF(0.0))
        grad_h = jnp.where(own, g_att, BF(0.0))
        query_h = jnp.where(own, query, BF(0.0))
        inner = jnp.sum(product[h * head : (h + 1) * head, :], axis=0, keepdims=True)
        key_h = key_t[h * head : (h + 1) * head, :]
        parts = []
        for b in range(2):
            span = NB + (b + 1) * half
            cols = slice(b * half, (b + 1) * half)
            probs = probs_of(h, slice(0, span), cols)
            dprob = dot(values[:span, :], grad_t[:, cols])
            dscore = (probs.astype(F32) * (dprob - inner[:, cols])).astype(BF)
            parts.append(dot(key_h[:, :span], dscore))
            val_part = dot(probs, grad_h[cols, :])
            key_part = dot(dscore, query_h[cols, :])
            val_grad[0] = val_grad[0] + val_part[:low, :]
            key_grad[0] = key_grad[0] + key_part[:low, :]
            if b == 1:
                val_grad[1] = val_grad[1] + val_part[low:, :]
                key_grad[1] = key_grad[1] + key_part[low:, :]
        query_grads.append(jnp.concatenate(parts, axis=1))
        between(h)
    query_grad = (jnp.concatenate(query_grads, axis=0) * scale).astype(BF).T
    key_grad = jnp.concatenate(key_grad, axis=0) * scale
    return query_grad, key_grad, jnp.concatenate(val_grad, axis=0)


def backward_kernel(
    tokens_ref,
    cots_ref,
    fwd_out_ref,
    res_ref,
    wa_ref,
    wu_ref,
    wd_ref,
    vec_ref,
    hmt_ref,
    h2t_ref,
    coef_ref,
    inv_ref,
    meta_ref,
    prob_ref,
    key_ref,
    val_ref,
    query_ref,
    att_ref,
    act_ref,
    slope_ref,
    outs_ref,
    tgs_ref,
    past_ref,
    gv_mem_ref,
    side_out_ref,
    attn_out_ref,
    mlp_out_ref,
    *scratch,
    head,
):
    (
        tok_ref,
        cot_ref,
        cott_ref,
        gres_ref,
        acc_ref,
        proj_ref,
        gv_ref,
        ggv_ref,
        gmem_ref,
        wide_ref,
        side_ref,
        attn_ref,
        mlp_ref,
    ) = scratch[:13]
    buffers = scratch[13:28]
    block_sems, sems, lsend, lrecv, lown, gsend, grecv, gown, load_sem = scratch[28:]
    step = pl.program_id(0)
    rows, width = tok_ref.shape
    local = query_ref.shape[2]
    items = past_ref.shape[0]
    place = Place()
    side, attn, mlp = [
        Collect(place, grads, out, buffers[i::3], (block_sems.at[i], sems.at[i]))
        for i, (grads, out) in enumerate(
            ((side_ref, side_out_ref), (attn_ref, attn_out_ref), (mlp_ref, mlp_out_ref))
        )
    ]
    outs = Line(place, fwd_out_ref, outs_ref, lsend.at[0], lrecv.at[0], lown.at[0])
    tgs = Line(place, cot_ref, tgs_ref, lsend.at[1], lrecv.at[1], lown.at[1])
    mem = Spread(place, side_out_ref.at[0, 0:8, :], gmem_ref, gsend, grecv, gown)
    mine = pl.ds(place.z * rows, rows)

    def load(ref, m, slot, which):
        return pltpu.make_async_copy(ref.at[m], wide_ref.at[slot, which], load_sem.at[slot, which])

    def bring(i, src, dst):
        return pltpu.make_async_copy(src, dst, load_sem.at[2, i])

    bring_cot = bring(0, cots_ref.at[mine, :], cot_ref)
    bring_tok = bring(1, tokens_ref.at[mine, :], tok_ref)
    bring_res = pltpu.make_async_copy(res_ref, gres_ref, load_sem.at[3, 0])
    at_step = {}

    @pl.when(step == 0)
    def _():
        bring_cot.start()
        bring_tok.start()
        bring_res.start()
        load(wu_ref, 0, 0, 0).start()
        load(wd_ref, 0, 0, 1).start()
        greet(place)
        outs.first()
        acc_ref[...] = jnp.zeros_like(acc_ref)
        gv_ref[...] = jnp.zeros_like(gv_ref)
        bring_cot.wait()
        bring_tok.wait()
        bring_res.wait()
        cott_ref[...] = cot_ref[...].T

    @pl.when(step < LINE)
    def _():
        m = step
        slot = lax.rem(m, 2)
        load(wu_ref, m, slot, 0).wait()
        load(wd_ref, m, slot, 1).wait()

        @pl.when(m < LINE - 1)
        def _():
            load(wu_ref, m + 1, 1 - slot, 0).start()
            load(wd_ref, m + 1, 1 - slot, 1).start()

        @pl.when(m == LINE - 1)
        def _():
            load(wa_ref, 0, 0, 0).start()

        upstream = cot_ref[...]
        grad = (dot(upstream, wide_ref[slot, 1]) * slope_ref[0].astype(F32)).astype(BF)
        mlp_ref[m, 1] = dot(cott_ref[...], act_ref[0]).astype(BF)
        mlp_ref[m, 0] = dot(h2t_ref[...], grad).astype(BF)
        mlp.begin(m)
        ggv_ref[m, 1:2, :] = col_sum(grad.astype(F32))
        acc_ref[NB:, :] += dot_nt(grad, wide_ref[slot, 0])

    @pl.when(step == 3)
    def _():
        outs.step(1)

    @pl.when(step == LINE)
    def _():
        for i in range(2):
            mlp.corner(i)
        upstream = cot_ref[...].astype(F32)
        normed, inverse = norm_parts(gres_ref[...])
        grad = acc_ref[NB:, :]
        g_res = upstream + norm_back(grad, normed, inverse, vec_ref[0, 2:3, :])
        gres_ref[...] = g_res
        g_attn = g_res.astype(BF)
        gv_ref[2:3, :] = col_sum(grad * normed)
        gv_ref[3:4, :] = col_sum(grad)
        gv_ref[4:5, :] = col_sum(g_attn.astype(F32))
        gv_ref[5:6, :] = col_sum(upstream)
        cott_ref[...] = g_attn.T
        acc_ref[...] = jnp.zeros_like(acc_ref)
        proj_ref[0:NB, :] = jnp.zeros((NB, proj_ref.shape[1]), BF)
        for i in range(2, 4):
            mlp.corner(i)

    part = functools.partial
    plan = {
        (0, 0): [part(mlp.sides, 0), part(mlp.sides, 1)],
        (0, 1): [part(mlp.sides, 2), part(mlp.sides, 3)],
        (1, 0): [part(mlp.relay, 0)],
        (1, 1): [part(mlp.relay, 1)],
        (2, 0): [part(outs.step, 2)],
        (2, 1): [part(mlp.relay, 2)],
        (2, 2): [part(mlp.relay, 3)],
        (3, 0): [part(mlp.line, 0)],
        (3, 2): [part(mlp.line, 1)],
    }

    @pl.when(step >= LINE)
    def _():
        m = step - LINE
        slot = lax.rem(m, 2)
        load(wa_ref, m, slot, 0).wait()

        @pl.when(m < LINE - 1)
        def _():
            load(wa_ref, m + 1, 1 - slot, 0).start()

        def between(h):
            for (at, position), steps in plan.items():
                if position == h:

                    @pl.when(m == at)
                    def _():
                        for one in steps:
                            one()

        def probs_of(h, lines, columns):
            return prob_ref[0, h, lines, columns]

        g_attn = gres_ref[...].astype(BF)
        g_att = dot(g_attn, wide_ref[slot, 0, :, 3 * local :]).astype(BF)
        att_t = att_ref[0]
        query_grad, key_grad, val_grad = attend_back(
            g_att, att_t, key_ref[0], val_ref[0], query_ref[0], probs_of, head, between
        )
        proj_ref[NB:, 0:local] = query_grad
        proj_ref[:, local : 2 * local] = key_grad.astype(BF)
        proj_ref[:, 2 * local :] = val_grad.astype(BF)
        proj = proj_ref[...]
        ggv_ref[m, 0:1, 0 : 3 * local] = col_sum(proj.astype(F32))
        ggv_ref[m, 0:1, 3 * local :] = jnp.zeros((1, width - 3 * local), F32)
        attn_ref[m, 0, :, 0 : 3 * local] = dot(hmt_ref[...], proj).astype(BF)
        attn_ref[m, 0, :, 3 * local :] = dot_nt(cott_ref[...], att_t).astype(BF)
        attn.begin(m)
        acc_ref[...] += dot_nt(proj, wide_ref[slot, 0, :, : 3 * local])

    @pl.when(step == 2 * LINE - 1)
    def _():
        grad = acc_ref[NB:, :]
        normed, inverse = norm_parts(tok_ref[...].astype(F32))
        back = norm_back(grad, normed, inverse, vec_ref[0, 0:1, :])
        cot_ref[...] = (gres_ref[...] + back).astype(BF)
        tgs.first()
        gv_ref[0:1, :] = col_sum(grad * normed)
        gv_ref[1:2, :] = col_sum(grad)
        for m in range(LINE):
            below = jnp.concatenate([gv_ref[0:6, :], ggv_ref[m, 0:2, :]], axis=0)
            for s in range(PLANE):
                top = (m * PLANE + s) * 8
                block = jnp.concatenate([acc_ref[top : top + 8, :], below], axis=0)
                side_ref[m, 0, s * 16 : (s + 1) * 16, :] = block.astype(BF)
            side.begin(m)

        @pl.loop(0, LINE)
        def _(i):
            side.corner(i)

        @pl.loop(0, LINE)
        def _(i):
            side.sides(i)

        @pl.loop(0, LINE)
        def _(i):
            attn.corner(i)

        @pl.loop(2, LINE)
        def _(i):
            mlp.line(i)

        outs.step(3)

        @pl.loop(0, LINE)
        def _(i):
            side.relay(i)

        @pl.loop(0, LINE)
        def _(i):
            attn.sides(i)

        @pl.loop(0, LINE)
        def _(i):
            side.line(i)

        mlp.result()
        tgs.step(1)
        side.result()
        mem.first()

        @pl.loop(0, LINE)
        def _(i):
            attn.relay(i)

        for one in mem.stages()[1]:
            one()
        for one in mem.stages()[2]:
            one()
        for one in mem.stages()[3]:
            one()
        tgs.step(2)

        @pl.loop(0, LINE)
        def _(i):
            attn.line(i)

        mem.own.wait()
        for m in range(LINE):
            mem.close(m)
        gmem = jnp.concatenate([gmem_ref[m] for m in range(LINE)], axis=0)
        give_past(gmem, coef_ref, vec_ref, inv_ref, meta_ref, past_ref, gv_mem_ref)
        attn.result()
        tgs.step(3)
        mem.settle()
        for part_ in (side, attn, mlp):
            part_.settle()
        outs.finish()
        tgs.finish()


def backward_pass(tokens, cots, out, meta, vec, inverse, coef, saved, wide, items, past_shape, head):
    res, hmt, h2t, prob, keys, vals, query, att, act, slope = saved
    rows, width = out.shape
    local = width // LINE
    hidden = wide[1].shape[2]
    heads = local // head
    keyed = NB + rows
    first = lambda i: jnp.minimum(i, LINE - 1)
    second = lambda i: jnp.maximum(i - LINE, 0)
    anywhere = pl.BlockSpec(memory_space=pl.ANY)
    vmem = pl.BlockSpec(memory_space=pltpu.VMEM)
    dma = pltpu.SemaphoreType.DMA
    shape = jax.ShapeDtypeStruct
    blocks = ((1, 16, width), (1, width // PLANE, width), (2, width // PLANE, width))
    return pl.pallas_call(
        functools.partial(backward_kernel, head=head),
        grid=(2 * LINE,),
        in_specs=[anywhere] * 7
        + [vmem] * 6
        + [
            pl.BlockSpec((1, heads, keyed, rows), lambda i: (second(i), 0, 0, 0)),
            pl.BlockSpec((1, keyed, local), lambda i: (second(i), 0, 0)),
            pl.BlockSpec((1, keyed, local), lambda i: (second(i), 0, 0)),
            pl.BlockSpec((1, rows, local), lambda i: (second(i), 0, 0)),
            pl.BlockSpec((1, local, rows), lambda i: (second(i), 0, 0)),
            pl.BlockSpec((1, rows, hidden), lambda i: (first(i), 0, 0)),
            pl.BlockSpec((1, rows, hidden), lambda i: (first(i), 0, 0)),
        ],
        out_specs=[anywhere, anywhere, vmem, vmem, vmem, vmem, vmem],
        out_shape=[
            shape((LINE, rows, width), BF),
            shape((LINE, rows, width), BF),
            shape(past_shape, F32),
            shape((8, width), F32),
        ]
        + [shape(b, F32) for b in blocks],
        scratch_shapes=[
            pltpu.VMEM((rows, width), BF),
            pltpu.VMEM((rows, width), BF),
            pltpu.VMEM((width, rows), BF),
            pltpu.VMEM((rows, width), F32),
            pltpu.VMEM((keyed, width), F32),
            pltpu.VMEM((keyed, 3 * local), BF),
            pltpu.VMEM((8, width), F32),
            pltpu.VMEM((LINE, 8, hidden), F32),
            pltpu.VMEM((LINE, PLANE * 8, width), F32),
            pltpu.VMEM((2, 2, width, width), BF),
        ]
        + [pltpu.VMEM((LINE, b[0], PLANE * b[1], b[2]), BF) for b in blocks]
        + [pltpu.VMEM(lead + b, BF) for lead in BUFFERS for b in blocks]
        + [
            dma((3, 2, 4, LINE)),
            dma((3, 9, LINE)),
            dma((2, 2, LINE)),
            dma((2, LINE)),
            dma((2,)),
            dma((5, LINE * 4)),
            dma((LINE * PLANE,)),
            dma(()),
            dma((4, 2)),
        ],
        compiler_params=pltpu.CompilerParams(
            collective_id=2, has_side_effects=True, vmem_limit_bytes=MAX_VMEM
        ),
        name="backward_pass",
    )(
        tokens,
        cots,
        out,
        res,
        *wide,
        vec,
        hmt,
        h2t,
        coef,
        inverse,
        meta,
        prob,
        keys,
        vals,
        query,
        att,
        act,
        slope,
    )


def plain_backward_kernel(
    tok_ref,
    cot_ref,
    res_ref,
    vec_ref,
    hm_ref,
    h2_ref,
    prob_ref,
    key_ref,
    val_ref,
    query_ref,
    att_ref,
    act_ref,
    slope_ref,
    wa_ref,
    wu_ref,
    wd_ref,
    tg_ref,
    gmem_ref,
    gup_ref,
    gdown_ref,
    gatt_ref,
    gv_ref,
    ggv_ref,
    acc_ref,
    hmt_ref,
    h2t_ref,
    cott_ref,
    gres_ref,
    proj_ref,
    *,
    groups,
    head,
):
    step = pl.program_id(0)
    rows, width = tok_ref.shape
    local = query_ref.shape[2]

    @pl.when(step == 0)
    def _():
        acc_ref[...] = jnp.zeros_like(acc_ref)
        h2t_ref[...] = h2_ref[...].T
        cott_ref[...] = cot_ref[...].T
        gv_ref[...] = jnp.zeros_like(gv_ref)

    @pl.when(step < groups)
    def _():
        upstream = cot_ref[...]
        grad = (dot(upstream, wd_ref[0]) * slope_ref[0].astype(F32)).astype(BF)
        gdown_ref[0] = dot(cott_ref[...], act_ref[0]).astype(BF)
        gup_ref[0] = dot(h2t_ref[...], grad).astype(BF)
        ggv_ref[0] = jnp.zeros_like(ggv_ref[0])
        ggv_ref[0, 0:1, :] = col_sum(grad.astype(F32))
        acc_ref[NB:, :] += dot_nt(grad, wu_ref[0])

    @pl.when(step == groups)
    def _():
        upstream = cot_ref[...].astype(F32)
        normed, inverse = norm_parts(res_ref[...])
        grad = acc_ref[NB:, :]
        g_res = upstream + norm_back(grad, normed, inverse, vec_ref[2:3, :])
        gres_ref[...] = g_res
        g_attn = g_res.astype(BF)
        gv_ref[2:3, :] = col_sum(grad * normed)
        gv_ref[3:4, :] = col_sum(grad)
        gv_ref[4:5, :] = col_sum(g_attn.astype(F32))
        gv_ref[5:6, :] = col_sum(upstream)
        cott_ref[...] = g_attn.T
        hmt_ref[...] = hm_ref[...].T
        acc_ref[...] = jnp.zeros_like(acc_ref)
        proj_ref[0:NB, :] = jnp.zeros((NB, proj_ref.shape[1]), BF)

    @pl.when(step >= groups)
    def _():
        weights = wa_ref[0]
        g_attn = gres_ref[...].astype(BF)
        g_att = dot(g_attn, weights[:, 3 * local :]).astype(BF)
        att_t = att_ref[0]
        query_grad, key_grad, val_grad = attend_back(
            g_att,
            att_t,
            key_ref[0],
            val_ref[0],
            query_ref[0],
            lambda h, lines, columns: prob_ref[0, h, lines, columns],
            head,
            lambda h: None,
        )
        key_grad, val_grad = key_grad.astype(BF), val_grad.astype(BF)
        proj_ref[NB:, 0:local] = query_grad
        proj_ref[:, local : 2 * local] = key_grad
        proj_ref[:, 2 * local :] = val_grad
        proj = proj_ref[...]
        ggv_ref[0] = jnp.zeros_like(ggv_ref[0])
        ggv_ref[0, 0:1, 0 : 3 * local] = col_sum(proj.astype(F32))
        gatt_ref[0, :, 0 : 3 * local] = dot(hmt_ref[...], proj).astype(BF)
        gatt_ref[0, :, 3 * local :] = dot_nt(cott_ref[...], att_t).astype(BF)
        acc_ref[...] += dot_nt(proj, weights[:, : 3 * local])

    @pl.when(step == 2 * groups - 1)
    def _():
        gmem_ref[...] = acc_ref[0:NB, :]
        grad = acc_ref[NB:, :]
        normed, inverse = norm_parts(tok_ref[...].astype(F32))
        part = norm_back(grad, normed, inverse, vec_ref[0:1, :])
        tg_ref[...] = (gres_ref[...] + part).astype(BF)
        gv_ref[0:1, :] = col_sum(grad * normed)
        gv_ref[1:2, :] = col_sum(grad)


def plain_backward(tok, cot, vec, saved, wide, head):
    res, hm, h2, prob, keys, vals, query, att, act, slope = saved
    rows, width = tok.shape
    groups = wide[0].shape[0]
    local = width // groups
    hidden = wide[1].shape[2]
    heads = local // head
    keyed = NB + rows
    first = lambda i: jnp.minimum(i, groups - 1)
    second = lambda i: jnp.maximum(i - groups, 0)
    whole = lambda shape: pl.BlockSpec(shape, lambda i: (0,) * len(shape))
    return pl.pallas_call(
        functools.partial(plain_backward_kernel, groups=groups, head=head),
        grid=(2 * groups,),
        in_specs=[
            whole((rows, width)),
            whole((rows, width)),
            whole((rows, width)),
            whole((16, width)),
            whole((keyed, width)),
            whole((rows, width)),
            pl.BlockSpec((1, heads, keyed, rows), lambda i: (second(i), 0, 0, 0)),
            pl.BlockSpec((1, keyed, local), lambda i: (second(i), 0, 0)),
            pl.BlockSpec((1, keyed, local), lambda i: (second(i), 0, 0)),
            pl.BlockSpec((1, rows, local), lambda i: (second(i), 0, 0)),
            pl.BlockSpec((1, local, rows), lambda i: (second(i), 0, 0)),
            pl.BlockSpec((1, rows, hidden), lambda i: (first(i), 0, 0)),
            pl.BlockSpec((1, rows, hidden), lambda i: (first(i), 0, 0)),
            pl.BlockSpec((1, width, width), lambda i: (second(i), 0, 0)),
            pl.BlockSpec((1, width, hidden), lambda i: (first(i), 0, 0)),
            pl.BlockSpec((1, width, hidden), lambda i: (first(i), 0, 0)),
        ],
        out_specs=[
            whole((rows, width)),
            whole((NB, width)),
            pl.BlockSpec((1, width, hidden), lambda i: (first(i), 0, 0)),
            pl.BlockSpec((1, width, hidden), lambda i: (first(i), 0, 0)),
            pl.BlockSpec((1, width, width), lambda i: (second(i), 0, 0)),
            whole((8, width)),
            pl.BlockSpec((1, 8, hidden), lambda i: (i, 0, 0)),
        ],
        out_shape=[
            jax.ShapeDtypeStruct((rows, width), BF),
            jax.ShapeDtypeStruct((NB, width), F32),
            jax.ShapeDtypeStruct((groups, width, hidden), BF),
            jax.ShapeDtypeStruct((groups, width, hidden), BF),
            jax.ShapeDtypeStruct((groups, width, width), BF),
            jax.ShapeDtypeStruct((8, width), F32),
            jax.ShapeDtypeStruct((2 * groups, 8, hidden), F32),
        ],
        scratch_shapes=[
            pltpu.VMEM((keyed, width), F32),
            pltpu.VMEM((width, keyed), BF),
            pltpu.VMEM((width, rows), BF),
            pltpu.VMEM((width, rows), BF),
            pltpu.VMEM((rows, width), F32),
            pltpu.VMEM((keyed, 3 * local), BF),
        ],
        compiler_params=pltpu.CompilerParams(vmem_limit_bytes=BIG_VMEM),
        name="plain_backward",
    )(
        tok, cot, res, vec, hm, h2, prob, keys, vals, query, att, act, slope, *wide
    )


def local(
    tokens,
    cotangent,
    past_state,
    positions,
    counts,
    ln1_gain,
    ln1_bias,
    w_qkv,
    b_qv,
    w_out,
    b_out,
    ln2_gain,
    ln2_bias,
    w_up,
    b_up,
    w_down,
    b_down,
):
    seq, mp = lax.axis_size("seq"), lax.axis_size("mp")
    seq_index, mp_index = lax.axis_index("seq"), lax.axis_index("mp")
    item_count, seg_len, local_width = past_state.shape
    slots = positions.shape[1]
    total = item_count * seq
    width = tokens.shape[1]
    part = width // seq
    heads_local, piece = b_qv.shape[1], b_qv.shape[2]
    head = piece * seq
    hidden = w_up.shape[1]
    rows = tokens.shape[0] // mp
    direct = seq == PLANE and mp == LINE and part % 16 == 0 and hidden == width

    items = (seq_index * item_count + jnp.arange(item_count)).astype(F32)
    spots = positions.astype(F32)
    places = (items[:, None] + (spots + 0.5) / seg_len) / total
    used = (jnp.arange(slots)[None, :] < counts[:, None]).astype(F32)
    meta = jnp.concatenate([places, used, spots, jnp.zeros((8 - 3 * item_count, slots), F32)])

    here = (jnp.arange(seq) == seq_index).astype(BF)
    vectors = jnp.stack([ln1_gain, ln1_bias, ln2_gain, ln2_bias, b_out, b_down])
    vectors = (vectors[:, None, :] * here[None, :, None]).reshape(6, width)
    bias_qv = (b_qv[:, :, None, :] * here[None, None, :, None]).reshape(2, local_width)
    bias_qv = jnp.concatenate([bias_qv, jnp.zeros((2, local_width), BF)], axis=1)
    bias_up = (b_up[:, None, :] * here[None, :, None]).reshape(1, hidden)
    room = jnp.concatenate([vectors, bias_qv.reshape(1, width), bias_up, jnp.zeros((8, width), BF)])
    attn = jnp.concatenate([w_qkv[0], w_qkv[1], w_qkv[2], w_out.T], axis=1)

    if direct:
        results = forward_pass(tokens, past_state, meta, room, attn, w_up, w_down.T, head)
        wide, forward, (vec, inverse, coef) = results[:3], results[3:14], results[14:]
    else:
        sampled = sample_rows(past_state, meta)
        all_sampled = lax.all_gather(sampled, "seq", axis=0)
        all_meta = lax.all_gather(meta, "seq", axis=0)
        coef_part, inverse = solve_memory(all_sampled, all_meta, item_count)
        coef = lax.all_gather(coef_part, "mp", axis=0).transpose(1, 0, 2).reshape(NB, width)
        wide = [
            lax.all_gather(lax.all_gather(shard, "seq", axis=0, tiled=True), "mp", axis=0)
            for shard in (attn, w_up, w_down.T)
        ]
        vec = lax.psum(room.astype(F32), "seq")
        vec = lax.all_gather(vec, "mp", axis=0)
        tok = lax.dynamic_slice_in_dim(tokens, mp_index * rows, rows, 0)
        cot = lax.dynamic_slice_in_dim(cotangent, mp_index * rows, rows, 0)
        forward = plain_forward(tok, coef, vec, wide, head)
    if direct:
        block_out, block_grad, past_grad, gv_mem, side, attn, mlp = backward_pass(
            tokens,
            cotangent,
            forward[0],
            meta,
            vec,
            inverse,
            coef,
            forward[1:],
            wide,
            item_count,
            past_state.shape,
            head,
        )
        block_out = block_out.reshape(mp * rows, width)
        block_grad = block_grad.reshape(mp * rows, width)
        own, attn, up_grad, down_grad = side[0, 8:], attn[0], mlp[0], mlp[1]
    else:
        block_out = lax.all_gather(forward[0], "mp", axis=0, tiled=True)
        tok_grad, gmem, g_up, g_down, g_attn, gv, ggv = plain_backward(
            tok, cot, vec[0], forward[1:], wide, head
        )
        tail = jnp.concatenate(
            [jnp.broadcast_to(gv[None, :6], (mp, 6, width)), ggv[mp:, :1], ggv[:mp, :1]], axis=1
        )
        block_grad = lax.all_gather(tok_grad, "mp", axis=0, tiled=True)
        gmem, tail = lax.psum((gmem, tail), ("seq", "mp"))
        own = lax.dynamic_index_in_dim(tail, mp_index, 0, keepdims=False)
        attn, up_grad, down_grad = (
            lax.psum_scatter(
                lax.psum_scatter(g, "mp", scatter_dimension=0, tiled=False),
                "seq",
                scatter_dimension=0,
                tiled=True,
            ).astype(F32)
            for g in (g_attn, g_up, g_down)
        )
        past_grad, gv_mem = past_grads(
            gmem, coef, vec, inverse, meta, item_count, seg_len, local_width
        )
    own = own + jnp.concatenate([gv_mem[:2], jnp.zeros((6, width), F32)])
    vec_own = lax.dynamic_slice_in_dim(own[:6], seq_index * part, part, 1)
    qv = jnp.stack([own[6, :local_width], own[6, 2 * local_width : 3 * local_width]])
    qv = qv.reshape(2, heads_local, head)
    qv = lax.dynamic_slice_in_dim(qv, seq_index * piece, piece, 2)
    up = lax.dynamic_slice_in_dim(own[7].reshape(-1, head), seq_index * piece, piece, 1)
    qkv_grad = jnp.stack([attn[:, i * local_width : (i + 1) * local_width] for i in range(3)])
    return (
        block_out,
        block_grad,
        past_grad,
        vec_own[0],
        vec_own[1],
        qkv_grad,
        qv,
        attn[:, 3 * local_width :].T,
        vec_own[4],
        vec_own[2],
        vec_own[3],
        up_grad,
        up,
        down_grad.T,
        vec_own[5],
    )


def solution(mesh):
    row = P("seq", None)
    placed = (
        row,
        row,
        P("seq", None, "mp"),
        row,
        P("seq"),
        P("seq"),
        P("seq"),
        P(None, "seq", "mp"),
        P(None, "mp", "seq"),
        P("mp", "seq"),
        P("seq"),
        P("seq"),
        P("seq"),
        P("seq", "mp"),
        P("mp", "seq"),
        P("mp", "seq"),
        P("seq"),
    )
    return jax.shard_map(
        local,
        mesh=mesh,
        in_specs=placed,
        out_specs=(row, row, placed[2]) + placed[5:],
        check_vma=False,
    )
```

```python
import functools
import math

import jax
import jax.numpy as jnp
from jax import lax
from jax.experimental import pallas as pl
from jax.experimental.pallas import tpu as pltpu
from jax.sharding import PartitionSpec as P

NB = 256
PIVOTS = 32
NORM_EPSILON = 1e-05
RIDGE_WEIGHT = 1.0
NARROW_WIDTH = 0.01
BROAD_WIDTH = 0.05
GELU_SCALE = 0.7978845608028654
GELU_CUBIC = 0.044715

BF = jnp.bfloat16
F32 = jnp.float32
HIGHEST = lax.Precision.HIGHEST
BIG_VMEM = 60 * 1024 * 1024
MAX_VMEM = 67043328


def dot(a, b):
    return jnp.dot(a, b, preferred_element_type=F32)


def dot_nt(a, b):
    return lax.dot_general(a, b, (((1,), (1,)), ((), ())), preferred_element_type=F32)


def dot_tn(a, b, precision=None):
    return lax.dot_general(
        a, b, (((0,), (0,)), ((), ())), preferred_element_type=F32, precision=precision
    )


def norm_parts(values):
    centered = values - jnp.mean(values, axis=-1, keepdims=True)
    inverse = lax.rsqrt(jnp.mean(centered * centered, axis=-1, keepdims=True) + NORM_EPSILON)
    return centered * inverse, inverse


def norm_back(upstream, normed, inverse, gain):
    scaled = upstream * gain
    inner = scaled - jnp.mean(scaled, axis=-1, keepdims=True)
    inner = inner - normed * jnp.mean(scaled * normed, axis=-1, keepdims=True)
    return inner * inverse


def col_sum(values):
    return jnp.sum(values, axis=0, keepdims=True)


def basis_of(places, used):
    column = lax.broadcasted_iota(jnp.int32, (places.shape[0], NB), 1)
    centers = (column.astype(F32) + 0.5) / NB
    widths = jnp.where(column % 2 == 0, NARROW_WIDTH, BROAD_WIDTH).astype(F32)
    scaled = (places - centers) / widths
    return jnp.exp(-0.5 * (scaled * scaled)) * used


def position_of(column, i, items):
    return column[:, 2 * items + i : 2 * items + i + 1].astype(jnp.int32)


def inverse_2(a, b, c, d):
    scale = 1.0 / (a * d - b * c)
    return d * scale, -(b * scale), -(c * scale), a * scale


def product_2(x, y):
    return (
        x[0] * y[0] + x[1] * y[2],
        x[0] * y[1] + x[1] * y[3],
        x[2] * y[0] + x[3] * y[2],
        x[2] * y[1] + x[3] * y[3],
    )


def invert_step(mat_ref):
    block = PIVOTS
    lane = lax.broadcasted_iota(jnp.int32, (block, NB), 1)
    line = lax.broadcasted_iota(jnp.int32, (block, NB), 0)
    panel = mat_ref[0:block, :]
    for k in range(0, block, 4):
        cols = [jnp.broadcast_to(panel[:, k + j : k + j + 1], panel.shape) for j in range(4)]
        at = [[cols[j][k + i : k + i + 1] for j in range(4)] for i in range(4)]
        head = inverse_2(at[0][0], at[0][1], at[1][0], at[1][1])
        upper = (at[0][2], at[0][3], at[1][2], at[1][3])
        lower = (at[2][0], at[2][1], at[3][0], at[3][1])
        right, left = product_2(head, upper), product_2(lower, head)
        minus = product_2(lower, right)
        tail = inverse_2(
            at[2][2] - minus[0], at[2][3] - minus[1], at[3][2] - minus[2], at[3][3] - minus[3]
        )
        rt, tl = product_2(right, tail), product_2(tail, left)
        back = product_2(rt, left)
        inverse = (
            (head[0] + back[0], head[1] + back[1], -rt[0], -rt[1]),
            (head[2] + back[2], head[3] + back[3], -rt[2], -rt[3]),
            (-tl[0], -tl[1], tail[0], tail[1]),
            (-tl[2], -tl[3], tail[2], tail[3]),
        )
        inside = (lane >= k) & (lane < k + 4)
        rows = [
            jnp.where(inside[0:1], (lane[0:1] == k + j).astype(F32), panel[k + j : k + j + 1])
            for j in range(4)
        ]
        new = [
            (m[0] * rows[0] + m[1] * rows[1]) + (m[2] * rows[2] + m[3] * rows[3]) for m in inverse
        ]
        rest = jnp.where(inside, 0.0, panel) - (
            (cols[0] * new[0] + cols[1] * new[1]) + (cols[2] * new[2] + cols[3] * new[3])
        )
        for i in range(4):
            rest = jnp.where(line == k + i, new[i], rest)
        panel = rest
    mat_ref[0:block, :] = panel
    row = lax.broadcasted_iota(jnp.int32, (NB, NB), 0)
    col = lax.broadcasted_iota(jnp.int32, (NB, NB), 1)
    mat = mat_ref[...]
    inside_row = row < block
    inside_col = col < block
    left = jnp.where(inside_col & ~inside_row, mat, 0.0)
    right = jnp.where(inside_row, mat, 0.0)
    update = jnp.dot(left, right, preferred_element_type=F32, precision=HIGHEST)
    mat = jnp.where(inside_row, mat, jnp.where(inside_col, 0.0, mat) - update)
    mat = pltpu.roll(mat, NB - block, 1)
    mat_ref[0 : NB - block, :] = mat[block:, :]
    mat_ref[NB - block :, :] = mat[:block, :]


def owner_basis(meta, items):
    column = meta.T
    rows = [
        basis_of(column[:, i : i + 1], column[:, items + i : items + i + 1]) for i in range(items)
    ]
    return jnp.concatenate(rows, axis=0)


def clear_moments(mat_ref, mom_ref):
    row = lax.broadcasted_iota(jnp.int32, (NB, NB), 0)
    col = lax.broadcasted_iota(jnp.int32, (NB, NB), 1)
    mat_ref[...] = jnp.where(row == col, RIDGE_WEIGHT, 0.0)
    mom_ref[...] = jnp.zeros_like(mom_ref)


def coefficients(mat_ref, mom_ref):
    return jnp.dot(mat_ref[...], mom_ref[...], preferred_element_type=F32, precision=HIGHEST)


def pick_samples(past, meta, items):
    slots, seg_len = meta.shape[1], past.shape[1]
    column = meta.T
    at = lax.broadcasted_iota(jnp.int32, (slots, seg_len), 1)
    rows = []
    for i in range(items):
        pick = (at == position_of(column, i, items)).astype(F32).astype(BF)
        rows.append(dot(pick, past[i]).astype(BF))
    return jnp.concatenate(rows, axis=0)


def sample_kernel(past_ref, meta_ref, out_ref, *, items):
    out_ref[...] = pick_samples(past_ref[...], meta_ref[...], items)


def sample_rows(past, meta):
    items, seg_len, width = past.shape
    return pl.pallas_call(
        functools.partial(sample_kernel, items=items),
        out_shape=jax.ShapeDtypeStruct((items * meta.shape[1], width), BF),
        name="sample_rows",
    )(past, meta)


def solve_kernel(sampled_ref, meta_ref, coef_ref, inv_ref, mat_ref, mom_ref, *, items):
    clear_moments(mat_ref, mom_ref)

    def owner(s, carry):
        rows = owner_basis(meta_ref[s], items)
        mat_ref[...] += dot_tn(rows, rows, HIGHEST)
        mom_ref[...] += dot_tn(rows, sampled_ref[s].astype(F32), HIGHEST)
        return carry

    lax.fori_loop(0, meta_ref.shape[0], owner, 0)

    def step(s, carry):
        invert_step(mat_ref)
        return carry

    lax.fori_loop(0, NB // PIVOTS, step, 0)
    inv_ref[...] = mat_ref[...]
    coef_ref[...] = coefficients(mat_ref, mom_ref).astype(BF)


def solve_memory(sampled, meta, items):
    width = sampled.shape[-1]
    return pl.pallas_call(
        functools.partial(solve_kernel, items=items),
        out_shape=(
            jax.ShapeDtypeStruct((NB, width), BF),
            jax.ShapeDtypeStruct((NB, NB), F32),
        ),
        scratch_shapes=[pltpu.VMEM((NB, NB), F32), pltpu.VMEM((NB, width), F32)],
        compiler_params=pltpu.CompilerParams(vmem_limit_bytes=BIG_VMEM),
        name="solve_memory",
    )(sampled, meta)


def give_past(gmem, coef_ref, vec_ref, inv_ref, meta_ref, out_ref, gv_ref):
    slots = meta_ref.shape[1]
    item_count, seg_len, width = out_ref.shape
    normed, inverse = norm_parts(coef_ref[...].astype(F32))
    coef_grad = norm_back(gmem, normed, inverse, vec_ref[0, 0:1, :])
    gv_ref[...] = jnp.zeros_like(gv_ref)
    gv_ref[0:1, :] = col_sum(gmem * normed)
    gv_ref[1:2, :] = col_sum(gmem)
    features = coef_grad.shape[1]
    part = lax.axis_index("mp")
    row = lax.broadcasted_iota(jnp.int32, (features, width), 0)
    col = lax.broadcasted_iota(jnp.int32, (features, width), 1)
    pick = (row == col + part * width).astype(F32)
    mine = jnp.dot(coef_grad, pick, preferred_element_type=F32, precision=HIGHEST)
    moment = jnp.dot(inv_ref[...], mine, preferred_element_type=F32, precision=HIGHEST)
    at = lax.broadcasted_iota(jnp.int32, (slots, seg_len), 1)
    column = meta_ref[...].T
    for i in range(item_count):
        rows = basis_of(column[:, i : i + 1], column[:, item_count + i : item_count + i + 1])
        sampled = jnp.dot(rows, moment, preferred_element_type=F32, precision=HIGHEST)
        spread = (at == position_of(column, i, item_count)).astype(F32)
        out_ref[i] = dot_tn(spread, sampled, HIGHEST)


def past_kernel(gmem_ref, coef_ref, vec_ref, inv_ref, meta_ref, out_ref, gv_ref):
    give_past(gmem_ref[...], coef_ref, vec_ref, inv_ref, meta_ref, out_ref, gv_ref)


def past_grads(gmem, coef, vec, inv, meta, items, seg_len, width):
    return pl.pallas_call(
        past_kernel,
        out_shape=(
            jax.ShapeDtypeStruct((items, seg_len, width), F32),
            jax.ShapeDtypeStruct((8, coef.shape[1]), F32),
        ),
        compiler_params=pltpu.CompilerParams(vmem_limit_bytes=BIG_VMEM),
        name="past_grads",
    )(gmem, coef, vec, inv, meta)


MESH = pl.DeviceIdType.MESH
LINE = 4
PLANE = 8
NEAR = (0, -1, 1, -2, 2, -3, 3)


class Place:
    def __init__(self):
        self.s = lax.axis_index("seq")
        self.z = lax.axis_index("mp")
        core = lax.rem(self.s, 2)
        x = lax.rem(self.s // 2, 2)
        y = self.s // 4
        self.turn = 1 - 2 * core
        self.partner = self.s + self.turn
        self.sx = self.s + 2 - 4 * x
        self.sy = self.s + 4 - 8 * y
        self.sd = self.sx + 4 - 8 * y
        self.low = self.z > 0
        self.high = self.z < LINE - 1
        self.near = [
            (
                d,
                valid(self.z + d),
                self.z + d,
                lax.rem(self.z + d + LINE, 2) == 1,
                lax.rem(self.z + d + LINE, 2) == 0,
            )
            for d in NEAR
        ]


def valid(m):
    return (m >= 0) & (m < LINE)


def when(conditions, act):
    conditions = [c for c in conditions if c is not None]
    if conditions:
        pl.when(functools.reduce(lambda a, b: a & b, conditions))(act)
    else:
        act()


def greet(place, line=True, plane=True):
    barrier = pltpu.get_barrier_semaphore()

    def signal(seq, z):
        pl.semaphore_signal(barrier, inc=1, device_id=(seq, z), device_id_type=MESH)

    if plane:
        for seq in (place.partner, place.sx, place.sy):
            signal(seq, place.z)
    if line:
        pl.when(place.low)(lambda: signal(place.s, place.z - 1))
        pl.when(place.high)(lambda: signal(place.s, place.z + 1))
    peers = 3 if plane else 0
    if line:
        peers = peers + (place.z + LINE - 1) // LINE + (2 * LINE - 2 - place.z) // LINE
    pl.semaphore_wait(barrier, peers)


UP, DOWN, ACROSS_X, ACROSS_Y, PARTNER = range(5)


class Spread:
    def __init__(self, place, src, dst, send, recv, local, line=True):
        self.p, self.src, self.dst = place, src, dst
        self.send, self.recv, self.line = send, recv, line
        self.rows = src.shape[0]
        self.sent = []
        self.mine = place.z if line else 0
        self.around = place.near if line else [(0, None, 0, None, None)]
        self.own = pltpu.make_async_copy(src, self.at(self.mine, place.s), local)

    def at(self, m, s):
        return self.dst.at[m, pl.ds(s * self.rows, self.rows), :]

    def copy(self, direction, m, s, own=False):
        p = self.p
        device = (
            (p.s, p.z + 1),
            (p.s, p.z - 1),
            (p.sx, p.z),
            (p.sy, p.z),
            (p.partner, p.z),
        )[direction]
        return pltpu.make_async_remote_copy(
            src_ref=self.src if own else self.at(m, s),
            dst_ref=self.at(m, s),
            send_sem=self.send.at[direction, m * 4 + s // 2],
            recv_sem=self.recv.at[m * PLANE + s],
            device_id=device,
            device_id_type=MESH,
        )

    def start(self, conditions, *what, **how):
        when(conditions, lambda: self.copy(*what, **how).start())
        self.sent.append((conditions, what, how))

    def arrived(self, m, s):
        self.copy(PARTNER, m, s).wait_recv()

    def first(self):
        p, m = self.p, self.mine
        self.own.start()
        if self.line:
            self.start((p.high,), UP, m, p.s, own=True)
            self.start((p.low,), DOWN, m, p.s, own=True)
        for direction in (ACROSS_X, ACROSS_Y, PARTNER):
            self.start((), direction, m, p.s, own=True)

    def along(self, d, ok, m, odd, even):
        p = self.p
        when((ok,), lambda: self.arrived(m, p.s))
        if d < 0:
            self.start((ok, p.high), UP, m, p.s)
        else:
            self.start((ok, p.low), DOWN, m, p.s)
        for direction in (ACROSS_X, ACROSS_Y, PARTNER):
            self.start((ok,), direction, m, p.s)

    def across(self, d, ok, m, odd, even):
        p = self.p
        when((ok,), lambda: self.arrived(m, p.sx))
        if self.line:
            self.start((ok, odd), ACROSS_Y, m, p.sx)
        self.start((ok,), PARTNER, m, p.sx)
        when((ok,), lambda: self.arrived(m, p.sy))
        if self.line:
            self.start((ok, even), ACROSS_X, m, p.sy)
        else:
            self.start((), ACROSS_X, m, p.sy)
        self.start((ok,), PARTNER, m, p.sy)

    def corner(self, d, ok, m, odd, even):
        p = self.p
        when((ok,), lambda: self.arrived(m, p.sd))
        self.start((ok,), PARTNER, m, p.sd)

    def part(self, kind, d):
        if kind == 0:
            return self.first
        act = (self.along, self.across, self.corner)[kind - 1]
        return functools.partial(act, *self.around[NEAR.index(d)])

    def steps(self, kind):
        return [self.part(kind, d) for d in NEAR if d or kind > 1]

    def close(self, m):
        p = self.p
        for s in (p.s, p.sx, p.sy, p.sd):
            self.arrived(m, s + p.turn)

    def settle(self):
        for conditions, what, how in self.sent:
            when(conditions, lambda: self.copy(*what, **how).wait_send())


class Line:
    def __init__(self, place, src, dst, send, recv, local):
        self.p, self.src, self.dst = place, src, dst
        self.send, self.recv = send, recv
        self.sent = []
        self.own = pltpu.make_async_copy(src, dst.at[place.z], local)

    def copy(self, up, m, own=False):
        p = self.p
        return pltpu.make_async_remote_copy(
            src_ref=self.src if own else self.dst.at[m],
            dst_ref=self.dst.at[m],
            send_sem=self.send.at[1 if up else 0, m],
            recv_sem=self.recv.at[m],
            device_id=(p.s, p.z + 1 if up else p.z - 1),
            device_id_type=MESH,
        )

    def start(self, conditions, *what, **how):
        when(conditions, lambda: self.copy(*what, **how).start())
        self.sent.append((conditions, what, how))

    def first(self):
        p = self.p
        self.own.start()
        self.start((p.high,), True, p.z, own=True)
        self.start((p.low,), False, p.z, own=True)

    def step(self, distance):
        p = self.p
        for d, ok, m, odd, even in p.near:
            if abs(d) != distance:
                continue
            when((ok,), lambda: self.copy(True, m).wait_recv())
            if d < 0:
                self.start((ok, p.high), True, m)
            else:
                self.start((ok, p.low), False, m)

    def finish_sends(self):
        for conditions, what, how in self.sent:
            when(conditions, lambda: self.copy(*what, **how).wait_send())

    def finish(self):
        self.finish_sends()
        self.own.wait()


class Collect:
    OWN, SIDE_X, SIDE_Y, CORNER = range(4)

    def __init__(self, place, grads, out, buffers, sems):
        self.p, self.grads, self.out = place, grads, out
        self.pin, self.din, self.xin, self.yin, self.zin = buffers
        self.block_sems, self.sems = sems
        self.rows = out.shape[1]
        self.columns = (place.s, place.sx, place.sy, place.sd)

    def plane(self, i):
        upper = self.p.z // 2
        return (1 - upper) * (LINE - 1 - i) + upper * i

    def unit(self, c, m, turn=0):
        s = self.columns[c] + turn
        return self.grads.at[m, :, pl.ds(s * self.rows, self.rows), :]

    def remote(self, src, dst, send, recv, device):
        return pltpu.make_async_remote_copy(
            src_ref=src,
            dst_ref=dst,
            send_sem=send,
            recv_sem=recv,
            device_id=device,
            device_id_type=MESH,
        )

    def swap(self, c, m):
        p = self.p
        return self.remote(
            self.unit(c, m, p.turn),
            self.pin.at[c, m],
            self.block_sems.at[0, c, m],
            self.block_sems.at[1, c, m],
            (p.partner, p.z),
        )

    def hop(self, kind, m, by_x=True):
        p = self.p
        src, dst, device = (
            (self.CORNER, self.din, (p.sx if by_x else p.sy, p.z)),
            (self.SIDE_X, self.xin, (p.sx, p.z)),
            (self.SIDE_Y, self.yin, (p.sy, p.z)),
        )[kind]
        return self.remote(
            self.unit(src, m),
            dst.at[m],
            self.sems.at[kind, m],
            self.sems.at[4 + kind, m],
            device,
        )

    def slot(self, m, z):
        ends = 1 // (1 + z - m)
        return m + (LINE - m) * ends

    def climb(self, m, up):
        p = self.p
        return self.remote(
            self.unit(self.OWN, m),
            self.zin.at[m if up else self.slot(m, p.z - 1)],
            self.sems.at[3, m],
            self.sems.at[7 if up else 8, m],
            (p.s, p.z + 1 if up else p.z - 1),
        )

    def climbed(self, m, up):
        zin = self.zin.at[m if up else self.slot(m, self.p.z)]
        return self.remote(
            zin, zin, self.sems.at[3, m], self.sems.at[7 if up else 8, m], (self.p.partner, self.p.z)
        )

    def add(self, c, m, *others):
        mine = self.unit(c, m)
        total = mine[...].astype(F32)
        for other in others:
            total = total + other[m].astype(F32)
        mine[...] = total.astype(BF)

    def begin(self, m):
        for c in (self.CORNER, self.SIDE_X, self.SIDE_Y, self.OWN):
            self.swap(c, m).start()

    def join(self, c, m):
        self.swap(c, m).wait_recv()
        self.add(c, m, self.pin.at[c])

    def corner(self, i):
        m = self.plane(i)
        self.join(self.CORNER, m)
        even = lax.rem(m, 2) == 0
        pl.when(even)(lambda: self.hop(0, m, True).start())
        pl.when(~even)(lambda: self.hop(0, m, False).start())

    def sides(self, i):
        m = self.plane(i)
        even = lax.rem(m, 2) == 0
        self.join(self.SIDE_X, m)
        self.join(self.SIDE_Y, m)
        pl.when(even)(lambda: self.hop(1, m).start())
        pl.when(~even)(lambda: self.hop(2, m).start())

    def relay(self, i):
        m = self.plane(i)
        even = lax.rem(m, 2) == 0
        self.hop(0, m).wait_recv()

        @pl.when(even)
        def _():
            self.add(self.SIDE_Y, m, self.din)
            self.hop(2, m).start()

        @pl.when(~even)
        def _():
            self.add(self.SIDE_X, m, self.din)
            self.hop(1, m).start()

    def line(self, i):
        p = self.p
        m = self.plane(i)
        self.join(self.OWN, m)
        self.hop(1, m).wait_recv()
        self.hop(2, m).wait_recv()
        self.add(self.OWN, m, self.xin, self.yin)

        @pl.when(m > p.z)
        def _():
            @pl.when(p.low)
            def _():
                self.climbed(m, True).wait_recv()
                self.add(self.OWN, m, self.zin)

            self.climb(m, True).start()

        @pl.when(m < p.z)
        def _():
            @pl.when(p.high)
            def _():
                self.climbed(m, False).wait_recv()
                self.add(self.OWN, m, self.zin)

            self.climb(m, False).start()

    def result(self):
        p = self.p
        self.out[...] = self.unit(self.OWN, p.z)[...].astype(F32)

        @pl.when(p.low)
        def _():
            self.climbed(p.z, True).wait_recv()
            self.out[...] += self.zin[p.z].astype(F32)

        @pl.when(p.high)
        def _():
            self.climbed(p.z, False).wait_recv()
            self.out[...] += self.zin[LINE].astype(F32)

    def settle(self):
        @pl.loop(0, LINE)
        def _(m):
            for c in range(4):
                self.swap(c, m).wait_send()
            for kind in range(3):
                self.hop(kind, m).wait_send()
            pl.when(m != self.p.z)(lambda: self.climb(m, True).wait_send())


BUFFERS = ((4, LINE), (LINE,), (LINE,), (LINE,), (LINE + 1,))


def project(rows, weights, bias, local):
    return (dot(rows, weights[:, : 3 * local]) + bias[:, : 3 * local]).astype(BF)


def attend(query, keys, values, head, store, between):
    rows, local = query.shape
    half = rows // 2
    query_t = query.T * BF(1.0 / math.sqrt(head))
    value_t = values.T
    line = lax.broadcasted_iota(jnp.int32, (local, rows), 0)
    heads = []
    for h in range(local // head):
        own = (line >= h * head) & (line < (h + 1) * head)
        masked = jnp.where(own, query_t, BF(0.0))
        value_h = value_t[h * head : (h + 1) * head, :]
        parts = []
        for b in range(2):
            span = NB + (b + 1) * half
            scores = dot(keys[:span, :], masked[:, b * half : (b + 1) * half])
            key_at = lax.broadcasted_iota(jnp.int32, (half, half), 0)
            row_at = lax.broadcasted_iota(jnp.int32, (half, half), 1)
            edge = jnp.where(key_at <= row_at, scores[span - half :, :], -1e30)
            scores = jnp.concatenate([scores[: span - half, :], edge], axis=0)
            scores = jnp.exp(scores - jnp.max(scores, axis=0, keepdims=True))
            probs = (scores * (1.0 / jnp.sum(scores, axis=0, keepdims=True))).astype(BF)
            store(h, slice(0, span), slice(b * half, (b + 1) * half), probs)
            parts.append(dot(value_h[:, :span], probs))
        heads.append(jnp.concatenate(parts, axis=1).astype(BF))
        between(h)
    return jnp.concatenate(heads, axis=0)


def gelu_parts(pre):
    square = pre * pre
    inner = jnp.tanh(GELU_SCALE * (pre + GELU_CUBIC * pre * square))
    half_up = 0.5 * (1.0 + inner)
    slope = GELU_SCALE * (1.0 + 3.0 * GELU_CUBIC * square)
    return (pre * half_up).astype(BF), half_up + 0.5 * pre * (1.0 - inner * inner) * slope


def forward_kernel(
    tokens_ref,
    past_ref,
    meta_ref,
    room_ref,
    attn_ref,
    up_ref,
    down_ref,
    wa_ref,
    wu_ref,
    wd_ref,
    out_ref,
    res_ref,
    hmt_ref,
    h2t_ref,
    prob_ref,
    key_ref,
    val_ref,
    query_ref,
    att_ref,
    act_ref,
    slope_ref,
    vec_ref,
    inv_ref,
    coef_ref,
    hm_ref,
    h2_ref,
    tok_ref,
    acc_ref,
    mom_ref,
    sampled_ref,
    all_sampled_ref,
    basis_ref,
    all_meta_ref,
    all_room_ref,
    coef_part_ref,
    all_coef_ref,
    wide_ref,
    past_vmem,
    flat_send,
    flat_recv,
    flat_local,
    send,
    recv,
    own_sem,
    line_send,
    line_recv,
    line_own,
    load_sem,
    *,
    items,
    head,
):
    step = pl.program_id(0)
    rows, width = tok_ref.shape
    local = query_ref.shape[2]
    place = Place()
    flat = [
        Spread(
            place, src, dst, flat_send.at[i], flat_recv.at[i], flat_local.at[i], line=False
        )
        for i, (src, dst) in enumerate(
            ((meta_ref, all_meta_ref), (sampled_ref, all_sampled_ref))
        )
    ]
    wide = [
        Spread(place, src, dst, send.at[i], recv.at[i], own_sem.at[i])
        for i, (src, dst) in enumerate(
            ((room_ref, all_room_ref), (attn_ref, wa_ref), (up_ref, wu_ref), (down_ref, wd_ref))
        )
    ]
    room, attn, up, down = wide
    line = Line(place, coef_part_ref, all_coef_ref, line_send, line_recv, line_own)

    attn_at = SOLVE_STEPS
    mlp_at = attn_at + LINE
    last = mlp_at + LINE - 1
    plan = {
        slot: [wide[i].part(kind, d) for i, kind, d in steps] for slot, steps in FORWARD_PLAN
    }

    def transfers(at, position):
        if plan.get((at, position)):

            @pl.when(step == at)
            def _():
                for one in plan[(at, position)]:
                    one()

    def load(ref, m, slot, which):
        return pltpu.make_async_copy(ref.at[m], wide_ref.at[slot, which], load_sem.at[slot, which])

    @pl.when(step == 0)
    def _():
        bring_tok = pltpu.make_async_copy(
            tokens_ref.at[pl.ds(place.z * rows, rows), :], tok_ref, load_sem.at[0, 0]
        )
        bring_past = pltpu.make_async_copy(past_ref, past_vmem, load_sem.at[0, 1])
        bring_tok.start()
        bring_past.start()
        greet(place)
        bring_past.wait()
        sampled_ref[...] = pick_samples(past_vmem[...], meta_ref[...], items)
        for part in flat:
            part.first()
        bring_tok.wait()
        acc_ref[...] = jnp.zeros_like(acc_ref)
        clear_moments(inv_ref, mom_ref)

    transfers(0, 0)

    meta, samples = flat

    @pl.when(step == 1)
    def _():
        for kind in (2, 3):
            meta.part(kind, 0)()
        samples.part(2, 0)()
        meta.own.wait()
        meta.close(0)

    transfers(1, 0)

    @pl.when(step == 1)
    def _():
        def owner(s, carry):
            rows = owner_basis(all_meta_ref[0, pl.ds(s * 8, 8), :], items)
            basis_ref[s] = rows
            inv_ref[...] += dot_tn(rows, rows, HIGHEST)
            return carry

        lax.fori_loop(0, PLANE, owner, 0)
        samples.part(3, 0)()
        samples.own.wait()
        samples.close(0)

    transfers(1, 1)

    @pl.when(step == 1)
    def _():
        def owner(s, carry):
            count = sampled_ref.shape[0]
            rows = all_sampled_ref[0, pl.ds(s * count, count), :]
            mom_ref[...] += dot_tn(basis_ref[s], rows.astype(F32), HIGHEST)
            return carry

        lax.fori_loop(0, PLANE, owner, 0)

    transfers(1, 2)

    inverse_end = 2 + NB // PIVOTS

    @pl.when((step >= 2) & (step < inverse_end))
    def _():
        invert_step(inv_ref)

    for at in range(2, inverse_end):
        transfers(at, 0)

    @pl.when(step == inverse_end)
    def _():
        coef_part_ref[...] = coefficients(inv_ref, mom_ref).astype(BF)
        line.first()

    transfers(inverse_end, 0)

    @pl.when(step == inverse_end)
    def _():
        room.own.wait()
        for m in range(LINE):
            room.close(m)
            total = all_room_ref[m, 0:16, :].astype(F32)
            for s in range(1, PLANE):
                total = total + all_room_ref[m, s * 16 : (s + 1) * 16, :].astype(F32)
            vec_ref[m] = total
        gain, bias = vec_ref[0, 0:1, :], vec_ref[0, 1:2, :]
        normed, _ = norm_parts(tok_ref[...].astype(F32))
        hm_ref[NB:, :] = (normed * gain + bias).astype(BF)
        hmt_ref[:, NB:] = hm_ref[NB:, :].T
        line.step(1)

    transfers(inverse_end, 1)

    @pl.when(step == inverse_end)
    def _():
        attn.own.wait()
        attn.close(0)
        load(wa_ref, 0, 0, 0).start()
        line.step(2)

    transfers(inverse_end, 2)

    @pl.when(step == inverse_end)
    def _():
        line.step(3)
        line.own.wait()
        gain, bias = vec_ref[0, 0:1, :], vec_ref[0, 1:2, :]
        for m in range(LINE):
            coef_ref[:, m * local : (m + 1) * local] = all_coef_ref[m]
        normed, _ = norm_parts(coef_ref[...].astype(F32))
        hm_ref[0:NB, :] = (normed * gain + bias).astype(BF)
        hmt_ref[:, 0:NB] = hm_ref[0:NB, :].T

    @pl.when((step >= attn_at) & (step < mlp_at))
    def _():
        m = step - attn_at
        slot = lax.rem(m, 2)
        load(wa_ref, m, slot, 0).wait()

        @pl.when(m < LINE - 1)
        def _():
            attn.close(m + 1)
            load(wa_ref, m + 1, 1 - slot, 0).start()

        weights = wide_ref[slot, 0]
        projected = project(hm_ref[...], weights, vec_ref[m, 6:7, :], local)
        query = projected[NB:, :local]
        keys = projected[:, local : 2 * local]
        values = projected[:, 2 * local :]
        query_ref[0] = query
        key_ref[0] = keys
        val_ref[0] = values

        def store(h, lines, columns, probs):
            prob_ref[0, h, lines, columns] = probs

        def between(h):
            for at in range(attn_at, mlp_at):
                transfers(at, h)

        attended = attend(query, keys, values, head, store, between)
        att_ref[0] = attended
        acc_ref[...] += dot_nt(attended.T, wide_ref[slot, 0, :, 3 * local :])

    transfers(mlp_at, 0)

    @pl.when(step == mlp_at)
    def _():
        for part in (up, down):
            part.own.wait()
            part.close(0)
        load(wu_ref, 0, 0, 0).start()
        load(wd_ref, 0, 0, 1).start()
        residual = tok_ref[...].astype(F32) + acc_ref[...] + vec_ref[0, 4:5, :]
        res_ref[...] = residual
        normed, _ = norm_parts(residual)
        h2_ref[...] = (normed * vec_ref[0, 2:3, :] + vec_ref[0, 3:4, :]).astype(BF)
        h2t_ref[...] = h2_ref[...].T
        acc_ref[...] = jnp.zeros_like(acc_ref)

    @pl.when(step >= mlp_at)
    def _():
        m = step - mlp_at
        slot = lax.rem(m, 2)
        load(wu_ref, m, slot, 0).wait()
        load(wd_ref, m, slot, 1).wait()

        @pl.when(m < LINE - 1)
        def _():
            up.close(m + 1)
            down.close(m + 1)
            load(wu_ref, m + 1, 1 - slot, 0).start()
            load(wd_ref, m + 1, 1 - slot, 1).start()

        pre = dot(h2_ref[...], wide_ref[slot, 0]) + vec_ref[m, 7:8, :]
        act, slope = gelu_parts(pre)
        act_ref[0] = act
        slope_ref[0] = slope.astype(BF)
        acc_ref[...] += dot_nt(act, wide_ref[slot, 1])

    @pl.when(step == last)
    def _():
        out_ref[...] = (res_ref[...] + acc_ref[...] + vec_ref[0, 5:6, :]).astype(BF)
        for part in flat + wide:
            part.settle()
        line.finish_sends()


SOLVE_STEPS = 3 + NB // PIVOTS


FORWARD_PLAN = (
    (
        (0, 0),
        ((0, 0, 0),),
    ),
    (
        (1, 0),
        ((1, 0, 0), (0, 1, 1), (0, 1, -1),),
    ),
    (
        (1, 1),
        ((0, 1, -2), (0, 1, 2), (1, 1, -1), (1, 1, 1),),
    ),
    (
        (1, 2),
        ((0, 1, -3), (0, 1, 3), (3, 0, 0),),
    ),
    (
        (2, 0),
        ((1, 1, 2), (1, 1, -2),),
    ),
    (
        (4, 0),
        ((0, 2, -3), (0, 2, 3), (1, 2, 0), (0, 2, -1), (0, 2, 1),),
    ),
    (
        (5, 0),
        ((0, 2, 0), (0, 2, -2), (0, 2, 2), (1, 1, -3), (1, 1, 3), (2, 0, 0),),
    ),
    (
        (7, 0),
        ((1, 2, -2), (1, 2, 2), (1, 2, 1), (1, 2, -1),),
    ),
    (
        (8, 0),
        ((3, 1, 1), (3, 1, -1),),
    ),
    (
        (9, 0),
        ((0, 3, 3), (0, 3, -3),),
    ),
    (
        (10, 0),
        ((0, 3, 1), (0, 3, -1), (1, 2, 3), (1, 2, -3), (0, 3, 0), (0, 3, 2), (0, 3, -2), (3, 1, -2), (3, 1, 2),),
    ),
    (
        (10, 1),
        ((3, 1, 3), (3, 1, -3), (1, 3, 0), (1, 3, 1), (1, 3, -2), (1, 3, 3), (1, 3, -1), (1, 3, 2), (1, 3, -3),),
    ),
    (
        (10, 2),
        ((2, 1, -1), (2, 1, 1),),
    ),
    (
        (11, 0),
        ((2, 1, -2), (2, 1, 2),),
    ),
    (
        (11, 1),
        ((2, 1, 3), (2, 1, -3), (3, 2, 0),),
    ),
    (
        (12, 0),
        ((2, 2, 1), (2, 2, -1), (2, 2, 0),),
    ),
    (
        (12, 1),
        ((2, 2, -3), (2, 2, 3), (3, 2, -2), (3, 2, 2),),
    ),
    (
        (13, 0),
        ((3, 2, -1), (3, 2, 1), (2, 2, 2), (2, 2, -2),),
    ),
    (
        (13, 1),
        ((2, 3, -1), (2, 3, 1), (3, 2, 3), (3, 2, -3), (2, 3, 0),),
    ),
    (
        (13, 2),
        ((3, 3, 0), (2, 3, 3), (2, 3, -3),),
    ),
    (
        (14, 1),
        ((3, 3, 1), (3, 3, -1), (3, 3, 2), (3, 3, -2), (2, 3, -2), (2, 3, 2), (3, 3, 3), (3, 3, -3),),
    ),
)


def forward_pass(tokens, past, meta, room, attn, up, down, head):
    width = tokens.shape[1]
    rows = tokens.shape[0] // LINE
    items = past.shape[0]
    local = width // LINE
    hidden = up.shape[1]
    heads = local // head
    keyed = NB + rows
    samples = items * meta.shape[1]
    attn_at = SOLVE_STEPS
    mlp_at = attn_at + LINE
    first = lambda i: jnp.clip(i - attn_at, 0, LINE - 1)
    second = lambda i: jnp.clip(i - mlp_at, 0, LINE - 1)
    whole = lambda shape: pl.BlockSpec(shape, lambda i: (0,) * len(shape))
    anywhere = pl.BlockSpec(memory_space=pl.ANY)
    vmem = pl.BlockSpec(memory_space=pltpu.VMEM)
    dma = pltpu.SemaphoreType.DMA
    shape = jax.ShapeDtypeStruct
    return pl.pallas_call(
        functools.partial(forward_kernel, items=items, head=head),
        grid=(mlp_at + LINE,),
        in_specs=[anywhere, anywhere, vmem, vmem, anywhere, anywhere, anywhere],
        out_specs=[
            anywhere,
            anywhere,
            anywhere,
            whole((rows, width)),
            whole((rows, width)),
            whole((width, keyed)),
            whole((width, rows)),
            pl.BlockSpec((1, heads, keyed, rows), lambda i: (first(i), 0, 0, 0)),
            pl.BlockSpec((1, keyed, local), lambda i: (first(i), 0, 0)),
            pl.BlockSpec((1, keyed, local), lambda i: (first(i), 0, 0)),
            pl.BlockSpec((1, rows, local), lambda i: (first(i), 0, 0)),
            pl.BlockSpec((1, local, rows), lambda i: (first(i), 0, 0)),
            pl.BlockSpec((1, rows, hidden), lambda i: (second(i), 0, 0)),
            pl.BlockSpec((1, rows, hidden), lambda i: (second(i), 0, 0)),
            whole((LINE, 16, width)),
            whole((NB, NB)),
            whole((NB, width)),
        ],
        out_shape=[
            shape((LINE, width, width), BF),
            shape((LINE, width, hidden), BF),
            shape((LINE, width, hidden), BF),
            shape((rows, width), BF),
            shape((rows, width), F32),
            shape((width, keyed), BF),
            shape((width, rows), BF),
            shape((LINE, heads, keyed, rows), BF),
            shape((LINE, keyed, local), BF),
            shape((LINE, keyed, local), BF),
            shape((LINE, rows, local), BF),
            shape((LINE, local, rows), BF),
            shape((LINE, rows, hidden), BF),
            shape((LINE, rows, hidden), BF),
            shape((LINE, 16, width), F32),
            shape((NB, NB), F32),
            shape((NB, width), BF),
        ],
        scratch_shapes=[
            pltpu.VMEM((keyed, width), BF),
            pltpu.VMEM((rows, width), BF),
            pltpu.VMEM((rows, width), BF),
            pltpu.VMEM((rows, width), F32),
            pltpu.VMEM((NB, local), F32),
            pltpu.VMEM((samples, local), BF),
            pltpu.VMEM((1, PLANE * samples, local), BF),
            pltpu.VMEM((PLANE, samples, NB), F32),
            pltpu.VMEM((1, PLANE * 8, meta.shape[1]), F32),
            pltpu.VMEM((LINE, PLANE * 16, width), BF),
            pltpu.VMEM((NB, local), BF),
            pltpu.VMEM((LINE, NB, local), BF),
            pltpu.VMEM((2, 2, width, width), BF),
            pltpu.VMEM(past.shape, BF),
            dma((2, 5, 4)),
            dma((2, PLANE)),
            dma((2,)),
            dma((4, 5, LINE * 4)),
            dma((4, LINE * PLANE)),
            dma((4,)),
            dma((2, LINE)),
            dma((LINE,)),
            dma(()),
            dma((2, 2)),
        ],
        compiler_params=pltpu.CompilerParams(
            collective_id=1, has_side_effects=True, vmem_limit_bytes=BIG_VMEM
        ),
        name="forward_pass",
    )(tokens, past, meta, room, attn, up, down)


def plain_forward_kernel(
    tok_ref,
    coef_ref,
    vec_ref,
    wa_ref,
    wu_ref,
    wd_ref,
    out_ref,
    res_ref,
    hm_ref,
    h2_ref,
    prob_ref,
    key_ref,
    val_ref,
    query_ref,
    att_ref,
    act_ref,
    slope_ref,
    acc_ref,
    *,
    groups,
    head,
):
    step = pl.program_id(0)
    rows, width = tok_ref.shape
    local = query_ref.shape[2]

    @pl.when(step == 0)
    def _():
        gain, bias = vec_ref[0, 0:1, :], vec_ref[0, 1:2, :]
        normed, _ = norm_parts(coef_ref[...].astype(F32))
        hm_ref[0:NB, :] = (normed * gain + bias).astype(BF)
        normed, _ = norm_parts(tok_ref[...].astype(F32))
        hm_ref[NB:, :] = (normed * gain + bias).astype(BF)
        acc_ref[...] = jnp.zeros_like(acc_ref)

    @pl.when(step < groups)
    def _():
        weights = wa_ref[0]
        projected = project(hm_ref[...], weights, vec_ref[step, 6:7, :], local)
        query = projected[NB:, :local]
        keys = projected[:, local : 2 * local]
        values = projected[:, 2 * local :]
        query_ref[0] = query
        key_ref[0] = keys
        val_ref[0] = values

        def store(h, lines, columns, probs):
            prob_ref[0, h, lines, columns] = probs

        attended = attend(query, keys, values, head, store, lambda h: None)
        att_ref[0] = attended
        acc_ref[...] += dot_nt(attended.T, weights[:, 3 * local :])

    @pl.when(step == groups)
    def _():
        residual = tok_ref[...].astype(F32) + acc_ref[...] + vec_ref[0, 4:5, :]
        res_ref[...] = residual
        normed, _ = norm_parts(residual)
        h2_ref[...] = (normed * vec_ref[0, 2:3, :] + vec_ref[0, 3:4, :]).astype(BF)
        acc_ref[...] = jnp.zeros_like(acc_ref)

    @pl.when(step >= groups)
    def _():
        pre = dot(h2_ref[...], wu_ref[0]) + vec_ref[step - groups, 7:8, :]
        act, slope = gelu_parts(pre)
        act_ref[0] = act
        slope_ref[0] = slope.astype(BF)
        acc_ref[...] += dot_nt(act, wd_ref[0])

    @pl.when(step == 2 * groups - 1)
    def _():
        out_ref[...] = (res_ref[...] + acc_ref[...] + vec_ref[0, 5:6, :]).astype(BF)


def plain_forward(tok, coef, vec, wide, head):
    rows, width = tok.shape
    groups = wide[0].shape[0]
    local = width // groups
    hidden = wide[1].shape[2]
    heads = local // head
    keyed = NB + rows
    first = lambda i: jnp.minimum(i, groups - 1)
    second = lambda i: jnp.maximum(i - groups, 0)
    whole = lambda shape: pl.BlockSpec(shape, lambda i: (0,) * len(shape))
    shape = jax.ShapeDtypeStruct
    return pl.pallas_call(
        functools.partial(plain_forward_kernel, groups=groups, head=head),
        grid=(2 * groups,),
        in_specs=[
            whole((rows, width)),
            whole((NB, width)),
            whole((groups, 16, width)),
            pl.BlockSpec((1, width, width), lambda i: (first(i), 0, 0)),
            pl.BlockSpec((1, width, hidden), lambda i: (second(i), 0, 0)),
            pl.BlockSpec((1, width, hidden), lambda i: (second(i), 0, 0)),
        ],
        out_specs=[
            whole((rows, width)),
            whole((rows, width)),
            whole((keyed, width)),
            whole((rows, width)),
            pl.BlockSpec((1, heads, keyed, rows), lambda i: (first(i), 0, 0, 0)),
            pl.BlockSpec((1, keyed, local), lambda i: (first(i), 0, 0)),
            pl.BlockSpec((1, keyed, local), lambda i: (first(i), 0, 0)),
            pl.BlockSpec((1, rows, local), lambda i: (first(i), 0, 0)),
            pl.BlockSpec((1, local, rows), lambda i: (first(i), 0, 0)),
            pl.BlockSpec((1, rows, hidden), lambda i: (second(i), 0, 0)),
            pl.BlockSpec((1, rows, hidden), lambda i: (second(i), 0, 0)),
        ],
        out_shape=[
            shape((rows, width), BF),
            shape((rows, width), F32),
            shape((keyed, width), BF),
            shape((rows, width), BF),
            shape((groups, heads, keyed, rows), BF),
            shape((groups, keyed, local), BF),
            shape((groups, keyed, local), BF),
            shape((groups, rows, local), BF),
            shape((groups, local, rows), BF),
            shape((groups, rows, hidden), BF),
            shape((groups, rows, hidden), BF),
        ],
        scratch_shapes=[pltpu.VMEM((rows, width), F32)],
        compiler_params=pltpu.CompilerParams(vmem_limit_bytes=BIG_VMEM),
        name="plain_forward",
    )(tok, coef, vec, *wide)


def attend_back(g_att, att_t, keys, values, query, probs_of, head, between):
    rows, local = g_att.shape
    half = rows // 2
    low = NB + rows - half
    g_att_t = g_att.T
    product = g_att_t.astype(F32) * att_t.astype(F32)
    key_t = keys.T
    scale = 1.0 / math.sqrt(head)
    line = lax.broadcasted_iota(jnp.int32, (local, rows), 0)
    lane = lax.broadcasted_iota(jnp.int32, (rows, local), 1)
    key_grad = [jnp.zeros((low, local), F32), jnp.zeros((half, local), F32)]
    val_grad = [jnp.zeros((low, local), F32), jnp.zeros((half, local), F32)]
    query_grads = []
    for h in range(local // head):
        own_t = (line >= h * head) & (line < (h + 1) * head)
        own = (lane >= h * head) & (lane < (h + 1) * head)
        grad_t = jnp.where(own_t, g_att_t, BF(0.0))
        grad_h = jnp.where(own, g_att, BF(0.0))
        query_h = jnp.where(own, query, BF(0.0))
        inner = jnp.sum(product[h * head : (h + 1) * head, :], axis=0, keepdims=True)
        key_h = key_t[h * head : (h + 1) * head, :]
        parts = []
        for b in range(2):
            span = NB + (b + 1) * half
            cols = slice(b * half, (b + 1) * half)
            probs = probs_of(h, slice(0, span), cols)
            dprob = dot(values[:span, :], grad_t[:, cols])
            dscore = (probs.astype(F32) * (dprob - inner[:, cols])).astype(BF)
            parts.append(dot(key_h[:, :span], dscore))
            val_part = dot(probs, grad_h[cols, :])
            key_part = dot(dscore, query_h[cols, :])
            val_grad[0] = val_grad[0] + val_part[:low, :]
            key_grad[0] = key_grad[0] + key_part[:low, :]
            if b == 1:
                val_grad[1] = val_grad[1] + val_part[low:, :]
                key_grad[1] = key_grad[1] + key_part[low:, :]
        query_grads.append(jnp.concatenate(parts, axis=1))
        between(h)
    query_grad = (jnp.concatenate(query_grads, axis=0) * scale).astype(BF).T
    key_grad = jnp.concatenate(key_grad, axis=0) * scale
    return query_grad, key_grad, jnp.concatenate(val_grad, axis=0)


def backward_kernel(
    tokens_ref,
    cots_ref,
    fwd_out_ref,
    res_ref,
    wa_ref,
    wu_ref,
    wd_ref,
    vec_ref,
    hmt_ref,
    h2t_ref,
    coef_ref,
    inv_ref,
    meta_ref,
    prob_ref,
    key_ref,
    val_ref,
    query_ref,
    att_ref,
    act_ref,
    slope_ref,
    outs_ref,
    tgs_ref,
    past_ref,
    gv_mem_ref,
    side_out_ref,
    attn_out_ref,
    mlp_out_ref,
    *scratch,
    head,
):
    (
        tok_ref,
        cot_ref,
        cott_ref,
        gres_ref,
        acc_ref,
        proj_ref,
        gv_ref,
        ggv_ref,
        gmem_ref,
        wide_ref,
        side_ref,
        attn_ref,
        mlp_ref,
    ) = scratch[:13]
    buffers = scratch[13:28]
    block_sems, sems, lsend, lrecv, lown, gsend, grecv, gown, load_sem = scratch[28:]
    step = pl.program_id(0)
    rows, width = tok_ref.shape
    local = query_ref.shape[2]
    items = past_ref.shape[0]
    place = Place()
    side, attn, mlp = [
        Collect(place, grads, out, buffers[i::3], (block_sems.at[i], sems.at[i]))
        for i, (grads, out) in enumerate(
            ((side_ref, side_out_ref), (attn_ref, attn_out_ref), (mlp_ref, mlp_out_ref))
        )
    ]
    outs = Line(place, fwd_out_ref, outs_ref, lsend.at[0], lrecv.at[0], lown.at[0])
    tgs = Line(place, cot_ref, tgs_ref, lsend.at[1], lrecv.at[1], lown.at[1])
    mem = Spread(place, side_out_ref.at[0, 0:8, :], gmem_ref, gsend, grecv, gown)
    mine = pl.ds(place.z * rows, rows)

    def load(ref, m, slot, which):
        return pltpu.make_async_copy(ref.at[m], wide_ref.at[slot, which], load_sem.at[slot, which])

    def bring(i, src, dst):
        return pltpu.make_async_copy(src, dst, load_sem.at[2, i])

    bring_cot = bring(0, cots_ref.at[mine, :], cot_ref)
    bring_tok = bring(1, tokens_ref.at[mine, :], tok_ref)
    bring_res = pltpu.make_async_copy(res_ref, gres_ref, load_sem.at[3, 0])
    at_step = {}

    @pl.when(step == 0)
    def _():
        bring_cot.start()
        bring_tok.start()
        bring_res.start()
        load(wu_ref, 0, 0, 0).start()
        load(wd_ref, 0, 0, 1).start()
        greet(place)
        outs.first()
        acc_ref[...] = jnp.zeros_like(acc_ref)
        gv_ref[...] = jnp.zeros_like(gv_ref)
        bring_cot.wait()
        bring_tok.wait()
        bring_res.wait()
        cott_ref[...] = cot_ref[...].T

    @pl.when(step < LINE)
    def _():
        m = step
        slot = lax.rem(m, 2)
        load(wu_ref, m, slot, 0).wait()
        load(wd_ref, m, slot, 1).wait()

        @pl.when(m < LINE - 1)
        def _():
            load(wu_ref, m + 1, 1 - slot, 0).start()
            load(wd_ref, m + 1, 1 - slot, 1).start()

        @pl.when(m == LINE - 1)
        def _():
            load(wa_ref, 0, 0, 0).start()

        upstream = cot_ref[...]
        grad = (dot(upstream, wide_ref[slot, 1]) * slope_ref[0].astype(F32)).astype(BF)
        mlp_ref[m, 1] = dot(cott_ref[...], act_ref[0]).astype(BF)
        mlp_ref[m, 0] = dot(h2t_ref[...], grad).astype(BF)
        mlp.begin(m)
        ggv_ref[m, 1:2, :] = col_sum(grad.astype(F32))
        acc_ref[NB:, :] += dot_nt(grad, wide_ref[slot, 0])

    @pl.when(step == 3)
    def _():
        outs.step(1)

    @pl.when(step == LINE)
    def _():
        for i in range(2):
            mlp.corner(i)
        upstream = cot_ref[...].astype(F32)
        normed, inverse = norm_parts(gres_ref[...])
        grad = acc_ref[NB:, :]
        g_res = upstream + norm_back(grad, normed, inverse, vec_ref[0, 2:3, :])
        gres_ref[...] = g_res
        g_attn = g_res.astype(BF)
        gv_ref[2:3, :] = col_sum(grad * normed)
        gv_ref[3:4, :] = col_sum(grad)
        gv_ref[4:5, :] = col_sum(g_attn.astype(F32))
        gv_ref[5:6, :] = col_sum(upstream)
        cott_ref[...] = g_attn.T
        acc_ref[...] = jnp.zeros_like(acc_ref)
        proj_ref[0:NB, :] = jnp.zeros((NB, proj_ref.shape[1]), BF)
        for i in range(2, 4):
            mlp.corner(i)

    part = functools.partial
    plan = {
        (0, 0): [part(mlp.sides, 0), part(mlp.sides, 1)],
        (0, 1): [part(mlp.sides, 2), part(mlp.sides, 3)],
        (1, 0): [part(mlp.relay, 0)],
        (1, 1): [part(mlp.relay, 1)],
        (2, 0): [part(outs.step, 2)],
        (2, 1): [part(mlp.relay, 2)],
        (2, 2): [part(mlp.relay, 3)],
        (3, 0): [part(mlp.line, 0)],
        (3, 2): [part(mlp.line, 1)],
    }

    @pl.when(step >= LINE)
    def _():
        m = step - LINE
        slot = lax.rem(m, 2)
        load(wa_ref, m, slot, 0).wait()

        @pl.when(m < LINE - 1)
        def _():
            load(wa_ref, m + 1, 1 - slot, 0).start()

        def between(h):
            for (at, position), steps in plan.items():
                if position == h:

                    @pl.when(m == at)
                    def _():
                        for one in steps:
                            one()

        def probs_of(h, lines, columns):
            return prob_ref[0, h, lines, columns]

        g_attn = gres_ref[...].astype(BF)
        g_att = dot(g_attn, wide_ref[slot, 0, :, 3 * local :]).astype(BF)
        att_t = att_ref[0]
        query_grad, key_grad, val_grad = attend_back(
            g_att, att_t, key_ref[0], val_ref[0], query_ref[0], probs_of, head, between
        )
        proj_ref[NB:, 0:local] = query_grad
        proj_ref[:, local : 2 * local] = key_grad.astype(BF)
        proj_ref[:, 2 * local :] = val_grad.astype(BF)
        proj = proj_ref[...]
        ggv_ref[m, 0:1, 0 : 3 * local] = col_sum(proj.astype(F32))
        ggv_ref[m, 0:1, 3 * local :] = jnp.zeros((1, width - 3 * local), F32)
        attn_ref[m, 0, :, 0 : 3 * local] = dot(hmt_ref[...], proj).astype(BF)
        attn_ref[m, 0, :, 3 * local :] = dot_nt(cott_ref[...], att_t).astype(BF)
        attn.begin(m)
        acc_ref[...] += dot_nt(proj, wide_ref[slot, 0, :, : 3 * local])

    @pl.when(step == 2 * LINE - 1)
    def _():
        grad = acc_ref[NB:, :]
        normed, inverse = norm_parts(tok_ref[...].astype(F32))
        back = norm_back(grad, normed, inverse, vec_ref[0, 0:1, :])
        cot_ref[...] = (gres_ref[...] + back).astype(BF)
        tgs.first()
        gv_ref[0:1, :] = col_sum(grad * normed)
        gv_ref[1:2, :] = col_sum(grad)
        for m in range(LINE):
            below = jnp.concatenate([gv_ref[0:6, :], ggv_ref[m, 0:2, :]], axis=0)
            for s in range(PLANE):
                top = (m * PLANE + s) * 8
                block = jnp.concatenate([acc_ref[top : top + 8, :], below], axis=0)
                side_ref[m, 0, s * 16 : (s + 1) * 16, :] = block.astype(BF)
            side.begin(m)

        @pl.loop(0, LINE)
        def _(i):
            side.corner(i)

        @pl.loop(0, LINE)
        def _(i):
            side.sides(i)

        @pl.loop(0, LINE)
        def _(i):
            attn.corner(i)

        @pl.loop(2, LINE)
        def _(i):
            mlp.line(i)

        outs.step(3)

        @pl.loop(0, LINE)
        def _(i):
            side.relay(i)

        @pl.loop(0, LINE)
        def _(i):
            attn.sides(i)

        @pl.loop(0, LINE)
        def _(i):
            side.line(i)

        mlp.result()
        tgs.step(1)
        side.result()
        mem.first()

        @pl.loop(0, LINE)
        def _(i):
            attn.relay(i)

        for kind in (1, 2, 3):
            for one in mem.steps(kind):
                one()
        tgs.step(2)

        @pl.loop(0, LINE)
        def _(i):
            attn.line(i)

        mem.own.wait()
        for m in range(LINE):
            mem.close(m)
        gmem = jnp.concatenate([gmem_ref[m] for m in range(LINE)], axis=0)
        give_past(gmem, coef_ref, vec_ref, inv_ref, meta_ref, past_ref, gv_mem_ref)
        attn.result()
        tgs.step(3)
        mem.settle()
        for part_ in (side, attn, mlp):
            part_.settle()
        outs.finish()
        tgs.finish()


def backward_pass(tokens, cots, out, meta, vec, inverse, coef, saved, wide, items, past_shape, head):
    res, hmt, h2t, prob, keys, vals, query, att, act, slope = saved
    rows, width = out.shape
    local = width // LINE
    hidden = wide[1].shape[2]
    heads = local // head
    keyed = NB + rows
    first = lambda i: jnp.minimum(i, LINE - 1)
    second = lambda i: jnp.maximum(i - LINE, 0)
    anywhere = pl.BlockSpec(memory_space=pl.ANY)
    vmem = pl.BlockSpec(memory_space=pltpu.VMEM)
    dma = pltpu.SemaphoreType.DMA
    shape = jax.ShapeDtypeStruct
    blocks = ((1, 16, width), (1, width // PLANE, width), (2, width // PLANE, width))
    return pl.pallas_call(
        functools.partial(backward_kernel, head=head),
        grid=(2 * LINE,),
        in_specs=[anywhere] * 7
        + [vmem] * 6
        + [
            pl.BlockSpec((1, heads, keyed, rows), lambda i: (second(i), 0, 0, 0)),
            pl.BlockSpec((1, keyed, local), lambda i: (second(i), 0, 0)),
            pl.BlockSpec((1, keyed, local), lambda i: (second(i), 0, 0)),
            pl.BlockSpec((1, rows, local), lambda i: (second(i), 0, 0)),
            pl.BlockSpec((1, local, rows), lambda i: (second(i), 0, 0)),
            pl.BlockSpec((1, rows, hidden), lambda i: (first(i), 0, 0)),
            pl.BlockSpec((1, rows, hidden), lambda i: (first(i), 0, 0)),
        ],
        out_specs=[anywhere, anywhere, vmem, vmem, vmem, vmem, vmem],
        out_shape=[
            shape((LINE, rows, width), BF),
            shape((LINE, rows, width), BF),
            shape(past_shape, F32),
            shape((8, width), F32),
        ]
        + [shape(b, F32) for b in blocks],
        scratch_shapes=[
            pltpu.VMEM((rows, width), BF),
            pltpu.VMEM((rows, width), BF),
            pltpu.VMEM((width, rows), BF),
            pltpu.VMEM((rows, width), F32),
            pltpu.VMEM((keyed, width), F32),
            pltpu.VMEM((keyed, 3 * local), BF),
            pltpu.VMEM((8, width), F32),
            pltpu.VMEM((LINE, 8, hidden), F32),
            pltpu.VMEM((LINE, PLANE * 8, width), F32),
            pltpu.VMEM((2, 2, width, width), BF),
        ]
        + [pltpu.VMEM((LINE, b[0], PLANE * b[1], b[2]), BF) for b in blocks]
        + [pltpu.VMEM(lead + b, BF) for lead in BUFFERS for b in blocks]
        + [
            dma((3, 2, 4, LINE)),
            dma((3, 9, LINE)),
            dma((2, 2, LINE)),
            dma((2, LINE)),
            dma((2,)),
            dma((5, LINE * 4)),
            dma((LINE * PLANE,)),
            dma(()),
            dma((4, 2)),
        ],
        compiler_params=pltpu.CompilerParams(
            collective_id=2, has_side_effects=True, vmem_limit_bytes=MAX_VMEM
        ),
        name="backward_pass",
    )(
        tokens,
        cots,
        out,
        res,
        *wide,
        vec,
        hmt,
        h2t,
        coef,
        inverse,
        meta,
        prob,
        keys,
        vals,
        query,
        att,
        act,
        slope,
    )


def plain_backward_kernel(
    tok_ref,
    cot_ref,
    res_ref,
    vec_ref,
    hm_ref,
    h2_ref,
    prob_ref,
    key_ref,
    val_ref,
    query_ref,
    att_ref,
    act_ref,
    slope_ref,
    wa_ref,
    wu_ref,
    wd_ref,
    tg_ref,
    gmem_ref,
    gup_ref,
    gdown_ref,
    gatt_ref,
    gv_ref,
    ggv_ref,
    acc_ref,
    hmt_ref,
    h2t_ref,
    cott_ref,
    gres_ref,
    proj_ref,
    *,
    groups,
    head,
):
    step = pl.program_id(0)
    rows, width = tok_ref.shape
    local = query_ref.shape[2]

    @pl.when(step == 0)
    def _():
        acc_ref[...] = jnp.zeros_like(acc_ref)
        h2t_ref[...] = h2_ref[...].T
        cott_ref[...] = cot_ref[...].T
        gv_ref[...] = jnp.zeros_like(gv_ref)

    @pl.when(step < groups)
    def _():
        upstream = cot_ref[...]
        grad = (dot(upstream, wd_ref[0]) * slope_ref[0].astype(F32)).astype(BF)
        gdown_ref[0] = dot(cott_ref[...], act_ref[0]).astype(BF)
        gup_ref[0] = dot(h2t_ref[...], grad).astype(BF)
        ggv_ref[0] = jnp.zeros_like(ggv_ref[0])
        ggv_ref[0, 0:1, :] = col_sum(grad.astype(F32))
        acc_ref[NB:, :] += dot_nt(grad, wu_ref[0])

    @pl.when(step == groups)
    def _():
        upstream = cot_ref[...].astype(F32)
        normed, inverse = norm_parts(res_ref[...])
        grad = acc_ref[NB:, :]
        g_res = upstream + norm_back(grad, normed, inverse, vec_ref[2:3, :])
        gres_ref[...] = g_res
        g_attn = g_res.astype(BF)
        gv_ref[2:3, :] = col_sum(grad * normed)
        gv_ref[3:4, :] = col_sum(grad)
        gv_ref[4:5, :] = col_sum(g_attn.astype(F32))
        gv_ref[5:6, :] = col_sum(upstream)
        cott_ref[...] = g_attn.T
        hmt_ref[...] = hm_ref[...].T
        acc_ref[...] = jnp.zeros_like(acc_ref)
        proj_ref[0:NB, :] = jnp.zeros((NB, proj_ref.shape[1]), BF)

    @pl.when(step >= groups)
    def _():
        weights = wa_ref[0]
        g_attn = gres_ref[...].astype(BF)
        g_att = dot(g_attn, weights[:, 3 * local :]).astype(BF)
        att_t = att_ref[0]
        query_grad, key_grad, val_grad = attend_back(
            g_att,
            att_t,
            key_ref[0],
            val_ref[0],
            query_ref[0],
            lambda h, lines, columns: prob_ref[0, h, lines, columns],
            head,
            lambda h: None,
        )
        key_grad, val_grad = key_grad.astype(BF), val_grad.astype(BF)
        proj_ref[NB:, 0:local] = query_grad
        proj_ref[:, local : 2 * local] = key_grad
        proj_ref[:, 2 * local :] = val_grad
        proj = proj_ref[...]
        ggv_ref[0] = jnp.zeros_like(ggv_ref[0])
        ggv_ref[0, 0:1, 0 : 3 * local] = col_sum(proj.astype(F32))
        gatt_ref[0, :, 0 : 3 * local] = dot(hmt_ref[...], proj).astype(BF)
        gatt_ref[0, :, 3 * local :] = dot_nt(cott_ref[...], att_t).astype(BF)
        acc_ref[...] += dot_nt(proj, weights[:, : 3 * local])

    @pl.when(step == 2 * groups - 1)
    def _():
        gmem_ref[...] = acc_ref[0:NB, :]
        grad = acc_ref[NB:, :]
        normed, inverse = norm_parts(tok_ref[...].astype(F32))
        part = norm_back(grad, normed, inverse, vec_ref[0:1, :])
        tg_ref[...] = (gres_ref[...] + part).astype(BF)
        gv_ref[0:1, :] = col_sum(grad * normed)
        gv_ref[1:2, :] = col_sum(grad)


def plain_backward(tok, cot, vec, saved, wide, head):
    res, hm, h2, prob, keys, vals, query, att, act, slope = saved
    rows, width = tok.shape
    groups = wide[0].shape[0]
    local = width // groups
    hidden = wide[1].shape[2]
    heads = local // head
    keyed = NB + rows
    first = lambda i: jnp.minimum(i, groups - 1)
    second = lambda i: jnp.maximum(i - groups, 0)
    whole = lambda shape: pl.BlockSpec(shape, lambda i: (0,) * len(shape))
    return pl.pallas_call(
        functools.partial(plain_backward_kernel, groups=groups, head=head),
        grid=(2 * groups,),
        in_specs=[
            whole((rows, width)),
            whole((rows, width)),
            whole((rows, width)),
            whole((16, width)),
            whole((keyed, width)),
            whole((rows, width)),
            pl.BlockSpec((1, heads, keyed, rows), lambda i: (second(i), 0, 0, 0)),
            pl.BlockSpec((1, keyed, local), lambda i: (second(i), 0, 0)),
            pl.BlockSpec((1, keyed, local), lambda i: (second(i), 0, 0)),
            pl.BlockSpec((1, rows, local), lambda i: (second(i), 0, 0)),
            pl.BlockSpec((1, local, rows), lambda i: (second(i), 0, 0)),
            pl.BlockSpec((1, rows, hidden), lambda i: (first(i), 0, 0)),
            pl.BlockSpec((1, rows, hidden), lambda i: (first(i), 0, 0)),
            pl.BlockSpec((1, width, width), lambda i: (second(i), 0, 0)),
            pl.BlockSpec((1, width, hidden), lambda i: (first(i), 0, 0)),
            pl.BlockSpec((1, width, hidden), lambda i: (first(i), 0, 0)),
        ],
        out_specs=[
            whole((rows, width)),
            whole((NB, width)),
            pl.BlockSpec((1, width, hidden), lambda i: (first(i), 0, 0)),
            pl.BlockSpec((1, width, hidden), lambda i: (first(i), 0, 0)),
            pl.BlockSpec((1, width, width), lambda i: (second(i), 0, 0)),
            whole((8, width)),
            pl.BlockSpec((1, 8, hidden), lambda i: (i, 0, 0)),
        ],
        out_shape=[
            jax.ShapeDtypeStruct((rows, width), BF),
            jax.ShapeDtypeStruct((NB, width), F32),
            jax.ShapeDtypeStruct((groups, width, hidden), BF),
            jax.ShapeDtypeStruct((groups, width, hidden), BF),
            jax.ShapeDtypeStruct((groups, width, width), BF),
            jax.ShapeDtypeStruct((8, width), F32),
            jax.ShapeDtypeStruct((2 * groups, 8, hidden), F32),
        ],
        scratch_shapes=[
            pltpu.VMEM((keyed, width), F32),
            pltpu.VMEM((width, keyed), BF),
            pltpu.VMEM((width, rows), BF),
            pltpu.VMEM((width, rows), BF),
            pltpu.VMEM((rows, width), F32),
            pltpu.VMEM((keyed, 3 * local), BF),
        ],
        compiler_params=pltpu.CompilerParams(vmem_limit_bytes=BIG_VMEM),
        name="plain_backward",
    )(
        tok, cot, res, vec, hm, h2, prob, keys, vals, query, att, act, slope, *wide
    )


def local(
    tokens,
    cotangent,
    past_state,
    positions,
    counts,
    ln1_gain,
    ln1_bias,
    w_qkv,
    b_qv,
    w_out,
    b_out,
    ln2_gain,
    ln2_bias,
    w_up,
    b_up,
    w_down,
    b_down,
):
    seq, mp = lax.axis_size("seq"), lax.axis_size("mp")
    seq_index, mp_index = lax.axis_index("seq"), lax.axis_index("mp")
    item_count, seg_len, local_width = past_state.shape
    slots = positions.shape[1]
    total = item_count * seq
    width = tokens.shape[1]
    part = width // seq
    heads_local, piece = b_qv.shape[1], b_qv.shape[2]
    head = piece * seq
    hidden = w_up.shape[1]
    rows = tokens.shape[0] // mp
    direct = seq == PLANE and mp == LINE and part % 16 == 0 and hidden == width

    items = (seq_index * item_count + jnp.arange(item_count)).astype(F32)
    spots = positions.astype(F32)
    places = (items[:, None] + (spots + 0.5) / seg_len) / total
    used = (jnp.arange(slots)[None, :] < counts[:, None]).astype(F32)
    meta = jnp.concatenate([places, used, spots, jnp.zeros((8 - 3 * item_count, slots), F32)])

    here = (jnp.arange(seq) == seq_index).astype(BF)
    vectors = jnp.stack([ln1_gain, ln1_bias, ln2_gain, ln2_bias, b_out, b_down])
    vectors = (vectors[:, None, :] * here[None, :, None]).reshape(6, width)
    bias_qv = (b_qv[:, :, None, :] * here[None, None, :, None]).reshape(2, local_width)
    bias_qv = jnp.concatenate([bias_qv, jnp.zeros((2, local_width), BF)], axis=1)
    bias_up = (b_up[:, None, :] * here[None, :, None]).reshape(1, hidden)
    room = jnp.concatenate([vectors, bias_qv.reshape(1, width), bias_up, jnp.zeros((8, width), BF)])
    attn = jnp.concatenate([w_qkv[0], w_qkv[1], w_qkv[2], w_out.T], axis=1)

    if direct:
        results = forward_pass(tokens, past_state, meta, room, attn, w_up, w_down.T, head)
        wide, forward, (vec, inverse, coef) = results[:3], results[3:14], results[14:]
    else:
        sampled = sample_rows(past_state, meta)
        all_sampled = lax.all_gather(sampled, "seq", axis=0)
        all_meta = lax.all_gather(meta, "seq", axis=0)
        coef_part, inverse = solve_memory(all_sampled, all_meta, item_count)
        coef = lax.all_gather(coef_part, "mp", axis=0).transpose(1, 0, 2).reshape(NB, width)
        wide = [
            lax.all_gather(lax.all_gather(shard, "seq", axis=0, tiled=True), "mp", axis=0)
            for shard in (attn, w_up, w_down.T)
        ]
        vec = lax.psum(room.astype(F32), "seq")
        vec = lax.all_gather(vec, "mp", axis=0)
        tok = lax.dynamic_slice_in_dim(tokens, mp_index * rows, rows, 0)
        cot = lax.dynamic_slice_in_dim(cotangent, mp_index * rows, rows, 0)
        forward = plain_forward(tok, coef, vec, wide, head)
    if direct:
        block_out, block_grad, past_grad, gv_mem, side, attn, mlp = backward_pass(
            tokens,
            cotangent,
            forward[0],
            meta,
            vec,
            inverse,
            coef,
            forward[1:],
            wide,
            item_count,
            past_state.shape,
            head,
        )
        block_out = block_out.reshape(mp * rows, width)
        block_grad = block_grad.reshape(mp * rows, width)
        own, attn, up_grad, down_grad = side[0, 8:], attn[0], mlp[0], mlp[1]
    else:
        block_out = lax.all_gather(forward[0], "mp", axis=0, tiled=True)
        tok_grad, gmem, g_up, g_down, g_attn, gv, ggv = plain_backward(
            tok, cot, vec[0], forward[1:], wide, head
        )
        tail = jnp.concatenate(
            [jnp.broadcast_to(gv[None, :6], (mp, 6, width)), ggv[mp:, :1], ggv[:mp, :1]], axis=1
        )
        block_grad = lax.all_gather(tok_grad, "mp", axis=0, tiled=True)
        gmem, tail = lax.psum((gmem, tail), ("seq", "mp"))
        own = lax.dynamic_index_in_dim(tail, mp_index, 0, keepdims=False)
        attn, up_grad, down_grad = (
            lax.psum_scatter(
                lax.psum_scatter(g, "mp", scatter_dimension=0, tiled=False),
                "seq",
                scatter_dimension=0,
                tiled=True,
            ).astype(F32)
            for g in (g_attn, g_up, g_down)
        )
        past_grad, gv_mem = past_grads(
            gmem, coef, vec, inverse, meta, item_count, seg_len, local_width
        )
    own = own + jnp.concatenate([gv_mem[:2], jnp.zeros((6, width), F32)])
    vec_own = lax.dynamic_slice_in_dim(own[:6], seq_index * part, part, 1)
    qv = jnp.stack([own[6, :local_width], own[6, 2 * local_width : 3 * local_width]])
    qv = qv.reshape(2, heads_local, head)
    qv = lax.dynamic_slice_in_dim(qv, seq_index * piece, piece, 2)
    up = lax.dynamic_slice_in_dim(own[7].reshape(-1, head), seq_index * piece, piece, 1)
    qkv_grad = jnp.stack([attn[:, i * local_width : (i + 1) * local_width] for i in range(3)])
    return (
        block_out,
        block_grad,
        past_grad,
        vec_own[0],
        vec_own[1],
        qkv_grad,
        qv,
        attn[:, 3 * local_width :].T,
        vec_own[4],
        vec_own[2],
        vec_own[3],
        up_grad,
        up,
        down_grad.T,
        vec_own[5],
    )


def solution(mesh):
    row = P("seq", None)
    placed = (
        row,
        row,
        P("seq", None, "mp"),
        row,
        P("seq"),
        P("seq"),
        P("seq"),
        P(None, "seq", "mp"),
        P(None, "mp", "seq"),
        P("mp", "seq"),
        P("seq"),
        P("seq"),
        P("seq"),
        P("seq", "mp"),
        P("mp", "seq"),
        P("mp", "seq"),
        P("seq"),
    )
    return jax.shard_map(
        local,
        mesh=mesh,
        in_specs=placed,
        out_specs=(row, row, placed[2]) + placed[5:],
        check_vma=False,
    )
```

```python
import functools
import math

import jax
import jax.numpy as jnp
from jax import lax
from jax.experimental import pallas as pl
from jax.experimental.pallas import tpu as pltpu
from jax.sharding import PartitionSpec as P

NB = 256
PIVOTS = 32
NORM_EPSILON = 1e-05
RIDGE_WEIGHT = 1.0
NARROW_WIDTH = 0.01
BROAD_WIDTH = 0.05
GELU_SCALE = 0.7978845608028654
GELU_CUBIC = 0.044715

BF = jnp.bfloat16
F32 = jnp.float32
HIGHEST = lax.Precision.HIGHEST
BIG_VMEM = 60 * 1024 * 1024
MAX_VMEM = 67043328


def dot(a, b):
    return jnp.dot(a, b, preferred_element_type=F32)


def dot_nt(a, b):
    return lax.dot_general(a, b, (((1,), (1,)), ((), ())), preferred_element_type=F32)


def dot_tn(a, b, precision=None):
    return lax.dot_general(
        a, b, (((0,), (0,)), ((), ())), preferred_element_type=F32, precision=precision
    )


def norm_parts(values):
    centered = values - jnp.mean(values, axis=-1, keepdims=True)
    inverse = lax.rsqrt(jnp.mean(centered * centered, axis=-1, keepdims=True) + NORM_EPSILON)
    return centered * inverse, inverse


def norm_back(upstream, normed, inverse, gain):
    scaled = upstream * gain
    inner = scaled - jnp.mean(scaled, axis=-1, keepdims=True)
    inner = inner - normed * jnp.mean(scaled * normed, axis=-1, keepdims=True)
    return inner * inverse


def col_sum(values):
    return jnp.sum(values, axis=0, keepdims=True)


def basis_of(places, used):
    column = lax.broadcasted_iota(jnp.int32, (places.shape[0], NB), 1)
    centers = (column.astype(F32) + 0.5) / NB
    widths = jnp.where(column % 2 == 0, NARROW_WIDTH, BROAD_WIDTH).astype(F32)
    scaled = (places - centers) / widths
    return jnp.exp(-0.5 * (scaled * scaled)) * used


def meta_rows(positions, counts_ref, first, total, seg_len):
    items, slots = positions.shape
    slot = lax.broadcasted_iota(jnp.int32, (1, slots), 1)
    places, used, spots = [], [], []
    for i in range(items):
        spot = positions[i : i + 1, :].astype(F32)
        item = (first + i).astype(F32)
        places.append((item + (spot + 0.5) / seg_len) / total)
        used.append((slot < counts_ref[i]).astype(F32))
        spots.append(spot)
    return jnp.concatenate(
        places + used + spots + [jnp.zeros((8 - 3 * items, slots), F32)], axis=0
    )


def iotas(shape):
    return lax.broadcasted_iota(jnp.int32, shape, 0), lax.broadcasted_iota(jnp.int32, shape, 1)


def small_rows(stack, b_qv, b_up_t, s, width, head):
    part, piece = stack.shape[1], b_up_t.shape[0]
    row, lane = iotas((part, width))
    rows = [jnp.dot(stack, (lane == s * part + row).astype(F32), preferred_element_type=F32)]
    row, lane = iotas((piece, width))
    repeat = (lax.rem(lane, piece) == row).astype(F32)
    _, lane = iotas((1, width))
    half = width // 2
    bias = jnp.zeros((1, width), F32)
    for h in range(b_qv.shape[0]):
        spread = jnp.dot(b_qv[h], repeat, preferred_element_type=F32)
        for t in range(2):
            at = h * head + t * half + s * piece
            bias = bias + jnp.where((lane >= at) & (lane < at + piece), spread[t : t + 1], 0.0)
    row, lane = iotas((b_up_t.shape[1], width))
    spread = jnp.dot(b_up_t, (lane // head == row).astype(F32), preferred_element_type=F32)
    row, lane = iotas((piece, width))
    up = jnp.sum(jnp.where(lax.rem(lane, head) == s * piece + row, spread, 0.0), axis=0, keepdims=True)
    return jnp.concatenate(rows + [bias, up, jnp.zeros((8, width), F32)], axis=0).astype(BF)


def small_pieces(own, s, part, piece, head, heads):
    width = own.shape[1]
    half = width // 2

    def pick(values, mask):
        return jnp.dot(values, mask.astype(F32), preferred_element_type=F32, precision=HIGHEST)

    row, lane = iotas((width, part))
    vectors = pick(own, row == s * part + lane)
    biases = []
    row, lane = iotas((width, piece))
    for h in range(heads):
        two = [
            pick(own, row == h * head + t * half + s * piece + lane)[6:7] for t in range(2)
        ]
        biases.append(jnp.concatenate(two, axis=0))
    row, lane = iotas((piece, width))
    masked = jnp.where(lax.rem(lane, head) == s * piece + row, own[7:8], 0.0)
    row, lane = iotas((width, width // head))
    return vectors, biases, pick(masked, row // head == lane)


def position_of(column, i, items):
    return column[:, 2 * items + i : 2 * items + i + 1].astype(jnp.int32)


def inverse_2(a, b, c, d):
    scale = 1.0 / (a * d - b * c)
    return d * scale, -(b * scale), -(c * scale), a * scale


def product_2(x, y):
    return (
        x[0] * y[0] + x[1] * y[2],
        x[0] * y[1] + x[1] * y[3],
        x[2] * y[0] + x[3] * y[2],
        x[2] * y[1] + x[3] * y[3],
    )


def invert_step(mat_ref):
    block = PIVOTS
    lane = lax.broadcasted_iota(jnp.int32, (block, NB), 1)
    line = lax.broadcasted_iota(jnp.int32, (block, NB), 0)
    panel = mat_ref[0:block, :]
    for k in range(0, block, 4):
        cols = [jnp.broadcast_to(panel[:, k + j : k + j + 1], panel.shape) for j in range(4)]
        at = [[cols[j][k + i : k + i + 1] for j in range(4)] for i in range(4)]
        head = inverse_2(at[0][0], at[0][1], at[1][0], at[1][1])
        upper = (at[0][2], at[0][3], at[1][2], at[1][3])
        lower = (at[2][0], at[2][1], at[3][0], at[3][1])
        right, left = product_2(head, upper), product_2(lower, head)
        minus = product_2(lower, right)
        tail = inverse_2(
            at[2][2] - minus[0], at[2][3] - minus[1], at[3][2] - minus[2], at[3][3] - minus[3]
        )
        rt, tl = product_2(right, tail), product_2(tail, left)
        back = product_2(rt, left)
        inverse = (
            (head[0] + back[0], head[1] + back[1], -rt[0], -rt[1]),
            (head[2] + back[2], head[3] + back[3], -rt[2], -rt[3]),
            (-tl[0], -tl[1], tail[0], tail[1]),
            (-tl[2], -tl[3], tail[2], tail[3]),
        )
        inside = (lane >= k) & (lane < k + 4)
        rows = [
            jnp.where(inside[0:1], (lane[0:1] == k + j).astype(F32), panel[k + j : k + j + 1])
            for j in range(4)
        ]
        new = [
            (m[0] * rows[0] + m[1] * rows[1]) + (m[2] * rows[2] + m[3] * rows[3]) for m in inverse
        ]
        rest = jnp.where(inside, 0.0, panel) - (
            (cols[0] * new[0] + cols[1] * new[1]) + (cols[2] * new[2] + cols[3] * new[3])
        )
        for i in range(4):
            rest = jnp.where(line == k + i, new[i], rest)
        panel = rest
    mat_ref[0:block, :] = panel
    row = lax.broadcasted_iota(jnp.int32, (NB, NB), 0)
    col = lax.broadcasted_iota(jnp.int32, (NB, NB), 1)
    mat = mat_ref[...]
    inside_row = row < block
    inside_col = col < block
    left = jnp.where(inside_col & ~inside_row, mat, 0.0)
    right = jnp.where(inside_row, mat, 0.0)
    update = jnp.dot(left, right, preferred_element_type=F32, precision=HIGHEST)
    mat = jnp.where(inside_row, mat, jnp.where(inside_col, 0.0, mat) - update)
    mat = pltpu.roll(mat, NB - block, 1)
    mat_ref[0 : NB - block, :] = mat[block:, :]
    mat_ref[NB - block :, :] = mat[:block, :]


def owner_basis(meta, items):
    column = meta.T
    rows = [
        basis_of(column[:, i : i + 1], column[:, items + i : items + i + 1]) for i in range(items)
    ]
    return jnp.concatenate(rows, axis=0)


def clear_moments(mat_ref, mom_ref):
    row = lax.broadcasted_iota(jnp.int32, (NB, NB), 0)
    col = lax.broadcasted_iota(jnp.int32, (NB, NB), 1)
    mat_ref[...] = jnp.where(row == col, RIDGE_WEIGHT, 0.0)
    mom_ref[...] = jnp.zeros_like(mom_ref)


def coefficients(mat_ref, mom_ref):
    return jnp.dot(mat_ref[...], mom_ref[...], preferred_element_type=F32, precision=HIGHEST)


def pick_samples(past, meta, items):
    slots, seg_len = meta.shape[1], past.shape[2]
    column = meta.T
    at = lax.broadcasted_iota(jnp.int32, (slots, seg_len), 1)
    rows = []
    for i in range(items):
        pick = (at == position_of(column, i, items)).astype(F32).astype(BF)
        rows.append(dot_nt(pick, past[i]).astype(BF))
    return jnp.concatenate(rows, axis=0)


def sample_kernel(past_ref, meta_ref, out_ref, *, items):
    out_ref[...] = pick_samples(past_ref[...], meta_ref[...], items)


def sample_rows(past, meta):
    items, width, seg_len = past.shape
    return pl.pallas_call(
        functools.partial(sample_kernel, items=items),
        out_shape=jax.ShapeDtypeStruct((items * meta.shape[1], width), BF),
        name="sample_rows",
    )(past, meta)


def solve_kernel(sampled_ref, meta_ref, coef_ref, inv_ref, mat_ref, mom_ref, *, items):
    clear_moments(mat_ref, mom_ref)

    def owner(s, carry):
        rows = owner_basis(meta_ref[s], items)
        mat_ref[...] += dot_tn(rows, rows, HIGHEST)
        mom_ref[...] += dot_tn(rows, sampled_ref[s].astype(F32), HIGHEST)
        return carry

    lax.fori_loop(0, meta_ref.shape[0], owner, 0)

    def step(s, carry):
        invert_step(mat_ref)
        return carry

    lax.fori_loop(0, NB // PIVOTS, step, 0)
    inv_ref[...] = mat_ref[...]
    coef_ref[...] = coefficients(mat_ref, mom_ref).astype(BF)


def solve_memory(sampled, meta, items):
    width = sampled.shape[-1]
    return pl.pallas_call(
        functools.partial(solve_kernel, items=items),
        out_shape=(
            jax.ShapeDtypeStruct((NB, width), BF),
            jax.ShapeDtypeStruct((NB, NB), F32),
        ),
        scratch_shapes=[pltpu.VMEM((NB, NB), F32), pltpu.VMEM((NB, width), F32)],
        compiler_params=pltpu.CompilerParams(vmem_limit_bytes=BIG_VMEM),
        name="solve_memory",
    )(sampled, meta)


def give_past(gmem, coef_ref, vec_ref, inv_ref, meta_ref, out_ref, gv_ref):
    slots = meta_ref.shape[1]
    item_count, width, seg_len = out_ref.shape
    normed, inverse = norm_parts(coef_ref[...].astype(F32))
    coef_grad = norm_back(gmem, normed, inverse, vec_ref[0, 0:1, :])
    gv_ref[...] = jnp.zeros_like(gv_ref)
    gv_ref[0:1, :] = col_sum(gmem * normed)
    gv_ref[1:2, :] = col_sum(gmem)
    features = coef_grad.shape[1]
    part = lax.axis_index("mp")
    row = lax.broadcasted_iota(jnp.int32, (features, width), 0)
    col = lax.broadcasted_iota(jnp.int32, (features, width), 1)
    pick = (row == col + part * width).astype(F32)
    mine = jnp.dot(coef_grad, pick, preferred_element_type=F32, precision=HIGHEST)
    moment = jnp.dot(inv_ref[...], mine, preferred_element_type=F32, precision=HIGHEST)
    at = lax.broadcasted_iota(jnp.int32, (slots, seg_len), 1)
    column = meta_ref[...].T
    for i in range(item_count):
        rows = basis_of(column[:, i : i + 1], column[:, item_count + i : item_count + i + 1])
        sampled = jnp.dot(rows, moment, preferred_element_type=F32, precision=HIGHEST)
        spread = (at == position_of(column, i, item_count)).astype(F32)
        out_ref[i] = dot_tn(sampled, spread, HIGHEST)


def past_kernel(gmem_ref, coef_ref, vec_ref, inv_ref, meta_ref, out_ref, gv_ref):
    give_past(gmem_ref[...], coef_ref, vec_ref, inv_ref, meta_ref, out_ref, gv_ref)


def past_grads(gmem, coef, vec, inv, meta, items, seg_len, width):
    return pl.pallas_call(
        past_kernel,
        out_shape=(
            jax.ShapeDtypeStruct((items, width, seg_len), F32),
            jax.ShapeDtypeStruct((8, coef.shape[1]), F32),
        ),
        compiler_params=pltpu.CompilerParams(vmem_limit_bytes=BIG_VMEM),
        name="past_grads",
    )(gmem, coef, vec, inv, meta)


MESH = pl.DeviceIdType.MESH
LINE = 4
PLANE = 8
NEAR = (0, -1, 1, -2, 2, -3, 3)


class Place:
    def __init__(self):
        self.s = lax.axis_index("seq")
        self.z = lax.axis_index("mp")
        core = lax.rem(self.s, 2)
        x = lax.rem(self.s // 2, 2)
        y = self.s // 4
        self.turn = 1 - 2 * core
        self.partner = self.s + self.turn
        self.sx = self.s + 2 - 4 * x
        self.sy = self.s + 4 - 8 * y
        self.sd = self.sx + 4 - 8 * y
        self.low = self.z > 0
        self.high = self.z < LINE - 1
        self.near = [
            (
                d,
                valid(self.z + d),
                self.z + d,
                lax.rem(self.z + d + LINE, 2) == 1,
                lax.rem(self.z + d + LINE, 2) == 0,
            )
            for d in NEAR
        ]


def valid(m):
    return (m >= 0) & (m < LINE)


def when(conditions, act):
    conditions = [c for c in conditions if c is not None]
    if conditions:
        pl.when(functools.reduce(lambda a, b: a & b, conditions))(act)
    else:
        act()


def greet(place, whole_line=False):
    barrier = pltpu.get_barrier_semaphore()

    def signal(seq, z):
        pl.semaphore_signal(barrier, inc=1, device_id=(seq, z), device_id_type=MESH)

    for seq in (place.partner, place.sx, place.sy):
        signal(seq, place.z)
    for d, ok, m, odd, even in place.near[1:]:
        if whole_line or abs(d) == 1:
            when((ok,), lambda: signal(place.s, m))
    if whole_line:
        peers = LINE - 1
    else:
        peers = (place.z + LINE - 1) // LINE + (2 * LINE - 2 - place.z) // LINE
    pl.semaphore_wait(barrier, 3 + peers)


UP, DOWN, ACROSS_X, ACROSS_Y, PARTNER = range(5)


class Spread:
    def __init__(self, place, src, dst, send, recv, local, line=True):
        self.p, self.src, self.dst = place, src, dst
        self.send, self.recv, self.line = send, recv, line
        self.rows = src.shape[0]
        self.sent = []
        self.mine = place.z if line else 0
        self.around = place.near if line else [(0, None, 0, None, None)]
        self.own = pltpu.make_async_copy(src, self.at(self.mine, place.s), local)

    def at(self, m, s):
        return self.dst.at[m, pl.ds(s * self.rows, self.rows), :]

    def copy(self, direction, m, s, own=False):
        p = self.p
        device = (
            (p.s, p.z + 1),
            (p.s, p.z - 1),
            (p.sx, p.z),
            (p.sy, p.z),
            (p.partner, p.z),
        )[direction]
        return pltpu.make_async_remote_copy(
            src_ref=self.src if own else self.at(m, s),
            dst_ref=self.at(m, s),
            send_sem=self.send.at[direction, m * 4 + s // 2],
            recv_sem=self.recv.at[m * PLANE + s],
            device_id=device,
            device_id_type=MESH,
        )

    def start(self, conditions, *what, **how):
        when(conditions, lambda: self.copy(*what, **how).start())
        self.sent.append((conditions, what, how))

    def arrived(self, m, s):
        self.copy(PARTNER, m, s).wait_recv()

    def first(self):
        p, m = self.p, self.mine
        self.own.start()
        if self.line:
            self.start((p.high,), UP, m, p.s, own=True)
            self.start((p.low,), DOWN, m, p.s, own=True)
        for direction in (ACROSS_X, ACROSS_Y, PARTNER):
            self.start((), direction, m, p.s, own=True)

    def along(self, d, ok, m, odd, even):
        p = self.p
        when((ok,), lambda: self.arrived(m, p.s))
        if d < 0:
            self.start((ok, p.high), UP, m, p.s)
        else:
            self.start((ok, p.low), DOWN, m, p.s)
        for direction in (ACROSS_X, ACROSS_Y, PARTNER):
            self.start((ok,), direction, m, p.s)

    def across(self, d, ok, m, odd, even):
        p = self.p
        when((ok,), lambda: self.arrived(m, p.sx))
        if self.line:
            self.start((ok, odd), ACROSS_Y, m, p.sx)
        self.start((ok,), PARTNER, m, p.sx)
        when((ok,), lambda: self.arrived(m, p.sy))
        if self.line:
            self.start((ok, even), ACROSS_X, m, p.sy)
        else:
            self.start((), ACROSS_X, m, p.sy)
        self.start((ok,), PARTNER, m, p.sy)

    def corner(self, d, ok, m, odd, even):
        p = self.p
        when((ok,), lambda: self.arrived(m, p.sd))
        self.start((ok,), PARTNER, m, p.sd)

    def part(self, kind, d):
        if kind == 0:
            return self.first
        act = (self.along, self.across, self.corner)[kind - 1]
        return functools.partial(act, *self.around[NEAR.index(d)])

    def steps(self, kind):
        return [self.part(kind, d) for d in NEAR if d or kind > 1]

    def close(self, m):
        p = self.p
        for s in (p.s, p.sx, p.sy, p.sd):
            self.arrived(m, s + p.turn)

    def settle(self):
        for conditions, what, how in self.sent:
            when(conditions, lambda: self.copy(*what, **how).wait_send())


class DirectSpread(Spread):
    def throw(self, m):
        p = self.p
        return pltpu.make_async_remote_copy(
            src_ref=self.src,
            dst_ref=self.at(self.mine, p.s),
            send_sem=self.send.at[UP, m],
            recv_sem=self.recv.at[self.mine * PLANE + p.s],
            device_id=(p.s, m),
            device_id_type=MESH,
        )

    def first(self):
        p, m = self.p, self.mine
        self.own.start()
        for d, ok, to, odd, even in self.around[1:]:
            when((ok,), lambda: self.throw(to).start())
        for direction in (ACROSS_X, ACROSS_Y, PARTNER):
            self.start((), direction, m, p.s, own=True)

    def along(self, d, ok, m, odd, even):
        when((ok,), lambda: self.arrived(m, self.p.s))
        for direction in (ACROSS_X, ACROSS_Y, PARTNER):
            self.start((ok,), direction, m, self.p.s)

    def settle(self):
        super().settle()
        for d, ok, m, odd, even in self.around[1:]:
            when((ok,), lambda: self.throw(m).wait_send())


class Line:
    def __init__(self, place, src, dst, send, recv, local):
        self.p, self.src, self.dst = place, src, dst
        self.send, self.recv = send, recv
        self.sent = []
        self.own = pltpu.make_async_copy(src, dst.at[place.z], local)

    def copy(self, up, m, own=False):
        p = self.p
        return pltpu.make_async_remote_copy(
            src_ref=self.src if own else self.dst.at[m],
            dst_ref=self.dst.at[m],
            send_sem=self.send.at[1 if up else 0, m],
            recv_sem=self.recv.at[m],
            device_id=(p.s, p.z + 1 if up else p.z - 1),
            device_id_type=MESH,
        )

    def start(self, conditions, *what, **how):
        when(conditions, lambda: self.copy(*what, **how).start())
        self.sent.append((conditions, what, how))

    def first(self):
        p = self.p
        self.own.start()
        self.start((p.high,), True, p.z, own=True)
        self.start((p.low,), False, p.z, own=True)

    def step(self, distance):
        p = self.p
        for d, ok, m, odd, even in p.near:
            if abs(d) != distance:
                continue
            when((ok,), lambda: self.copy(True, m).wait_recv())
            if d < 0:
                self.start((ok, p.high), True, m)
            else:
                self.start((ok, p.low), False, m)

    def finish_sends(self):
        for conditions, what, how in self.sent:
            when(conditions, lambda: self.copy(*what, **how).wait_send())

    def finish(self):
        self.finish_sends()
        self.own.wait()


class Collect:
    OWN, SIDE_X, SIDE_Y, CORNER = range(4)

    def __init__(self, place, grads, out, buffers, sems):
        self.p, self.grads, self.out = place, grads, out
        self.pin, self.din, self.xin, self.yin, self.zin = buffers
        self.block_sems, self.sems = sems
        self.rows = out.shape[1]
        self.columns = (place.s, place.sx, place.sy, place.sd)

    def plane(self, i):
        upper = self.p.z // 2
        return (1 - upper) * (LINE - 1 - i) + upper * i

    def unit(self, c, m, turn=0):
        s = self.columns[c] + turn
        return self.grads.at[m, :, pl.ds(s * self.rows, self.rows), :]

    def remote(self, src, dst, send, recv, device):
        return pltpu.make_async_remote_copy(
            src_ref=src,
            dst_ref=dst,
            send_sem=send,
            recv_sem=recv,
            device_id=device,
            device_id_type=MESH,
        )

    def swap(self, c, m):
        p = self.p
        return self.remote(
            self.unit(c, m, p.turn),
            self.pin.at[c, m],
            self.block_sems.at[0, c, m],
            self.block_sems.at[1, c, m],
            (p.partner, p.z),
        )

    def hop(self, kind, m, by_x=True):
        p = self.p
        src, dst, device = (
            (self.CORNER, self.din, (p.sx if by_x else p.sy, p.z)),
            (self.SIDE_X, self.xin, (p.sx, p.z)),
            (self.SIDE_Y, self.yin, (p.sy, p.z)),
        )[kind]
        return self.remote(
            self.unit(src, m),
            dst.at[m],
            self.sems.at[kind, m],
            self.sems.at[4 + kind, m],
            device,
        )

    def slot(self, m, z):
        ends = 1 // (1 + z - m)
        return m + (LINE - m) * ends

    def climb(self, m, up):
        p = self.p
        return self.remote(
            self.unit(self.OWN, m),
            self.zin.at[m if up else self.slot(m, p.z - 1)],
            self.sems.at[3, m],
            self.sems.at[7 if up else 8, m],
            (p.s, p.z + 1 if up else p.z - 1),
        )

    def climbed(self, m, up):
        zin = self.zin.at[m if up else self.slot(m, self.p.z)]
        return self.remote(
            zin, zin, self.sems.at[3, m], self.sems.at[7 if up else 8, m], (self.p.partner, self.p.z)
        )

    def add(self, c, m, *others):
        size = min(32, self.rows)
        pieces = self.rows // size

        @pl.loop(0, self.grads.shape[1] * pieces)
        def _(j):
            l = j // pieces
            at = lax.rem(j, pieces) * size
            here = pl.ds(pl.multiple_of(self.columns[c] * self.rows + at, 16), size)
            there = pl.ds(pl.multiple_of(at, 16), size)
            total = self.grads[m, l, here, :].astype(F32)
            for other in others:
                total = total + other[m, l, there, :].astype(F32)
            self.grads[m, l, here, :] = total.astype(self.grads.dtype)

    def begin(self, m):
        for c in (self.CORNER, self.SIDE_X, self.SIDE_Y, self.OWN):
            self.swap(c, m).start()

    def join(self, c, m):
        self.swap(c, m).wait_recv()
        self.add(c, m, self.pin.at[c])

    def corner(self, i):
        m = self.plane(i)
        self.join(self.CORNER, m)
        even = lax.rem(m, 2) == 0
        pl.when(even)(lambda: self.hop(0, m, True).start())
        pl.when(~even)(lambda: self.hop(0, m, False).start())

    def sides(self, i):
        m = self.plane(i)
        even = lax.rem(m, 2) == 0
        self.join(self.SIDE_X, m)
        self.join(self.SIDE_Y, m)
        pl.when(even)(lambda: self.hop(1, m).start())
        pl.when(~even)(lambda: self.hop(2, m).start())

    def relay(self, i):
        m = self.plane(i)
        even = lax.rem(m, 2) == 0
        self.hop(0, m).wait_recv()

        @pl.when(even)
        def _():
            self.add(self.SIDE_Y, m, self.din)
            self.hop(2, m).start()

        @pl.when(~even)
        def _():
            self.add(self.SIDE_X, m, self.din)
            self.hop(1, m).start()

    def line(self, i):
        p = self.p
        m = self.plane(i)
        self.join(self.OWN, m)
        self.hop(1, m).wait_recv()
        self.hop(2, m).wait_recv()
        self.add(self.OWN, m, self.xin, self.yin)

        @pl.when(m > p.z)
        def _():
            @pl.when(p.low)
            def _():
                self.climbed(m, True).wait_recv()
                self.add(self.OWN, m, self.zin)

            self.climb(m, True).start()

        @pl.when(m < p.z)
        def _():
            @pl.when(p.high)
            def _():
                self.climbed(m, False).wait_recv()
                self.add(self.OWN, m, self.zin)

            self.climb(m, False).start()

    def result(self):
        p = self.p
        self.out[...] = self.unit(self.OWN, p.z)[...].astype(F32)

        @pl.when(p.low)
        def _():
            self.climbed(p.z, True).wait_recv()
            self.out[...] += self.zin[p.z].astype(F32)

        @pl.when(p.high)
        def _():
            self.climbed(p.z, False).wait_recv()
            self.out[...] += self.zin[LINE].astype(F32)

    def part(self, kind, i):
        if kind == 4:
            return self.result
        return functools.partial((self.corner, self.sides, self.relay, self.line)[kind], i)

    def settle(self):
        @pl.loop(0, LINE)
        def _(m):
            for c in range(4):
                self.swap(c, m).wait_send()
            for kind in range(3):
                self.hop(kind, m).wait_send()
            pl.when(m != self.p.z)(lambda: self.climb(m, True).wait_send())


class DirectCollect(Collect):
    def throw(self, m):
        p = self.p
        return self.remote(
            self.unit(self.OWN, m),
            self.zin.at[p.z],
            self.sems.at[3, m],
            self.sems.at[7, p.z],
            (p.s, m),
        )

    def line(self, i):
        m = self.plane(i)
        self.join(self.OWN, m)
        self.hop(1, m).wait_recv()
        self.hop(2, m).wait_recv()
        self.add(self.OWN, m, self.xin, self.yin)
        pl.when(m != self.p.z)(lambda: self.throw(m).start())

    def result(self):
        p = self.p
        self.out[...] = self.unit(self.OWN, p.z)[...].astype(F32)
        for m in range(LINE):

            @pl.when(m != p.z)
            def _():
                zin = self.zin.at[m]
                self.remote(
                    zin, zin, self.sems.at[3, m], self.sems.at[7, m], (p.partner, p.z)
                ).wait_recv()
                self.out[...] += self.zin[m].astype(F32)


BUFFERS = ((4, LINE), (LINE,), (LINE,), (LINE,), (LINE + 1,))


def project(rows, weights, bias, local):
    return (dot(rows, weights[:, : 3 * local]) + bias[:, : 3 * local]).astype(BF)


def attend(query, keys, values, head, store, between):
    rows, local = query.shape
    half = rows // 2
    query_t = query.T * BF(1.0 / math.sqrt(head))
    value_t = values.T
    line = lax.broadcasted_iota(jnp.int32, (local, rows), 0)
    heads = []
    for h in range(local // head):
        own = (line >= h * head) & (line < (h + 1) * head)
        masked = jnp.where(own, query_t, BF(0.0))
        value_h = value_t[h * head : (h + 1) * head, :]
        parts = []
        for b in range(2):
            span = NB + (b + 1) * half
            scores = dot(keys[:span, :], masked[:, b * half : (b + 1) * half])
            key_at = lax.broadcasted_iota(jnp.int32, (half, half), 0)
            row_at = lax.broadcasted_iota(jnp.int32, (half, half), 1)
            edge = jnp.where(key_at <= row_at, scores[span - half :, :], -1e30)
            scores = jnp.concatenate([scores[: span - half, :], edge], axis=0)
            scores = jnp.exp(scores - jnp.max(scores, axis=0, keepdims=True))
            probs = (scores * (1.0 / jnp.sum(scores, axis=0, keepdims=True))).astype(BF)
            store(h, slice(0, span), slice(b * half, (b + 1) * half), probs)
            parts.append(dot(value_h[:, :span], probs))
        heads.append(jnp.concatenate(parts, axis=1).astype(BF))
        between(h)
    return jnp.concatenate(heads, axis=0)


def gelu_parts(pre):
    square = pre * pre
    inner = jnp.tanh(GELU_SCALE * (pre + GELU_CUBIC * pre * square))
    half_up = 0.5 * (1.0 + inner)
    slope = GELU_SCALE * (1.0 + 3.0 * GELU_CUBIC * square)
    return (pre * half_up).astype(BF), half_up + 0.5 * pre * (1.0 - inner * inner) * slope


def forward_kernel(
    tokens_ref,
    past_ref,
    pos_ref,
    counts_ref,
    stack_ref,
    b_qv_ref,
    b_up_ref,
    w_qkv_ref,
    w_out_ref,
    up_ref,
    down_ref,
    wa_ref,
    wu_ref,
    wd_ref,
    out_ref,
    res_ref,
    hmt_ref,
    h2t_ref,
    prob_ref,
    key_ref,
    val_ref,
    query_ref,
    att_ref,
    act_ref,
    slope_ref,
    vec_ref,
    inv_ref,
    coef_ref,
    meta_ref,
    hm_ref,
    h2_ref,
    room_ref,
    attn_ref,
    tok_ref,
    acc_ref,
    mom_ref,
    sampled_ref,
    all_sampled_ref,
    basis_ref,
    all_meta_ref,
    all_room_ref,
    coef_part_ref,
    all_coef_ref,
    wide_ref,
    past_vmem,
    flat_send,
    flat_recv,
    flat_local,
    send,
    recv,
    own_sem,
    line_send,
    line_recv,
    line_own,
    load_sem,
    *,
    items,
    head,
):
    step = pl.program_id(0)
    rows, width = tok_ref.shape
    local = query_ref.shape[2]
    place = Place()
    flat = [
        Spread(
            place, src, dst, flat_send.at[i], flat_recv.at[i], flat_local.at[i], line=False
        )
        for i, (src, dst) in enumerate(
            ((meta_ref, all_meta_ref), (sampled_ref, all_sampled_ref))
        )
    ]
    wide = [
        Spread(place, src, dst, send.at[i], recv.at[i], own_sem.at[i])
        for i, (src, dst) in enumerate(
            ((room_ref, all_room_ref), (attn_ref, wa_ref), (up_ref, wu_ref), (down_ref, wd_ref))
        )
    ]
    room, attn, up, down = wide
    line = Line(place, coef_part_ref, all_coef_ref, line_send, line_recv, line_own)

    attn_at = SOLVE_STEPS
    mlp_at = attn_at + LINE
    last = mlp_at + LINE - 1
    plan = {
        slot: [wide[i].part(kind, d) for i, kind, d in steps] for slot, steps in FORWARD_PLAN
    }

    def transfers(at, position):
        if plan.get((at, position)):

            @pl.when(step == at)
            def _():
                for one in plan[(at, position)]:
                    one()

    def load(ref, m, slot, which):
        return pltpu.make_async_copy(ref.at[m], wide_ref.at[slot, which], load_sem.at[slot, which])

    @pl.when(step == 0)
    def _():
        bring_tok = pltpu.make_async_copy(
            tokens_ref.at[pl.ds(place.z * rows, rows), :], tok_ref, load_sem.at[0, 0]
        )
        bring_past = pltpu.make_async_copy(past_ref, past_vmem, load_sem.at[0, 1])
        bring_tok.start()
        bring_past.start()
        greet(place)
        meta_ref[...] = meta_rows(
            pos_ref[...], counts_ref, place.s * items, PLANE * items, past_ref.shape[2]
        )
        bring_past.wait()
        sampled_ref[...] = pick_samples(past_vmem[...], meta_ref[...], items)
        for part in flat:
            part.first()
        room_ref[...] = small_rows(
            stack_ref[...].astype(F32),
            b_qv_ref[...].astype(F32),
            b_up_ref[...].astype(F32),
            place.s,
            width,
            head,
        )
        for i in range(3):
            attn_ref[:, i * local : (i + 1) * local] = w_qkv_ref[i]
        row, lane = iotas((w_out_ref.shape[1], w_out_ref.shape[1]))
        unit = (row == lane).astype(F32).astype(BF)
        attn_ref[:, 3 * local :] = dot_nt(unit, w_out_ref[...]).astype(BF)
        bring_tok.wait()
        acc_ref[...] = jnp.zeros_like(acc_ref)
        clear_moments(inv_ref, mom_ref)

    transfers(0, 0)

    meta, samples = flat

    @pl.when(step == 1)
    def _():
        for kind in (2, 3):
            meta.part(kind, 0)()
        samples.part(2, 0)()
        meta.own.wait()
        meta.close(0)

    transfers(1, 0)

    @pl.when(step == 1)
    def _():
        def owner(s, carry):
            rows = owner_basis(all_meta_ref[0, pl.ds(s * 8, 8), :], items)
            basis_ref[s] = rows
            inv_ref[...] += dot_tn(rows, rows, HIGHEST)
            return carry

        lax.fori_loop(0, PLANE, owner, 0)
        samples.part(3, 0)()
        samples.own.wait()
        samples.close(0)

    transfers(1, 1)

    @pl.when(step == 1)
    def _():
        def owner(s, carry):
            count = sampled_ref.shape[0]
            rows = all_sampled_ref[0, pl.ds(s * count, count), :]
            mom_ref[...] += dot_tn(basis_ref[s], rows.astype(F32), HIGHEST)
            return carry

        lax.fori_loop(0, PLANE, owner, 0)

    transfers(1, 2)

    inverse_end = 2 + NB // PIVOTS

    @pl.when((step >= 2) & (step < inverse_end))
    def _():
        invert_step(inv_ref)

    for at in range(2, inverse_end):
        transfers(at, 0)

    @pl.when(step == inverse_end)
    def _():
        coef_part_ref[...] = coefficients(inv_ref, mom_ref).astype(BF)
        line.first()

    transfers(inverse_end, 0)

    @pl.when(step == inverse_end)
    def _():
        room.own.wait()
        for m in range(LINE):
            room.close(m)
            total = all_room_ref[m, 0:16, :].astype(F32)
            for s in range(1, PLANE):
                total = total + all_room_ref[m, s * 16 : (s + 1) * 16, :].astype(F32)
            vec_ref[m] = total
        gain, bias = vec_ref[0, 0:1, :], vec_ref[0, 1:2, :]
        normed, _ = norm_parts(tok_ref[...].astype(F32))
        hm_ref[NB:, :] = (normed * gain + bias).astype(BF)
        hmt_ref[:, NB:] = hm_ref[NB:, :].T
        line.step(1)

    transfers(inverse_end, 1)

    @pl.when(step == inverse_end)
    def _():
        attn.own.wait()
        attn.close(0)
        load(wa_ref, 0, 0, 0).start()
        line.step(2)

    transfers(inverse_end, 2)

    @pl.when(step == inverse_end)
    def _():
        line.step(3)
        line.own.wait()
        gain, bias = vec_ref[0, 0:1, :], vec_ref[0, 1:2, :]
        for m in range(LINE):
            coef_ref[:, m * local : (m + 1) * local] = all_coef_ref[m]
        normed, _ = norm_parts(coef_ref[...].astype(F32))
        hm_ref[0:NB, :] = (normed * gain + bias).astype(BF)
        hmt_ref[:, 0:NB] = hm_ref[0:NB, :].T

    @pl.when((step >= attn_at) & (step < mlp_at))
    def _():
        m = step - attn_at
        slot = lax.rem(m, 2)
        load(wa_ref, m, slot, 0).wait()

        @pl.when(m < LINE - 1)
        def _():
            attn.close(m + 1)
            load(wa_ref, m + 1, 1 - slot, 0).start()

        weights = wide_ref[slot, 0]
        projected = project(hm_ref[...], weights, vec_ref[m, 6:7, :], local)
        query = projected[NB:, :local]
        keys = projected[:, local : 2 * local]
        values = projected[:, 2 * local :]
        query_ref[0] = query
        key_ref[0] = keys
        val_ref[0] = values

        def store(h, lines, columns, probs):
            prob_ref[0, h, lines, columns] = probs

        def between(h):
            for at in range(attn_at, mlp_at):
                transfers(at, h)

        attended = attend(query, keys, values, head, store, between)
        att_ref[0] = attended
        acc_ref[...] += dot_nt(attended.T, wide_ref[slot, 0, :, 3 * local :])

    transfers(mlp_at, 0)

    @pl.when(step == mlp_at)
    def _():
        for part in (up, down):
            part.own.wait()
            part.close(0)
        load(wu_ref, 0, 0, 0).start()
        load(wd_ref, 0, 0, 1).start()
        residual = tok_ref[...].astype(F32) + acc_ref[...] + vec_ref[0, 4:5, :]
        res_ref[...] = residual
        normed, _ = norm_parts(residual)
        h2_ref[...] = (normed * vec_ref[0, 2:3, :] + vec_ref[0, 3:4, :]).astype(BF)
        h2t_ref[...] = h2_ref[...].T
        acc_ref[...] = jnp.zeros_like(acc_ref)

    @pl.when(step >= mlp_at)
    def _():
        m = step - mlp_at
        slot = lax.rem(m, 2)
        load(wu_ref, m, slot, 0).wait()
        load(wd_ref, m, slot, 1).wait()

        @pl.when(m < LINE - 1)
        def _():
            up.close(m + 1)
            down.close(m + 1)
            load(wu_ref, m + 1, 1 - slot, 0).start()
            load(wd_ref, m + 1, 1 - slot, 1).start()

        pre = dot(h2_ref[...], wide_ref[slot, 0]) + vec_ref[m, 7:8, :]
        act, slope = gelu_parts(pre)
        act_ref[0] = act
        slope_ref[0] = slope.astype(BF)
        acc_ref[...] += dot_nt(act, wide_ref[slot, 1])

    @pl.when(step == last)
    def _():
        out_ref[...] = (res_ref[...] + acc_ref[...] + vec_ref[0, 5:6, :]).astype(BF)
        for part in flat + wide:
            part.settle()
        line.finish_sends()


SOLVE_STEPS = 3 + NB // PIVOTS


FORWARD_PLAN = (
    (
        (0, 0),
        ((0, 0, 0),),
    ),
    (
        (1, 0),
        ((1, 0, 0), (0, 1, 1), (0, 1, -1),),
    ),
    (
        (1, 1),
        ((0, 1, -2), (0, 1, 2), (1, 1, -1), (1, 1, 1),),
    ),
    (
        (1, 2),
        ((0, 1, -3), (0, 1, 3), (3, 0, 0),),
    ),
    (
        (2, 0),
        ((1, 1, 2), (1, 1, -2),),
    ),
    (
        (4, 0),
        ((0, 2, -3), (0, 2, 3), (1, 2, 0), (0, 2, -1), (0, 2, 1),),
    ),
    (
        (5, 0),
        ((0, 2, 0), (0, 2, -2), (0, 2, 2), (1, 1, -3), (1, 1, 3), (2, 0, 0),),
    ),
    (
        (7, 0),
        ((1, 2, -2), (1, 2, 2), (1, 2, 1), (1, 2, -1),),
    ),
    (
        (8, 0),
        ((3, 1, 1), (3, 1, -1),),
    ),
    (
        (9, 0),
        ((0, 3, 3), (0, 3, -3),),
    ),
    (
        (10, 0),
        ((0, 3, 1), (0, 3, -1), (1, 2, 3), (1, 2, -3), (0, 3, 0), (0, 3, 2), (0, 3, -2), (3, 1, -2), (3, 1, 2),),
    ),
    (
        (10, 1),
        ((3, 1, 3), (3, 1, -3), (1, 3, 0), (1, 3, 1), (1, 3, -2), (1, 3, 3), (1, 3, -1), (1, 3, 2), (1, 3, -3),),
    ),
    (
        (10, 2),
        ((2, 1, -1), (2, 1, 1),),
    ),
    (
        (11, 0),
        ((2, 1, -2), (2, 1, 2),),
    ),
    (
        (11, 1),
        ((2, 1, 3), (2, 1, -3), (3, 2, 0),),
    ),
    (
        (12, 0),
        ((2, 2, 1), (2, 2, -1), (2, 2, 0),),
    ),
    (
        (12, 1),
        ((2, 2, -3), (2, 2, 3), (3, 2, -2), (3, 2, 2),),
    ),
    (
        (13, 0),
        ((3, 2, -1), (3, 2, 1), (2, 2, 2), (2, 2, -2),),
    ),
    (
        (13, 1),
        ((2, 3, -1), (2, 3, 1), (3, 2, 3), (3, 2, -3), (2, 3, 0),),
    ),
    (
        (13, 2),
        ((3, 3, 0), (2, 3, 3), (2, 3, -3),),
    ),
    (
        (14, 1),
        ((3, 3, 1), (3, 3, -1), (3, 3, 2), (3, 3, -2), (2, 3, -2), (2, 3, 2), (3, 3, 3), (3, 3, -3),),
    ),
)


def forward_pass(tokens, past, positions, counts, stack, b_qv, b_up, w_qkv, w_out, up, down, head):
    width = tokens.shape[1]
    rows = tokens.shape[0] // LINE
    items = past.shape[0]
    local = width // LINE
    hidden = up.shape[1]
    heads = local // head
    keyed = NB + rows
    slots = positions.shape[1]
    samples = items * slots
    part = up.shape[0]
    attn_at = SOLVE_STEPS
    mlp_at = attn_at + LINE
    first = lambda i: jnp.clip(i - attn_at, 0, LINE - 1)
    second = lambda i: jnp.clip(i - mlp_at, 0, LINE - 1)
    whole = lambda shape: pl.BlockSpec(shape, lambda i: (0,) * len(shape))
    anywhere = pl.BlockSpec(memory_space=pl.ANY)
    vmem = pl.BlockSpec(memory_space=pltpu.VMEM)
    dma = pltpu.SemaphoreType.DMA
    shape = jax.ShapeDtypeStruct
    return pl.pallas_call(
        functools.partial(forward_kernel, items=items, head=head),
        grid=(mlp_at + LINE,),
        in_specs=[anywhere, anywhere, vmem, pl.BlockSpec(memory_space=pltpu.SMEM)]
        + [vmem] * 5
        + [anywhere, anywhere],
        out_specs=[
            anywhere,
            anywhere,
            anywhere,
            whole((rows, width)),
            whole((rows, width)),
            whole((width, keyed)),
            whole((width, rows)),
            pl.BlockSpec((1, heads, keyed, rows), lambda i: (first(i), 0, 0, 0)),
            pl.BlockSpec((1, keyed, local), lambda i: (first(i), 0, 0)),
            pl.BlockSpec((1, keyed, local), lambda i: (first(i), 0, 0)),
            pl.BlockSpec((1, rows, local), lambda i: (first(i), 0, 0)),
            pl.BlockSpec((1, local, rows), lambda i: (first(i), 0, 0)),
            pl.BlockSpec((1, rows, hidden), lambda i: (second(i), 0, 0)),
            pl.BlockSpec((1, rows, hidden), lambda i: (second(i), 0, 0)),
            whole((LINE, 16, width)),
            whole((NB, NB)),
            whole((NB, width)),
            whole((8, slots)),
        ],
        out_shape=[
            shape((LINE, width, width), BF),
            shape((LINE, width, hidden), BF),
            shape((LINE, width, hidden), BF),
            shape((rows, width), BF),
            shape((rows, width), F32),
            shape((width, keyed), BF),
            shape((width, rows), BF),
            shape((LINE, heads, keyed, rows), BF),
            shape((LINE, keyed, local), BF),
            shape((LINE, keyed, local), BF),
            shape((LINE, rows, local), BF),
            shape((LINE, local, rows), BF),
            shape((LINE, rows, hidden), BF),
            shape((LINE, rows, hidden), BF),
            shape((LINE, 16, width), F32),
            shape((NB, NB), F32),
            shape((NB, width), BF),
            shape((8, slots), F32),
        ],
        scratch_shapes=[
            pltpu.VMEM((keyed, width), BF),
            pltpu.VMEM((rows, width), BF),
            pltpu.VMEM((16, width), BF),
            pltpu.VMEM((part, width), BF),
            pltpu.VMEM((rows, width), BF),
            pltpu.VMEM((rows, width), F32),
            pltpu.VMEM((NB, local), F32),
            pltpu.VMEM((samples, local), BF),
            pltpu.VMEM((1, PLANE * samples, local), BF),
            pltpu.VMEM((PLANE, samples, NB), F32),
            pltpu.VMEM((1, PLANE * 8, slots), F32),
            pltpu.VMEM((LINE, PLANE * 16, width), BF),
            pltpu.VMEM((NB, local), BF),
            pltpu.VMEM((LINE, NB, local), BF),
            pltpu.VMEM((2, 2, width, width), BF),
            pltpu.VMEM(past.shape, BF),
            dma((2, 5, 4)),
            dma((2, PLANE)),
            dma((2,)),
            dma((4, 5, LINE * 4)),
            dma((4, LINE * PLANE)),
            dma((4,)),
            dma((2, LINE)),
            dma((LINE,)),
            dma(()),
            dma((2, 2)),
        ],
        compiler_params=pltpu.CompilerParams(
            collective_id=1, has_side_effects=True, vmem_limit_bytes=BIG_VMEM
        ),
        name="forward_pass",
    )(tokens, past, positions, counts, stack, b_qv, b_up, w_qkv, w_out, up, down)


def plain_forward_kernel(
    tok_ref,
    coef_ref,
    vec_ref,
    wa_ref,
    wu_ref,
    wd_ref,
    out_ref,
    res_ref,
    hm_ref,
    h2_ref,
    prob_ref,
    key_ref,
    val_ref,
    query_ref,
    att_ref,
    act_ref,
    slope_ref,
    acc_ref,
    *,
    groups,
    head,
):
    step = pl.program_id(0)
    rows, width = tok_ref.shape
    local = query_ref.shape[2]

    @pl.when(step == 0)
    def _():
        gain, bias = vec_ref[0, 0:1, :], vec_ref[0, 1:2, :]
        normed, _ = norm_parts(coef_ref[...].astype(F32))
        hm_ref[0:NB, :] = (normed * gain + bias).astype(BF)
        normed, _ = norm_parts(tok_ref[...].astype(F32))
        hm_ref[NB:, :] = (normed * gain + bias).astype(BF)
        acc_ref[...] = jnp.zeros_like(acc_ref)

    @pl.when(step < groups)
    def _():
        weights = wa_ref[0]
        projected = project(hm_ref[...], weights, vec_ref[step, 6:7, :], local)
        query = projected[NB:, :local]
        keys = projected[:, local : 2 * local]
        values = projected[:, 2 * local :]
        query_ref[0] = query
        key_ref[0] = keys
        val_ref[0] = values

        def store(h, lines, columns, probs):
            prob_ref[0, h, lines, columns] = probs

        attended = attend(query, keys, values, head, store, lambda h: None)
        att_ref[0] = attended
        acc_ref[...] += dot_nt(attended.T, weights[:, 3 * local :])

    @pl.when(step == groups)
    def _():
        residual = tok_ref[...].astype(F32) + acc_ref[...] + vec_ref[0, 4:5, :]
        res_ref[...] = residual
        normed, _ = norm_parts(residual)
        h2_ref[...] = (normed * vec_ref[0, 2:3, :] + vec_ref[0, 3:4, :]).astype(BF)
        acc_ref[...] = jnp.zeros_like(acc_ref)

    @pl.when(step >= groups)
    def _():
        pre = dot(h2_ref[...], wu_ref[0]) + vec_ref[step - groups, 7:8, :]
        act, slope = gelu_parts(pre)
        act_ref[0] = act
        slope_ref[0] = slope.astype(BF)
        acc_ref[...] += dot_nt(act, wd_ref[0])

    @pl.when(step == 2 * groups - 1)
    def _():
        out_ref[...] = (res_ref[...] + acc_ref[...] + vec_ref[0, 5:6, :]).astype(BF)


def plain_forward(tok, coef, vec, wide, head):
    rows, width = tok.shape
    groups = wide[0].shape[0]
    local = width // groups
    hidden = wide[1].shape[2]
    heads = local // head
    keyed = NB + rows
    first = lambda i: jnp.minimum(i, groups - 1)
    second = lambda i: jnp.maximum(i - groups, 0)
    whole = lambda shape: pl.BlockSpec(shape, lambda i: (0,) * len(shape))
    shape = jax.ShapeDtypeStruct
    return pl.pallas_call(
        functools.partial(plain_forward_kernel, groups=groups, head=head),
        grid=(2 * groups,),
        in_specs=[
            whole((rows, width)),
            whole((NB, width)),
            whole((groups, 16, width)),
            pl.BlockSpec((1, width, width), lambda i: (first(i), 0, 0)),
            pl.BlockSpec((1, width, hidden), lambda i: (second(i), 0, 0)),
            pl.BlockSpec((1, width, hidden), lambda i: (second(i), 0, 0)),
        ],
        out_specs=[
            whole((rows, width)),
            whole((rows, width)),
            whole((keyed, width)),
            whole((rows, width)),
            pl.BlockSpec((1, heads, keyed, rows), lambda i: (first(i), 0, 0, 0)),
            pl.BlockSpec((1, keyed, local), lambda i: (first(i), 0, 0)),
            pl.BlockSpec((1, keyed, local), lambda i: (first(i), 0, 0)),
            pl.BlockSpec((1, rows, local), lambda i: (first(i), 0, 0)),
            pl.BlockSpec((1, local, rows), lambda i: (first(i), 0, 0)),
            pl.BlockSpec((1, rows, hidden), lambda i: (second(i), 0, 0)),
            pl.BlockSpec((1, rows, hidden), lambda i: (second(i), 0, 0)),
        ],
        out_shape=[
            shape((rows, width), BF),
            shape((rows, width), F32),
            shape((keyed, width), BF),
            shape((rows, width), BF),
            shape((groups, heads, keyed, rows), BF),
            shape((groups, keyed, local), BF),
            shape((groups, keyed, local), BF),
            shape((groups, rows, local), BF),
            shape((groups, local, rows), BF),
            shape((groups, rows, hidden), BF),
            shape((groups, rows, hidden), BF),
        ],
        scratch_shapes=[pltpu.VMEM((rows, width), F32)],
        compiler_params=pltpu.CompilerParams(vmem_limit_bytes=BIG_VMEM),
        name="plain_forward",
    )(tok, coef, vec, *wide)


def attend_back(g_att, att_t, keys, values, query, probs_of, head, between):
    rows, local = g_att.shape
    half = rows // 2
    low = NB + rows - half
    g_att_t = g_att.T
    product = g_att_t.astype(F32) * att_t.astype(F32)
    key_t = keys.T
    scale = 1.0 / math.sqrt(head)
    line = lax.broadcasted_iota(jnp.int32, (local, rows), 0)
    lane = lax.broadcasted_iota(jnp.int32, (rows, local), 1)
    key_grad = [jnp.zeros((low, local), F32), jnp.zeros((half, local), F32)]
    val_grad = [jnp.zeros((low, local), F32), jnp.zeros((half, local), F32)]
    query_grads = []
    for h in range(local // head):
        own_t = (line >= h * head) & (line < (h + 1) * head)
        own = (lane >= h * head) & (lane < (h + 1) * head)
        grad_t = jnp.where(own_t, g_att_t, BF(0.0))
        grad_h = jnp.where(own, g_att, BF(0.0))
        query_h = jnp.where(own, query, BF(0.0))
        inner = jnp.sum(product[h * head : (h + 1) * head, :], axis=0, keepdims=True)
        key_h = key_t[h * head : (h + 1) * head, :]
        parts = []
        for b in range(2):
            span = NB + (b + 1) * half
            cols = slice(b * half, (b + 1) * half)
            probs = probs_of(h, slice(0, span), cols)
            dprob = dot(values[:span, :], grad_t[:, cols])
            dscore = (probs.astype(F32) * (dprob - inner[:, cols])).astype(BF)
            parts.append(dot(key_h[:, :span], dscore))
            val_part = dot(probs, grad_h[cols, :])
            key_part = dot(dscore, query_h[cols, :])
            val_grad[0] = val_grad[0] + val_part[:low, :]
            key_grad[0] = key_grad[0] + key_part[:low, :]
            if b == 1:
                val_grad[1] = val_grad[1] + val_part[low:, :]
                key_grad[1] = key_grad[1] + key_part[low:, :]
        query_grads.append(jnp.concatenate(parts, axis=1))
        between(h)
    query_grad = (jnp.concatenate(query_grads, axis=0) * scale).astype(BF).T
    key_grad = jnp.concatenate(key_grad, axis=0) * scale
    return query_grad, key_grad, jnp.concatenate(val_grad, axis=0)


def backward_kernel(
    tokens_ref,
    cots_ref,
    fwd_out_ref,
    res_ref,
    wa_ref,
    wu_ref,
    wd_ref,
    vec_ref,
    hmt_ref,
    h2t_ref,
    coef_ref,
    inv_ref,
    meta_ref,
    prob_ref,
    key_ref,
    val_ref,
    query_ref,
    att_ref,
    act_ref,
    slope_ref,
    outs_ref,
    tgs_ref,
    past_ref,
    vectors_ref,
    bias_ref,
    bias_up_ref,
    qkv_out_ref,
    wo_out_ref,
    up_out_ref,
    down_out_ref,
    *scratch,
    head,
):
    (
        tok_ref,
        cot_ref,
        cott_ref,
        gres_ref,
        acc_ref,
        proj_ref,
        gv_ref,
        ggv_ref,
        gmem_ref,
        wide_ref,
        side_ref,
        attn_ref,
        mlp_ref,
        gv_mem_ref,
        side_out_ref,
        attn_out_ref,
        mlp_out_ref,
    ) = scratch[:17]
    buffers = scratch[17:32]
    block_sems, sems, lsend, lrecv, lown, gsend, grecv, gown, load_sem = scratch[32:]
    step = pl.program_id(0)
    rows, width = tok_ref.shape
    local = query_ref.shape[2]
    items = past_ref.shape[0]
    place = Place()
    side, attn, mlp = [
        kind(place, grads, out, buffers[i::3], (block_sems.at[i], sems.at[i]))
        for i, (kind, grads, out) in enumerate(
            (
                (DirectCollect, side_ref, side_out_ref),
                (Collect, attn_ref, attn_out_ref),
                (Collect, mlp_ref, mlp_out_ref),
            )
        )
    ]
    outs, tgs = [
        [
            Line(
                place,
                src.at[pl.ds(h * (rows // count), rows // count), :],
                dst.at[:, pl.ds(h * (rows // count), rows // count), :],
                lsend.at[first + h],
                lrecv.at[first + h],
                lown.at[first + h],
            )
            for h in range(count)
        ]
        for src, dst, first, count in (
            (fwd_out_ref, outs_ref, 0, OUT_PIECES),
            (cot_ref, tgs_ref, OUT_PIECES, GRAD_PIECES),
        )
    ]
    mem = DirectSpread(place, side_out_ref.at[0, 0:8, :], gmem_ref, gsend, grecv, gown)
    mine = pl.ds(place.z * rows, rows)

    def load(ref, m, slot, which):
        return pltpu.make_async_copy(ref.at[m], wide_ref.at[slot, which], load_sem.at[slot, which])

    def bring(i, src, dst):
        return pltpu.make_async_copy(src, dst, load_sem.at[2, i])

    bring_cot = bring(0, cots_ref.at[mine, :], cot_ref)
    bring_tok = bring(1, tokens_ref.at[mine, :], tok_ref)
    bring_res = pltpu.make_async_copy(res_ref, gres_ref, load_sem.at[3, 0])

    def past():
        mem.own.wait()
        for m in range(LINE):
            mem.close(m)
        gmem = jnp.concatenate([gmem_ref[m] for m in range(LINE)], axis=0)
        give_past(gmem, coef_ref, vec_ref, inv_ref, meta_ref, past_ref, gv_mem_ref)
        own = side_out_ref[0, 8:16, :]
        own = jnp.concatenate([own[0:2] + gv_mem_ref[0:2, :], own[2:8]], axis=0)
        vectors, biases, bias_up = small_pieces(
            own, place.s, vectors_ref.shape[1], bias_ref.shape[2], head, bias_ref.shape[0]
        )
        vectors_ref[...] = vectors
        for h, bias in enumerate(biases):
            bias_ref[h] = bias
        bias_up_ref[...] = bias_up

    def give_attn():
        attn.result()
        for i in range(3):
            qkv_out_ref[i] = attn_out_ref[0, :, i * local : (i + 1) * local]
        row, lane = iotas((attn_out_ref.shape[1], attn_out_ref.shape[1]))
        unit = (row == lane).astype(F32)
        wo_out_ref[...] = dot_tn(attn_out_ref[0, :, 3 * local :], unit, HIGHEST)

    def give_mlp():
        mlp.result()
        up_out_ref[...] = mlp_out_ref[0]
        down_out_ref[...] = mlp_out_ref[1]

    def move(what, kind, i):
        if what == 1 and kind == 4:
            return [give_attn]
        if what == 2 and kind == 4:
            return [give_mlp]
        if what < 3:
            return [(side, attn, mlp)[what].part(kind, i)]
        if what == 3:
            return mem.steps(kind) if kind else [mem.first]
        if what == 4:
            return [past]
        line = (outs + tgs)[what - 5]
        return [functools.partial(line.step, i) if kind else line.first]

    plan = [[one for what in moves for one in move(*what)] for moves in BACKWARD_PLAN]

    def transfers(slot, condition=None):
        def go():
            for one in plan[slot]:
                one()

        if plan[slot]:
            when((condition,), go)

    @pl.when(step == 0)
    def _():
        bring_cot.start()
        bring_tok.start()
        bring_res.start()
        load(wu_ref, 0, 0, 0).start()
        load(wd_ref, 0, 0, 1).start()
        greet(place, whole_line=True)
        for line in outs:
            line.first()
        acc_ref[...] = jnp.zeros_like(acc_ref)
        gv_ref[...] = jnp.zeros_like(gv_ref)
        bring_cot.wait()
        bring_tok.wait()
        bring_res.wait()
        cott_ref[...] = cot_ref[...].T

    @pl.when(step < LINE)
    def _():
        m = step
        slot = lax.rem(m, 2)
        load(wu_ref, m, slot, 0).wait()
        load(wd_ref, m, slot, 1).wait()

        @pl.when(m < LINE - 1)
        def _():
            load(wu_ref, m + 1, 1 - slot, 0).start()
            load(wd_ref, m + 1, 1 - slot, 1).start()

        @pl.when(m == LINE - 1)
        def _():
            load(wa_ref, 0, 0, 0).start()

        upstream = cot_ref[...]
        grad = (dot(upstream, wide_ref[slot, 1]) * slope_ref[0].astype(F32)).astype(BF)
        mlp_ref[m, 1] = dot(cott_ref[...], act_ref[0]).astype(BF)
        mlp_ref[m, 0] = dot(h2t_ref[...], grad).astype(BF)
        mlp.begin(m)
        for at in range(LINE):
            transfers(at, step == at)
        ggv_ref[m, 1:2, :] = col_sum(grad.astype(F32))
        acc_ref[NB:, :] += dot_nt(grad, wide_ref[slot, 0])

    @pl.when(step == LINE)
    def _():
        transfers(LINE)
        upstream = cot_ref[...].astype(F32)
        normed, inverse = norm_parts(gres_ref[...])
        grad = acc_ref[NB:, :]
        g_res = upstream + norm_back(grad, normed, inverse, vec_ref[0, 2:3, :])
        gres_ref[...] = g_res
        g_attn = g_res.astype(BF)
        gv_ref[2:3, :] = col_sum(grad * normed)
        gv_ref[3:4, :] = col_sum(grad)
        gv_ref[4:5, :] = col_sum(g_attn.astype(F32))
        gv_ref[5:6, :] = col_sum(upstream)
        cott_ref[...] = g_attn.T
        acc_ref[...] = jnp.zeros_like(acc_ref)
        proj_ref[0:NB, :] = jnp.zeros((NB, proj_ref.shape[1]), BF)
        transfers(LINE + 1)

    @pl.when(step >= LINE)
    def _():
        m = step - LINE
        slot = lax.rem(m, 2)
        load(wa_ref, m, slot, 0).wait()

        @pl.when(m < LINE - 1)
        def _():
            load(wa_ref, m + 1, 1 - slot, 0).start()

        def between(h):
            for at in range(LINE):
                transfers(LINE + 2 + 4 * at + h, m == at)

        def probs_of(h, lines, columns):
            return prob_ref[0, h, lines, columns]

        g_attn = gres_ref[...].astype(BF)
        g_att = dot(g_attn, wide_ref[slot, 0, :, 3 * local :]).astype(BF)
        att_t = att_ref[0]
        query_grad, key_grad, val_grad = attend_back(
            g_att, att_t, key_ref[0], val_ref[0], query_ref[0], probs_of, head, between
        )
        proj_ref[NB:, 0:local] = query_grad
        proj_ref[:, local : 2 * local] = key_grad.astype(BF)
        proj_ref[:, 2 * local :] = val_grad.astype(BF)
        proj = proj_ref[...]
        ggv_ref[m, 0:1, 0 : 3 * local] = col_sum(proj.astype(F32))
        ggv_ref[m, 0:1, 3 * local :] = jnp.zeros((1, width - 3 * local), F32)
        attn_ref[m, 0, :, 0 : 3 * local] = dot(hmt_ref[...], proj).astype(BF)
        attn_ref[m, 0, :, 3 * local :] = dot_nt(cott_ref[...], att_t).astype(BF)
        attn.begin(m)
        acc_ref[...] += dot_nt(proj, wide_ref[slot, 0, :, : 3 * local])
        between(3)

    @pl.when(step == 2 * LINE - 1)
    def _():
        grad = acc_ref[NB:, :]
        normed, inverse = norm_parts(tok_ref[...].astype(F32))
        back = norm_back(grad, normed, inverse, vec_ref[0, 0:1, :])
        cot_ref[...] = (gres_ref[...] + back).astype(BF)
        tgs[0].first()
        gv_ref[0:1, :] = col_sum(grad * normed)
        gv_ref[1:2, :] = col_sum(grad)
        transfers(5 * LINE + 2)
        for m in range(LINE):
            below = jnp.concatenate([gv_ref[0:6, :], ggv_ref[m, 0:2, :]], axis=0)
            for s in range(PLANE):
                top = (m * PLANE + s) * 8
                side_ref[m, 0, s * 16 : s * 16 + 8, :] = acc_ref[top : top + 8, :]
                side_ref[m, 0, s * 16 + 8 : (s + 1) * 16, :] = below
            side.begin(m)
        transfers(5 * LINE + 3)
        mem.settle()
        for part in (side, attn, mlp):
            part.settle()
        for line in outs + tgs:
            line.finish()


OUT_PIECES, GRAD_PIECES = 2, 4

BACKWARD_PLAN = (
    (),
    (),
    ((5, 1, 1),),
    (),
    ((2, 0, 2),),
    (),
    (),
    ((2, 0, 0), (6, 1, 1),),
    (),
    (),
    (),
    ((2, 0, 1),),
    (),
    (),
    ((6, 1, 2), (5, 1, 2),),
    (),
    ((2, 0, 3),),
    (),
    (),
    (),
    (),
    ((1, 0, 2), (1, 0, 3),),
    ((2, 1, 0), (2, 2, 0), (1, 0, 0), (9, 0, 0), (1, 0, 1), (7, 1, 1), (8, 0, 0),),
    ((0, 0, 0), (0, 0, 1), (0, 0, 2), (0, 0, 3), (0, 1, 1), (0, 1, 2), (0, 1, 3), (0, 2, 1), (0, 2, 2), (0, 2, 3), (10, 0, 0), (0, 1, 0), (0, 2, 0), (1, 1, 0), (1, 2, 0), (2, 1, 1), (2, 2, 1), (1, 1, 1), (1, 2, 1), (5, 1, 3), (0, 3, 3), (2, 1, 3), (2, 2, 3), (0, 3, 0), (0, 3, 1), (9, 1, 1), (0, 3, 2), (0, 4, 0), (3, 0, 0), (10, 1, 1), (7, 1, 2), (8, 1, 1), (2, 3, 0), (10, 1, 2), (6, 1, 3), (3, 1, 0), (1, 1, 2), (1, 2, 2), (1, 3, 0), (9, 1, 2), (3, 2, 0), (2, 1, 2), (2, 2, 2), (8, 1, 2), (1, 3, 1), (1, 1, 3), (1, 2, 3), (2, 3, 3), (3, 3, 0), (2, 3, 1), (2, 3, 2), (1, 3, 2), (1, 3, 3), (4, 0, 0), (7, 1, 3), (8, 1, 3), (9, 1, 3), (10, 1, 3), (2, 4, 0), (1, 4, 0),),
)


def backward_pass(tokens, cots, out, meta, vec, inverse, coef, saved, wide, items, past_shape, head):
    res, hmt, h2t, prob, keys, vals, query, att, act, slope = saved
    rows, width = out.shape
    local = width // LINE
    hidden = wide[1].shape[2]
    heads = local // head
    keyed = NB + rows
    first = lambda i: jnp.minimum(i, LINE - 1)
    second = lambda i: jnp.maximum(i - LINE, 0)
    anywhere = pl.BlockSpec(memory_space=pl.ANY)
    vmem = pl.BlockSpec(memory_space=pltpu.VMEM)
    dma = pltpu.SemaphoreType.DMA
    shape = jax.ShapeDtypeStruct
    part = width // PLANE
    blocks = ((1, 16, width), (1, part, width), (2, part, width))
    kinds = (F32, BF, BF)
    pieces = OUT_PIECES + GRAD_PIECES
    return pl.pallas_call(
        functools.partial(backward_kernel, head=head),
        grid=(2 * LINE,),
        in_specs=[anywhere] * 7
        + [vmem] * 6
        + [
            pl.BlockSpec((1, heads, keyed, rows), lambda i: (second(i), 0, 0, 0)),
            pl.BlockSpec((1, keyed, local), lambda i: (second(i), 0, 0)),
            pl.BlockSpec((1, keyed, local), lambda i: (second(i), 0, 0)),
            pl.BlockSpec((1, rows, local), lambda i: (second(i), 0, 0)),
            pl.BlockSpec((1, local, rows), lambda i: (second(i), 0, 0)),
            pl.BlockSpec((1, rows, hidden), lambda i: (first(i), 0, 0)),
            pl.BlockSpec((1, rows, hidden), lambda i: (first(i), 0, 0)),
        ],
        out_specs=[anywhere, anywhere] + [vmem] * 8,
        out_shape=[
            shape((LINE, rows, width), BF),
            shape((LINE, rows, width), BF),
            shape(past_shape, F32),
            shape((8, part), F32),
            shape((local // head, 2, head // PLANE), F32),
            shape((head // PLANE, hidden // head), F32),
            shape((3, part, local), F32),
            shape((local, part), F32),
            shape((part, hidden), F32),
            shape((part, hidden), F32),
        ],
        scratch_shapes=[
            pltpu.VMEM((rows, width), BF),
            pltpu.VMEM((rows, width), BF),
            pltpu.VMEM((width, rows), BF),
            pltpu.VMEM((rows, width), F32),
            pltpu.VMEM((keyed, width), F32),
            pltpu.VMEM((keyed, 3 * local), BF),
            pltpu.VMEM((8, width), F32),
            pltpu.VMEM((LINE, 8, hidden), F32),
            pltpu.VMEM((LINE, PLANE * 8, width), F32),
            pltpu.VMEM((2, 2, width, width), BF),
        ]
        + [pltpu.VMEM((LINE, b[0], PLANE * b[1], b[2]), t) for b, t in zip(blocks, kinds)]
        + [pltpu.VMEM((8, width), F32)]
        + [pltpu.VMEM(b, F32) for b in blocks]
        + [pltpu.VMEM(lead + b, t) for lead in BUFFERS for b, t in zip(blocks, kinds)]
        + [
            dma((3, 2, 4, LINE)),
            dma((3, 9, LINE)),
            dma((pieces, 2, LINE)),
            dma((pieces, LINE)),
            dma((pieces,)),
            dma((5, LINE * 4)),
            dma((LINE * PLANE,)),
            dma(()),
            dma((4, 2)),
        ],
        compiler_params=pltpu.CompilerParams(
            collective_id=2, has_side_effects=True, vmem_limit_bytes=MAX_VMEM
        ),
        name="backward_pass",
    )(
        tokens,
        cots,
        out,
        res,
        *wide,
        vec,
        hmt,
        h2t,
        coef,
        inverse,
        meta,
        prob,
        keys,
        vals,
        query,
        att,
        act,
        slope,
    )


def plain_backward_kernel(
    tok_ref,
    cot_ref,
    res_ref,
    vec_ref,
    hm_ref,
    h2_ref,
    prob_ref,
    key_ref,
    val_ref,
    query_ref,
    att_ref,
    act_ref,
    slope_ref,
    wa_ref,
    wu_ref,
    wd_ref,
    tg_ref,
    gmem_ref,
    gup_ref,
    gdown_ref,
    gatt_ref,
    gv_ref,
    ggv_ref,
    acc_ref,
    hmt_ref,
    h2t_ref,
    cott_ref,
    gres_ref,
    proj_ref,
    *,
    groups,
    head,
):
    step = pl.program_id(0)
    rows, width = tok_ref.shape
    local = query_ref.shape[2]

    @pl.when(step == 0)
    def _():
        acc_ref[...] = jnp.zeros_like(acc_ref)
        h2t_ref[...] = h2_ref[...].T
        cott_ref[...] = cot_ref[...].T
        gv_ref[...] = jnp.zeros_like(gv_ref)

    @pl.when(step < groups)
    def _():
        upstream = cot_ref[...]
        grad = (dot(upstream, wd_ref[0]) * slope_ref[0].astype(F32)).astype(BF)
        gdown_ref[0] = dot(cott_ref[...], act_ref[0]).astype(BF)
        gup_ref[0] = dot(h2t_ref[...], grad).astype(BF)
        ggv_ref[0] = jnp.zeros_like(ggv_ref[0])
        ggv_ref[0, 0:1, :] = col_sum(grad.astype(F32))
        acc_ref[NB:, :] += dot_nt(grad, wu_ref[0])

    @pl.when(step == groups)
    def _():
        upstream = cot_ref[...].astype(F32)
        normed, inverse = norm_parts(res_ref[...])
        grad = acc_ref[NB:, :]
        g_res = upstream + norm_back(grad, normed, inverse, vec_ref[2:3, :])
        gres_ref[...] = g_res
        g_attn = g_res.astype(BF)
        gv_ref[2:3, :] = col_sum(grad * normed)
        gv_ref[3:4, :] = col_sum(grad)
        gv_ref[4:5, :] = col_sum(g_attn.astype(F32))
        gv_ref[5:6, :] = col_sum(upstream)
        cott_ref[...] = g_attn.T
        hmt_ref[...] = hm_ref[...].T
        acc_ref[...] = jnp.zeros_like(acc_ref)
        proj_ref[0:NB, :] = jnp.zeros((NB, proj_ref.shape[1]), BF)

    @pl.when(step >= groups)
    def _():
        weights = wa_ref[0]
        g_attn = gres_ref[...].astype(BF)
        g_att = dot(g_attn, weights[:, 3 * local :]).astype(BF)
        att_t = att_ref[0]
        query_grad, key_grad, val_grad = attend_back(
            g_att,
            att_t,
            key_ref[0],
            val_ref[0],
            query_ref[0],
            lambda h, lines, columns: prob_ref[0, h, lines, columns],
            head,
            lambda h: None,
        )
        key_grad, val_grad = key_grad.astype(BF), val_grad.astype(BF)
        proj_ref[NB:, 0:local] = query_grad
        proj_ref[:, local : 2 * local] = key_grad
        proj_ref[:, 2 * local :] = val_grad
        proj = proj_ref[...]
        ggv_ref[0] = jnp.zeros_like(ggv_ref[0])
        ggv_ref[0, 0:1, 0 : 3 * local] = col_sum(proj.astype(F32))
        gatt_ref[0, :, 0 : 3 * local] = dot(hmt_ref[...], proj).astype(BF)
        gatt_ref[0, :, 3 * local :] = dot_nt(cott_ref[...], att_t).astype(BF)
        acc_ref[...] += dot_nt(proj, weights[:, : 3 * local])

    @pl.when(step == 2 * groups - 1)
    def _():
        gmem_ref[...] = acc_ref[0:NB, :]
        grad = acc_ref[NB:, :]
        normed, inverse = norm_parts(tok_ref[...].astype(F32))
        part = norm_back(grad, normed, inverse, vec_ref[0:1, :])
        tg_ref[...] = (gres_ref[...] + part).astype(BF)
        gv_ref[0:1, :] = col_sum(grad * normed)
        gv_ref[1:2, :] = col_sum(grad)


def plain_backward(tok, cot, vec, saved, wide, head):
    res, hm, h2, prob, keys, vals, query, att, act, slope = saved
    rows, width = tok.shape
    groups = wide[0].shape[0]
    local = width // groups
    hidden = wide[1].shape[2]
    heads = local // head
    keyed = NB + rows
    first = lambda i: jnp.minimum(i, groups - 1)
    second = lambda i: jnp.maximum(i - groups, 0)
    whole = lambda shape: pl.BlockSpec(shape, lambda i: (0,) * len(shape))
    return pl.pallas_call(
        functools.partial(plain_backward_kernel, groups=groups, head=head),
        grid=(2 * groups,),
        in_specs=[
            whole((rows, width)),
            whole((rows, width)),
            whole((rows, width)),
            whole((16, width)),
            whole((keyed, width)),
            whole((rows, width)),
            pl.BlockSpec((1, heads, keyed, rows), lambda i: (second(i), 0, 0, 0)),
            pl.BlockSpec((1, keyed, local), lambda i: (second(i), 0, 0)),
            pl.BlockSpec((1, keyed, local), lambda i: (second(i), 0, 0)),
            pl.BlockSpec((1, rows, local), lambda i: (second(i), 0, 0)),
            pl.BlockSpec((1, local, rows), lambda i: (second(i), 0, 0)),
            pl.BlockSpec((1, rows, hidden), lambda i: (first(i), 0, 0)),
            pl.BlockSpec((1, rows, hidden), lambda i: (first(i), 0, 0)),
            pl.BlockSpec((1, width, width), lambda i: (second(i), 0, 0)),
            pl.BlockSpec((1, width, hidden), lambda i: (first(i), 0, 0)),
            pl.BlockSpec((1, width, hidden), lambda i: (first(i), 0, 0)),
        ],
        out_specs=[
            whole((rows, width)),
            whole((NB, width)),
            pl.BlockSpec((1, width, hidden), lambda i: (first(i), 0, 0)),
            pl.BlockSpec((1, width, hidden), lambda i: (first(i), 0, 0)),
            pl.BlockSpec((1, width, width), lambda i: (second(i), 0, 0)),
            whole((8, width)),
            pl.BlockSpec((1, 8, hidden), lambda i: (i, 0, 0)),
        ],
        out_shape=[
            jax.ShapeDtypeStruct((rows, width), BF),
            jax.ShapeDtypeStruct((NB, width), F32),
            jax.ShapeDtypeStruct((groups, width, hidden), BF),
            jax.ShapeDtypeStruct((groups, width, hidden), BF),
            jax.ShapeDtypeStruct((groups, width, width), BF),
            jax.ShapeDtypeStruct((8, width), F32),
            jax.ShapeDtypeStruct((2 * groups, 8, hidden), F32),
        ],
        scratch_shapes=[
            pltpu.VMEM((keyed, width), F32),
            pltpu.VMEM((width, keyed), BF),
            pltpu.VMEM((width, rows), BF),
            pltpu.VMEM((width, rows), BF),
            pltpu.VMEM((rows, width), F32),
            pltpu.VMEM((keyed, 3 * local), BF),
        ],
        compiler_params=pltpu.CompilerParams(vmem_limit_bytes=BIG_VMEM),
        name="plain_backward",
    )(
        tok, cot, res, vec, hm, h2, prob, keys, vals, query, att, act, slope, *wide
    )


def local(
    tokens,
    cotangent,
    past_state,
    positions,
    counts,
    ln1_gain,
    ln1_bias,
    w_qkv,
    b_qv,
    w_out,
    b_out,
    ln2_gain,
    ln2_bias,
    w_up,
    b_up,
    w_down,
    b_down,
):
    seq, mp = lax.axis_size("seq"), lax.axis_size("mp")
    seq_index, mp_index = lax.axis_index("seq"), lax.axis_index("mp")
    item_count, seg_len, local_width = past_state.shape
    slots = positions.shape[1]
    total = item_count * seq
    width = tokens.shape[1]
    part = width // seq
    heads_local, piece = b_qv.shape[1], b_qv.shape[2]
    head = piece * seq
    hidden = w_up.shape[1]
    rows = tokens.shape[0] // mp
    direct = seq == PLANE and mp == LINE and part % 16 == 0 and hidden == width

    past_t = past_state.transpose(0, 2, 1)

    vectors = jnp.stack([ln1_gain, ln1_bias, ln2_gain, ln2_bias, b_out, b_down])
    if direct:
        results = forward_pass(
            tokens,
            past_t,
            positions,
            counts,
            vectors,
            b_qv.transpose(1, 0, 2),
            b_up.T,
            w_qkv,
            w_out,
            w_up,
            w_down.T,
            head,
        )
        wide, forward, (vec, inverse, coef, meta) = results[:3], results[3:14], results[14:]
        block_out, block_grad, past_grad, vec_own, bias, bias_up, qkv_grad, out_grad, *mlp = (
            backward_pass(
                tokens,
                cotangent,
                forward[0],
                meta,
                vec,
                inverse,
                coef,
                forward[1:],
                wide,
                item_count,
                past_t.shape,
                head,
            )
        )
        block_out = block_out.reshape(mp * rows, width)
        block_grad = block_grad.reshape(mp * rows, width)
        qv, up, (up_grad, down_grad) = bias.transpose(1, 0, 2), bias_up.T, mlp
    else:
        items = (seq_index * item_count + jnp.arange(item_count)).astype(F32)
        spots = positions.astype(F32)
        places = (items[:, None] + (spots + 0.5) / seg_len) / total
        used = (jnp.arange(slots)[None, :] < counts[:, None]).astype(F32)
        meta = jnp.concatenate([places, used, spots, jnp.zeros((8 - 3 * item_count, slots), F32)])

        here = (jnp.arange(seq) == seq_index).astype(BF)
        vectors = (vectors[:, None, :] * here[None, :, None]).reshape(6, width)
        bias_qv = (b_qv[:, :, None, :] * here[None, None, :, None]).reshape(2, local_width)
        bias_qv = jnp.concatenate([bias_qv, jnp.zeros((2, local_width), BF)], axis=1)
        bias_up = (b_up[:, None, :] * here[None, :, None]).reshape(1, hidden)
        room = jnp.concatenate(
            [vectors, bias_qv.reshape(1, width), bias_up, jnp.zeros((8, width), BF)]
        )
        attn = jnp.concatenate([w_qkv[0], w_qkv[1], w_qkv[2], w_out.T], axis=1)
        sampled = sample_rows(past_t, meta)
        all_sampled = lax.all_gather(sampled, "seq", axis=0)
        all_meta = lax.all_gather(meta, "seq", axis=0)
        coef_part, inverse = solve_memory(all_sampled, all_meta, item_count)
        coef = lax.all_gather(coef_part, "mp", axis=0).transpose(1, 0, 2).reshape(NB, width)
        wide = [
            lax.all_gather(lax.all_gather(shard, "seq", axis=0, tiled=True), "mp", axis=0)
            for shard in (attn, w_up, w_down.T)
        ]
        vec = lax.psum(room.astype(F32), "seq")
        vec = lax.all_gather(vec, "mp", axis=0)
        tok = lax.dynamic_slice_in_dim(tokens, mp_index * rows, rows, 0)
        cot = lax.dynamic_slice_in_dim(cotangent, mp_index * rows, rows, 0)
        forward = plain_forward(tok, coef, vec, wide, head)
        block_out = lax.all_gather(forward[0], "mp", axis=0, tiled=True)
        tok_grad, gmem, g_up, g_down, g_attn, gv, ggv = plain_backward(
            tok, cot, vec[0], forward[1:], wide, head
        )
        tail = jnp.concatenate(
            [jnp.broadcast_to(gv[None, :6], (mp, 6, width)), ggv[mp:, :1], ggv[:mp, :1]], axis=1
        )
        block_grad = lax.all_gather(tok_grad, "mp", axis=0, tiled=True)
        gmem, tail = lax.psum((gmem, tail), ("seq", "mp"))
        own = lax.dynamic_index_in_dim(tail, mp_index, 0, keepdims=False)
        attn, up_grad, down_grad = (
            lax.psum_scatter(
                lax.psum_scatter(g, "mp", scatter_dimension=0, tiled=False),
                "seq",
                scatter_dimension=0,
                tiled=True,
            ).astype(F32)
            for g in (g_attn, g_up, g_down)
        )
        past_grad, gv_mem = past_grads(
            gmem, coef, vec, inverse, meta, item_count, seg_len, local_width
        )
        own = own + jnp.concatenate([gv_mem[:2], jnp.zeros((6, width), F32)])
        vec_own = lax.dynamic_slice_in_dim(own[:6], seq_index * part, part, 1)
        qv = jnp.stack([own[6, :local_width], own[6, 2 * local_width : 3 * local_width]])
        qv = qv.reshape(2, heads_local, head)
        qv = lax.dynamic_slice_in_dim(qv, seq_index * piece, piece, 2)
        up = lax.dynamic_slice_in_dim(own[7].reshape(-1, head), seq_index * piece, piece, 1)
        qkv_grad = jnp.stack([attn[:, i * local_width : (i + 1) * local_width] for i in range(3)])
        out_grad = attn[:, 3 * local_width :].T
    return (
        block_out,
        block_grad,
        past_grad.transpose(0, 2, 1),
        vec_own[0],
        vec_own[1],
        qkv_grad,
        qv,
        out_grad,
        vec_own[4],
        vec_own[2],
        vec_own[3],
        up_grad,
        up,
        down_grad.T,
        vec_own[5],
    )


def solution(mesh):
    row = P("seq", None)
    placed = (
        row,
        row,
        P("seq", None, "mp"),
        row,
        P("seq"),
        P("seq"),
        P("seq"),
        P(None, "seq", "mp"),
        P(None, "mp", "seq"),
        P("mp", "seq"),
        P("seq"),
        P("seq"),
        P("seq"),
        P("seq", "mp"),
        P("mp", "seq"),
        P("mp", "seq"),
        P("seq"),
    )
    return jax.shard_map(
        local,
        mesh=mesh,
        in_specs=placed,
        out_specs=(row, row, placed[2]) + placed[5:],
        check_vma=False,
    )
```

```python
import functools
import math

import jax
import jax.numpy as jnp
from jax import lax
from jax.experimental import pallas as pl
from jax.experimental.pallas import tpu as pltpu
from jax.sharding import PartitionSpec as P

NB = 256
PIVOTS = 32
NORM_EPSILON = 1e-05
RIDGE_WEIGHT = 1.0
NARROW_WIDTH = 0.01
BROAD_WIDTH = 0.05
GELU_SCALE = 0.7978845608028654
GELU_CUBIC = 0.044715

BF = jnp.bfloat16
F32 = jnp.float32
HIGHEST = lax.Precision.HIGHEST
BIG_VMEM = 60 * 1024 * 1024
MAX_VMEM = 67043328


def dot(a, b):
    return jnp.dot(a, b, preferred_element_type=F32)


def dot_nt(a, b):
    return lax.dot_general(a, b, (((1,), (1,)), ((), ())), preferred_element_type=F32)


def dot_tn(a, b, precision=None):
    return lax.dot_general(
        a, b, (((0,), (0,)), ((), ())), preferred_element_type=F32, precision=precision
    )


def norm_parts(values):
    centered = values - jnp.mean(values, axis=-1, keepdims=True)
    inverse = lax.rsqrt(jnp.mean(centered * centered, axis=-1, keepdims=True) + NORM_EPSILON)
    return centered * inverse, inverse


def norm_back(upstream, normed, inverse, gain):
    scaled = upstream * gain
    inner = scaled - jnp.mean(scaled, axis=-1, keepdims=True)
    inner = inner - normed * jnp.mean(scaled * normed, axis=-1, keepdims=True)
    return inner * inverse


def col_sum(values):
    return jnp.sum(values, axis=0, keepdims=True)


def basis_of(places, used):
    column = lax.broadcasted_iota(jnp.int32, (places.shape[0], NB), 1)
    centers = (column.astype(F32) + 0.5) / NB
    widths = jnp.where(column % 2 == 0, NARROW_WIDTH, BROAD_WIDTH).astype(F32)
    scaled = (places - centers) / widths
    return jnp.exp(-0.5 * (scaled * scaled)) * used


def meta_rows(positions, counts_ref, first, total, seg_len):
    items, slots = positions.shape
    slot = lax.broadcasted_iota(jnp.int32, (1, slots), 1)
    places, used, spots = [], [], []
    for i in range(items):
        spot = positions[i : i + 1, :].astype(F32)
        item = (first + i).astype(F32)
        places.append((item + (spot + 0.5) / seg_len) / total)
        used.append((slot < counts_ref[i]).astype(F32))
        spots.append(spot)
    return jnp.concatenate(
        places + used + spots + [jnp.zeros((8 - 3 * items, slots), F32)], axis=0
    )


def iotas(shape):
    return lax.broadcasted_iota(jnp.int32, shape, 0), lax.broadcasted_iota(jnp.int32, shape, 1)


def small_rows(stack, b_qv, b_up_t, s, width, head):
    part, piece = stack.shape[1], b_up_t.shape[0]
    row, lane = iotas((part, width))
    rows = [jnp.dot(stack, (lane == s * part + row).astype(F32), preferred_element_type=F32)]
    row, lane = iotas((piece, width))
    repeat = (lax.rem(lane, piece) == row).astype(F32)
    _, lane = iotas((1, width))
    half = width // 2
    bias = jnp.zeros((1, width), F32)
    for h in range(b_qv.shape[0]):
        spread = jnp.dot(b_qv[h], repeat, preferred_element_type=F32)
        for t in range(2):
            at = h * head + t * half + s * piece
            bias = bias + jnp.where((lane >= at) & (lane < at + piece), spread[t : t + 1], 0.0)
    row, lane = iotas((b_up_t.shape[1], width))
    spread = jnp.dot(b_up_t, (lane // head == row).astype(F32), preferred_element_type=F32)
    row, lane = iotas((piece, width))
    up = jnp.sum(jnp.where(lax.rem(lane, head) == s * piece + row, spread, 0.0), axis=0, keepdims=True)
    return jnp.concatenate(rows + [bias, up, jnp.zeros((8, width), F32)], axis=0).astype(BF)


def small_pieces(own, s, part, piece, head, heads):
    width = own.shape[1]
    half = width // 2
    row, lane = iotas((width, part + 2 * heads * piece))
    slot = lane - part
    spot = (slot // (2 * piece)) * head + (lax.rem(slot, 2 * piece) // piece) * half
    source = jnp.where(lane < part, s * part + lane, spot + s * piece + lax.rem(slot, piece))
    picked = jnp.dot(
        own, (row == source).astype(F32), preferred_element_type=F32, precision=HIGHEST
    )
    at = [part + i * piece for i in range(2 * heads)]
    flat = [picked[6:7, i : i + piece] for i in at]
    biases = [jnp.concatenate(flat[2 * h : 2 * h + 2], axis=0) for h in range(heads)]
    row, lane = iotas((piece, width))
    masked = jnp.where(lax.rem(lane, head) == s * piece + row, own[7:8], 0.0)
    row, lane = iotas((width, width // head))
    up = jnp.dot(
        masked, (row // head == lane).astype(F32), preferred_element_type=F32, precision=HIGHEST
    )
    return picked[:, :part], biases, up


def position_of(column, i, items):
    return column[:, 2 * items + i : 2 * items + i + 1].astype(jnp.int32)


def inverse_2(a, b, c, d):
    scale = 1.0 / (a * d - b * c)
    return d * scale, -(b * scale), -(c * scale), a * scale


def product_2(x, y):
    return (
        x[0] * y[0] + x[1] * y[2],
        x[0] * y[1] + x[1] * y[3],
        x[2] * y[0] + x[3] * y[2],
        x[2] * y[1] + x[3] * y[3],
    )


def invert_step(mat_ref):
    block = PIVOTS
    lane = lax.broadcasted_iota(jnp.int32, (block, NB), 1)
    line = lax.broadcasted_iota(jnp.int32, (block, NB), 0)
    panel = mat_ref[0:block, :]
    for k in range(0, block, 4):
        cols = [jnp.broadcast_to(panel[:, k + j : k + j + 1], panel.shape) for j in range(4)]
        at = [[cols[j][k + i : k + i + 1] for j in range(4)] for i in range(4)]
        head = inverse_2(at[0][0], at[0][1], at[1][0], at[1][1])
        upper = (at[0][2], at[0][3], at[1][2], at[1][3])
        lower = (at[2][0], at[2][1], at[3][0], at[3][1])
        right, left = product_2(head, upper), product_2(lower, head)
        minus = product_2(lower, right)
        tail = inverse_2(
            at[2][2] - minus[0], at[2][3] - minus[1], at[3][2] - minus[2], at[3][3] - minus[3]
        )
        rt, tl = product_2(right, tail), product_2(tail, left)
        back = product_2(rt, left)
        inverse = (
            (head[0] + back[0], head[1] + back[1], -rt[0], -rt[1]),
            (head[2] + back[2], head[3] + back[3], -rt[2], -rt[3]),
            (-tl[0], -tl[1], tail[0], tail[1]),
            (-tl[2], -tl[3], tail[2], tail[3]),
        )
        inside = (lane >= k) & (lane < k + 4)
        rows = [
            jnp.where(inside[0:1], (lane[0:1] == k + j).astype(F32), panel[k + j : k + j + 1])
            for j in range(4)
        ]
        new = [
            (m[0] * rows[0] + m[1] * rows[1]) + (m[2] * rows[2] + m[3] * rows[3]) for m in inverse
        ]
        rest = jnp.where(inside, 0.0, panel) - (
            (cols[0] * new[0] + cols[1] * new[1]) + (cols[2] * new[2] + cols[3] * new[3])
        )
        for i in range(4):
            rest = jnp.where(line == k + i, new[i], rest)
        panel = rest
    mat_ref[0:block, :] = panel
    row = lax.broadcasted_iota(jnp.int32, (NB, NB), 0)
    col = lax.broadcasted_iota(jnp.int32, (NB, NB), 1)
    mat = mat_ref[...]
    inside_row = row < block
    inside_col = col < block
    left = jnp.where(inside_col & ~inside_row, mat, 0.0)
    right = jnp.where(inside_row, mat, 0.0)
    update = jnp.dot(left, right, preferred_element_type=F32, precision=HIGHEST)
    mat = jnp.where(inside_row, mat, jnp.where(inside_col, 0.0, mat) - update)
    mat = pltpu.roll(mat, NB - block, 1)
    mat_ref[0 : NB - block, :] = mat[block:, :]
    mat_ref[NB - block :, :] = mat[:block, :]


def owner_basis(meta, items):
    column = meta.T
    rows = [
        basis_of(column[:, i : i + 1], column[:, items + i : items + i + 1]) for i in range(items)
    ]
    return jnp.concatenate(rows, axis=0)


def clear_moments(mat_ref, mom_ref):
    row = lax.broadcasted_iota(jnp.int32, (NB, NB), 0)
    col = lax.broadcasted_iota(jnp.int32, (NB, NB), 1)
    mat_ref[...] = jnp.where(row == col, RIDGE_WEIGHT, 0.0)
    mom_ref[...] = jnp.zeros_like(mom_ref)


def coefficients(mat_ref, mom_ref):
    return jnp.dot(mat_ref[...], mom_ref[...], preferred_element_type=F32, precision=HIGHEST)


def pick_samples(past, meta, items):
    slots, seg_len = meta.shape[1], past.shape[2]
    column = meta.T
    at = lax.broadcasted_iota(jnp.int32, (slots, seg_len), 1)
    rows = []
    for i in range(items):
        pick = (at == position_of(column, i, items)).astype(F32).astype(BF)
        rows.append(dot_nt(pick, past[i]).astype(BF))
    return jnp.concatenate(rows, axis=0)


def sample_kernel(past_ref, meta_ref, out_ref, *, items):
    out_ref[...] = pick_samples(past_ref[...], meta_ref[...], items)


def sample_rows(past, meta):
    items, width, seg_len = past.shape
    return pl.pallas_call(
        functools.partial(sample_kernel, items=items),
        out_shape=jax.ShapeDtypeStruct((items * meta.shape[1], width), BF),
        name="sample_rows",
    )(past, meta)


def solve_kernel(sampled_ref, meta_ref, coef_ref, inv_ref, mat_ref, mom_ref, *, items):
    clear_moments(mat_ref, mom_ref)

    def owner(s, carry):
        rows = owner_basis(meta_ref[s], items)
        mat_ref[...] += dot_tn(rows, rows, HIGHEST)
        mom_ref[...] += dot_tn(rows, sampled_ref[s].astype(F32), HIGHEST)
        return carry

    lax.fori_loop(0, meta_ref.shape[0], owner, 0)

    def step(s, carry):
        invert_step(mat_ref)
        return carry

    lax.fori_loop(0, NB // PIVOTS, step, 0)
    inv_ref[...] = mat_ref[...]
    coef_ref[...] = coefficients(mat_ref, mom_ref).astype(BF)


def solve_memory(sampled, meta, items):
    width = sampled.shape[-1]
    return pl.pallas_call(
        functools.partial(solve_kernel, items=items),
        out_shape=(
            jax.ShapeDtypeStruct((NB, width), BF),
            jax.ShapeDtypeStruct((NB, NB), F32),
        ),
        scratch_shapes=[pltpu.VMEM((NB, NB), F32), pltpu.VMEM((NB, width), F32)],
        compiler_params=pltpu.CompilerParams(vmem_limit_bytes=BIG_VMEM),
        name="solve_memory",
    )(sampled, meta)


def give_past(gmem, coef_ref, vec_ref, inv_ref, meta_ref, out_ref, gv_ref):
    slots = meta_ref.shape[1]
    item_count, width, seg_len = out_ref.shape
    normed, inverse = norm_parts(coef_ref[...].astype(F32))
    coef_grad = norm_back(gmem, normed, inverse, vec_ref[0, 0:1, :])
    gv_ref[...] = jnp.zeros_like(gv_ref)
    gv_ref[0:1, :] = col_sum(gmem * normed)
    gv_ref[1:2, :] = col_sum(gmem)
    part = lax.axis_index("mp")
    mine = jnp.zeros((coef_grad.shape[0], width), F32)
    for m in range(coef_grad.shape[1] // width):
        mine = jnp.where(part == m, coef_grad[:, m * width : (m + 1) * width], mine)
    moment = jnp.dot(inv_ref[...], mine, preferred_element_type=F32, precision=HIGHEST)
    at = lax.broadcasted_iota(jnp.int32, (slots, seg_len), 1)
    column = meta_ref[...].T
    for i in range(item_count):
        rows = basis_of(column[:, i : i + 1], column[:, item_count + i : item_count + i + 1])
        sampled = jnp.dot(rows, moment, preferred_element_type=F32, precision=HIGHEST)
        spread = (at == position_of(column, i, item_count)).astype(F32)
        out_ref[i] = dot_tn(sampled, spread, HIGHEST)


def past_kernel(gmem_ref, coef_ref, vec_ref, inv_ref, meta_ref, out_ref, gv_ref):
    give_past(gmem_ref[...], coef_ref, vec_ref, inv_ref, meta_ref, out_ref, gv_ref)


def past_grads(gmem, coef, vec, inv, meta, items, seg_len, width):
    return pl.pallas_call(
        past_kernel,
        out_shape=(
            jax.ShapeDtypeStruct((items, width, seg_len), F32),
            jax.ShapeDtypeStruct((8, coef.shape[1]), F32),
        ),
        compiler_params=pltpu.CompilerParams(vmem_limit_bytes=BIG_VMEM),
        name="past_grads",
    )(gmem, coef, vec, inv, meta)


MESH = pl.DeviceIdType.MESH
LINE = 4
PLANE = 8
NEAR = (0, -1, 1, -2, 2, -3, 3)


class Place:
    def __init__(self):
        self.s = lax.axis_index("seq")
        self.z = lax.axis_index("mp")
        core = lax.rem(self.s, 2)
        x = lax.rem(self.s // 2, 2)
        y = self.s // 4
        self.turn = 1 - 2 * core
        self.partner = self.s + self.turn
        self.sx = self.s + 2 - 4 * x
        self.sy = self.s + 4 - 8 * y
        self.sd = self.sx + 4 - 8 * y
        self.low = self.z > 0
        self.high = self.z < LINE - 1
        self.near = [
            (
                d,
                valid(self.z + d),
                self.z + d,
                lax.rem(self.z + d + LINE, 2) == 1,
                lax.rem(self.z + d + LINE, 2) == 0,
            )
            for d in NEAR
        ]


def valid(m):
    return (m >= 0) & (m < LINE)


def when(conditions, act):
    conditions = [c for c in conditions if c is not None]
    if conditions:
        pl.when(functools.reduce(lambda a, b: a & b, conditions))(act)
    else:
        act()


def greet(place, whole_line=False):
    barrier = pltpu.get_barrier_semaphore()

    def signal(seq, z):
        pl.semaphore_signal(barrier, inc=1, device_id=(seq, z), device_id_type=MESH)

    for seq in (place.partner, place.sx, place.sy):
        signal(seq, place.z)
    for d, ok, m, odd, even in place.near[1:]:
        if whole_line or abs(d) == 1:
            when((ok,), lambda: signal(place.s, m))
    if whole_line:
        peers = LINE - 1
    else:
        peers = (place.z + LINE - 1) // LINE + (2 * LINE - 2 - place.z) // LINE
    pl.semaphore_wait(barrier, 3 + peers)


UP, DOWN, ACROSS_X, ACROSS_Y, PARTNER = range(5)


class Spread:
    def __init__(self, place, src, dst, send, recv, local, line=True):
        self.p, self.src, self.dst = place, src, dst
        self.send, self.recv, self.line = send, recv, line
        self.rows = src.shape[0]
        self.sent = []
        self.mine = place.z if line else 0
        self.around = place.near if line else [(0, None, 0, None, None)]
        self.own = pltpu.make_async_copy(src, self.at(self.mine, place.s), local)

    def at(self, m, s):
        return self.dst.at[m, pl.ds(s * self.rows, self.rows), :]

    def copy(self, direction, m, s, own=False):
        p = self.p
        device = (
            (p.s, p.z + 1),
            (p.s, p.z - 1),
            (p.sx, p.z),
            (p.sy, p.z),
            (p.partner, p.z),
        )[direction]
        return pltpu.make_async_remote_copy(
            src_ref=self.src if own else self.at(m, s),
            dst_ref=self.at(m, s),
            send_sem=self.send.at[direction, m * 4 + s // 2],
            recv_sem=self.recv.at[m * PLANE + s],
            device_id=device,
            device_id_type=MESH,
        )

    def start(self, conditions, *what, **how):
        when(conditions, lambda: self.copy(*what, **how).start())
        self.sent.append((conditions, what, how))

    def arrived(self, m, s):
        self.copy(PARTNER, m, s).wait_recv()

    def first(self):
        p, m = self.p, self.mine
        self.own.start()
        if self.line:
            self.start((p.high,), UP, m, p.s, own=True)
            self.start((p.low,), DOWN, m, p.s, own=True)
        for direction in (ACROSS_X, ACROSS_Y, PARTNER):
            self.start((), direction, m, p.s, own=True)

    def along(self, d, ok, m, odd, even):
        p = self.p
        when((ok,), lambda: self.arrived(m, p.s))
        if d < 0:
            self.start((ok, p.high), UP, m, p.s)
        else:
            self.start((ok, p.low), DOWN, m, p.s)
        for direction in (ACROSS_X, ACROSS_Y, PARTNER):
            self.start((ok,), direction, m, p.s)

    def across(self, d, ok, m, odd, even):
        p = self.p
        when((ok,), lambda: self.arrived(m, p.sx))
        if self.line:
            self.start((ok, odd), ACROSS_Y, m, p.sx)
        self.start((ok,), PARTNER, m, p.sx)
        when((ok,), lambda: self.arrived(m, p.sy))
        if self.line:
            self.start((ok, even), ACROSS_X, m, p.sy)
        else:
            self.start((), ACROSS_X, m, p.sy)
        self.start((ok,), PARTNER, m, p.sy)

    def corner(self, d, ok, m, odd, even):
        p = self.p
        when((ok,), lambda: self.arrived(m, p.sd))
        self.start((ok,), PARTNER, m, p.sd)

    def part(self, kind, d):
        if kind == 0:
            return self.first
        act = (self.along, self.across, self.corner)[kind - 1]
        return functools.partial(act, *self.around[NEAR.index(d)])

    def steps(self, kind):
        return [self.part(kind, d) for d in NEAR if d or kind > 1]

    def close(self, m):
        p = self.p
        for s in (p.s, p.sx, p.sy, p.sd):
            self.arrived(m, s + p.turn)

    def settle(self):
        for conditions, what, how in self.sent:
            when(conditions, lambda: self.copy(*what, **how).wait_send())


class DirectSpread(Spread):
    def throw(self, m):
        p = self.p
        return pltpu.make_async_remote_copy(
            src_ref=self.src,
            dst_ref=self.at(self.mine, p.s),
            send_sem=self.send.at[UP, m],
            recv_sem=self.recv.at[self.mine * PLANE + p.s],
            device_id=(p.s, m),
            device_id_type=MESH,
        )

    def first(self):
        p, m = self.p, self.mine
        self.own.start()
        for d, ok, to, odd, even in self.around[1:]:
            when((ok,), lambda: self.throw(to).start())
        for direction in (ACROSS_X, ACROSS_Y, PARTNER):
            self.start((), direction, m, p.s, own=True)

    def along(self, d, ok, m, odd, even):
        when((ok,), lambda: self.arrived(m, self.p.s))
        for direction in (ACROSS_X, ACROSS_Y, PARTNER):
            self.start((ok,), direction, m, self.p.s)

    def settle(self):
        super().settle()
        for d, ok, m, odd, even in self.around[1:]:
            when((ok,), lambda: self.throw(m).wait_send())


class Line:
    def __init__(self, place, src, dst, send, recv, local):
        self.p, self.src, self.dst = place, src, dst
        self.send, self.recv = send, recv
        self.sent = []
        self.own = pltpu.make_async_copy(src, dst.at[place.z], local)

    def copy(self, up, m, own=False):
        p = self.p
        return pltpu.make_async_remote_copy(
            src_ref=self.src if own else self.dst.at[m],
            dst_ref=self.dst.at[m],
            send_sem=self.send.at[1 if up else 0, m],
            recv_sem=self.recv.at[m],
            device_id=(p.s, p.z + 1 if up else p.z - 1),
            device_id_type=MESH,
        )

    def start(self, conditions, *what, **how):
        when(conditions, lambda: self.copy(*what, **how).start())
        self.sent.append((conditions, what, how))

    def first(self):
        p = self.p
        self.own.start()
        self.start((p.high,), True, p.z, own=True)
        self.start((p.low,), False, p.z, own=True)

    def step(self, distance):
        p = self.p
        for d, ok, m, odd, even in p.near:
            if abs(d) != distance:
                continue
            when((ok,), lambda: self.copy(True, m).wait_recv())
            if d < 0:
                self.start((ok, p.high), True, m)
            else:
                self.start((ok, p.low), False, m)

    def finish_sends(self):
        for conditions, what, how in self.sent:
            when(conditions, lambda: self.copy(*what, **how).wait_send())

    def finish(self):
        self.finish_sends()
        self.own.wait()


class Collect:
    OWN, SIDE_X, SIDE_Y, CORNER = range(4)

    def __init__(self, place, grads, out, buffers, sems):
        self.p, self.grads, self.out = place, grads, out
        self.pin, self.din, self.xin, self.yin, self.zin = buffers
        self.block_sems, self.sems = sems
        self.rows = out.shape[1]
        self.columns = (place.s, place.sx, place.sy, place.sd)

    def plane(self, i):
        return i

    def unit(self, c, m, turn=0):
        s = self.columns[c] + turn
        return self.grads.at[m, :, pl.ds(s * self.rows, self.rows), :]

    def remote(self, src, dst, send, recv, device):
        return pltpu.make_async_remote_copy(
            src_ref=src,
            dst_ref=dst,
            send_sem=send,
            recv_sem=recv,
            device_id=device,
            device_id_type=MESH,
        )

    def swap(self, c, m):
        p = self.p
        return self.remote(
            self.unit(c, m, p.turn),
            self.pin.at[c, m],
            self.block_sems.at[0, c, m],
            self.block_sems.at[1, c, m],
            (p.partner, p.z),
        )

    def hop(self, kind, m, by_x=True):
        p = self.p
        src, dst, device = (
            (self.CORNER, self.din, (p.sx if by_x else p.sy, p.z)),
            (self.SIDE_X, self.xin, (p.sx, p.z)),
            (self.SIDE_Y, self.yin, (p.sy, p.z)),
        )[kind]
        return self.remote(
            self.unit(src, m),
            dst.at[m],
            self.sems.at[kind, m],
            self.sems.at[4 + kind, m],
            device,
        )

    def slot(self, m, z):
        ends = 1 // (1 + z - m)
        return m + (LINE - m) * ends

    def climb(self, m, up):
        p = self.p
        return self.remote(
            self.unit(self.OWN, m),
            self.zin.at[m if up else self.slot(m, p.z - 1)],
            self.sems.at[3, m],
            self.sems.at[7 if up else 8, m],
            (p.s, p.z + 1 if up else p.z - 1),
        )

    def climbed(self, m, up):
        zin = self.zin.at[m if up else self.slot(m, self.p.z)]
        return self.remote(
            zin, zin, self.sems.at[3, m], self.sems.at[7 if up else 8, m], (self.p.partner, self.p.z)
        )

    def add(self, c, m, *others):
        size = min(32, self.rows)
        pieces = self.rows // size

        @pl.loop(0, self.grads.shape[1] * pieces)
        def _(j):
            l = j // pieces
            at = lax.rem(j, pieces) * size
            here = pl.ds(pl.multiple_of(self.columns[c] * self.rows + at, 16), size)
            there = pl.ds(pl.multiple_of(at, 16), size)
            total = self.grads[m, l, here, :].astype(F32)
            for other in others:
                total = total + other[m, l, there, :].astype(F32)
            self.grads[m, l, here, :] = total.astype(self.grads.dtype)

    def begin(self, m):
        for c in (self.CORNER, self.SIDE_X, self.SIDE_Y, self.OWN):
            self.swap(c, m).start()

    def join(self, c, m):
        self.swap(c, m).wait_recv()
        self.add(c, m, self.pin.at[c])

    def corner(self, i):
        m = self.plane(i)
        self.join(self.CORNER, m)
        even = lax.rem(m, 2) == 0
        pl.when(even)(lambda: self.hop(0, m, True).start())
        pl.when(~even)(lambda: self.hop(0, m, False).start())

    def sides(self, i):
        m = self.plane(i)
        even = lax.rem(m, 2) == 0
        self.join(self.SIDE_X, m)
        self.join(self.SIDE_Y, m)
        pl.when(even)(lambda: self.hop(1, m).start())
        pl.when(~even)(lambda: self.hop(2, m).start())

    def relay(self, i):
        m = self.plane(i)
        even = lax.rem(m, 2) == 0
        self.hop(0, m).wait_recv()

        @pl.when(even)
        def _():
            self.add(self.SIDE_Y, m, self.din)
            self.hop(2, m).start()

        @pl.when(~even)
        def _():
            self.add(self.SIDE_X, m, self.din)
            self.hop(1, m).start()

    def line(self, i):
        p = self.p
        m = self.plane(i)
        self.join(self.OWN, m)
        self.hop(1, m).wait_recv()
        self.hop(2, m).wait_recv()
        self.add(self.OWN, m, self.xin, self.yin)

        @pl.when(m > p.z)
        def _():
            @pl.when(p.low)
            def _():
                self.climbed(m, True).wait_recv()
                self.add(self.OWN, m, self.zin)

            self.climb(m, True).start()

        @pl.when(m < p.z)
        def _():
            @pl.when(p.high)
            def _():
                self.climbed(m, False).wait_recv()
                self.add(self.OWN, m, self.zin)

            self.climb(m, False).start()

    def result(self):
        p = self.p
        self.out[...] = self.unit(self.OWN, p.z)[...].astype(F32)

        @pl.when(p.low)
        def _():
            self.climbed(p.z, True).wait_recv()
            self.out[...] += self.zin[p.z].astype(F32)

        @pl.when(p.high)
        def _():
            self.climbed(p.z, False).wait_recv()
            self.out[...] += self.zin[LINE].astype(F32)

    def part(self, kind, i):
        if kind == 4:
            return self.result
        return functools.partial((self.corner, self.sides, self.relay, self.line)[kind], i)

    def settle(self):
        @pl.loop(0, LINE)
        def _(m):
            for c in range(4):
                self.swap(c, m).wait_send()
            for kind in range(3):
                self.hop(kind, m).wait_send()
            pl.when(m != self.p.z)(lambda: self.climb(m, True).wait_send())


class DirectCollect(Collect):
    def throw(self, m):
        p = self.p
        return self.remote(
            self.unit(self.OWN, m),
            self.zin.at[p.z],
            self.sems.at[3, m],
            self.sems.at[7, p.z],
            (p.s, m),
        )

    def line(self, i):
        m = self.plane(i)
        self.join(self.OWN, m)
        self.hop(1, m).wait_recv()
        self.hop(2, m).wait_recv()
        self.add(self.OWN, m, self.xin, self.yin)
        pl.when(m != self.p.z)(lambda: self.throw(m).start())

    def result(self):
        p = self.p
        self.out[...] = self.unit(self.OWN, p.z)[...].astype(F32)
        for m in range(LINE):

            @pl.when(m != p.z)
            def _():
                zin = self.zin.at[m]
                self.remote(
                    zin, zin, self.sems.at[3, m], self.sems.at[7, m], (p.partner, p.z)
                ).wait_recv()
                self.out[...] += self.zin[m].astype(F32)


BUFFERS = ((4, LINE), (LINE,), (LINE,), (LINE,), (LINE + 1,))


def project(rows, weights, bias, local):
    return (dot(rows, weights[:, : 3 * local]) + bias[:, : 3 * local]).astype(BF)


def attend(query, keys, values, head, store, between):
    rows, local = query.shape
    half = rows // 2
    query_t = query.T * BF(1.0 / math.sqrt(head))
    value_t = values.T
    line = lax.broadcasted_iota(jnp.int32, (local, rows), 0)
    heads = []
    for h in range(local // head):
        own = (line >= h * head) & (line < (h + 1) * head)
        masked = jnp.where(own, query_t, BF(0.0))
        value_h = value_t[h * head : (h + 1) * head, :]
        parts = []
        for b in range(2):
            span = NB + (b + 1) * half
            scores = dot(keys[:span, :], masked[:, b * half : (b + 1) * half])
            key_at = lax.broadcasted_iota(jnp.int32, (half, half), 0)
            row_at = lax.broadcasted_iota(jnp.int32, (half, half), 1)
            edge = jnp.where(key_at <= row_at, scores[span - half :, :], -1e30)
            scores = jnp.concatenate([scores[: span - half, :], edge], axis=0)
            scores = jnp.exp(scores - jnp.max(scores, axis=0, keepdims=True))
            probs = (scores * (1.0 / jnp.sum(scores, axis=0, keepdims=True))).astype(BF)
            store(h, slice(0, span), slice(b * half, (b + 1) * half), probs)
            parts.append(dot(value_h[:, :span], probs))
        heads.append(jnp.concatenate(parts, axis=1).astype(BF))
        between(h)
    return jnp.concatenate(heads, axis=0)


def gelu_parts(pre):
    square = pre * pre
    inner = jnp.tanh(GELU_SCALE * (pre + GELU_CUBIC * pre * square))
    half_up = 0.5 * (1.0 + inner)
    slope = GELU_SCALE * (1.0 + 3.0 * GELU_CUBIC * square)
    return (pre * half_up).astype(BF), half_up + 0.5 * pre * (1.0 - inner * inner) * slope


def forward_kernel(
    tokens_ref,
    past_ref,
    pos_ref,
    counts_ref,
    stack_ref,
    b_qv_ref,
    b_up_ref,
    w_qkv_ref,
    w_out_ref,
    up_ref,
    down_ref,
    wa_ref,
    wu_ref,
    wd_ref,
    out_ref,
    res_ref,
    hmt_ref,
    h2t_ref,
    prob_ref,
    key_ref,
    val_ref,
    query_ref,
    att_ref,
    act_ref,
    slope_ref,
    vec_ref,
    inv_ref,
    coef_ref,
    meta_ref,
    hm_ref,
    h2_ref,
    room_ref,
    attn_ref,
    tok_ref,
    acc_ref,
    mom_ref,
    sampled_ref,
    all_sampled_ref,
    basis_ref,
    all_meta_ref,
    all_room_ref,
    coef_part_ref,
    all_coef_ref,
    wide_ref,
    past_vmem,
    flat_send,
    flat_recv,
    flat_local,
    send,
    recv,
    own_sem,
    line_send,
    line_recv,
    line_own,
    load_sem,
    *,
    items,
    head,
):
    step = pl.program_id(0)
    rows, width = tok_ref.shape
    local = query_ref.shape[2]
    place = Place()
    flat = [
        Spread(
            place, src, dst, flat_send.at[i], flat_recv.at[i], flat_local.at[i], line=False
        )
        for i, (src, dst) in enumerate(
            ((meta_ref, all_meta_ref), (sampled_ref, all_sampled_ref))
        )
    ]
    wide = [
        Spread(place, src, dst, send.at[i], recv.at[i], own_sem.at[i])
        for i, (src, dst) in enumerate(
            ((room_ref, all_room_ref), (attn_ref, wa_ref), (up_ref, wu_ref), (down_ref, wd_ref))
        )
    ]
    room, attn, up, down = wide
    line = Line(place, coef_part_ref, all_coef_ref, line_send, line_recv, line_own)

    attn_at = SOLVE_STEPS
    mlp_at = attn_at + LINE
    last = mlp_at + LINE - 1
    plan = {
        slot: [wide[i].part(kind, d) for i, kind, d in steps] for slot, steps in FORWARD_PLAN
    }

    def transfers(at, position):
        if plan.get((at, position)):

            @pl.when(step == at)
            def _():
                for one in plan[(at, position)]:
                    one()

    def load(ref, m, slot, which):
        return pltpu.make_async_copy(ref.at[m], wide_ref.at[slot, which], load_sem.at[slot, which])

    @pl.when(step == 0)
    def _():
        bring_tok = pltpu.make_async_copy(
            tokens_ref.at[pl.ds(place.z * rows, rows), :], tok_ref, load_sem.at[0, 0]
        )
        bring_past = pltpu.make_async_copy(past_ref, past_vmem, load_sem.at[0, 1])
        bring_tok.start()
        bring_past.start()
        greet(place)
        meta_ref[...] = meta_rows(
            pos_ref[...], counts_ref, place.s * items, PLANE * items, past_ref.shape[2]
        )
        bring_past.wait()
        sampled_ref[...] = pick_samples(past_vmem[...], meta_ref[...], items)
        for part in flat:
            part.first()
        room_ref[...] = small_rows(
            stack_ref[...].astype(F32),
            b_qv_ref[...].astype(F32),
            b_up_ref[...].astype(F32),
            place.s,
            width,
            head,
        )
        for i in range(3):
            attn_ref[:, i * local : (i + 1) * local] = w_qkv_ref[i]
        row, lane = iotas((w_out_ref.shape[1], w_out_ref.shape[1]))
        unit = (row == lane).astype(F32).astype(BF)
        attn_ref[:, 3 * local :] = dot_nt(unit, w_out_ref[...]).astype(BF)
        bring_tok.wait()
        acc_ref[...] = jnp.zeros_like(acc_ref)
        clear_moments(inv_ref, mom_ref)

    transfers(0, 0)

    meta, samples = flat

    @pl.when(step == 1)
    def _():
        for kind in (2, 3):
            meta.part(kind, 0)()
        samples.part(2, 0)()
        meta.own.wait()
        meta.close(0)

    transfers(1, 0)

    @pl.when(step == 1)
    def _():
        def owner(s, carry):
            rows = owner_basis(all_meta_ref[0, pl.ds(s * 8, 8), :], items)
            basis_ref[s] = rows
            inv_ref[...] += dot_tn(rows, rows, HIGHEST)
            return carry

        lax.fori_loop(0, PLANE, owner, 0)
        samples.part(3, 0)()
        samples.own.wait()
        samples.close(0)

    transfers(1, 1)

    @pl.when(step == 1)
    def _():
        def owner(s, carry):
            count = sampled_ref.shape[0]
            rows = all_sampled_ref[0, pl.ds(s * count, count), :]
            mom_ref[...] += dot_tn(basis_ref[s], rows.astype(F32), HIGHEST)
            return carry

        lax.fori_loop(0, PLANE, owner, 0)

    transfers(1, 2)

    inverse_end = 2 + NB // PIVOTS

    @pl.when((step >= 2) & (step < inverse_end))
    def _():
        invert_step(inv_ref)

    for at in range(2, inverse_end):
        transfers(at, 0)

    @pl.when(step == inverse_end)
    def _():
        coef_part_ref[...] = coefficients(inv_ref, mom_ref).astype(BF)
        line.first()

    transfers(inverse_end, 0)

    @pl.when(step == inverse_end)
    def _():
        room.own.wait()
        for m in range(LINE):
            room.close(m)
            total = all_room_ref[m, 0:16, :].astype(F32)
            for s in range(1, PLANE):
                total = total + all_room_ref[m, s * 16 : (s + 1) * 16, :].astype(F32)
            vec_ref[m] = total
        gain, bias = vec_ref[0, 0:1, :], vec_ref[0, 1:2, :]
        normed, _ = norm_parts(tok_ref[...].astype(F32))
        hm_ref[NB:, :] = (normed * gain + bias).astype(BF)
        hmt_ref[:, NB:] = hm_ref[NB:, :].T
        line.step(1)

    transfers(inverse_end, 1)

    @pl.when(step == inverse_end)
    def _():
        attn.own.wait()
        attn.close(0)
        load(wa_ref, 0, 0, 0).start()
        line.step(2)

    transfers(inverse_end, 2)

    @pl.when(step == inverse_end)
    def _():
        line.step(3)
        line.own.wait()
        gain, bias = vec_ref[0, 0:1, :], vec_ref[0, 1:2, :]
        for m in range(LINE):
            coef_ref[:, m * local : (m + 1) * local] = all_coef_ref[m]
        normed, _ = norm_parts(coef_ref[...].astype(F32))
        hm_ref[0:NB, :] = (normed * gain + bias).astype(BF)
        hmt_ref[:, 0:NB] = hm_ref[0:NB, :].T

    @pl.when((step >= attn_at) & (step < mlp_at))
    def _():
        m = step - attn_at
        slot = lax.rem(m, 2)
        load(wa_ref, m, slot, 0).wait()

        @pl.when(m < LINE - 1)
        def _():
            attn.close(m + 1)
            load(wa_ref, m + 1, 1 - slot, 0).start()

        weights = wide_ref[slot, 0]
        projected = project(hm_ref[...], weights, vec_ref[m, 6:7, :], local)
        query = projected[NB:, :local]
        keys = projected[:, local : 2 * local]
        values = projected[:, 2 * local :]
        query_ref[0] = query
        key_ref[0] = keys
        val_ref[0] = values

        def store(h, lines, columns, probs):
            prob_ref[0, h, lines, columns] = probs

        def between(h):
            for at in range(attn_at, mlp_at):
                transfers(at, h)

        attended = attend(query, keys, values, head, store, between)
        att_ref[0] = attended
        acc_ref[...] += dot_nt(attended.T, wide_ref[slot, 0, :, 3 * local :])

    transfers(mlp_at, 0)

    @pl.when(step == mlp_at)
    def _():
        for part in (up, down):
            part.own.wait()
            part.close(0)
        load(wu_ref, 0, 0, 0).start()
        load(wd_ref, 0, 0, 1).start()
        residual = tok_ref[...].astype(F32) + acc_ref[...] + vec_ref[0, 4:5, :]
        res_ref[...] = residual
        normed, _ = norm_parts(residual)
        h2_ref[...] = (normed * vec_ref[0, 2:3, :] + vec_ref[0, 3:4, :]).astype(BF)
        h2t_ref[...] = h2_ref[...].T
        acc_ref[...] = jnp.zeros_like(acc_ref)

    @pl.when(step >= mlp_at)
    def _():
        m = step - mlp_at
        slot = lax.rem(m, 2)
        load(wu_ref, m, slot, 0).wait()
        load(wd_ref, m, slot, 1).wait()

        @pl.when(m < LINE - 1)
        def _():
            up.close(m + 1)
            down.close(m + 1)
            load(wu_ref, m + 1, 1 - slot, 0).start()
            load(wd_ref, m + 1, 1 - slot, 1).start()

        pre = dot(h2_ref[...], wide_ref[slot, 0]) + vec_ref[m, 7:8, :]
        act, slope = gelu_parts(pre)
        act_ref[0] = act
        slope_ref[0] = slope.astype(BF)
        acc_ref[...] += dot_nt(act, wide_ref[slot, 1])

    @pl.when(step == last)
    def _():
        out_ref[...] = (res_ref[...] + acc_ref[...] + vec_ref[0, 5:6, :]).astype(BF)
        for part in flat + wide:
            part.settle()
        line.finish_sends()


SOLVE_STEPS = 3 + NB // PIVOTS


FORWARD_PLAN = (
    (
        (0, 0),
        ((0, 0, 0),),
    ),
    (
        (1, 0),
        ((1, 0, 0), (0, 1, 1), (0, 1, -1),),
    ),
    (
        (1, 1),
        ((0, 1, -2), (0, 1, 2), (1, 1, -1), (1, 1, 1),),
    ),
    (
        (1, 2),
        ((0, 1, -3), (0, 1, 3), (3, 0, 0),),
    ),
    (
        (2, 0),
        ((1, 1, 2), (1, 1, -2),),
    ),
    (
        (4, 0),
        ((0, 2, -3), (0, 2, 3), (1, 2, 0), (0, 2, -1), (0, 2, 1),),
    ),
    (
        (5, 0),
        ((0, 2, 0), (0, 2, -2), (0, 2, 2), (1, 1, -3), (1, 1, 3), (2, 0, 0),),
    ),
    (
        (7, 0),
        ((1, 2, -2), (1, 2, 2), (1, 2, 1), (1, 2, -1),),
    ),
    (
        (8, 0),
        ((3, 1, 1), (3, 1, -1),),
    ),
    (
        (9, 0),
        ((0, 3, 3), (0, 3, -3),),
    ),
    (
        (10, 0),
        ((0, 3, 1), (0, 3, -1), (1, 2, 3), (1, 2, -3), (0, 3, 0), (0, 3, 2), (0, 3, -2), (3, 1, -2), (3, 1, 2),),
    ),
    (
        (10, 1),
        ((3, 1, 3), (3, 1, -3), (1, 3, 0), (1, 3, 1), (1, 3, -2), (1, 3, 3), (1, 3, -1), (1, 3, 2), (1, 3, -3),),
    ),
    (
        (10, 2),
        ((2, 1, -1), (2, 1, 1),),
    ),
    (
        (11, 0),
        ((2, 1, -2), (2, 1, 2),),
    ),
    (
        (11, 1),
        ((2, 1, 3), (2, 1, -3), (3, 2, 0),),
    ),
    (
        (12, 0),
        ((2, 2, 1), (2, 2, -1), (2, 2, 0),),
    ),
    (
        (12, 1),
        ((2, 2, -3), (2, 2, 3), (3, 2, -2), (3, 2, 2),),
    ),
    (
        (13, 0),
        ((3, 2, -1), (3, 2, 1), (2, 2, 2), (2, 2, -2),),
    ),
    (
        (13, 1),
        ((2, 3, -1), (2, 3, 1), (3, 2, 3), (3, 2, -3), (2, 3, 0),),
    ),
    (
        (13, 2),
        ((3, 3, 0), (2, 3, 3), (2, 3, -3),),
    ),
    (
        (14, 1),
        ((3, 3, 1), (3, 3, -1), (3, 3, 2), (3, 3, -2), (2, 3, -2), (2, 3, 2), (3, 3, 3), (3, 3, -3),),
    ),
)


def forward_pass(tokens, past, positions, counts, stack, b_qv, b_up, w_qkv, w_out, up, down, head):
    width = tokens.shape[1]
    rows = tokens.shape[0] // LINE
    items = past.shape[0]
    local = width // LINE
    hidden = up.shape[1]
    heads = local // head
    keyed = NB + rows
    slots = positions.shape[1]
    samples = items * slots
    part = up.shape[0]
    attn_at = SOLVE_STEPS
    mlp_at = attn_at + LINE
    first = lambda i: jnp.clip(i - attn_at, 0, LINE - 1)
    second = lambda i: jnp.clip(i - mlp_at, 0, LINE - 1)
    whole = lambda shape: pl.BlockSpec(shape, lambda i: (0,) * len(shape))
    anywhere = pl.BlockSpec(memory_space=pl.ANY)
    vmem = pl.BlockSpec(memory_space=pltpu.VMEM)
    dma = pltpu.SemaphoreType.DMA
    shape = jax.ShapeDtypeStruct
    return pl.pallas_call(
        functools.partial(forward_kernel, items=items, head=head),
        grid=(mlp_at + LINE,),
        in_specs=[anywhere, anywhere, vmem, pl.BlockSpec(memory_space=pltpu.SMEM)]
        + [vmem] * 5
        + [anywhere, anywhere],
        out_specs=[
            anywhere,
            anywhere,
            anywhere,
            whole((rows, width)),
            whole((rows, width)),
            whole((width, keyed)),
            whole((width, rows)),
            pl.BlockSpec((1, heads, keyed, rows), lambda i: (first(i), 0, 0, 0)),
            pl.BlockSpec((1, keyed, local), lambda i: (first(i), 0, 0)),
            pl.BlockSpec((1, keyed, local), lambda i: (first(i), 0, 0)),
            pl.BlockSpec((1, rows, local), lambda i: (first(i), 0, 0)),
            pl.BlockSpec((1, local, rows), lambda i: (first(i), 0, 0)),
            pl.BlockSpec((1, rows, hidden), lambda i: (second(i), 0, 0)),
            pl.BlockSpec((1, rows, hidden), lambda i: (second(i), 0, 0)),
            whole((LINE, 16, width)),
            whole((NB, NB)),
            whole((NB, width)),
            whole((8, slots)),
        ],
        out_shape=[
            shape((LINE, width, width), BF),
            shape((LINE, width, hidden), BF),
            shape((LINE, width, hidden), BF),
            shape((rows, width), BF),
            shape((rows, width), F32),
            shape((width, keyed), BF),
            shape((width, rows), BF),
            shape((LINE, heads, keyed, rows), BF),
            shape((LINE, keyed, local), BF),
            shape((LINE, keyed, local), BF),
            shape((LINE, rows, local), BF),
            shape((LINE, local, rows), BF),
            shape((LINE, rows, hidden), BF),
            shape((LINE, rows, hidden), BF),
            shape((LINE, 16, width), F32),
            shape((NB, NB), F32),
            shape((NB, width), BF),
            shape((8, slots), F32),
        ],
        scratch_shapes=[
            pltpu.VMEM((keyed, width), BF),
            pltpu.VMEM((rows, width), BF),
            pltpu.VMEM((16, width), BF),
            pltpu.VMEM((part, width), BF),
            pltpu.VMEM((rows, width), BF),
            pltpu.VMEM((rows, width), F32),
            pltpu.VMEM((NB, local), F32),
            pltpu.VMEM((samples, local), BF),
            pltpu.VMEM((1, PLANE * samples, local), BF),
            pltpu.VMEM((PLANE, samples, NB), F32),
            pltpu.VMEM((1, PLANE * 8, slots), F32),
            pltpu.VMEM((LINE, PLANE * 16, width), BF),
            pltpu.VMEM((NB, local), BF),
            pltpu.VMEM((LINE, NB, local), BF),
            pltpu.VMEM((2, 2, width, width), BF),
            pltpu.VMEM(past.shape, BF),
            dma((2, 5, 4)),
            dma((2, PLANE)),
            dma((2,)),
            dma((4, 5, LINE * 4)),
            dma((4, LINE * PLANE)),
            dma((4,)),
            dma((2, LINE)),
            dma((LINE,)),
            dma(()),
            dma((2, 2)),
        ],
        compiler_params=pltpu.CompilerParams(
            collective_id=1, has_side_effects=True, vmem_limit_bytes=BIG_VMEM
        ),
        name="forward_pass",
    )(tokens, past, positions, counts, stack, b_qv, b_up, w_qkv, w_out, up, down)


def plain_forward_kernel(
    tok_ref,
    coef_ref,
    vec_ref,
    wa_ref,
    wu_ref,
    wd_ref,
    out_ref,
    res_ref,
    hm_ref,
    h2_ref,
    prob_ref,
    key_ref,
    val_ref,
    query_ref,
    att_ref,
    act_ref,
    slope_ref,
    acc_ref,
    *,
    groups,
    head,
):
    step = pl.program_id(0)
    rows, width = tok_ref.shape
    local = query_ref.shape[2]

    @pl.when(step == 0)
    def _():
        gain, bias = vec_ref[0, 0:1, :], vec_ref[0, 1:2, :]
        normed, _ = norm_parts(coef_ref[...].astype(F32))
        hm_ref[0:NB, :] = (normed * gain + bias).astype(BF)
        normed, _ = norm_parts(tok_ref[...].astype(F32))
        hm_ref[NB:, :] = (normed * gain + bias).astype(BF)
        acc_ref[...] = jnp.zeros_like(acc_ref)

    @pl.when(step < groups)
    def _():
        weights = wa_ref[0]
        projected = project(hm_ref[...], weights, vec_ref[step, 6:7, :], local)
        query = projected[NB:, :local]
        keys = projected[:, local : 2 * local]
        values = projected[:, 2 * local :]
        query_ref[0] = query
        key_ref[0] = keys
        val_ref[0] = values

        def store(h, lines, columns, probs):
            prob_ref[0, h, lines, columns] = probs

        attended = attend(query, keys, values, head, store, lambda h: None)
        att_ref[0] = attended
        acc_ref[...] += dot_nt(attended.T, weights[:, 3 * local :])

    @pl.when(step == groups)
    def _():
        residual = tok_ref[...].astype(F32) + acc_ref[...] + vec_ref[0, 4:5, :]
        res_ref[...] = residual
        normed, _ = norm_parts(residual)
        h2_ref[...] = (normed * vec_ref[0, 2:3, :] + vec_ref[0, 3:4, :]).astype(BF)
        acc_ref[...] = jnp.zeros_like(acc_ref)

    @pl.when(step >= groups)
    def _():
        pre = dot(h2_ref[...], wu_ref[0]) + vec_ref[step - groups, 7:8, :]
        act, slope = gelu_parts(pre)
        act_ref[0] = act
        slope_ref[0] = slope.astype(BF)
        acc_ref[...] += dot_nt(act, wd_ref[0])

    @pl.when(step == 2 * groups - 1)
    def _():
        out_ref[...] = (res_ref[...] + acc_ref[...] + vec_ref[0, 5:6, :]).astype(BF)


def plain_forward(tok, coef, vec, wide, head):
    rows, width = tok.shape
    groups = wide[0].shape[0]
    local = width // groups
    hidden = wide[1].shape[2]
    heads = local // head
    keyed = NB + rows
    first = lambda i: jnp.minimum(i, groups - 1)
    second = lambda i: jnp.maximum(i - groups, 0)
    whole = lambda shape: pl.BlockSpec(shape, lambda i: (0,) * len(shape))
    shape = jax.ShapeDtypeStruct
    return pl.pallas_call(
        functools.partial(plain_forward_kernel, groups=groups, head=head),
        grid=(2 * groups,),
        in_specs=[
            whole((rows, width)),
            whole((NB, width)),
            whole((groups, 16, width)),
            pl.BlockSpec((1, width, width), lambda i: (first(i), 0, 0)),
            pl.BlockSpec((1, width, hidden), lambda i: (second(i), 0, 0)),
            pl.BlockSpec((1, width, hidden), lambda i: (second(i), 0, 0)),
        ],
        out_specs=[
            whole((rows, width)),
            whole((rows, width)),
            whole((keyed, width)),
            whole((rows, width)),
            pl.BlockSpec((1, heads, keyed, rows), lambda i: (first(i), 0, 0, 0)),
            pl.BlockSpec((1, keyed, local), lambda i: (first(i), 0, 0)),
            pl.BlockSpec((1, keyed, local), lambda i: (first(i), 0, 0)),
            pl.BlockSpec((1, rows, local), lambda i: (first(i), 0, 0)),
            pl.BlockSpec((1, local, rows), lambda i: (first(i), 0, 0)),
            pl.BlockSpec((1, rows, hidden), lambda i: (second(i), 0, 0)),
            pl.BlockSpec((1, rows, hidden), lambda i: (second(i), 0, 0)),
        ],
        out_shape=[
            shape((rows, width), BF),
            shape((rows, width), F32),
            shape((keyed, width), BF),
            shape((rows, width), BF),
            shape((groups, heads, keyed, rows), BF),
            shape((groups, keyed, local), BF),
            shape((groups, keyed, local), BF),
            shape((groups, rows, local), BF),
            shape((groups, local, rows), BF),
            shape((groups, rows, hidden), BF),
            shape((groups, rows, hidden), BF),
        ],
        scratch_shapes=[pltpu.VMEM((rows, width), F32)],
        compiler_params=pltpu.CompilerParams(vmem_limit_bytes=BIG_VMEM),
        name="plain_forward",
    )(tok, coef, vec, *wide)


def attend_back(g_att, att_t, keys, values, query, probs_of, head, between):
    rows, local = g_att.shape
    half = rows // 2
    low = NB + rows - half
    g_att_t = g_att.T
    product = g_att_t.astype(F32) * att_t.astype(F32)
    key_t = keys.T
    scale = 1.0 / math.sqrt(head)
    line = lax.broadcasted_iota(jnp.int32, (local, rows), 0)
    lane = lax.broadcasted_iota(jnp.int32, (rows, local), 1)
    key_grad = [jnp.zeros((low, local), F32), jnp.zeros((half, local), F32)]
    val_grad = [jnp.zeros((low, local), F32), jnp.zeros((half, local), F32)]
    query_grads = []
    for h in range(local // head):
        own_t = (line >= h * head) & (line < (h + 1) * head)
        own = (lane >= h * head) & (lane < (h + 1) * head)
        grad_t = jnp.where(own_t, g_att_t, BF(0.0))
        grad_h = jnp.where(own, g_att, BF(0.0))
        query_h = jnp.where(own, query, BF(0.0))
        inner = jnp.sum(product[h * head : (h + 1) * head, :], axis=0, keepdims=True)
        key_h = key_t[h * head : (h + 1) * head, :]
        parts = []
        for b in range(2):
            span = NB + (b + 1) * half
            cols = slice(b * half, (b + 1) * half)
            probs = probs_of(h, slice(0, span), cols)
            dprob = dot(values[:span, :], grad_t[:, cols])
            dscore = (probs.astype(F32) * (dprob - inner[:, cols])).astype(BF)
            parts.append(dot(key_h[:, :span], dscore))
            val_part = dot(probs, grad_h[cols, :])
            key_part = dot(dscore, query_h[cols, :])
            val_grad[0] = val_grad[0] + val_part[:low, :]
            key_grad[0] = key_grad[0] + key_part[:low, :]
            if b == 1:
                val_grad[1] = val_grad[1] + val_part[low:, :]
                key_grad[1] = key_grad[1] + key_part[low:, :]
        query_grads.append(jnp.concatenate(parts, axis=1))
        between(h)
    query_grad = (jnp.concatenate(query_grads, axis=0) * scale).astype(BF).T
    key_grad = jnp.concatenate(key_grad, axis=0) * scale
    return query_grad, key_grad, jnp.concatenate(val_grad, axis=0)


def backward_kernel(
    tokens_ref,
    cots_ref,
    fwd_out_ref,
    res_ref,
    wa_ref,
    wu_ref,
    wd_ref,
    vec_ref,
    hmt_ref,
    h2t_ref,
    coef_ref,
    inv_ref,
    meta_ref,
    prob_ref,
    key_ref,
    val_ref,
    query_ref,
    att_ref,
    act_ref,
    slope_ref,
    outs_ref,
    tgs_ref,
    past_ref,
    vectors_ref,
    bias_ref,
    bias_up_ref,
    qkv_out_ref,
    wo_out_ref,
    up_out_ref,
    down_out_ref,
    *scratch,
    head,
):
    (
        tok_ref,
        cot_ref,
        cott_ref,
        gres_ref,
        acc_ref,
        proj_ref,
        gv_ref,
        ggv_ref,
        gmem_ref,
        wide_ref,
        side_ref,
        attn_ref,
        mlp_ref,
        gv_mem_ref,
        side_out_ref,
        attn_out_ref,
        mlp_out_ref,
    ) = scratch[:17]
    buffers = scratch[17:32]
    block_sems, sems, lsend, lrecv, lown, gsend, grecv, gown, load_sem = scratch[32:]
    step = pl.program_id(0)
    rows, width = tok_ref.shape
    local = query_ref.shape[2]
    items = past_ref.shape[0]
    place = Place()
    side, attn, mlp = [
        kind(place, grads, out, buffers[i::3], (block_sems.at[i], sems.at[i]))
        for i, (kind, grads, out) in enumerate(
            (
                (DirectCollect, side_ref, side_out_ref),
                (Collect, attn_ref, attn_out_ref),
                (Collect, mlp_ref, mlp_out_ref),
            )
        )
    ]
    outs, tgs = [
        [
            Line(
                place,
                src.at[pl.ds(h * (rows // count), rows // count), :],
                dst.at[:, pl.ds(h * (rows // count), rows // count), :],
                lsend.at[first + h],
                lrecv.at[first + h],
                lown.at[first + h],
            )
            for h in range(count)
        ]
        for src, dst, first, count in (
            (fwd_out_ref, outs_ref, 0, OUT_PIECES),
            (cot_ref, tgs_ref, OUT_PIECES, GRAD_PIECES),
        )
    ]
    mem = DirectSpread(place, side_out_ref.at[0, 0:8, :], gmem_ref, gsend, grecv, gown)
    mine = pl.ds(place.z * rows, rows)

    def load(ref, m, slot, which):
        return pltpu.make_async_copy(ref.at[m], wide_ref.at[slot, which], load_sem.at[slot, which])

    def bring(i, src, dst):
        return pltpu.make_async_copy(src, dst, load_sem.at[2, i])

    bring_cot = bring(0, cots_ref.at[mine, :], cot_ref)
    bring_tok = bring(1, tokens_ref.at[mine, :], tok_ref)
    bring_res = pltpu.make_async_copy(res_ref, gres_ref, load_sem.at[3, 0])

    def past():
        mem.own.wait()
        for m in range(LINE):
            mem.close(m)
        gmem = jnp.concatenate([gmem_ref[m] for m in range(LINE)], axis=0)
        give_past(gmem, coef_ref, vec_ref, inv_ref, meta_ref, past_ref, gv_mem_ref)
        own = side_out_ref[0, 8:16, :]
        own = jnp.concatenate([own[0:2] + gv_mem_ref[0:2, :], own[2:8]], axis=0)
        vectors, biases, bias_up = small_pieces(
            own, place.s, vectors_ref.shape[1], bias_ref.shape[2], head, bias_ref.shape[0]
        )
        vectors_ref[...] = vectors
        for h, bias in enumerate(biases):
            bias_ref[h] = bias
        bias_up_ref[...] = bias_up

    def give_attn():
        attn.result()
        for i in range(3):
            qkv_out_ref[i] = attn_out_ref[0, :, i * local : (i + 1) * local]
        row, lane = iotas((attn_out_ref.shape[1], attn_out_ref.shape[1]))
        unit = (row == lane).astype(F32)
        wo_out_ref[...] = dot_tn(attn_out_ref[0, :, 3 * local :], unit, HIGHEST)

    def give_mlp():
        mlp.result()
        up_out_ref[...] = mlp_out_ref[0]
        down_out_ref[...] = mlp_out_ref[1]

    def move(what, kind, i):
        if what == 1 and kind == 4:
            return [give_attn]
        if what == 2 and kind == 4:
            return [give_mlp]
        if what < 3:
            return [(side, attn, mlp)[what].part(kind, i)]
        if what == 3:
            return mem.steps(kind) if kind else [mem.first]
        if what == 4:
            return [past]
        line = (outs + tgs)[what - 5]
        return [functools.partial(line.step, i) if kind else line.first]

    plan = [[one for what in moves for one in move(*what)] for moves in BACKWARD_PLAN]

    def transfers(slot, condition=None):
        def go():
            for one in plan[slot]:
                one()

        if plan[slot]:
            when((condition,), go)

    @pl.when(step == 0)
    def _():
        bring_cot.start()
        bring_tok.start()
        bring_res.start()
        load(wu_ref, 0, 0, 0).start()
        load(wd_ref, 0, 0, 1).start()
        greet(place, whole_line=True)
        for line in outs:
            line.first()
        acc_ref[...] = jnp.zeros_like(acc_ref)
        gv_ref[...] = jnp.zeros_like(gv_ref)
        bring_cot.wait()
        bring_tok.wait()
        bring_res.wait()
        cott_ref[...] = cot_ref[...].T

    @pl.when(step < LINE)
    def _():
        m = step
        slot = lax.rem(m, 2)
        load(wu_ref, m, slot, 0).wait()
        load(wd_ref, m, slot, 1).wait()

        @pl.when(m < LINE - 1)
        def _():
            load(wu_ref, m + 1, 1 - slot, 0).start()
            load(wd_ref, m + 1, 1 - slot, 1).start()

        @pl.when(m == LINE - 1)
        def _():
            load(wa_ref, 0, 0, 0).start()

        upstream = cot_ref[...]
        grad = (dot(upstream, wide_ref[slot, 1]) * slope_ref[0].astype(F32)).astype(BF)
        mlp_ref[m, 1] = dot(cott_ref[...], act_ref[0]).astype(BF)
        mlp_ref[m, 0] = dot(h2t_ref[...], grad).astype(BF)
        mlp.begin(m)
        for at in range(LINE):
            transfers(at, step == at)
        ggv_ref[m, 1:2, :] = col_sum(grad.astype(F32))
        acc_ref[NB:, :] += dot_nt(grad, wide_ref[slot, 0])

    @pl.when(step == LINE)
    def _():
        transfers(LINE)
        upstream = cot_ref[...].astype(F32)
        normed, inverse = norm_parts(gres_ref[...])
        grad = acc_ref[NB:, :]
        g_res = upstream + norm_back(grad, normed, inverse, vec_ref[0, 2:3, :])
        gres_ref[...] = g_res
        g_attn = g_res.astype(BF)
        gv_ref[2:3, :] = col_sum(grad * normed)
        gv_ref[3:4, :] = col_sum(grad)
        gv_ref[4:5, :] = col_sum(g_attn.astype(F32))
        gv_ref[5:6, :] = col_sum(upstream)
        cott_ref[...] = g_attn.T
        acc_ref[...] = jnp.zeros_like(acc_ref)
        proj_ref[0:NB, :] = jnp.zeros((NB, proj_ref.shape[1]), BF)
        transfers(LINE + 1)

    @pl.when(step >= LINE)
    def _():
        m = step - LINE
        slot = lax.rem(m, 2)
        load(wa_ref, m, slot, 0).wait()

        @pl.when(m < LINE - 1)
        def _():
            load(wa_ref, m + 1, 1 - slot, 0).start()

        def between(h):
            for at in range(LINE):
                transfers(LINE + 2 + 4 * at + h, m == at)

        def probs_of(h, lines, columns):
            return prob_ref[0, h, lines, columns]

        g_attn = gres_ref[...].astype(BF)
        g_att = dot(g_attn, wide_ref[slot, 0, :, 3 * local :]).astype(BF)
        att_t = att_ref[0]
        query_grad, key_grad, val_grad = attend_back(
            g_att, att_t, key_ref[0], val_ref[0], query_ref[0], probs_of, head, between
        )
        proj_ref[NB:, 0:local] = query_grad
        proj_ref[:, local : 2 * local] = key_grad.astype(BF)
        proj_ref[:, 2 * local :] = val_grad.astype(BF)
        proj = proj_ref[...]
        ggv_ref[m, 0:1, 0 : 3 * local] = col_sum(proj.astype(F32))
        ggv_ref[m, 0:1, 3 * local :] = jnp.zeros((1, width - 3 * local), F32)
        attn_ref[m, 0, :, 0 : 3 * local] = dot(hmt_ref[...], proj).astype(BF)
        attn_ref[m, 0, :, 3 * local :] = dot_nt(cott_ref[...], att_t).astype(BF)
        attn.begin(m)
        acc_ref[...] += dot_nt(proj, wide_ref[slot, 0, :, : 3 * local])
        between(3)

    @pl.when(step == 2 * LINE - 1)
    def _():
        grad = acc_ref[NB:, :]
        normed, inverse = norm_parts(tok_ref[...].astype(F32))
        back = norm_back(grad, normed, inverse, vec_ref[0, 0:1, :])
        cot_ref[...] = (gres_ref[...] + back).astype(BF)
        tgs[0].first()
        gv_ref[0:1, :] = col_sum(grad * normed)
        gv_ref[1:2, :] = col_sum(grad)
        transfers(5 * LINE + 2)
        for m in range(LINE):
            below = jnp.concatenate([gv_ref[0:6, :], ggv_ref[m, 0:2, :]], axis=0)
            for s in range(PLANE):
                top = (m * PLANE + s) * 8
                side_ref[m, 0, s * 16 : s * 16 + 8, :] = acc_ref[top : top + 8, :]
                side_ref[m, 0, s * 16 + 8 : (s + 1) * 16, :] = below
            side.begin(m)
        transfers(5 * LINE + 3)
        mem.settle()
        for part in (side, attn, mlp):
            part.settle()
        for line in outs + tgs:
            line.finish()


OUT_PIECES, GRAD_PIECES = 2, 4

BACKWARD_PLAN = (
    (),
    (),
    (),
    (),
    ((5, 1, 1),),
    (),
    ((2, 0, 1),),
    ((6, 1, 1),),
    (),
    ((2, 0, 0),),
    ((2, 1, 0),),
    (),
    ((2, 0, 3),),
    ((5, 1, 2),),
    (),
    ((2, 2, 0),),
    ((1, 0, 1),),
    ((2, 0, 2), (6, 1, 2),),
    (),
    (),
    ((1, 0, 0),),
    (),
    ((8, 0, 0), (1, 0, 3), (1, 0, 2), (9, 0, 0), (10, 0, 0),),
    ((0, 0, 0), (0, 0, 1), (0, 0, 2), (0, 0, 3), (0, 1, 2), (1, 1, 2), (0, 1, 3), (1, 2, 2), (0, 2, 3), (0, 1, 1), (0, 2, 1), (0, 2, 2), (0, 1, 0), (0, 2, 0), (8, 1, 1), (1, 1, 1), (1, 2, 1), (0, 3, 1), (1, 1, 0), (1, 2, 0), (2, 1, 1), (2, 2, 1), (0, 3, 3), (0, 3, 2), (2, 1, 3), (2, 2, 3), (0, 3, 0), (2, 1, 2), (2, 2, 2), (7, 1, 1), (0, 4, 0), (3, 0, 0), (6, 1, 3), (10, 1, 1), (9, 1, 1), (5, 1, 3), (8, 1, 2), (1, 1, 3), (1, 2, 3), (2, 3, 0), (1, 3, 2), (3, 1, 0), (10, 1, 2), (1, 3, 0), (2, 3, 1), (7, 1, 2), (9, 1, 2), (2, 3, 3), (3, 2, 0), (3, 3, 0), (1, 3, 3), (2, 3, 2), (1, 3, 1), (4, 0, 0), (7, 1, 3), (8, 1, 3), (9, 1, 3), (10, 1, 3), (2, 4, 0), (1, 4, 0),),
)


def backward_pass(tokens, cots, out, meta, vec, inverse, coef, saved, wide, items, past_shape, head):
    res, hmt, h2t, prob, keys, vals, query, att, act, slope = saved
    rows, width = out.shape
    local = width // LINE
    hidden = wide[1].shape[2]
    heads = local // head
    keyed = NB + rows
    first = lambda i: jnp.minimum(i, LINE - 1)
    second = lambda i: jnp.maximum(i - LINE, 0)
    anywhere = pl.BlockSpec(memory_space=pl.ANY)
    vmem = pl.BlockSpec(memory_space=pltpu.VMEM)
    dma = pltpu.SemaphoreType.DMA
    shape = jax.ShapeDtypeStruct
    part = width // PLANE
    blocks = ((1, 16, width), (1, part, width), (2, part, width))
    kinds = (F32, BF, BF)
    pieces = OUT_PIECES + GRAD_PIECES
    return pl.pallas_call(
        functools.partial(backward_kernel, head=head),
        grid=(2 * LINE,),
        in_specs=[anywhere] * 7
        + [vmem] * 6
        + [
            pl.BlockSpec((1, heads, keyed, rows), lambda i: (second(i), 0, 0, 0)),
            pl.BlockSpec((1, keyed, local), lambda i: (second(i), 0, 0)),
            pl.BlockSpec((1, keyed, local), lambda i: (second(i), 0, 0)),
            pl.BlockSpec((1, rows, local), lambda i: (second(i), 0, 0)),
            pl.BlockSpec((1, local, rows), lambda i: (second(i), 0, 0)),
            pl.BlockSpec((1, rows, hidden), lambda i: (first(i), 0, 0)),
            pl.BlockSpec((1, rows, hidden), lambda i: (first(i), 0, 0)),
        ],
        out_specs=[anywhere, anywhere] + [vmem] * 8,
        out_shape=[
            shape((LINE, rows, width), BF),
            shape((LINE, rows, width), BF),
            shape(past_shape, F32),
            shape((8, part), F32),
            shape((local // head, 2, head // PLANE), F32),
            shape((head // PLANE, hidden // head), F32),
            shape((3, part, local), F32),
            shape((local, part), F32),
            shape((part, hidden), F32),
            shape((part, hidden), F32),
        ],
        scratch_shapes=[
            pltpu.VMEM((rows, width), BF),
            pltpu.VMEM((rows, width), BF),
            pltpu.VMEM((width, rows), BF),
            pltpu.VMEM((rows, width), F32),
            pltpu.VMEM((keyed, width), F32),
            pltpu.VMEM((keyed, 3 * local), BF),
            pltpu.VMEM((8, width), F32),
            pltpu.VMEM((LINE, 8, hidden), F32),
            pltpu.VMEM((LINE, PLANE * 8, width), F32),
            pltpu.VMEM((2, 2, width, width), BF),
        ]
        + [pltpu.VMEM((LINE, b[0], PLANE * b[1], b[2]), t) for b, t in zip(blocks, kinds)]
        + [pltpu.VMEM((8, width), F32)]
        + [pltpu.VMEM(b, F32) for b in blocks]
        + [pltpu.VMEM(lead + b, t) for lead in BUFFERS for b, t in zip(blocks, kinds)]
        + [
            dma((3, 2, 4, LINE)),
            dma((3, 9, LINE)),
            dma((pieces, 2, LINE)),
            dma((pieces, LINE)),
            dma((pieces,)),
            dma((5, LINE * 4)),
            dma((LINE * PLANE,)),
            dma(()),
            dma((4, 2)),
        ],
        compiler_params=pltpu.CompilerParams(
            collective_id=2, has_side_effects=True, vmem_limit_bytes=MAX_VMEM
        ),
        name="backward_pass",
    )(
        tokens,
        cots,
        out,
        res,
        *wide,
        vec,
        hmt,
        h2t,
        coef,
        inverse,
        meta,
        prob,
        keys,
        vals,
        query,
        att,
        act,
        slope,
    )


def plain_backward_kernel(
    tok_ref,
    cot_ref,
    res_ref,
    vec_ref,
    hm_ref,
    h2_ref,
    prob_ref,
    key_ref,
    val_ref,
    query_ref,
    att_ref,
    act_ref,
    slope_ref,
    wa_ref,
    wu_ref,
    wd_ref,
    tg_ref,
    gmem_ref,
    gup_ref,
    gdown_ref,
    gatt_ref,
    gv_ref,
    ggv_ref,
    acc_ref,
    hmt_ref,
    h2t_ref,
    cott_ref,
    gres_ref,
    proj_ref,
    *,
    groups,
    head,
):
    step = pl.program_id(0)
    rows, width = tok_ref.shape
    local = query_ref.shape[2]

    @pl.when(step == 0)
    def _():
        acc_ref[...] = jnp.zeros_like(acc_ref)
        h2t_ref[...] = h2_ref[...].T
        cott_ref[...] = cot_ref[...].T
        gv_ref[...] = jnp.zeros_like(gv_ref)

    @pl.when(step < groups)
    def _():
        upstream = cot_ref[...]
        grad = (dot(upstream, wd_ref[0]) * slope_ref[0].astype(F32)).astype(BF)
        gdown_ref[0] = dot(cott_ref[...], act_ref[0]).astype(BF)
        gup_ref[0] = dot(h2t_ref[...], grad).astype(BF)
        ggv_ref[0] = jnp.zeros_like(ggv_ref[0])
        ggv_ref[0, 0:1, :] = col_sum(grad.astype(F32))
        acc_ref[NB:, :] += dot_nt(grad, wu_ref[0])

    @pl.when(step == groups)
    def _():
        upstream = cot_ref[...].astype(F32)
        normed, inverse = norm_parts(res_ref[...])
        grad = acc_ref[NB:, :]
        g_res = upstream + norm_back(grad, normed, inverse, vec_ref[2:3, :])
        gres_ref[...] = g_res
        g_attn = g_res.astype(BF)
        gv_ref[2:3, :] = col_sum(grad * normed)
        gv_ref[3:4, :] = col_sum(grad)
        gv_ref[4:5, :] = col_sum(g_attn.astype(F32))
        gv_ref[5:6, :] = col_sum(upstream)
        cott_ref[...] = g_attn.T
        hmt_ref[...] = hm_ref[...].T
        acc_ref[...] = jnp.zeros_like(acc_ref)
        proj_ref[0:NB, :] = jnp.zeros((NB, proj_ref.shape[1]), BF)

    @pl.when(step >= groups)
    def _():
        weights = wa_ref[0]
        g_attn = gres_ref[...].astype(BF)
        g_att = dot(g_attn, weights[:, 3 * local :]).astype(BF)
        att_t = att_ref[0]
        query_grad, key_grad, val_grad = attend_back(
            g_att,
            att_t,
            key_ref[0],
            val_ref[0],
            query_ref[0],
            lambda h, lines, columns: prob_ref[0, h, lines, columns],
            head,
            lambda h: None,
        )
        key_grad, val_grad = key_grad.astype(BF), val_grad.astype(BF)
        proj_ref[NB:, 0:local] = query_grad
        proj_ref[:, local : 2 * local] = key_grad
        proj_ref[:, 2 * local :] = val_grad
        proj = proj_ref[...]
        ggv_ref[0] = jnp.zeros_like(ggv_ref[0])
        ggv_ref[0, 0:1, 0 : 3 * local] = col_sum(proj.astype(F32))
        gatt_ref[0, :, 0 : 3 * local] = dot(hmt_ref[...], proj).astype(BF)
        gatt_ref[0, :, 3 * local :] = dot_nt(cott_ref[...], att_t).astype(BF)
        acc_ref[...] += dot_nt(proj, weights[:, : 3 * local])

    @pl.when(step == 2 * groups - 1)
    def _():
        gmem_ref[...] = acc_ref[0:NB, :]
        grad = acc_ref[NB:, :]
        normed, inverse = norm_parts(tok_ref[...].astype(F32))
        part = norm_back(grad, normed, inverse, vec_ref[0:1, :])
        tg_ref[...] = (gres_ref[...] + part).astype(BF)
        gv_ref[0:1, :] = col_sum(grad * normed)
        gv_ref[1:2, :] = col_sum(grad)


def plain_backward(tok, cot, vec, saved, wide, head):
    res, hm, h2, prob, keys, vals, query, att, act, slope = saved
    rows, width = tok.shape
    groups = wide[0].shape[0]
    local = width // groups
    hidden = wide[1].shape[2]
    heads = local // head
    keyed = NB + rows
    first = lambda i: jnp.minimum(i, groups - 1)
    second = lambda i: jnp.maximum(i - groups, 0)
    whole = lambda shape: pl.BlockSpec(shape, lambda i: (0,) * len(shape))
    return pl.pallas_call(
        functools.partial(plain_backward_kernel, groups=groups, head=head),
        grid=(2 * groups,),
        in_specs=[
            whole((rows, width)),
            whole((rows, width)),
            whole((rows, width)),
            whole((16, width)),
            whole((keyed, width)),
            whole((rows, width)),
            pl.BlockSpec((1, heads, keyed, rows), lambda i: (second(i), 0, 0, 0)),
            pl.BlockSpec((1, keyed, local), lambda i: (second(i), 0, 0)),
            pl.BlockSpec((1, keyed, local), lambda i: (second(i), 0, 0)),
            pl.BlockSpec((1, rows, local), lambda i: (second(i), 0, 0)),
            pl.BlockSpec((1, local, rows), lambda i: (second(i), 0, 0)),
            pl.BlockSpec((1, rows, hidden), lambda i: (first(i), 0, 0)),
            pl.BlockSpec((1, rows, hidden), lambda i: (first(i), 0, 0)),
            pl.BlockSpec((1, width, width), lambda i: (second(i), 0, 0)),
            pl.BlockSpec((1, width, hidden), lambda i: (first(i), 0, 0)),
            pl.BlockSpec((1, width, hidden), lambda i: (first(i), 0, 0)),
        ],
        out_specs=[
            whole((rows, width)),
            whole((NB, width)),
            pl.BlockSpec((1, width, hidden), lambda i: (first(i), 0, 0)),
            pl.BlockSpec((1, width, hidden), lambda i: (first(i), 0, 0)),
            pl.BlockSpec((1, width, width), lambda i: (second(i), 0, 0)),
            whole((8, width)),
            pl.BlockSpec((1, 8, hidden), lambda i: (i, 0, 0)),
        ],
        out_shape=[
            jax.ShapeDtypeStruct((rows, width), BF),
            jax.ShapeDtypeStruct((NB, width), F32),
            jax.ShapeDtypeStruct((groups, width, hidden), BF),
            jax.ShapeDtypeStruct((groups, width, hidden), BF),
            jax.ShapeDtypeStruct((groups, width, width), BF),
            jax.ShapeDtypeStruct((8, width), F32),
            jax.ShapeDtypeStruct((2 * groups, 8, hidden), F32),
        ],
        scratch_shapes=[
            pltpu.VMEM((keyed, width), F32),
            pltpu.VMEM((width, keyed), BF),
            pltpu.VMEM((width, rows), BF),
            pltpu.VMEM((width, rows), BF),
            pltpu.VMEM((rows, width), F32),
            pltpu.VMEM((keyed, 3 * local), BF),
        ],
        compiler_params=pltpu.CompilerParams(vmem_limit_bytes=BIG_VMEM),
        name="plain_backward",
    )(
        tok, cot, res, vec, hm, h2, prob, keys, vals, query, att, act, slope, *wide
    )


def local(
    tokens,
    cotangent,
    past_state,
    positions,
    counts,
    ln1_gain,
    ln1_bias,
    w_qkv,
    b_qv,
    w_out,
    b_out,
    ln2_gain,
    ln2_bias,
    w_up,
    b_up,
    w_down,
    b_down,
):
    seq, mp = lax.axis_size("seq"), lax.axis_size("mp")
    seq_index, mp_index = lax.axis_index("seq"), lax.axis_index("mp")
    item_count, seg_len, local_width = past_state.shape
    slots = positions.shape[1]
    total = item_count * seq
    width = tokens.shape[1]
    part = width // seq
    heads_local, piece = b_qv.shape[1], b_qv.shape[2]
    head = piece * seq
    hidden = w_up.shape[1]
    rows = tokens.shape[0] // mp
    direct = seq == PLANE and mp == LINE and part % 16 == 0 and hidden == width

    past_t = past_state.transpose(0, 2, 1)

    vectors = jnp.stack([ln1_gain, ln1_bias, ln2_gain, ln2_bias, b_out, b_down])
    if direct:
        results = forward_pass(
            tokens,
            past_t,
            positions,
            counts,
            vectors,
            b_qv.transpose(1, 0, 2),
            b_up.T,
            w_qkv,
            w_out,
            w_up,
            w_down.T,
            head,
        )
        wide, forward, (vec, inverse, coef, meta) = results[:3], results[3:14], results[14:]
        block_out, block_grad, past_grad, vec_own, bias, bias_up, qkv_grad, out_grad, *mlp = (
            backward_pass(
                tokens,
                cotangent,
                forward[0],
                meta,
                vec,
                inverse,
                coef,
                forward[1:],
                wide,
                item_count,
                past_t.shape,
                head,
            )
        )
        block_out = block_out.reshape(mp * rows, width)
        block_grad = block_grad.reshape(mp * rows, width)
        qv, up, (up_grad, down_grad) = bias.transpose(1, 0, 2), bias_up.T, mlp
    else:
        items = (seq_index * item_count + jnp.arange(item_count)).astype(F32)
        spots = positions.astype(F32)
        places = (items[:, None] + (spots + 0.5) / seg_len) / total
        used = (jnp.arange(slots)[None, :] < counts[:, None]).astype(F32)
        meta = jnp.concatenate([places, used, spots, jnp.zeros((8 - 3 * item_count, slots), F32)])

        here = (jnp.arange(seq) == seq_index).astype(BF)
        vectors = (vectors[:, None, :] * here[None, :, None]).reshape(6, width)
        bias_qv = (b_qv[:, :, None, :] * here[None, None, :, None]).reshape(2, local_width)
        bias_qv = jnp.concatenate([bias_qv, jnp.zeros((2, local_width), BF)], axis=1)
        bias_up = (b_up[:, None, :] * here[None, :, None]).reshape(1, hidden)
        room = jnp.concatenate(
            [vectors, bias_qv.reshape(1, width), bias_up, jnp.zeros((8, width), BF)]
        )
        attn = jnp.concatenate([w_qkv[0], w_qkv[1], w_qkv[2], w_out.T], axis=1)
        sampled = sample_rows(past_t, meta)
        all_sampled = lax.all_gather(sampled, "seq", axis=0)
        all_meta = lax.all_gather(meta, "seq", axis=0)
        coef_part, inverse = solve_memory(all_sampled, all_meta, item_count)
        coef = lax.all_gather(coef_part, "mp", axis=0).transpose(1, 0, 2).reshape(NB, width)
        wide = [
            lax.all_gather(lax.all_gather(shard, "seq", axis=0, tiled=True), "mp", axis=0)
            for shard in (attn, w_up, w_down.T)
        ]
        vec = lax.psum(room.astype(F32), "seq")
        vec = lax.all_gather(vec, "mp", axis=0)
        tok = lax.dynamic_slice_in_dim(tokens, mp_index * rows, rows, 0)
        cot = lax.dynamic_slice_in_dim(cotangent, mp_index * rows, rows, 0)
        forward = plain_forward(tok, coef, vec, wide, head)
        block_out = lax.all_gather(forward[0], "mp", axis=0, tiled=True)
        tok_grad, gmem, g_up, g_down, g_attn, gv, ggv = plain_backward(
            tok, cot, vec[0], forward[1:], wide, head
        )
        tail = jnp.concatenate(
            [jnp.broadcast_to(gv[None, :6], (mp, 6, width)), ggv[mp:, :1], ggv[:mp, :1]], axis=1
        )
        block_grad = lax.all_gather(tok_grad, "mp", axis=0, tiled=True)
        gmem, tail = lax.psum((gmem, tail), ("seq", "mp"))
        own = lax.dynamic_index_in_dim(tail, mp_index, 0, keepdims=False)
        attn, up_grad, down_grad = (
            lax.psum_scatter(
                lax.psum_scatter(g, "mp", scatter_dimension=0, tiled=False),
                "seq",
                scatter_dimension=0,
                tiled=True,
            ).astype(F32)
            for g in (g_attn, g_up, g_down)
        )
        past_grad, gv_mem = past_grads(
            gmem, coef, vec, inverse, meta, item_count, seg_len, local_width
        )
        own = own + jnp.concatenate([gv_mem[:2], jnp.zeros((6, width), F32)])
        vec_own = lax.dynamic_slice_in_dim(own[:6], seq_index * part, part, 1)
        qv = jnp.stack([own[6, :local_width], own[6, 2 * local_width : 3 * local_width]])
        qv = qv.reshape(2, heads_local, head)
        qv = lax.dynamic_slice_in_dim(qv, seq_index * piece, piece, 2)
        up = lax.dynamic_slice_in_dim(own[7].reshape(-1, head), seq_index * piece, piece, 1)
        qkv_grad = jnp.stack([attn[:, i * local_width : (i + 1) * local_width] for i in range(3)])
        out_grad = attn[:, 3 * local_width :].T
    return (
        block_out,
        block_grad,
        past_grad.transpose(0, 2, 1),
        vec_own[0],
        vec_own[1],
        qkv_grad,
        qv,
        out_grad,
        vec_own[4],
        vec_own[2],
        vec_own[3],
        up_grad,
        up,
        down_grad.T,
        vec_own[5],
    )


def solution(mesh):
    row = P("seq", None)
    placed = (
        row,
        row,
        P("seq", None, "mp"),
        row,
        P("seq"),
        P("seq"),
        P("seq"),
        P(None, "seq", "mp"),
        P(None, "mp", "seq"),
        P("mp", "seq"),
        P("seq"),
        P("seq"),
        P("seq"),
        P("seq", "mp"),
        P("mp", "seq"),
        P("mp", "seq"),
        P("seq"),
    )
    return jax.shard_map(
        local,
        mesh=mesh,
        in_specs=placed,
        out_specs=(row, row, placed[2]) + placed[5:],
        check_vma=False,
    )
```

```python
import functools
import math

import jax
import jax.numpy as jnp
from jax import lax
from jax.experimental import pallas as pl
from jax.experimental.pallas import tpu as pltpu
from jax.sharding import PartitionSpec as P

NB = 256
PIVOTS = 32
NORM_EPSILON = 1e-05
RIDGE_WEIGHT = 1.0
NARROW_WIDTH = 0.01
BROAD_WIDTH = 0.05
GELU_SCALE = 0.7978845608028654
GELU_CUBIC = 0.044715

BF = jnp.bfloat16
F32 = jnp.float32
HIGHEST = lax.Precision.HIGHEST
BIG_VMEM = 60 * 1024 * 1024
MAX_VMEM = 67043328


def dot(a, b):
    return jnp.dot(a, b, preferred_element_type=F32)


def dot_nt(a, b):
    return lax.dot_general(a, b, (((1,), (1,)), ((), ())), preferred_element_type=F32)


def dot_tn(a, b, precision=None):
    return lax.dot_general(
        a, b, (((0,), (0,)), ((), ())), preferred_element_type=F32, precision=precision
    )


def norm_parts(values):
    centered = values - jnp.mean(values, axis=-1, keepdims=True)
    inverse = lax.rsqrt(jnp.mean(centered * centered, axis=-1, keepdims=True) + NORM_EPSILON)
    return centered * inverse, inverse


def norm_back(upstream, normed, inverse, gain):
    scaled = upstream * gain
    inner = scaled - jnp.mean(scaled, axis=-1, keepdims=True)
    inner = inner - normed * jnp.mean(scaled * normed, axis=-1, keepdims=True)
    return inner * inverse


def col_sum(values):
    return jnp.sum(values, axis=0, keepdims=True)


def basis_of(places, used):
    column = lax.broadcasted_iota(jnp.int32, (places.shape[0], NB), 1)
    centers = (column.astype(F32) + 0.5) / NB
    widths = jnp.where(column % 2 == 0, NARROW_WIDTH, BROAD_WIDTH).astype(F32)
    scaled = (places - centers) / widths
    return jnp.exp(-0.5 * (scaled * scaled)) * used


def meta_rows(positions, counts_ref, first, total, seg_len):
    items, slots = positions.shape
    slot = lax.broadcasted_iota(jnp.int32, (1, slots), 1)
    places, used, spots = [], [], []
    for i in range(items):
        spot = positions[i : i + 1, :].astype(F32)
        item = (first + i).astype(F32)
        places.append((item + (spot + 0.5) / seg_len) / total)
        used.append((slot < counts_ref[i]).astype(F32))
        spots.append(spot)
    return jnp.concatenate(
        places + used + spots + [jnp.zeros((8 - 3 * items, slots), F32)], axis=0
    )


def iotas(shape):
    return lax.broadcasted_iota(jnp.int32, shape, 0), lax.broadcasted_iota(jnp.int32, shape, 1)


def small_rows(stack, b_qv, b_up_t, s, width, head):
    part, piece = stack.shape[1], b_up_t.shape[0]
    row, lane = iotas((part, width))
    rows = [jnp.dot(stack, (lane == s * part + row).astype(F32), preferred_element_type=F32)]
    row, lane = iotas((piece, width))
    repeat = (lax.rem(lane, piece) == row).astype(F32)
    _, lane = iotas((1, width))
    half = width // 2
    bias = jnp.zeros((1, width), F32)
    for h in range(b_qv.shape[0]):
        spread = jnp.dot(b_qv[h], repeat, preferred_element_type=F32)
        for t in range(2):
            at = h * head + t * half + s * piece
            bias = bias + jnp.where((lane >= at) & (lane < at + piece), spread[t : t + 1], 0.0)
    row, lane = iotas((b_up_t.shape[1], width))
    spread = jnp.dot(b_up_t, (lane // head == row).astype(F32), preferred_element_type=F32)
    row, lane = iotas((piece, width))
    up = jnp.sum(jnp.where(lax.rem(lane, head) == s * piece + row, spread, 0.0), axis=0, keepdims=True)
    return jnp.concatenate(rows + [bias, up, jnp.zeros((8, width), F32)], axis=0).astype(BF)


def small_pieces(own, s, part, piece, head, heads):
    width = own.shape[1]
    half = width // 2
    row, lane = iotas((width, part + 2 * heads * piece))
    slot = lane - part
    spot = (slot // (2 * piece)) * head + (lax.rem(slot, 2 * piece) // piece) * half
    source = jnp.where(lane < part, s * part + lane, spot + s * piece + lax.rem(slot, piece))
    picked = jnp.dot(
        own, (row == source).astype(F32), preferred_element_type=F32, precision=HIGHEST
    )
    at = [part + i * piece for i in range(2 * heads)]
    flat = [picked[6:7, i : i + piece] for i in at]
    biases = [jnp.concatenate(flat[2 * h : 2 * h + 2], axis=0) for h in range(heads)]
    row, lane = iotas((piece, width))
    masked = jnp.where(lax.rem(lane, head) == s * piece + row, own[7:8], 0.0)
    row, lane = iotas((width, width // head))
    up = jnp.dot(
        masked, (row // head == lane).astype(F32), preferred_element_type=F32, precision=HIGHEST
    )
    return picked[:, :part], biases, up


def position_of(column, i, items):
    return column[:, 2 * items + i : 2 * items + i + 1].astype(jnp.int32)


def inverse_2(a, b, c, d):
    scale = 1.0 / (a * d - b * c)
    return d * scale, -(b * scale), -(c * scale), a * scale


def product_2(x, y):
    return (
        x[0] * y[0] + x[1] * y[2],
        x[0] * y[1] + x[1] * y[3],
        x[2] * y[0] + x[3] * y[2],
        x[2] * y[1] + x[3] * y[3],
    )


def invert_step(mat_ref):
    block = PIVOTS
    lane = lax.broadcasted_iota(jnp.int32, (block, NB), 1)
    line = lax.broadcasted_iota(jnp.int32, (block, NB), 0)
    panel = mat_ref[0:block, :]
    for k in range(0, block, 4):
        cols = [jnp.broadcast_to(panel[:, k + j : k + j + 1], panel.shape) for j in range(4)]
        at = [[cols[j][k + i : k + i + 1] for j in range(4)] for i in range(4)]
        head = inverse_2(at[0][0], at[0][1], at[1][0], at[1][1])
        upper = (at[0][2], at[0][3], at[1][2], at[1][3])
        lower = (at[2][0], at[2][1], at[3][0], at[3][1])
        right, left = product_2(head, upper), product_2(lower, head)
        minus = product_2(lower, right)
        tail = inverse_2(
            at[2][2] - minus[0], at[2][3] - minus[1], at[3][2] - minus[2], at[3][3] - minus[3]
        )
        rt, tl = product_2(right, tail), product_2(tail, left)
        back = product_2(rt, left)
        inverse = (
            (head[0] + back[0], head[1] + back[1], -rt[0], -rt[1]),
            (head[2] + back[2], head[3] + back[3], -rt[2], -rt[3]),
            (-tl[0], -tl[1], tail[0], tail[1]),
            (-tl[2], -tl[3], tail[2], tail[3]),
        )
        inside = (lane >= k) & (lane < k + 4)
        rows = [
            jnp.where(inside[0:1], (lane[0:1] == k + j).astype(F32), panel[k + j : k + j + 1])
            for j in range(4)
        ]
        new = [
            (m[0] * rows[0] + m[1] * rows[1]) + (m[2] * rows[2] + m[3] * rows[3]) for m in inverse
        ]
        rest = jnp.where(inside, 0.0, panel) - (
            (cols[0] * new[0] + cols[1] * new[1]) + (cols[2] * new[2] + cols[3] * new[3])
        )
        for i in range(4):
            rest = jnp.where(line == k + i, new[i], rest)
        panel = rest
    mat_ref[0:block, :] = panel
    row = lax.broadcasted_iota(jnp.int32, (NB, NB), 0)
    col = lax.broadcasted_iota(jnp.int32, (NB, NB), 1)
    mat = mat_ref[...]
    inside_row = row < block
    inside_col = col < block
    left = jnp.where(inside_col & ~inside_row, mat, 0.0)
    right = jnp.where(inside_row, mat, 0.0)
    update = jnp.dot(left, right, preferred_element_type=F32, precision=HIGHEST)
    mat = jnp.where(inside_row, mat, jnp.where(inside_col, 0.0, mat) - update)
    mat = pltpu.roll(mat, NB - block, 1)
    mat_ref[0 : NB - block, :] = mat[block:, :]
    mat_ref[NB - block :, :] = mat[:block, :]


def owner_basis(meta, items):
    column = meta.T
    rows = [
        basis_of(column[:, i : i + 1], column[:, items + i : items + i + 1]) for i in range(items)
    ]
    return jnp.concatenate(rows, axis=0)


def clear_moments(mat_ref, mom_ref):
    row = lax.broadcasted_iota(jnp.int32, (NB, NB), 0)
    col = lax.broadcasted_iota(jnp.int32, (NB, NB), 1)
    mat_ref[...] = jnp.where(row == col, RIDGE_WEIGHT, 0.0)
    mom_ref[...] = jnp.zeros_like(mom_ref)


def coefficients(mat_ref, mom_ref):
    return jnp.dot(mat_ref[...], mom_ref[...], preferred_element_type=F32, precision=HIGHEST)


def pick_samples(past, meta, items):
    slots, seg_len = meta.shape[1], past.shape[2]
    column = meta.T
    at = lax.broadcasted_iota(jnp.int32, (slots, seg_len), 1)
    rows = []
    for i in range(items):
        pick = (at == position_of(column, i, items)).astype(F32).astype(BF)
        rows.append(dot_nt(pick, past[i]).astype(BF))
    return jnp.concatenate(rows, axis=0)


def sample_kernel(past_ref, meta_ref, out_ref, *, items):
    out_ref[...] = pick_samples(past_ref[...], meta_ref[...], items)


def sample_rows(past, meta):
    items, width, seg_len = past.shape
    return pl.pallas_call(
        functools.partial(sample_kernel, items=items),
        out_shape=jax.ShapeDtypeStruct((items * meta.shape[1], width), BF),
        name="sample_rows",
    )(past, meta)


def solve_kernel(sampled_ref, meta_ref, coef_ref, inv_ref, mat_ref, mom_ref, *, items):
    clear_moments(mat_ref, mom_ref)

    def owner(s, carry):
        rows = owner_basis(meta_ref[s], items)
        mat_ref[...] += dot_tn(rows, rows, HIGHEST)
        mom_ref[...] += dot_tn(rows, sampled_ref[s].astype(F32), HIGHEST)
        return carry

    lax.fori_loop(0, meta_ref.shape[0], owner, 0)

    def step(s, carry):
        invert_step(mat_ref)
        return carry

    lax.fori_loop(0, NB // PIVOTS, step, 0)
    inv_ref[...] = mat_ref[...]
    coef_ref[...] = coefficients(mat_ref, mom_ref).astype(BF)


def solve_memory(sampled, meta, items):
    width = sampled.shape[-1]
    return pl.pallas_call(
        functools.partial(solve_kernel, items=items),
        out_shape=(
            jax.ShapeDtypeStruct((NB, width), BF),
            jax.ShapeDtypeStruct((NB, NB), F32),
        ),
        scratch_shapes=[pltpu.VMEM((NB, NB), F32), pltpu.VMEM((NB, width), F32)],
        compiler_params=pltpu.CompilerParams(vmem_limit_bytes=BIG_VMEM),
        name="solve_memory",
    )(sampled, meta)


def give_past(gmem, coef_ref, vec_ref, inv_ref, meta_ref, out_ref, gv_ref):
    slots = meta_ref.shape[1]
    item_count, width, seg_len = out_ref.shape
    normed, inverse = norm_parts(coef_ref[...].astype(F32))
    coef_grad = norm_back(gmem, normed, inverse, vec_ref[0, 0:1, :])
    gv_ref[...] = jnp.zeros_like(gv_ref)
    gv_ref[0:1, :] = col_sum(gmem * normed)
    gv_ref[1:2, :] = col_sum(gmem)
    part = lax.axis_index("mp")
    mine = jnp.zeros((coef_grad.shape[0], width), F32)
    for m in range(coef_grad.shape[1] // width):
        mine = jnp.where(part == m, coef_grad[:, m * width : (m + 1) * width], mine)
    moment = jnp.dot(inv_ref[...], mine, preferred_element_type=F32, precision=HIGHEST)
    at = lax.broadcasted_iota(jnp.int32, (slots, seg_len), 1)
    column = meta_ref[...].T
    for i in range(item_count):
        rows = basis_of(column[:, i : i + 1], column[:, item_count + i : item_count + i + 1])
        sampled = jnp.dot(rows, moment, preferred_element_type=F32, precision=HIGHEST)
        spread = (at == position_of(column, i, item_count)).astype(F32)
        out_ref[i] = dot_tn(sampled, spread, HIGHEST)


def past_kernel(gmem_ref, coef_ref, vec_ref, inv_ref, meta_ref, out_ref, gv_ref):
    give_past(gmem_ref[...], coef_ref, vec_ref, inv_ref, meta_ref, out_ref, gv_ref)


def past_grads(gmem, coef, vec, inv, meta, items, seg_len, width):
    return pl.pallas_call(
        past_kernel,
        out_shape=(
            jax.ShapeDtypeStruct((items, width, seg_len), F32),
            jax.ShapeDtypeStruct((8, coef.shape[1]), F32),
        ),
        compiler_params=pltpu.CompilerParams(vmem_limit_bytes=BIG_VMEM),
        name="past_grads",
    )(gmem, coef, vec, inv, meta)


MESH = pl.DeviceIdType.MESH
LINE = 4
PLANE = 8
NEAR = (0, -1, 1, -2, 2, -3, 3)


class Place:
    def __init__(self):
        self.s = lax.axis_index("seq")
        self.z = lax.axis_index("mp")
        core = lax.rem(self.s, 2)
        x = lax.rem(self.s // 2, 2)
        y = self.s // 4
        self.turn = 1 - 2 * core
        self.partner = self.s + self.turn
        self.sx = self.s + 2 - 4 * x
        self.sy = self.s + 4 - 8 * y
        self.sd = self.sx + 4 - 8 * y
        self.low = self.z > 0
        self.high = self.z < LINE - 1
        self.near = [
            (
                d,
                valid(self.z + d),
                self.z + d,
                lax.rem(self.z + d + LINE, 2) == 1,
                lax.rem(self.z + d + LINE, 2) == 0,
            )
            for d in NEAR
        ]


def valid(m):
    return (m >= 0) & (m < LINE)


def when(conditions, act):
    conditions = [c for c in conditions if c is not None]
    if conditions:
        pl.when(functools.reduce(lambda a, b: a & b, conditions))(act)
    else:
        act()


def greet(place, whole_line=False):
    barrier = pltpu.get_barrier_semaphore()

    def signal(seq, z):
        pl.semaphore_signal(barrier, inc=1, device_id=(seq, z), device_id_type=MESH)

    for seq in (place.partner, place.sx, place.sy):
        signal(seq, place.z)
    for d, ok, m, odd, even in place.near[1:]:
        if whole_line or abs(d) == 1:
            when((ok,), lambda: signal(place.s, m))
    if whole_line:
        peers = LINE - 1
    else:
        peers = (place.z + LINE - 1) // LINE + (2 * LINE - 2 - place.z) // LINE
    pl.semaphore_wait(barrier, 3 + peers)


UP, DOWN, ACROSS_X, ACROSS_Y, PARTNER = range(5)


class Spread:
    def __init__(self, place, src, dst, send, recv, local, line=True):
        self.p, self.src, self.dst = place, src, dst
        self.send, self.recv, self.line = send, recv, line
        self.rows = src.shape[0]
        self.sent = []
        self.mine = place.z if line else 0
        self.around = place.near if line else [(0, None, 0, None, None)]
        self.own = pltpu.make_async_copy(src, self.at(self.mine, place.s), local)

    def at(self, m, s):
        return self.dst.at[m, pl.ds(s * self.rows, self.rows), :]

    def copy(self, direction, m, s, own=False):
        p = self.p
        device = (
            (p.s, p.z + 1),
            (p.s, p.z - 1),
            (p.sx, p.z),
            (p.sy, p.z),
            (p.partner, p.z),
        )[direction]
        return pltpu.make_async_remote_copy(
            src_ref=self.src if own else self.at(m, s),
            dst_ref=self.at(m, s),
            send_sem=self.send.at[direction, m * 4 + s // 2],
            recv_sem=self.recv.at[m * PLANE + s],
            device_id=device,
            device_id_type=MESH,
        )

    def start(self, conditions, *what, **how):
        when(conditions, lambda: self.copy(*what, **how).start())
        self.sent.append((conditions, what, how))

    def arrived(self, m, s):
        self.copy(PARTNER, m, s).wait_recv()

    def first(self):
        p, m = self.p, self.mine
        self.own.start()
        if self.line:
            self.start((p.high,), UP, m, p.s, own=True)
            self.start((p.low,), DOWN, m, p.s, own=True)
        for direction in (ACROSS_X, ACROSS_Y, PARTNER):
            self.start((), direction, m, p.s, own=True)

    def along(self, d, ok, m, odd, even):
        p = self.p
        when((ok,), lambda: self.arrived(m, p.s))
        if d < 0:
            self.start((ok, p.high), UP, m, p.s)
        else:
            self.start((ok, p.low), DOWN, m, p.s)
        for direction in (ACROSS_X, ACROSS_Y, PARTNER):
            self.start((ok,), direction, m, p.s)

    def across(self, d, ok, m, odd, even):
        p = self.p
        when((ok,), lambda: self.arrived(m, p.sx))
        if self.line:
            self.start((ok, odd), ACROSS_Y, m, p.sx)
        self.start((ok,), PARTNER, m, p.sx)
        when((ok,), lambda: self.arrived(m, p.sy))
        if self.line:
            self.start((ok, even), ACROSS_X, m, p.sy)
        else:
            self.start((), ACROSS_X, m, p.sy)
        self.start((ok,), PARTNER, m, p.sy)

    def corner(self, d, ok, m, odd, even):
        p = self.p
        when((ok,), lambda: self.arrived(m, p.sd))
        self.start((ok,), PARTNER, m, p.sd)

    def part(self, kind, d):
        if kind == 0:
            return self.first
        act = (self.along, self.across, self.corner)[kind - 1]
        return functools.partial(act, *self.around[NEAR.index(d)])

    def steps(self, kind):
        return [self.part(kind, d) for d in NEAR if d or kind > 1]

    def close(self, m):
        p = self.p
        for s in (p.s, p.sx, p.sy, p.sd):
            self.arrived(m, s + p.turn)

    def settle(self):
        for conditions, what, how in self.sent:
            when(conditions, lambda: self.copy(*what, **how).wait_send())


class DirectSpread(Spread):
    def throw(self, m):
        p = self.p
        return pltpu.make_async_remote_copy(
            src_ref=self.src,
            dst_ref=self.at(self.mine, p.s),
            send_sem=self.send.at[UP, m],
            recv_sem=self.recv.at[self.mine * PLANE + p.s],
            device_id=(p.s, m),
            device_id_type=MESH,
        )

    def first(self):
        p, m = self.p, self.mine
        self.own.start()
        for d, ok, to, odd, even in self.around[1:]:
            when((ok,), lambda: self.throw(to).start())
        for direction in (ACROSS_X, ACROSS_Y, PARTNER):
            self.start((), direction, m, p.s, own=True)

    def along(self, d, ok, m, odd, even):
        when((ok,), lambda: self.arrived(m, self.p.s))
        for direction in (ACROSS_X, ACROSS_Y, PARTNER):
            self.start((ok,), direction, m, self.p.s)

    def settle(self):
        super().settle()
        for d, ok, m, odd, even in self.around[1:]:
            when((ok,), lambda: self.throw(m).wait_send())


class Line:
    def __init__(self, place, src, dst, send, recv, local):
        self.p, self.src, self.dst = place, src, dst
        self.send, self.recv = send, recv
        self.sent = []
        self.own = pltpu.make_async_copy(src, dst.at[place.z], local)

    def copy(self, up, m, own=False):
        p = self.p
        return pltpu.make_async_remote_copy(
            src_ref=self.src if own else self.dst.at[m],
            dst_ref=self.dst.at[m],
            send_sem=self.send.at[1 if up else 0, m],
            recv_sem=self.recv.at[m],
            device_id=(p.s, p.z + 1 if up else p.z - 1),
            device_id_type=MESH,
        )

    def start(self, conditions, *what, **how):
        when(conditions, lambda: self.copy(*what, **how).start())
        self.sent.append((conditions, what, how))

    def first(self):
        p = self.p
        self.own.start()
        self.start((p.high,), True, p.z, own=True)
        self.start((p.low,), False, p.z, own=True)

    def step(self, distance):
        p = self.p
        for d, ok, m, odd, even in p.near:
            if abs(d) != distance:
                continue
            when((ok,), lambda: self.copy(True, m).wait_recv())
            if d < 0:
                self.start((ok, p.high), True, m)
            else:
                self.start((ok, p.low), False, m)

    def finish_sends(self):
        for conditions, what, how in self.sent:
            when(conditions, lambda: self.copy(*what, **how).wait_send())

    def finish(self):
        self.finish_sends()
        self.own.wait()


class Collect:
    OWN, SIDE_X, SIDE_Y, CORNER = range(4)

    def __init__(self, place, grads, out, buffers, sems):
        self.p, self.grads, self.out = place, grads, out
        self.pin, self.din, self.xin, self.yin, self.zin = buffers
        self.block_sems, self.sems = sems
        self.rows = out.shape[1]
        self.columns = (place.s, place.sx, place.sy, place.sd)

    def plane(self, i):
        return i

    def unit(self, c, m, turn=0):
        s = self.columns[c] + turn
        return self.grads.at[m, :, pl.ds(s * self.rows, self.rows), :]

    def remote(self, src, dst, send, recv, device):
        return pltpu.make_async_remote_copy(
            src_ref=src,
            dst_ref=dst,
            send_sem=send,
            recv_sem=recv,
            device_id=device,
            device_id_type=MESH,
        )

    def swap(self, c, m):
        p = self.p
        return self.remote(
            self.unit(c, m, p.turn),
            self.pin.at[c, m],
            self.block_sems.at[0, c, m],
            self.block_sems.at[1, c, m],
            (p.partner, p.z),
        )

    def hop(self, kind, m, by_x=True):
        p = self.p
        src, dst, device = (
            (self.CORNER, self.din, (p.sx if by_x else p.sy, p.z)),
            (self.SIDE_X, self.xin, (p.sx, p.z)),
            (self.SIDE_Y, self.yin, (p.sy, p.z)),
        )[kind]
        return self.remote(
            self.unit(src, m),
            dst.at[m],
            self.sems.at[kind, m],
            self.sems.at[4 + kind, m],
            device,
        )

    def slot(self, m, z):
        ends = 1 // (1 + z - m)
        return m + (LINE - m) * ends

    def climb(self, m, up):
        p = self.p
        return self.remote(
            self.unit(self.OWN, m),
            self.zin.at[m if up else self.slot(m, p.z - 1)],
            self.sems.at[3, m],
            self.sems.at[7 if up else 8, m],
            (p.s, p.z + 1 if up else p.z - 1),
        )

    def climbed(self, m, up):
        zin = self.zin.at[m if up else self.slot(m, self.p.z)]
        return self.remote(
            zin, zin, self.sems.at[3, m], self.sems.at[7 if up else 8, m], (self.p.partner, self.p.z)
        )

    def add(self, c, m, *others):
        size = min(32, self.rows)
        pieces = self.rows // size

        @pl.loop(0, self.grads.shape[1] * pieces)
        def _(j):
            l = j // pieces
            at = lax.rem(j, pieces) * size
            here = pl.ds(pl.multiple_of(self.columns[c] * self.rows + at, 16), size)
            there = pl.ds(pl.multiple_of(at, 16), size)
            total = self.grads[m, l, here, :].astype(F32)
            for other in others:
                total = total + other[m, l, there, :].astype(F32)
            self.grads[m, l, here, :] = total.astype(self.grads.dtype)

    def begin(self, m):
        for c in (self.CORNER, self.SIDE_X, self.SIDE_Y, self.OWN):
            self.swap(c, m).start()

    def join(self, c, m):
        self.swap(c, m).wait_recv()
        self.add(c, m, self.pin.at[c])

    def corner(self, i):
        m = self.plane(i)
        self.join(self.CORNER, m)
        even = lax.rem(m, 2) == 0
        pl.when(even)(lambda: self.hop(0, m, True).start())
        pl.when(~even)(lambda: self.hop(0, m, False).start())

    def sides(self, i):
        m = self.plane(i)
        even = lax.rem(m, 2) == 0
        self.join(self.SIDE_X, m)
        self.join(self.SIDE_Y, m)
        pl.when(even)(lambda: self.hop(1, m).start())
        pl.when(~even)(lambda: self.hop(2, m).start())

    def relay(self, i):
        m = self.plane(i)
        even = lax.rem(m, 2) == 0
        self.hop(0, m).wait_recv()

        @pl.when(even)
        def _():
            self.add(self.SIDE_Y, m, self.din)
            self.hop(2, m).start()

        @pl.when(~even)
        def _():
            self.add(self.SIDE_X, m, self.din)
            self.hop(1, m).start()

    def line(self, i):
        p = self.p
        m = self.plane(i)
        self.join(self.OWN, m)
        self.hop(1, m).wait_recv()
        self.hop(2, m).wait_recv()
        self.add(self.OWN, m, self.xin, self.yin)

        @pl.when(m > p.z)
        def _():
            @pl.when(p.low)
            def _():
                self.climbed(m, True).wait_recv()
                self.add(self.OWN, m, self.zin)

            self.climb(m, True).start()

        @pl.when(m < p.z)
        def _():
            @pl.when(p.high)
            def _():
                self.climbed(m, False).wait_recv()
                self.add(self.OWN, m, self.zin)

            self.climb(m, False).start()

    def result(self):
        p = self.p
        self.out[...] = self.unit(self.OWN, p.z)[...].astype(F32)

        @pl.when(p.low)
        def _():
            self.climbed(p.z, True).wait_recv()
            self.out[...] += self.zin[p.z].astype(F32)

        @pl.when(p.high)
        def _():
            self.climbed(p.z, False).wait_recv()
            self.out[...] += self.zin[LINE].astype(F32)

    def part(self, kind, i):
        if kind == 4:
            return self.result
        return functools.partial((self.corner, self.sides, self.relay, self.line)[kind], i)

    def settle(self):
        @pl.loop(0, LINE)
        def _(m):
            for c in range(4):
                self.swap(c, m).wait_send()
            for kind in range(3):
                self.hop(kind, m).wait_send()
            pl.when(m != self.p.z)(lambda: self.climb(m, True).wait_send())


class DirectCollect(Collect):
    def throw(self, m):
        p = self.p
        return self.remote(
            self.unit(self.OWN, m),
            self.zin.at[p.z],
            self.sems.at[3, m],
            self.sems.at[7, p.z],
            (p.s, m),
        )

    def line(self, i):
        m = self.plane(i)
        self.join(self.OWN, m)
        self.hop(1, m).wait_recv()
        self.hop(2, m).wait_recv()
        self.add(self.OWN, m, self.xin, self.yin)
        pl.when(m != self.p.z)(lambda: self.throw(m).start())

    def result(self):
        p = self.p
        self.out[...] = self.unit(self.OWN, p.z)[...].astype(F32)
        for m in range(LINE):

            @pl.when(m != p.z)
            def _():
                zin = self.zin.at[m]
                self.remote(
                    zin, zin, self.sems.at[3, m], self.sems.at[7, m], (p.partner, p.z)
                ).wait_recv()
                self.out[...] += self.zin[m].astype(F32)


BUFFERS = ((4, LINE), (LINE,), (LINE,), (LINE,), (LINE + 1,))


def project(rows, weights, bias, local):
    return (dot(rows, weights[:, : 3 * local]) + bias[:, : 3 * local]).astype(BF)


def attend(query, keys, values, head, store, between):
    rows, local = query.shape
    half = rows // 2
    query_t = query.T * BF(1.0 / math.sqrt(head))
    value_t = values.T
    line = lax.broadcasted_iota(jnp.int32, (local, rows), 0)
    heads = []
    for h in range(local // head):
        own = (line >= h * head) & (line < (h + 1) * head)
        masked = jnp.where(own, query_t, BF(0.0))
        value_h = value_t[h * head : (h + 1) * head, :]
        parts = []
        for b in range(2):
            span = NB + (b + 1) * half
            scores = dot(keys[:span, :], masked[:, b * half : (b + 1) * half])
            key_at = lax.broadcasted_iota(jnp.int32, (half, half), 0)
            row_at = lax.broadcasted_iota(jnp.int32, (half, half), 1)
            edge = jnp.where(key_at <= row_at, scores[span - half :, :], -1e30)
            scores = jnp.concatenate([scores[: span - half, :], edge], axis=0)
            scores = jnp.exp(scores - jnp.max(scores, axis=0, keepdims=True))
            probs = (scores * (1.0 / jnp.sum(scores, axis=0, keepdims=True))).astype(BF)
            store(h, slice(0, span), slice(b * half, (b + 1) * half), probs)
            parts.append(dot(value_h[:, :span], probs))
        heads.append(jnp.concatenate(parts, axis=1).astype(BF))
        between(h)
    return jnp.concatenate(heads, axis=0)


def gelu_parts(pre):
    square = pre * pre
    inner = jnp.tanh(GELU_SCALE * (pre + GELU_CUBIC * pre * square))
    half_up = 0.5 * (1.0 + inner)
    slope = GELU_SCALE * (1.0 + 3.0 * GELU_CUBIC * square)
    return (pre * half_up).astype(BF), half_up + 0.5 * pre * (1.0 - inner * inner) * slope


def forward_kernel(
    tokens_ref,
    past_ref,
    pos_ref,
    counts_ref,
    stack_ref,
    b_qv_ref,
    b_up_ref,
    w_qkv_ref,
    w_out_ref,
    up_ref,
    down_ref,
    wa_ref,
    wu_ref,
    wd_ref,
    out_ref,
    res_ref,
    hmt_ref,
    h2t_ref,
    prob_ref,
    key_ref,
    val_ref,
    query_ref,
    att_ref,
    act_ref,
    slope_ref,
    vec_ref,
    inv_ref,
    coef_ref,
    meta_ref,
    hm_ref,
    h2_ref,
    room_ref,
    attn_ref,
    tok_ref,
    acc_ref,
    mom_ref,
    sampled_ref,
    all_sampled_ref,
    basis_ref,
    all_meta_ref,
    all_room_ref,
    coef_part_ref,
    all_coef_ref,
    wide_ref,
    past_vmem,
    flat_send,
    flat_recv,
    flat_local,
    send,
    recv,
    own_sem,
    line_send,
    line_recv,
    line_own,
    load_sem,
    *,
    items,
    head,
):
    step = pl.program_id(0)
    rows, width = tok_ref.shape
    local = query_ref.shape[2]
    place = Place()
    flat = [
        Spread(
            place, src, dst, flat_send.at[i], flat_recv.at[i], flat_local.at[i], line=False
        )
        for i, (src, dst) in enumerate(
            ((meta_ref, all_meta_ref), (sampled_ref, all_sampled_ref))
        )
    ]
    wide = [
        Spread(place, src, dst, send.at[i], recv.at[i], own_sem.at[i])
        for i, (src, dst) in enumerate(
            ((room_ref, all_room_ref), (attn_ref, wa_ref), (up_ref, wu_ref), (down_ref, wd_ref))
        )
    ]
    room, attn, up, down = wide
    line = Line(place, coef_part_ref, all_coef_ref, line_send, line_recv, line_own)

    attn_at = SOLVE_STEPS
    mlp_at = attn_at + LINE
    last = mlp_at + LINE - 1
    plan = {
        slot: [wide[i].part(kind, d) for i, kind, d in steps] for slot, steps in FORWARD_PLAN
    }

    def transfers(at, position):
        if plan.get((at, position)):

            @pl.when(step == at)
            def _():
                for one in plan[(at, position)]:
                    one()

    def load(ref, m, slot, which):
        return pltpu.make_async_copy(ref.at[m], wide_ref.at[slot, which], load_sem.at[slot, which])

    @pl.when(step == 0)
    def _():
        bring_tok = pltpu.make_async_copy(
            tokens_ref.at[pl.ds(place.z * rows, rows), :], tok_ref, load_sem.at[0, 0]
        )
        bring_past = pltpu.make_async_copy(past_ref, past_vmem, load_sem.at[0, 1])
        bring_tok.start()
        bring_past.start()
        greet(place)
        meta_ref[...] = meta_rows(
            pos_ref[...], counts_ref, place.s * items, PLANE * items, past_ref.shape[2]
        )
        bring_past.wait()
        sampled_ref[...] = pick_samples(past_vmem[...], meta_ref[...], items)
        for part in flat:
            part.first()
        room_ref[...] = small_rows(
            stack_ref[...].astype(F32),
            b_qv_ref[...].astype(F32),
            b_up_ref[...].astype(F32),
            place.s,
            width,
            head,
        )
        for i in range(3):
            attn_ref[:, i * local : (i + 1) * local] = w_qkv_ref[i]
        row, lane = iotas((w_out_ref.shape[1], w_out_ref.shape[1]))
        unit = (row == lane).astype(F32).astype(BF)
        attn_ref[:, 3 * local :] = dot_nt(unit, w_out_ref[...]).astype(BF)
        bring_tok.wait()
        acc_ref[...] = jnp.zeros_like(acc_ref)
        clear_moments(inv_ref, mom_ref)

    transfers(0, 0)

    meta, samples = flat

    @pl.when(step == 1)
    def _():
        for kind in (2, 3):
            meta.part(kind, 0)()
        samples.part(2, 0)()
        meta.own.wait()
        meta.close(0)

    transfers(1, 0)

    @pl.when(step == 1)
    def _():
        def owner(s, carry):
            rows = owner_basis(all_meta_ref[0, pl.ds(s * 8, 8), :], items)
            basis_ref[s] = rows
            inv_ref[...] += dot_tn(rows, rows, HIGHEST)
            return carry

        lax.fori_loop(0, PLANE, owner, 0)
        samples.part(3, 0)()
        samples.own.wait()
        samples.close(0)

    transfers(1, 1)

    @pl.when(step == 1)
    def _():
        def owner(s, carry):
            count = sampled_ref.shape[0]
            rows = all_sampled_ref[0, pl.ds(s * count, count), :]
            mom_ref[...] += dot_tn(basis_ref[s], rows.astype(F32), HIGHEST)
            return carry

        lax.fori_loop(0, PLANE, owner, 0)

    transfers(1, 2)

    inverse_end = 2 + NB // PIVOTS

    @pl.when((step >= 2) & (step < inverse_end))
    def _():
        invert_step(inv_ref)

    for at in range(2, inverse_end):
        transfers(at, 0)

    @pl.when(step == inverse_end)
    def _():
        coef_part_ref[...] = coefficients(inv_ref, mom_ref).astype(BF)
        line.first()

    transfers(inverse_end, 0)

    @pl.when(step == inverse_end)
    def _():
        room.own.wait()
        for m in range(LINE):
            room.close(m)
            total = all_room_ref[m, 0:16, :].astype(F32)
            for s in range(1, PLANE):
                total = total + all_room_ref[m, s * 16 : (s + 1) * 16, :].astype(F32)
            vec_ref[m] = total
        gain, bias = vec_ref[0, 0:1, :], vec_ref[0, 1:2, :]
        normed, _ = norm_parts(tok_ref[...].astype(F32))
        hm_ref[NB:, :] = (normed * gain + bias).astype(BF)
        hmt_ref[:, NB:] = hm_ref[NB:, :].T
        line.step(1)

    transfers(inverse_end, 1)

    @pl.when(step == inverse_end)
    def _():
        attn.own.wait()
        attn.close(0)
        load(wa_ref, 0, 0, 0).start()
        line.step(2)

    transfers(inverse_end, 2)

    @pl.when(step == inverse_end)
    def _():
        line.step(3)
        line.own.wait()
        gain, bias = vec_ref[0, 0:1, :], vec_ref[0, 1:2, :]
        for m in range(LINE):
            coef_ref[:, m * local : (m + 1) * local] = all_coef_ref[m]
        normed, _ = norm_parts(coef_ref[...].astype(F32))
        hm_ref[0:NB, :] = (normed * gain + bias).astype(BF)
        hmt_ref[:, 0:NB] = hm_ref[0:NB, :].T

    @pl.when((step >= attn_at) & (step < mlp_at))
    def _():
        m = step - attn_at
        slot = lax.rem(m, 2)
        load(wa_ref, m, slot, 0).wait()

        @pl.when(m < LINE - 1)
        def _():
            attn.close(m + 1)
            load(wa_ref, m + 1, 1 - slot, 0).start()

        weights = wide_ref[slot, 0]
        projected = project(hm_ref[...], weights, vec_ref[m, 6:7, :], local)
        query = projected[NB:, :local]
        keys = projected[:, local : 2 * local]
        values = projected[:, 2 * local :]
        query_ref[0] = query
        key_ref[0] = keys
        val_ref[0] = values

        def store(h, lines, columns, probs):
            prob_ref[0, h, lines, columns] = probs

        def between(h):
            for at in range(attn_at, mlp_at):
                transfers(at, h)

        attended = attend(query, keys, values, head, store, between)
        att_ref[0] = attended
        acc_ref[...] += dot_nt(attended.T, wide_ref[slot, 0, :, 3 * local :])

    transfers(mlp_at, 0)

    @pl.when(step == mlp_at)
    def _():
        for part in (up, down):
            part.own.wait()
            part.close(0)
        load(wu_ref, 0, 0, 0).start()
        load(wd_ref, 0, 0, 1).start()
        residual = tok_ref[...].astype(F32) + acc_ref[...] + vec_ref[0, 4:5, :]
        res_ref[...] = residual
        normed, _ = norm_parts(residual)
        h2_ref[...] = (normed * vec_ref[0, 2:3, :] + vec_ref[0, 3:4, :]).astype(BF)
        h2t_ref[...] = h2_ref[...].T
        acc_ref[...] = jnp.zeros_like(acc_ref)

    @pl.when(step >= mlp_at)
    def _():
        m = step - mlp_at
        slot = lax.rem(m, 2)
        load(wu_ref, m, slot, 0).wait()
        load(wd_ref, m, slot, 1).wait()

        @pl.when(m < LINE - 1)
        def _():
            up.close(m + 1)
            down.close(m + 1)
            load(wu_ref, m + 1, 1 - slot, 0).start()
            load(wd_ref, m + 1, 1 - slot, 1).start()

        pre = dot(h2_ref[...], wide_ref[slot, 0]) + vec_ref[m, 7:8, :]
        act, slope = gelu_parts(pre)
        act_ref[0] = act
        slope_ref[0] = slope.astype(BF)
        acc_ref[...] += dot_nt(act, wide_ref[slot, 1])

    @pl.when(step == last)
    def _():
        out_ref[...] = (res_ref[...] + acc_ref[...] + vec_ref[0, 5:6, :]).astype(BF)
        for part in flat + wide:
            part.settle()
        line.finish_sends()


SOLVE_STEPS = 3 + NB // PIVOTS


FORWARD_PLAN = (
    (
        (0, 0),
        ((0, 0, 0),),
    ),
    (
        (1, 0),
        ((1, 0, 0), (0, 1, 1), (0, 1, -1),),
    ),
    (
        (1, 1),
        ((0, 1, -2), (0, 1, 2), (1, 1, -1), (1, 1, 1),),
    ),
    (
        (1, 2),
        ((0, 1, -3), (0, 1, 3), (3, 0, 0),),
    ),
    (
        (2, 0),
        ((1, 1, 2), (1, 1, -2),),
    ),
    (
        (4, 0),
        ((0, 2, -3), (0, 2, 3), (1, 2, 0), (0, 2, -1), (0, 2, 1),),
    ),
    (
        (5, 0),
        ((0, 2, 0), (0, 2, -2), (0, 2, 2), (1, 1, -3), (1, 1, 3), (2, 0, 0),),
    ),
    (
        (7, 0),
        ((1, 2, -2), (1, 2, 2), (1, 2, 1), (1, 2, -1),),
    ),
    (
        (8, 0),
        ((3, 1, 1), (3, 1, -1),),
    ),
    (
        (9, 0),
        ((0, 3, 3), (0, 3, -3),),
    ),
    (
        (10, 0),
        ((0, 3, 1), (0, 3, -1), (1, 2, 3), (1, 2, -3), (0, 3, 0), (0, 3, 2), (0, 3, -2), (3, 1, -2), (3, 1, 2),),
    ),
    (
        (10, 1),
        ((3, 1, 3), (3, 1, -3), (1, 3, 0), (1, 3, 1), (1, 3, -2), (1, 3, 3), (1, 3, -1), (1, 3, 2), (1, 3, -3),),
    ),
    (
        (10, 2),
        ((2, 1, -1), (2, 1, 1),),
    ),
    (
        (11, 0),
        ((2, 1, -2), (2, 1, 2),),
    ),
    (
        (11, 1),
        ((2, 1, 3), (2, 1, -3), (3, 2, 0),),
    ),
    (
        (12, 0),
        ((2, 2, 1), (2, 2, -1), (2, 2, 0),),
    ),
    (
        (12, 1),
        ((2, 2, -3), (2, 2, 3), (3, 2, -2), (3, 2, 2),),
    ),
    (
        (13, 0),
        ((3, 2, -1), (3, 2, 1), (2, 2, 2), (2, 2, -2),),
    ),
    (
        (13, 1),
        ((2, 3, -1), (2, 3, 1), (3, 2, 3), (3, 2, -3), (2, 3, 0),),
    ),
    (
        (13, 2),
        ((3, 3, 0), (2, 3, 3), (2, 3, -3),),
    ),
    (
        (14, 1),
        ((3, 3, 1), (3, 3, -1), (3, 3, 2), (3, 3, -2), (2, 3, -2), (2, 3, 2), (3, 3, 3), (3, 3, -3),),
    ),
)


def forward_pass(tokens, past, positions, counts, stack, b_qv, b_up, w_qkv, w_out, up, down, head):
    width = tokens.shape[1]
    rows = tokens.shape[0] // LINE
    items = past.shape[0]
    local = width // LINE
    hidden = up.shape[1]
    heads = local // head
    keyed = NB + rows
    slots = positions.shape[1]
    samples = items * slots
    part = up.shape[0]
    attn_at = SOLVE_STEPS
    mlp_at = attn_at + LINE
    first = lambda i: jnp.clip(i - attn_at, 0, LINE - 1)
    second = lambda i: jnp.clip(i - mlp_at, 0, LINE - 1)
    whole = lambda shape: pl.BlockSpec(shape, lambda i: (0,) * len(shape))
    anywhere = pl.BlockSpec(memory_space=pl.ANY)
    vmem = pl.BlockSpec(memory_space=pltpu.VMEM)
    dma = pltpu.SemaphoreType.DMA
    shape = jax.ShapeDtypeStruct
    return pl.pallas_call(
        functools.partial(forward_kernel, items=items, head=head),
        grid=(mlp_at + LINE,),
        in_specs=[anywhere, anywhere, vmem, pl.BlockSpec(memory_space=pltpu.SMEM)]
        + [vmem] * 5
        + [anywhere, anywhere],
        out_specs=[
            anywhere,
            anywhere,
            anywhere,
            whole((rows, width)),
            whole((rows, width)),
            whole((width, keyed)),
            whole((width, rows)),
            pl.BlockSpec((1, heads, keyed, rows), lambda i: (first(i), 0, 0, 0)),
            pl.BlockSpec((1, keyed, local), lambda i: (first(i), 0, 0)),
            pl.BlockSpec((1, keyed, local), lambda i: (first(i), 0, 0)),
            pl.BlockSpec((1, rows, local), lambda i: (first(i), 0, 0)),
            pl.BlockSpec((1, local, rows), lambda i: (first(i), 0, 0)),
            pl.BlockSpec((1, rows, hidden), lambda i: (second(i), 0, 0)),
            pl.BlockSpec((1, rows, hidden), lambda i: (second(i), 0, 0)),
            whole((LINE, 16, width)),
            whole((NB, NB)),
            whole((NB, width)),
            whole((8, slots)),
        ],
        out_shape=[
            shape((LINE, width, width), BF),
            shape((LINE, width, hidden), BF),
            shape((LINE, width, hidden), BF),
            shape((rows, width), BF),
            shape((rows, width), F32),
            shape((width, keyed), BF),
            shape((width, rows), BF),
            shape((LINE, heads, keyed, rows), BF),
            shape((LINE, keyed, local), BF),
            shape((LINE, keyed, local), BF),
            shape((LINE, rows, local), BF),
            shape((LINE, local, rows), BF),
            shape((LINE, rows, hidden), BF),
            shape((LINE, rows, hidden), BF),
            shape((LINE, 16, width), F32),
            shape((NB, NB), F32),
            shape((NB, width), BF),
            shape((8, slots), F32),
        ],
        scratch_shapes=[
            pltpu.VMEM((keyed, width), BF),
            pltpu.VMEM((rows, width), BF),
            pltpu.VMEM((16, width), BF),
            pltpu.VMEM((part, width), BF),
            pltpu.VMEM((rows, width), BF),
            pltpu.VMEM((rows, width), F32),
            pltpu.VMEM((NB, local), F32),
            pltpu.VMEM((samples, local), BF),
            pltpu.VMEM((1, PLANE * samples, local), BF),
            pltpu.VMEM((PLANE, samples, NB), F32),
            pltpu.VMEM((1, PLANE * 8, slots), F32),
            pltpu.VMEM((LINE, PLANE * 16, width), BF),
            pltpu.VMEM((NB, local), BF),
            pltpu.VMEM((LINE, NB, local), BF),
            pltpu.VMEM((2, 2, width, width), BF),
            pltpu.VMEM(past.shape, BF),
            dma((2, 5, 4)),
            dma((2, PLANE)),
            dma((2,)),
            dma((4, 5, LINE * 4)),
            dma((4, LINE * PLANE)),
            dma((4,)),
            dma((2, LINE)),
            dma((LINE,)),
            dma(()),
            dma((2, 2)),
        ],
        compiler_params=pltpu.CompilerParams(
            collective_id=1, has_side_effects=True, vmem_limit_bytes=BIG_VMEM
        ),
        name="forward_pass",
    )(tokens, past, positions, counts, stack, b_qv, b_up, w_qkv, w_out, up, down)


def plain_forward_kernel(
    tok_ref,
    coef_ref,
    vec_ref,
    wa_ref,
    wu_ref,
    wd_ref,
    out_ref,
    res_ref,
    hm_ref,
    h2_ref,
    prob_ref,
    key_ref,
    val_ref,
    query_ref,
    att_ref,
    act_ref,
    slope_ref,
    acc_ref,
    *,
    groups,
    head,
):
    step = pl.program_id(0)
    rows, width = tok_ref.shape
    local = query_ref.shape[2]

    @pl.when(step == 0)
    def _():
        gain, bias = vec_ref[0, 0:1, :], vec_ref[0, 1:2, :]
        normed, _ = norm_parts(coef_ref[...].astype(F32))
        hm_ref[0:NB, :] = (normed * gain + bias).astype(BF)
        normed, _ = norm_parts(tok_ref[...].astype(F32))
        hm_ref[NB:, :] = (normed * gain + bias).astype(BF)
        acc_ref[...] = jnp.zeros_like(acc_ref)

    @pl.when(step < groups)
    def _():
        weights = wa_ref[0]
        projected = project(hm_ref[...], weights, vec_ref[step, 6:7, :], local)
        query = projected[NB:, :local]
        keys = projected[:, local : 2 * local]
        values = projected[:, 2 * local :]
        query_ref[0] = query
        key_ref[0] = keys
        val_ref[0] = values

        def store(h, lines, columns, probs):
            prob_ref[0, h, lines, columns] = probs

        attended = attend(query, keys, values, head, store, lambda h: None)
        att_ref[0] = attended
        acc_ref[...] += dot_nt(attended.T, weights[:, 3 * local :])

    @pl.when(step == groups)
    def _():
        residual = tok_ref[...].astype(F32) + acc_ref[...] + vec_ref[0, 4:5, :]
        res_ref[...] = residual
        normed, _ = norm_parts(residual)
        h2_ref[...] = (normed * vec_ref[0, 2:3, :] + vec_ref[0, 3:4, :]).astype(BF)
        acc_ref[...] = jnp.zeros_like(acc_ref)

    @pl.when(step >= groups)
    def _():
        pre = dot(h2_ref[...], wu_ref[0]) + vec_ref[step - groups, 7:8, :]
        act, slope = gelu_parts(pre)
        act_ref[0] = act
        slope_ref[0] = slope.astype(BF)
        acc_ref[...] += dot_nt(act, wd_ref[0])

    @pl.when(step == 2 * groups - 1)
    def _():
        out_ref[...] = (res_ref[...] + acc_ref[...] + vec_ref[0, 5:6, :]).astype(BF)


def plain_forward(tok, coef, vec, wide, head):
    rows, width = tok.shape
    groups = wide[0].shape[0]
    local = width // groups
    hidden = wide[1].shape[2]
    heads = local // head
    keyed = NB + rows
    first = lambda i: jnp.minimum(i, groups - 1)
    second = lambda i: jnp.maximum(i - groups, 0)
    whole = lambda shape: pl.BlockSpec(shape, lambda i: (0,) * len(shape))
    shape = jax.ShapeDtypeStruct
    return pl.pallas_call(
        functools.partial(plain_forward_kernel, groups=groups, head=head),
        grid=(2 * groups,),
        in_specs=[
            whole((rows, width)),
            whole((NB, width)),
            whole((groups, 16, width)),
            pl.BlockSpec((1, width, width), lambda i: (first(i), 0, 0)),
            pl.BlockSpec((1, width, hidden), lambda i: (second(i), 0, 0)),
            pl.BlockSpec((1, width, hidden), lambda i: (second(i), 0, 0)),
        ],
        out_specs=[
            whole((rows, width)),
            whole((rows, width)),
            whole((keyed, width)),
            whole((rows, width)),
            pl.BlockSpec((1, heads, keyed, rows), lambda i: (first(i), 0, 0, 0)),
            pl.BlockSpec((1, keyed, local), lambda i: (first(i), 0, 0)),
            pl.BlockSpec((1, keyed, local), lambda i: (first(i), 0, 0)),
            pl.BlockSpec((1, rows, local), lambda i: (first(i), 0, 0)),
            pl.BlockSpec((1, local, rows), lambda i: (first(i), 0, 0)),
            pl.BlockSpec((1, rows, hidden), lambda i: (second(i), 0, 0)),
            pl.BlockSpec((1, rows, hidden), lambda i: (second(i), 0, 0)),
        ],
        out_shape=[
            shape((rows, width), BF),
            shape((rows, width), F32),
            shape((keyed, width), BF),
            shape((rows, width), BF),
            shape((groups, heads, keyed, rows), BF),
            shape((groups, keyed, local), BF),
            shape((groups, keyed, local), BF),
            shape((groups, rows, local), BF),
            shape((groups, local, rows), BF),
            shape((groups, rows, hidden), BF),
            shape((groups, rows, hidden), BF),
        ],
        scratch_shapes=[pltpu.VMEM((rows, width), F32)],
        compiler_params=pltpu.CompilerParams(vmem_limit_bytes=BIG_VMEM),
        name="plain_forward",
    )(tok, coef, vec, *wide)


def attend_back(g_att, att_t, keys, values, query, probs_of, head, between):
    rows, local = g_att.shape
    half = rows // 2
    low = NB + rows - half
    g_att_t = g_att.T
    product = g_att_t.astype(F32) * att_t.astype(F32)
    key_t = keys.T
    scale = 1.0 / math.sqrt(head)
    line = lax.broadcasted_iota(jnp.int32, (local, rows), 0)
    lane = lax.broadcasted_iota(jnp.int32, (rows, local), 1)
    key_grad = [jnp.zeros((low, local), F32), jnp.zeros((half, local), F32)]
    val_grad = [jnp.zeros((low, local), F32), jnp.zeros((half, local), F32)]
    query_grads = []
    for h in range(local // head):
        own_t = (line >= h * head) & (line < (h + 1) * head)
        own = (lane >= h * head) & (lane < (h + 1) * head)
        grad_t = jnp.where(own_t, g_att_t, BF(0.0))
        grad_h = jnp.where(own, g_att, BF(0.0))
        query_h = jnp.where(own, query, BF(0.0))
        inner = jnp.sum(product[h * head : (h + 1) * head, :], axis=0, keepdims=True)
        key_h = key_t[h * head : (h + 1) * head, :]
        parts = []
        for b in range(2):
            span = NB + (b + 1) * half
            cols = slice(b * half, (b + 1) * half)
            probs = probs_of(h, slice(0, span), cols)
            dprob = dot(values[:span, :], grad_t[:, cols])
            dscore = (probs.astype(F32) * (dprob - inner[:, cols])).astype(BF)
            parts.append(dot(key_h[:, :span], dscore))
            val_part = dot(probs, grad_h[cols, :])
            key_part = dot(dscore, query_h[cols, :])
            val_grad[0] = val_grad[0] + val_part[:low, :]
            key_grad[0] = key_grad[0] + key_part[:low, :]
            if b == 1:
                val_grad[1] = val_grad[1] + val_part[low:, :]
                key_grad[1] = key_grad[1] + key_part[low:, :]
        query_grads.append(jnp.concatenate(parts, axis=1))
        between(h)
    query_grad = (jnp.concatenate(query_grads, axis=0) * scale).astype(BF).T
    key_grad = jnp.concatenate(key_grad, axis=0) * scale
    return query_grad, key_grad, jnp.concatenate(val_grad, axis=0)


def backward_kernel(
    tokens_ref,
    cots_ref,
    fwd_out_ref,
    res_ref,
    wa_ref,
    wu_ref,
    wd_ref,
    vec_ref,
    hmt_ref,
    h2t_ref,
    coef_ref,
    inv_ref,
    meta_ref,
    prob_ref,
    key_ref,
    val_ref,
    query_ref,
    att_ref,
    act_ref,
    slope_ref,
    outs_ref,
    tgs_ref,
    past_ref,
    vectors_ref,
    bias_ref,
    bias_up_ref,
    qkv_out_ref,
    wo_out_ref,
    up_out_ref,
    down_out_ref,
    *scratch,
    head,
):
    (
        tok_ref,
        cot_ref,
        cott_ref,
        gres_ref,
        acc_ref,
        proj_ref,
        gv_ref,
        ggv_ref,
        gmem_ref,
        wide_ref,
        side_ref,
        attn_ref,
        mlp_ref,
        gv_mem_ref,
        side_out_ref,
        attn_out_ref,
        mlp_out_ref,
    ) = scratch[:17]
    buffers = scratch[17:32]
    block_sems, sems, lsend, lrecv, lown, gsend, grecv, gown, load_sem = scratch[32:]
    step = pl.program_id(0)
    rows, width = tok_ref.shape
    local = query_ref.shape[2]
    items = past_ref.shape[0]
    place = Place()
    side, attn, mlp = [
        kind(place, grads, out, buffers[i::3], (block_sems.at[i], sems.at[i]))
        for i, (kind, grads, out) in enumerate(
            (
                (DirectCollect, side_ref, side_out_ref),
                (Collect, attn_ref, attn_out_ref),
                (Collect, mlp_ref, mlp_out_ref),
            )
        )
    ]
    outs, tgs = [
        [
            Line(
                place,
                src.at[pl.ds(h * (rows // count), rows // count), :],
                dst.at[:, pl.ds(h * (rows // count), rows // count), :],
                lsend.at[first + h],
                lrecv.at[first + h],
                lown.at[first + h],
            )
            for h in range(count)
        ]
        for src, dst, first, count in (
            (fwd_out_ref, outs_ref, 0, OUT_PIECES),
            (cot_ref, tgs_ref, OUT_PIECES, GRAD_PIECES),
        )
    ]
    mem = DirectSpread(place, side_out_ref.at[0, 0:8, :], gmem_ref, gsend, grecv, gown)
    mine = pl.ds(place.z * rows, rows)

    def load(ref, m, slot, which):
        return pltpu.make_async_copy(ref.at[m], wide_ref.at[slot, which], load_sem.at[slot, which])

    def bring(i, src, dst):
        return pltpu.make_async_copy(src, dst, load_sem.at[2, i])

    bring_cot = bring(0, cots_ref.at[mine, :], cot_ref)
    bring_tok = bring(1, tokens_ref.at[mine, :], tok_ref)
    bring_res = pltpu.make_async_copy(res_ref, gres_ref, load_sem.at[3, 0])

    def past():
        mem.own.wait()
        for m in range(LINE):
            mem.close(m)
        gmem = jnp.concatenate([gmem_ref[m] for m in range(LINE)], axis=0)
        give_past(gmem, coef_ref, vec_ref, inv_ref, meta_ref, past_ref, gv_mem_ref)
        own = side_out_ref[0, 8:16, :]
        own = jnp.concatenate([own[0:2] + gv_mem_ref[0:2, :], own[2:8]], axis=0)
        vectors, biases, bias_up = small_pieces(
            own, place.s, vectors_ref.shape[1], bias_ref.shape[2], head, bias_ref.shape[0]
        )
        vectors_ref[...] = vectors
        for h, bias in enumerate(biases):
            bias_ref[h] = bias
        bias_up_ref[...] = bias_up

    def give_attn():
        attn.result()
        for i in range(3):
            qkv_out_ref[i] = attn_out_ref[0, :, i * local : (i + 1) * local]
        row, lane = iotas((attn_out_ref.shape[1], attn_out_ref.shape[1]))
        unit = (row == lane).astype(F32)
        wo_out_ref[...] = dot_tn(attn_out_ref[0, :, 3 * local :], unit, HIGHEST)

    def give_mlp():
        mlp.result()
        up_out_ref[...] = mlp_out_ref[0]
        down_out_ref[...] = mlp_out_ref[1]

    def move(what, kind, i):
        if what == 1 and kind == 4:
            return [give_attn]
        if what == 2 and kind == 4:
            return [give_mlp]
        if what < 3:
            return [(side, attn, mlp)[what].part(kind, i)]
        if what == 3:
            return mem.steps(kind) if kind else [mem.first]
        if what == 4:
            return [past]
        line = (outs + tgs)[what - 5]
        return [functools.partial(line.step, i) if kind else line.first]

    plan = [[one for what in moves for one in move(*what)] for moves in BACKWARD_PLAN]

    def transfers(slot, condition=None):
        def go():
            for one in plan[slot]:
                one()

        if plan[slot]:
            when((condition,), go)

    @pl.when(step == 0)
    def _():
        bring_cot.start()
        bring_tok.start()
        bring_res.start()
        load(wu_ref, 0, 0, 0).start()
        load(wd_ref, 0, 0, 1).start()
        greet(place, whole_line=True)
        for line in outs:
            line.first()
        acc_ref[...] = jnp.zeros_like(acc_ref)
        gv_ref[...] = jnp.zeros_like(gv_ref)
        bring_cot.wait()
        bring_tok.wait()
        bring_res.wait()
        cott_ref[...] = cot_ref[...].T

    @pl.when(step < LINE)
    def _():
        m = step
        slot = lax.rem(m, 2)
        load(wu_ref, m, slot, 0).wait()
        load(wd_ref, m, slot, 1).wait()

        @pl.when(m < LINE - 1)
        def _():
            load(wu_ref, m + 1, 1 - slot, 0).start()
            load(wd_ref, m + 1, 1 - slot, 1).start()

        @pl.when(m == LINE - 1)
        def _():
            load(wa_ref, 0, 0, 0).start()

        upstream = cot_ref[...]
        grad = (dot(upstream, wide_ref[slot, 1]) * slope_ref[0].astype(F32)).astype(BF)
        mlp_ref[m, 1] = dot(cott_ref[...], act_ref[0]).astype(BF)
        mlp_ref[m, 0] = dot(h2t_ref[...], grad).astype(BF)
        mlp.begin(m)
        for at in range(LINE):
            transfers(at, step == at)
        ggv_ref[m, 1:2, :] = col_sum(grad.astype(F32))
        acc_ref[NB:, :] += dot_nt(grad, wide_ref[slot, 0])

    @pl.when(step == LINE)
    def _():
        transfers(LINE)
        upstream = cot_ref[...].astype(F32)
        normed, inverse = norm_parts(gres_ref[...])
        grad = acc_ref[NB:, :]
        g_res = upstream + norm_back(grad, normed, inverse, vec_ref[0, 2:3, :])
        gres_ref[...] = g_res
        g_attn = g_res.astype(BF)
        gv_ref[2:3, :] = col_sum(grad * normed)
        gv_ref[3:4, :] = col_sum(grad)
        gv_ref[4:5, :] = col_sum(g_attn.astype(F32))
        gv_ref[5:6, :] = col_sum(upstream)
        cott_ref[...] = g_attn.T
        acc_ref[...] = jnp.zeros_like(acc_ref)
        proj_ref[0:NB, :] = jnp.zeros((NB, proj_ref.shape[1]), BF)
        transfers(LINE + 1)

    @pl.when(step >= LINE)
    def _():
        m = step - LINE
        slot = lax.rem(m, 2)
        load(wa_ref, m, slot, 0).wait()

        @pl.when(m < LINE - 1)
        def _():
            load(wa_ref, m + 1, 1 - slot, 0).start()

        def between(h):
            for at in range(LINE):
                transfers(LINE + 2 + 4 * at + h, m == at)

        def probs_of(h, lines, columns):
            return prob_ref[0, h, lines, columns]

        g_attn = gres_ref[...].astype(BF)
        g_att = dot(g_attn, wide_ref[slot, 0, :, 3 * local :]).astype(BF)
        att_t = att_ref[0]
        query_grad, key_grad, val_grad = attend_back(
            g_att, att_t, key_ref[0], val_ref[0], query_ref[0], probs_of, head, between
        )
        proj_ref[NB:, 0:local] = query_grad
        proj_ref[:, local : 2 * local] = key_grad.astype(BF)
        proj_ref[:, 2 * local :] = val_grad.astype(BF)
        proj = proj_ref[...]
        ggv_ref[m, 0:1, 0 : 3 * local] = col_sum(proj.astype(F32))
        ggv_ref[m, 0:1, 3 * local :] = jnp.zeros((1, width - 3 * local), F32)
        attn_ref[m, 0, :, 0 : 3 * local] = dot(hmt_ref[...], proj).astype(BF)
        attn_ref[m, 0, :, 3 * local :] = dot_nt(cott_ref[...], att_t).astype(BF)
        attn.begin(m)
        acc_ref[...] += dot_nt(proj, wide_ref[slot, 0, :, : 3 * local])
        between(3)

    @pl.when(step == 2 * LINE - 1)
    def _():
        grad = acc_ref[NB:, :]
        normed, inverse = norm_parts(tok_ref[...].astype(F32))
        back = norm_back(grad, normed, inverse, vec_ref[0, 0:1, :])
        cot_ref[...] = (gres_ref[...] + back).astype(BF)
        tgs[0].first()
        gv_ref[0:1, :] = col_sum(grad * normed)
        gv_ref[1:2, :] = col_sum(grad)
        transfers(5 * LINE + 2)
        for m in range(LINE):
            below = jnp.concatenate([gv_ref[0:6, :], ggv_ref[m, 0:2, :]], axis=0)
            for s in range(PLANE):
                top = (m * PLANE + s) * 8
                side_ref[m, 0, s * 16 : s * 16 + 8, :] = acc_ref[top : top + 8, :]
                side_ref[m, 0, s * 16 + 8 : (s + 1) * 16, :] = below
            side.begin(m)
        transfers(5 * LINE + 3)
        mem.settle()
        for part in (side, attn, mlp):
            part.settle()
        for line in outs + tgs:
            line.finish()


OUT_PIECES, GRAD_PIECES = 2, 4

BACKWARD_PLAN = (
    (),
    (),
    (),
    (),
    ((5, 1, 1),),
    (),
    ((2, 0, 1),),
    ((6, 1, 1),),
    (),
    ((2, 0, 0),),
    ((2, 1, 0),),
    (),
    ((2, 0, 3),),
    ((5, 1, 2),),
    (),
    ((2, 2, 0),),
    ((1, 0, 1),),
    ((2, 0, 2), (6, 1, 2),),
    (),
    (),
    ((1, 0, 0),),
    (),
    ((8, 0, 0), (1, 0, 3), (1, 0, 2), (9, 0, 0), (10, 0, 0),),
    ((0, 0, 0), (0, 0, 1), (0, 0, 2), (0, 0, 3), (0, 1, 2), (1, 1, 2), (0, 1, 3), (1, 2, 2), (0, 2, 3), (0, 1, 1), (0, 2, 1), (0, 2, 2), (0, 1, 0), (0, 2, 0), (8, 1, 1), (1, 1, 1), (1, 2, 1), (0, 3, 1), (1, 1, 0), (1, 2, 0), (2, 1, 1), (2, 2, 1), (0, 3, 3), (0, 3, 2), (2, 1, 3), (2, 2, 3), (0, 3, 0), (2, 1, 2), (2, 2, 2), (7, 1, 1), (0, 4, 0), (3, 0, 0), (6, 1, 3), (10, 1, 1), (9, 1, 1), (5, 1, 3), (8, 1, 2), (1, 1, 3), (1, 2, 3), (2, 3, 0), (1, 3, 2), (3, 1, 0), (10, 1, 2), (1, 3, 0), (2, 3, 1), (7, 1, 2), (9, 1, 2), (2, 3, 3), (3, 2, 0), (3, 3, 0), (1, 3, 3), (2, 3, 2), (1, 3, 1), (4, 0, 0), (7, 1, 3), (8, 1, 3), (9, 1, 3), (10, 1, 3), (2, 4, 0), (1, 4, 0),),
)


def backward_pass(tokens, cots, out, meta, vec, inverse, coef, saved, wide, items, past_shape, head):
    res, hmt, h2t, prob, keys, vals, query, att, act, slope = saved
    rows, width = out.shape
    local = width // LINE
    hidden = wide[1].shape[2]
    heads = local // head
    keyed = NB + rows
    first = lambda i: jnp.minimum(i, LINE - 1)
    second = lambda i: jnp.maximum(i - LINE, 0)
    anywhere = pl.BlockSpec(memory_space=pl.ANY)
    vmem = pl.BlockSpec(memory_space=pltpu.VMEM)
    dma = pltpu.SemaphoreType.DMA
    shape = jax.ShapeDtypeStruct
    part = width // PLANE
    blocks = ((1, 16, width), (1, part, width), (2, part, width))
    kinds = (F32, BF, BF)
    pieces = OUT_PIECES + GRAD_PIECES
    return pl.pallas_call(
        functools.partial(backward_kernel, head=head),
        grid=(2 * LINE,),
        in_specs=[anywhere] * 7
        + [vmem] * 6
        + [
            pl.BlockSpec((1, heads, keyed, rows), lambda i: (second(i), 0, 0, 0)),
            pl.BlockSpec((1, keyed, local), lambda i: (second(i), 0, 0)),
            pl.BlockSpec((1, keyed, local), lambda i: (second(i), 0, 0)),
            pl.BlockSpec((1, rows, local), lambda i: (second(i), 0, 0)),
            pl.BlockSpec((1, local, rows), lambda i: (second(i), 0, 0)),
            pl.BlockSpec((1, rows, hidden), lambda i: (first(i), 0, 0)),
            pl.BlockSpec((1, rows, hidden), lambda i: (first(i), 0, 0)),
        ],
        out_specs=[anywhere, anywhere] + [vmem] * 8,
        out_shape=[
            shape((LINE, rows, width), BF),
            shape((LINE, rows, width), BF),
            shape(past_shape, F32),
            shape((8, part), F32),
            shape((local // head, 2, head // PLANE), F32),
            shape((head // PLANE, hidden // head), F32),
            shape((3, part, local), F32),
            shape((local, part), F32),
            shape((part, hidden), F32),
            shape((part, hidden), F32),
        ],
        scratch_shapes=[
            pltpu.VMEM((rows, width), BF),
            pltpu.VMEM((rows, width), BF),
            pltpu.VMEM((width, rows), BF),
            pltpu.VMEM((rows, width), F32),
            pltpu.VMEM((keyed, width), F32),
            pltpu.VMEM((keyed, 3 * local), BF),
            pltpu.VMEM((8, width), F32),
            pltpu.VMEM((LINE, 8, hidden), F32),
            pltpu.VMEM((LINE, PLANE * 8, width), F32),
            pltpu.VMEM((2, 2, width, width), BF),
        ]
        + [pltpu.VMEM((LINE, b[0], PLANE * b[1], b[2]), t) for b, t in zip(blocks, kinds)]
        + [pltpu.VMEM((8, width), F32)]
        + [pltpu.VMEM(b, F32) for b in blocks]
        + [pltpu.VMEM(lead + b, t) for lead in BUFFERS for b, t in zip(blocks, kinds)]
        + [
            dma((3, 2, 4, LINE)),
            dma((3, 9, LINE)),
            dma((pieces, 2, LINE)),
            dma((pieces, LINE)),
            dma((pieces,)),
            dma((5, LINE * 4)),
            dma((LINE * PLANE,)),
            dma(()),
            dma((4, 2)),
        ],
        compiler_params=pltpu.CompilerParams(
            collective_id=2, has_side_effects=True, vmem_limit_bytes=MAX_VMEM
        ),
        name="backward_pass",
    )(
        tokens,
        cots,
        out,
        res,
        *wide,
        vec,
        hmt,
        h2t,
        coef,
        inverse,
        meta,
        prob,
        keys,
        vals,
        query,
        att,
        act,
        slope,
    )


def plain_backward_kernel(
    tok_ref,
    cot_ref,
    res_ref,
    vec_ref,
    hm_ref,
    h2_ref,
    prob_ref,
    key_ref,
    val_ref,
    query_ref,
    att_ref,
    act_ref,
    slope_ref,
    wa_ref,
    wu_ref,
    wd_ref,
    tg_ref,
    gmem_ref,
    gup_ref,
    gdown_ref,
    gatt_ref,
    gv_ref,
    ggv_ref,
    acc_ref,
    hmt_ref,
    h2t_ref,
    cott_ref,
    gres_ref,
    proj_ref,
    *,
    groups,
    head,
):
    step = pl.program_id(0)
    rows, width = tok_ref.shape
    local = query_ref.shape[2]

    @pl.when(step == 0)
    def _():
        acc_ref[...] = jnp.zeros_like(acc_ref)
        h2t_ref[...] = h2_ref[...].T
        cott_ref[...] = cot_ref[...].T
        gv_ref[...] = jnp.zeros_like(gv_ref)

    @pl.when(step < groups)
    def _():
        upstream = cot_ref[...]
        grad = (dot(upstream, wd_ref[0]) * slope_ref[0].astype(F32)).astype(BF)
        gdown_ref[0] = dot(cott_ref[...], act_ref[0]).astype(BF)
        gup_ref[0] = dot(h2t_ref[...], grad).astype(BF)
        ggv_ref[0] = jnp.zeros_like(ggv_ref[0])
        ggv_ref[0, 0:1, :] = col_sum(grad.astype(F32))
        acc_ref[NB:, :] += dot_nt(grad, wu_ref[0])

    @pl.when(step == groups)
    def _():
        upstream = cot_ref[...].astype(F32)
        normed, inverse = norm_parts(res_ref[...])
        grad = acc_ref[NB:, :]
        g_res = upstream + norm_back(grad, normed, inverse, vec_ref[2:3, :])
        gres_ref[...] = g_res
        g_attn = g_res.astype(BF)
        gv_ref[2:3, :] = col_sum(grad * normed)
        gv_ref[3:4, :] = col_sum(grad)
        gv_ref[4:5, :] = col_sum(g_attn.astype(F32))
        gv_ref[5:6, :] = col_sum(upstream)
        cott_ref[...] = g_attn.T
        hmt_ref[...] = hm_ref[...].T
        acc_ref[...] = jnp.zeros_like(acc_ref)
        proj_ref[0:NB, :] = jnp.zeros((NB, proj_ref.shape[1]), BF)

    @pl.when(step >= groups)
    def _():
        weights = wa_ref[0]
        g_attn = gres_ref[...].astype(BF)
        g_att = dot(g_attn, weights[:, 3 * local :]).astype(BF)
        att_t = att_ref[0]
        query_grad, key_grad, val_grad = attend_back(
            g_att,
            att_t,
            key_ref[0],
            val_ref[0],
            query_ref[0],
            lambda h, lines, columns: prob_ref[0, h, lines, columns],
            head,
            lambda h: None,
        )
        key_grad, val_grad = key_grad.astype(BF), val_grad.astype(BF)
        proj_ref[NB:, 0:local] = query_grad
        proj_ref[:, local : 2 * local] = key_grad
        proj_ref[:, 2 * local :] = val_grad
        proj = proj_ref[...]
        ggv_ref[0] = jnp.zeros_like(ggv_ref[0])
        ggv_ref[0, 0:1, 0 : 3 * local] = col_sum(proj.astype(F32))
        gatt_ref[0, :, 0 : 3 * local] = dot(hmt_ref[...], proj).astype(BF)
        gatt_ref[0, :, 3 * local :] = dot_nt(cott_ref[...], att_t).astype(BF)
        acc_ref[...] += dot_nt(proj, weights[:, : 3 * local])

    @pl.when(step == 2 * groups - 1)
    def _():
        gmem_ref[...] = acc_ref[0:NB, :]
        grad = acc_ref[NB:, :]
        normed, inverse = norm_parts(tok_ref[...].astype(F32))
        part = norm_back(grad, normed, inverse, vec_ref[0:1, :])
        tg_ref[...] = (gres_ref[...] + part).astype(BF)
        gv_ref[0:1, :] = col_sum(grad * normed)
        gv_ref[1:2, :] = col_sum(grad)


def plain_backward(tok, cot, vec, saved, wide, head):
    res, hm, h2, prob, keys, vals, query, att, act, slope = saved
    rows, width = tok.shape
    groups = wide[0].shape[0]
    local = width // groups
    hidden = wide[1].shape[2]
    heads = local // head
    keyed = NB + rows
    first = lambda i: jnp.minimum(i, groups - 1)
    second = lambda i: jnp.maximum(i - groups, 0)
    whole = lambda shape: pl.BlockSpec(shape, lambda i: (0,) * len(shape))
    return pl.pallas_call(
        functools.partial(plain_backward_kernel, groups=groups, head=head),
        grid=(2 * groups,),
        in_specs=[
            whole((rows, width)),
            whole((rows, width)),
            whole((rows, width)),
            whole((16, width)),
            whole((keyed, width)),
            whole((rows, width)),
            pl.BlockSpec((1, heads, keyed, rows), lambda i: (second(i), 0, 0, 0)),
            pl.BlockSpec((1, keyed, local), lambda i: (second(i), 0, 0)),
            pl.BlockSpec((1, keyed, local), lambda i: (second(i), 0, 0)),
            pl.BlockSpec((1, rows, local), lambda i: (second(i), 0, 0)),
            pl.BlockSpec((1, local, rows), lambda i: (second(i), 0, 0)),
            pl.BlockSpec((1, rows, hidden), lambda i: (first(i), 0, 0)),
            pl.BlockSpec((1, rows, hidden), lambda i: (first(i), 0, 0)),
            pl.BlockSpec((1, width, width), lambda i: (second(i), 0, 0)),
            pl.BlockSpec((1, width, hidden), lambda i: (first(i), 0, 0)),
            pl.BlockSpec((1, width, hidden), lambda i: (first(i), 0, 0)),
        ],
        out_specs=[
            whole((rows, width)),
            whole((NB, width)),
            pl.BlockSpec((1, width, hidden), lambda i: (first(i), 0, 0)),
            pl.BlockSpec((1, width, hidden), lambda i: (first(i), 0, 0)),
            pl.BlockSpec((1, width, width), lambda i: (second(i), 0, 0)),
            whole((8, width)),
            pl.BlockSpec((1, 8, hidden), lambda i: (i, 0, 0)),
        ],
        out_shape=[
            jax.ShapeDtypeStruct((rows, width), BF),
            jax.ShapeDtypeStruct((NB, width), F32),
            jax.ShapeDtypeStruct((groups, width, hidden), BF),
            jax.ShapeDtypeStruct((groups, width, hidden), BF),
            jax.ShapeDtypeStruct((groups, width, width), BF),
            jax.ShapeDtypeStruct((8, width), F32),
            jax.ShapeDtypeStruct((2 * groups, 8, hidden), F32),
        ],
        scratch_shapes=[
            pltpu.VMEM((keyed, width), F32),
            pltpu.VMEM((width, keyed), BF),
            pltpu.VMEM((width, rows), BF),
            pltpu.VMEM((width, rows), BF),
            pltpu.VMEM((rows, width), F32),
            pltpu.VMEM((keyed, 3 * local), BF),
        ],
        compiler_params=pltpu.CompilerParams(vmem_limit_bytes=BIG_VMEM),
        name="plain_backward",
    )(
        tok, cot, res, vec, hm, h2, prob, keys, vals, query, att, act, slope, *wide
    )


def hand_over_kernel(*refs):
    half = len(refs) // 2
    for src, dst in zip(refs[:2], refs[half : half + 2]):
        dst[...] = src[0]

    @pl.when(pl.program_id(0) == 0)
    def _():
        for src, dst in zip(refs[2:half], refs[half + 2 :]):
            dst[...] = src[...]


def hand_over(rows, others):
    count, n, width = rows[0].shape
    whole = [pl.BlockSpec(a.shape, lambda i, r=a.ndim: (0,) * r) for a in others]
    return pl.pallas_call(
        hand_over_kernel,
        grid=(count,),
        in_specs=[pl.BlockSpec((1, n, width), lambda i: (i, 0, 0))] * len(rows) + whole,
        out_specs=[pl.BlockSpec((n, width), lambda i: (i, 0))] * len(rows) + whole,
        out_shape=[jax.ShapeDtypeStruct((count * n, width), a.dtype) for a in rows]
        + [jax.ShapeDtypeStruct(a.shape, a.dtype) for a in others],
        name="hand_over",
    )(*rows, *others)


def local(
    tokens,
    cotangent,
    past_state,
    positions,
    counts,
    ln1_gain,
    ln1_bias,
    w_qkv,
    b_qv,
    w_out,
    b_out,
    ln2_gain,
    ln2_bias,
    w_up,
    b_up,
    w_down,
    b_down,
):
    seq, mp = lax.axis_size("seq"), lax.axis_size("mp")
    seq_index, mp_index = lax.axis_index("seq"), lax.axis_index("mp")
    item_count, seg_len, local_width = past_state.shape
    slots = positions.shape[1]
    total = item_count * seq
    width = tokens.shape[1]
    part = width // seq
    heads_local, piece = b_qv.shape[1], b_qv.shape[2]
    head = piece * seq
    hidden = w_up.shape[1]
    rows = tokens.shape[0] // mp
    direct = seq == PLANE and mp == LINE and part % 16 == 0 and hidden == width

    past_t = past_state.transpose(0, 2, 1)

    vectors = jnp.stack([ln1_gain, ln1_bias, ln2_gain, ln2_bias, b_out, b_down])
    if direct:
        results = forward_pass(
            tokens,
            past_t,
            positions,
            counts,
            vectors,
            b_qv.transpose(1, 0, 2),
            b_up.T,
            w_qkv,
            w_out,
            w_up,
            w_down.T,
            head,
        )
        wide, forward, (vec, inverse, coef, meta) = results[:3], results[3:14], results[14:]
        block_out, block_grad, *others = backward_pass(
            tokens,
            cotangent,
            forward[0],
            meta,
            vec,
            inverse,
            coef,
            forward[1:],
            wide,
            item_count,
            past_t.shape,
            head,
        )
        vec_own = others.pop(1)
        (block_out, block_grad, past_grad, bias, bias_up, qkv_grad, out_grad, *mlp) = hand_over(
            [block_out, block_grad], others
        )
        qv, up, (up_grad, down_grad) = bias.transpose(1, 0, 2), bias_up.T, mlp
    else:
        items = (seq_index * item_count + jnp.arange(item_count)).astype(F32)
        spots = positions.astype(F32)
        places = (items[:, None] + (spots + 0.5) / seg_len) / total
        used = (jnp.arange(slots)[None, :] < counts[:, None]).astype(F32)
        meta = jnp.concatenate([places, used, spots, jnp.zeros((8 - 3 * item_count, slots), F32)])

        here = (jnp.arange(seq) == seq_index).astype(BF)
        vectors = (vectors[:, None, :] * here[None, :, None]).reshape(6, width)
        bias_qv = (b_qv[:, :, None, :] * here[None, None, :, None]).reshape(2, local_width)
        bias_qv = jnp.concatenate([bias_qv, jnp.zeros((2, local_width), BF)], axis=1)
        bias_up = (b_up[:, None, :] * here[None, :, None]).reshape(1, hidden)
        room = jnp.concatenate(
            [vectors, bias_qv.reshape(1, width), bias_up, jnp.zeros((8, width), BF)]
        )
        attn = jnp.concatenate([w_qkv[0], w_qkv[1], w_qkv[2], w_out.T], axis=1)
        sampled = sample_rows(past_t, meta)
        all_sampled = lax.all_gather(sampled, "seq", axis=0)
        all_meta = lax.all_gather(meta, "seq", axis=0)
        coef_part, inverse = solve_memory(all_sampled, all_meta, item_count)
        coef = lax.all_gather(coef_part, "mp", axis=0).transpose(1, 0, 2).reshape(NB, width)
        wide = [
            lax.all_gather(lax.all_gather(shard, "seq", axis=0, tiled=True), "mp", axis=0)
            for shard in (attn, w_up, w_down.T)
        ]
        vec = lax.psum(room.astype(F32), "seq")
        vec = lax.all_gather(vec, "mp", axis=0)
        tok = lax.dynamic_slice_in_dim(tokens, mp_index * rows, rows, 0)
        cot = lax.dynamic_slice_in_dim(cotangent, mp_index * rows, rows, 0)
        forward = plain_forward(tok, coef, vec, wide, head)
        block_out = lax.all_gather(forward[0], "mp", axis=0, tiled=True)
        tok_grad, gmem, g_up, g_down, g_attn, gv, ggv = plain_backward(
            tok, cot, vec[0], forward[1:], wide, head
        )
        tail = jnp.concatenate(
            [jnp.broadcast_to(gv[None, :6], (mp, 6, width)), ggv[mp:, :1], ggv[:mp, :1]], axis=1
        )
        block_grad = lax.all_gather(tok_grad, "mp", axis=0, tiled=True)
        gmem, tail = lax.psum((gmem, tail), ("seq", "mp"))
        own = lax.dynamic_index_in_dim(tail, mp_index, 0, keepdims=False)
        attn, up_grad, down_grad = (
            lax.psum_scatter(
                lax.psum_scatter(g, "mp", scatter_dimension=0, tiled=False),
                "seq",
                scatter_dimension=0,
                tiled=True,
            ).astype(F32)
            for g in (g_attn, g_up, g_down)
        )
        past_grad, gv_mem = past_grads(
            gmem, coef, vec, inverse, meta, item_count, seg_len, local_width
        )
        own = own + jnp.concatenate([gv_mem[:2], jnp.zeros((6, width), F32)])
        vec_own = lax.dynamic_slice_in_dim(own[:6], seq_index * part, part, 1)
        qv = jnp.stack([own[6, :local_width], own[6, 2 * local_width : 3 * local_width]])
        qv = qv.reshape(2, heads_local, head)
        qv = lax.dynamic_slice_in_dim(qv, seq_index * piece, piece, 2)
        up = lax.dynamic_slice_in_dim(own[7].reshape(-1, head), seq_index * piece, piece, 1)
        qkv_grad = jnp.stack([attn[:, i * local_width : (i + 1) * local_width] for i in range(3)])
        out_grad = attn[:, 3 * local_width :].T
    return (
        block_out,
        block_grad,
        past_grad.transpose(0, 2, 1),
        vec_own[0],
        vec_own[1],
        qkv_grad,
        qv,
        out_grad,
        vec_own[4],
        vec_own[2],
        vec_own[3],
        up_grad,
        up,
        down_grad.T,
        vec_own[5],
    )


def solution(mesh):
    row = P("seq", None)
    placed = (
        row,
        row,
        P("seq", None, "mp"),
        row,
        P("seq"),
        P("seq"),
        P("seq"),
        P(None, "seq", "mp"),
        P(None, "mp", "seq"),
        P("mp", "seq"),
        P("seq"),
        P("seq"),
        P("seq"),
        P("seq", "mp"),
        P("mp", "seq"),
        P("mp", "seq"),
        P("seq"),
    )
    return jax.shard_map(
        local,
        mesh=mesh,
        in_specs=placed,
        out_specs=(row, row, placed[2]) + placed[5:],
        check_vma=False,
    )
```

```python
import functools
import math

import jax
import jax.numpy as jnp
from jax import lax
from jax.experimental import pallas as pl
from jax.experimental.pallas import tpu as pltpu
from jax.sharding import PartitionSpec as P

NB = 256
PIVOTS = 32
NORM_EPSILON = 1e-05
RIDGE_WEIGHT = 1.0
NARROW_WIDTH = 0.01
BROAD_WIDTH = 0.05
GELU_SCALE = 0.7978845608028654
GELU_CUBIC = 0.044715

BF = jnp.bfloat16
F32 = jnp.float32
HIGHEST = lax.Precision.HIGHEST
BIG_VMEM = 60 * 1024 * 1024
MAX_VMEM = 67043328


def dot(a, b):
    return jnp.dot(a, b, preferred_element_type=F32)


def dot_nt(a, b):
    return lax.dot_general(a, b, (((1,), (1,)), ((), ())), preferred_element_type=F32)


def dot_tn(a, b, precision=None):
    return lax.dot_general(
        a, b, (((0,), (0,)), ((), ())), preferred_element_type=F32, precision=precision
    )


def norm_parts(values):
    centered = values - jnp.mean(values, axis=-1, keepdims=True)
    inverse = lax.rsqrt(jnp.mean(centered * centered, axis=-1, keepdims=True) + NORM_EPSILON)
    return centered * inverse, inverse


def norm_back(upstream, normed, inverse, gain):
    scaled = upstream * gain
    inner = scaled - jnp.mean(scaled, axis=-1, keepdims=True)
    inner = inner - normed * jnp.mean(scaled * normed, axis=-1, keepdims=True)
    return inner * inverse


def col_sum(values):
    return jnp.sum(values, axis=0, keepdims=True)


def basis_of(places, used):
    column = lax.broadcasted_iota(jnp.int32, (places.shape[0], NB), 1)
    centers = (column.astype(F32) + 0.5) / NB
    widths = jnp.where(column % 2 == 0, NARROW_WIDTH, BROAD_WIDTH).astype(F32)
    scaled = (places - centers) / widths
    return jnp.exp(-0.5 * (scaled * scaled)) * used


def meta_rows(positions, counts_ref, first, total, seg_len):
    items, slots = positions.shape
    slot = lax.broadcasted_iota(jnp.int32, (1, slots), 1)
    places, used, spots = [], [], []
    for i in range(items):
        spot = positions[i : i + 1, :].astype(F32)
        item = (first + i).astype(F32)
        places.append((item + (spot + 0.5) / seg_len) / total)
        used.append((slot < counts_ref[i]).astype(F32))
        spots.append(spot)
    return jnp.concatenate(
        places + used + spots + [jnp.zeros((8 - 3 * items, slots), F32)], axis=0
    )


def iotas(shape):
    return lax.broadcasted_iota(jnp.int32, shape, 0), lax.broadcasted_iota(jnp.int32, shape, 1)


def small_rows(stack, b_qv, b_up_t, s, width, head):
    part, piece = stack.shape[1], b_up_t.shape[0]
    row, lane = iotas((part, width))
    rows = [jnp.dot(stack, (lane == s * part + row).astype(F32), preferred_element_type=F32)]
    row, lane = iotas((piece, width))
    repeat = (lax.rem(lane, piece) == row).astype(F32)
    _, lane = iotas((1, width))
    half = width // 2
    bias = jnp.zeros((1, width), F32)
    for h in range(b_qv.shape[0]):
        spread = jnp.dot(b_qv[h], repeat, preferred_element_type=F32)
        for t in range(2):
            at = h * head + t * half + s * piece
            bias = bias + jnp.where((lane >= at) & (lane < at + piece), spread[t : t + 1], 0.0)
    row, lane = iotas((b_up_t.shape[1], width))
    spread = jnp.dot(b_up_t, (lane // head == row).astype(F32), preferred_element_type=F32)
    row, lane = iotas((piece, width))
    up = jnp.sum(jnp.where(lax.rem(lane, head) == s * piece + row, spread, 0.0), axis=0, keepdims=True)
    return jnp.concatenate(rows + [bias, up, jnp.zeros((8, width), F32)], axis=0).astype(BF)


def small_pieces(own, s, part, piece, head, heads):
    width = own.shape[1]
    half = width // 2
    row, lane = iotas((width, part + 2 * heads * piece))
    slot = lane - part
    spot = (slot // (2 * piece)) * head + (lax.rem(slot, 2 * piece) // piece) * half
    source = jnp.where(lane < part, s * part + lane, spot + s * piece + lax.rem(slot, piece))
    picked = jnp.dot(
        own, (row == source).astype(F32), preferred_element_type=F32, precision=HIGHEST
    )
    at = [part + i * piece for i in range(2 * heads)]
    flat = [picked[6:7, i : i + piece] for i in at]
    biases = [jnp.concatenate(flat[2 * h : 2 * h + 2], axis=0) for h in range(heads)]
    row, lane = iotas((piece, width))
    masked = jnp.where(lax.rem(lane, head) == s * piece + row, own[7:8], 0.0)
    row, lane = iotas((width, width // head))
    up = jnp.dot(
        masked, (row // head == lane).astype(F32), preferred_element_type=F32, precision=HIGHEST
    )
    return picked[:, :part], biases, up


def position_of(column, i, items):
    return column[:, 2 * items + i : 2 * items + i + 1].astype(jnp.int32)


def inverse_2(a, b, c, d):
    scale = 1.0 / (a * d - b * c)
    return d * scale, -(b * scale), -(c * scale), a * scale


def product_2(x, y):
    return (
        x[0] * y[0] + x[1] * y[2],
        x[0] * y[1] + x[1] * y[3],
        x[2] * y[0] + x[3] * y[2],
        x[2] * y[1] + x[3] * y[3],
    )


def invert_step(mat_ref):
    block = PIVOTS
    lane = lax.broadcasted_iota(jnp.int32, (block, NB), 1)
    line = lax.broadcasted_iota(jnp.int32, (block, NB), 0)
    panel = mat_ref[0:block, :]
    for k in range(0, block, 4):
        cols = [jnp.broadcast_to(panel[:, k + j : k + j + 1], panel.shape) for j in range(4)]
        at = [[cols[j][k + i : k + i + 1] for j in range(4)] for i in range(4)]
        head = inverse_2(at[0][0], at[0][1], at[1][0], at[1][1])
        upper = (at[0][2], at[0][3], at[1][2], at[1][3])
        lower = (at[2][0], at[2][1], at[3][0], at[3][1])
        right, left = product_2(head, upper), product_2(lower, head)
        minus = product_2(lower, right)
        tail = inverse_2(
            at[2][2] - minus[0], at[2][3] - minus[1], at[3][2] - minus[2], at[3][3] - minus[3]
        )
        rt, tl = product_2(right, tail), product_2(tail, left)
        back = product_2(rt, left)
        inverse = (
            (head[0] + back[0], head[1] + back[1], -rt[0], -rt[1]),
            (head[2] + back[2], head[3] + back[3], -rt[2], -rt[3]),
            (-tl[0], -tl[1], tail[0], tail[1]),
            (-tl[2], -tl[3], tail[2], tail[3]),
        )
        inside = (lane >= k) & (lane < k + 4)
        rows = [
            jnp.where(inside[0:1], (lane[0:1] == k + j).astype(F32), panel[k + j : k + j + 1])
            for j in range(4)
        ]
        new = [
            (m[0] * rows[0] + m[1] * rows[1]) + (m[2] * rows[2] + m[3] * rows[3]) for m in inverse
        ]
        rest = jnp.where(inside, 0.0, panel) - (
            (cols[0] * new[0] + cols[1] * new[1]) + (cols[2] * new[2] + cols[3] * new[3])
        )
        for i in range(4):
            rest = jnp.where(line == k + i, new[i], rest)
        panel = rest
    mat_ref[0:block, :] = panel
    row = lax.broadcasted_iota(jnp.int32, (NB, NB), 0)
    col = lax.broadcasted_iota(jnp.int32, (NB, NB), 1)
    mat = mat_ref[...]
    inside_row = row < block
    inside_col = col < block
    left = jnp.where(inside_col & ~inside_row, mat, 0.0)
    right = jnp.where(inside_row, mat, 0.0)
    update = jnp.dot(left, right, preferred_element_type=F32, precision=HIGHEST)
    mat = jnp.where(inside_row, mat, jnp.where(inside_col, 0.0, mat) - update)
    mat = pltpu.roll(mat, NB - block, 1)
    mat_ref[0 : NB - block, :] = mat[block:, :]
    mat_ref[NB - block :, :] = mat[:block, :]


def owner_basis(meta, items):
    column = meta.T
    rows = [
        basis_of(column[:, i : i + 1], column[:, items + i : items + i + 1]) for i in range(items)
    ]
    return jnp.concatenate(rows, axis=0)


def clear_moments(mat_ref, mom_ref):
    row = lax.broadcasted_iota(jnp.int32, (NB, NB), 0)
    col = lax.broadcasted_iota(jnp.int32, (NB, NB), 1)
    mat_ref[...] = jnp.where(row == col, RIDGE_WEIGHT, 0.0)
    mom_ref[...] = jnp.zeros_like(mom_ref)


def coefficients(mat_ref, mom_ref):
    return jnp.dot(mat_ref[...], mom_ref[...], preferred_element_type=F32, precision=HIGHEST)


def pick_samples(past, meta, items):
    slots, seg_len = meta.shape[1], past.shape[2]
    column = meta.T
    at = lax.broadcasted_iota(jnp.int32, (slots, seg_len), 1)
    rows = []
    for i in range(items):
        pick = (at == position_of(column, i, items)).astype(F32).astype(BF)
        rows.append(dot_nt(pick, past[i]).astype(BF))
    return jnp.concatenate(rows, axis=0)


def sample_kernel(past_ref, meta_ref, out_ref, *, items):
    out_ref[...] = pick_samples(past_ref[...], meta_ref[...], items)


def sample_rows(past, meta):
    items, width, seg_len = past.shape
    return pl.pallas_call(
        functools.partial(sample_kernel, items=items),
        out_shape=jax.ShapeDtypeStruct((items * meta.shape[1], width), BF),
        name="sample_rows",
    )(past, meta)


def solve_kernel(sampled_ref, meta_ref, coef_ref, inv_ref, mat_ref, mom_ref, *, items):
    clear_moments(mat_ref, mom_ref)

    def owner(s, carry):
        rows = owner_basis(meta_ref[s], items)
        mat_ref[...] += dot_tn(rows, rows, HIGHEST)
        mom_ref[...] += dot_tn(rows, sampled_ref[s].astype(F32), HIGHEST)
        return carry

    lax.fori_loop(0, meta_ref.shape[0], owner, 0)

    def step(s, carry):
        invert_step(mat_ref)
        return carry

    lax.fori_loop(0, NB // PIVOTS, step, 0)
    inv_ref[...] = mat_ref[...]
    coef_ref[...] = coefficients(mat_ref, mom_ref).astype(BF)


def solve_memory(sampled, meta, items):
    width = sampled.shape[-1]
    return pl.pallas_call(
        functools.partial(solve_kernel, items=items),
        out_shape=(
            jax.ShapeDtypeStruct((NB, width), BF),
            jax.ShapeDtypeStruct((NB, NB), F32),
        ),
        scratch_shapes=[pltpu.VMEM((NB, NB), F32), pltpu.VMEM((NB, width), F32)],
        compiler_params=pltpu.CompilerParams(vmem_limit_bytes=BIG_VMEM),
        name="solve_memory",
    )(sampled, meta)


def give_past(gmem, coef_ref, vec_ref, inv_ref, meta_ref, out_ref, gv_ref):
    slots = meta_ref.shape[1]
    item_count, width, seg_len = out_ref.shape
    normed, inverse = norm_parts(coef_ref[...].astype(F32))
    coef_grad = norm_back(gmem, normed, inverse, vec_ref[0, 0:1, :])
    gv_ref[...] = jnp.zeros_like(gv_ref)
    gv_ref[0:1, :] = col_sum(gmem * normed)
    gv_ref[1:2, :] = col_sum(gmem)
    part = lax.axis_index("mp")
    mine = jnp.zeros((coef_grad.shape[0], width), F32)
    for m in range(coef_grad.shape[1] // width):
        mine = jnp.where(part == m, coef_grad[:, m * width : (m + 1) * width], mine)
    moment = jnp.dot(inv_ref[...], mine, preferred_element_type=F32, precision=HIGHEST)
    at = lax.broadcasted_iota(jnp.int32, (slots, seg_len), 1)
    column = meta_ref[...].T
    for i in range(item_count):
        rows = basis_of(column[:, i : i + 1], column[:, item_count + i : item_count + i + 1])
        sampled = jnp.dot(rows, moment, preferred_element_type=F32, precision=HIGHEST)
        spread = (at == position_of(column, i, item_count)).astype(F32)
        out_ref[i] = dot_tn(sampled, spread, HIGHEST)


def past_kernel(gmem_ref, coef_ref, vec_ref, inv_ref, meta_ref, out_ref, gv_ref):
    give_past(gmem_ref[...], coef_ref, vec_ref, inv_ref, meta_ref, out_ref, gv_ref)


def past_grads(gmem, coef, vec, inv, meta, items, seg_len, width):
    return pl.pallas_call(
        past_kernel,
        out_shape=(
            jax.ShapeDtypeStruct((items, width, seg_len), F32),
            jax.ShapeDtypeStruct((8, coef.shape[1]), F32),
        ),
        compiler_params=pltpu.CompilerParams(vmem_limit_bytes=BIG_VMEM),
        name="past_grads",
    )(gmem, coef, vec, inv, meta)


MESH = pl.DeviceIdType.MESH
LINE = 4
PLANE = 8
NEAR = (0, -1, 1, -2, 2, -3, 3)


class Place:
    def __init__(self):
        self.s = lax.axis_index("seq")
        self.z = lax.axis_index("mp")
        core = lax.rem(self.s, 2)
        x = lax.rem(self.s // 2, 2)
        y = self.s // 4
        self.turn = 1 - 2 * core
        self.partner = self.s + self.turn
        self.sx = self.s + 2 - 4 * x
        self.sy = self.s + 4 - 8 * y
        self.sd = self.sx + 4 - 8 * y
        self.low = self.z > 0
        self.high = self.z < LINE - 1
        self.near = [
            (
                d,
                valid(self.z + d),
                self.z + d,
                lax.rem(self.z + d + LINE, 2) == 1,
                lax.rem(self.z + d + LINE, 2) == 0,
            )
            for d in NEAR
        ]


def valid(m):
    return (m >= 0) & (m < LINE)


def when(conditions, act):
    conditions = [c for c in conditions if c is not None]
    if conditions:
        pl.when(functools.reduce(lambda a, b: a & b, conditions))(act)
    else:
        act()


def greet(place, whole_line=False):
    barrier = pltpu.get_barrier_semaphore()

    def signal(seq, z):
        pl.semaphore_signal(barrier, inc=1, device_id=(seq, z), device_id_type=MESH)

    for seq in (place.partner, place.sx, place.sy):
        signal(seq, place.z)
    for d, ok, m, odd, even in place.near[1:]:
        if whole_line or abs(d) == 1:
            when((ok,), lambda: signal(place.s, m))
    if whole_line:
        peers = LINE - 1
    else:
        peers = (place.z + LINE - 1) // LINE + (2 * LINE - 2 - place.z) // LINE
    pl.semaphore_wait(barrier, 3 + peers)


UP, DOWN, ACROSS_X, ACROSS_Y, PARTNER = range(5)


class Spread:
    def __init__(self, place, src, dst, send, recv, local, line=True):
        self.p, self.src, self.dst = place, src, dst
        self.send, self.recv, self.line = send, recv, line
        self.rows = src.shape[0]
        self.sent = []
        self.mine = place.z if line else 0
        self.around = place.near if line else [(0, None, 0, None, None)]
        self.own = pltpu.make_async_copy(src, self.at(self.mine, place.s), local)

    def at(self, m, s):
        return self.dst.at[m, pl.ds(s * self.rows, self.rows), :]

    def copy(self, direction, m, s, own=False):
        p = self.p
        device = (
            (p.s, p.z + 1),
            (p.s, p.z - 1),
            (p.sx, p.z),
            (p.sy, p.z),
            (p.partner, p.z),
        )[direction]
        return pltpu.make_async_remote_copy(
            src_ref=self.src if own else self.at(m, s),
            dst_ref=self.at(m, s),
            send_sem=self.send.at[direction, m * 4 + s // 2],
            recv_sem=self.recv.at[m * PLANE + s],
            device_id=device,
            device_id_type=MESH,
        )

    def start(self, conditions, *what, **how):
        when(conditions, lambda: self.copy(*what, **how).start())
        self.sent.append((conditions, what, how))

    def arrived(self, m, s):
        self.copy(PARTNER, m, s).wait_recv()

    def first(self):
        p, m = self.p, self.mine
        self.own.start()
        if self.line:
            self.start((p.high,), UP, m, p.s, own=True)
            self.start((p.low,), DOWN, m, p.s, own=True)
        for direction in (ACROSS_X, ACROSS_Y, PARTNER):
            self.start((), direction, m, p.s, own=True)

    def along(self, d, ok, m, odd, even):
        p = self.p
        when((ok,), lambda: self.arrived(m, p.s))
        if d < 0:
            self.start((ok, p.high), UP, m, p.s)
        else:
            self.start((ok, p.low), DOWN, m, p.s)
        for direction in (ACROSS_X, ACROSS_Y, PARTNER):
            self.start((ok,), direction, m, p.s)

    def across(self, d, ok, m, odd, even):
        p = self.p
        when((ok,), lambda: self.arrived(m, p.sx))
        if self.line:
            self.start((ok, odd), ACROSS_Y, m, p.sx)
        self.start((ok,), PARTNER, m, p.sx)
        when((ok,), lambda: self.arrived(m, p.sy))
        if self.line:
            self.start((ok, even), ACROSS_X, m, p.sy)
        else:
            self.start((), ACROSS_X, m, p.sy)
        self.start((ok,), PARTNER, m, p.sy)

    def corner(self, d, ok, m, odd, even):
        p = self.p
        when((ok,), lambda: self.arrived(m, p.sd))
        self.start((ok,), PARTNER, m, p.sd)

    def part(self, kind, d):
        if kind == 0:
            return self.first
        act = (self.along, self.across, self.corner)[kind - 1]
        return functools.partial(act, *self.around[NEAR.index(d)])

    def steps(self, kind):
        return [self.part(kind, d) for d in NEAR if d or kind > 1]

    def close(self, m):
        p = self.p
        for s in (p.s, p.sx, p.sy, p.sd):
            self.arrived(m, s + p.turn)

    def settle(self):
        for conditions, what, how in self.sent:
            when(conditions, lambda: self.copy(*what, **how).wait_send())


class DirectSpread(Spread):
    def throw(self, m):
        p = self.p
        return pltpu.make_async_remote_copy(
            src_ref=self.src,
            dst_ref=self.at(self.mine, p.s),
            send_sem=self.send.at[UP, m],
            recv_sem=self.recv.at[self.mine * PLANE + p.s],
            device_id=(p.s, m),
            device_id_type=MESH,
        )

    def first(self):
        p, m = self.p, self.mine
        self.own.start()
        for d, ok, to, odd, even in self.around[1:]:
            when((ok,), lambda: self.throw(to).start())
        for direction in (ACROSS_X, ACROSS_Y, PARTNER):
            self.start((), direction, m, p.s, own=True)

    def along(self, d, ok, m, odd, even):
        when((ok,), lambda: self.arrived(m, self.p.s))
        for direction in (ACROSS_X, ACROSS_Y, PARTNER):
            self.start((ok,), direction, m, self.p.s)

    def settle(self):
        super().settle()
        for d, ok, m, odd, even in self.around[1:]:
            when((ok,), lambda: self.throw(m).wait_send())


class Line:
    def __init__(self, place, src, dst, send, recv, local):
        self.p, self.src, self.dst = place, src, dst
        self.send, self.recv = send, recv
        self.sent = []
        self.own = pltpu.make_async_copy(src, dst.at[place.z], local)

    def copy(self, up, m, own=False):
        p = self.p
        return pltpu.make_async_remote_copy(
            src_ref=self.src if own else self.dst.at[m],
            dst_ref=self.dst.at[m],
            send_sem=self.send.at[1 if up else 0, m],
            recv_sem=self.recv.at[m],
            device_id=(p.s, p.z + 1 if up else p.z - 1),
            device_id_type=MESH,
        )

    def start(self, conditions, *what, **how):
        when(conditions, lambda: self.copy(*what, **how).start())
        self.sent.append((conditions, what, how))

    def first(self):
        p = self.p
        self.own.start()
        self.start((p.high,), True, p.z, own=True)
        self.start((p.low,), False, p.z, own=True)

    def step(self, distance):
        p = self.p
        for d, ok, m, odd, even in p.near:
            if abs(d) != distance:
                continue
            when((ok,), lambda: self.copy(True, m).wait_recv())
            if d < 0:
                self.start((ok, p.high), True, m)
            else:
                self.start((ok, p.low), False, m)

    def finish_sends(self):
        for conditions, what, how in self.sent:
            when(conditions, lambda: self.copy(*what, **how).wait_send())

    def finish(self):
        self.finish_sends()
        self.own.wait()


class Collect:
    OWN, SIDE_X, SIDE_Y, CORNER = range(4)

    def __init__(self, place, grads, out, buffers, sems):
        self.p, self.grads, self.out = place, grads, out
        self.pin, self.din, self.xin, self.yin, self.zin = buffers
        self.block_sems, self.sems = sems
        self.rows = out.shape[1]
        self.columns = (place.s, place.sx, place.sy, place.sd)

    def plane(self, i):
        return i

    def unit(self, c, m, turn=0):
        s = self.columns[c] + turn
        return self.grads.at[m, :, pl.ds(s * self.rows, self.rows), :]

    def remote(self, src, dst, send, recv, device):
        return pltpu.make_async_remote_copy(
            src_ref=src,
            dst_ref=dst,
            send_sem=send,
            recv_sem=recv,
            device_id=device,
            device_id_type=MESH,
        )

    def swap(self, c, m):
        p = self.p
        return self.remote(
            self.unit(c, m, p.turn),
            self.pin.at[c, m],
            self.block_sems.at[0, c, m],
            self.block_sems.at[1, c, m],
            (p.partner, p.z),
        )

    def hop(self, kind, m, by_x=True):
        p = self.p
        src, dst, device = (
            (self.CORNER, self.din, (p.sx if by_x else p.sy, p.z)),
            (self.SIDE_X, self.xin, (p.sx, p.z)),
            (self.SIDE_Y, self.yin, (p.sy, p.z)),
        )[kind]
        return self.remote(
            self.unit(src, m),
            dst.at[m],
            self.sems.at[kind, m],
            self.sems.at[4 + kind, m],
            device,
        )

    def slot(self, m, z):
        ends = 1 // (1 + z - m)
        return m + (LINE - m) * ends

    def climb(self, m, up):
        p = self.p
        return self.remote(
            self.unit(self.OWN, m),
            self.zin.at[m if up else self.slot(m, p.z - 1)],
            self.sems.at[3, m],
            self.sems.at[7 if up else 8, m],
            (p.s, p.z + 1 if up else p.z - 1),
        )

    def climbed(self, m, up):
        zin = self.zin.at[m if up else self.slot(m, self.p.z)]
        return self.remote(
            zin, zin, self.sems.at[3, m], self.sems.at[7 if up else 8, m], (self.p.partner, self.p.z)
        )

    def add(self, c, m, *others):
        size = min(32, self.rows)
        pieces = self.rows // size

        @pl.loop(0, self.grads.shape[1] * pieces)
        def _(j):
            l = j // pieces
            at = lax.rem(j, pieces) * size
            here = pl.ds(pl.multiple_of(self.columns[c] * self.rows + at, 16), size)
            there = pl.ds(pl.multiple_of(at, 16), size)
            total = self.grads[m, l, here, :].astype(F32)
            for other in others:
                total = total + other[m, l, there, :].astype(F32)
            self.grads[m, l, here, :] = total.astype(self.grads.dtype)

    def begin(self, m):
        for c in (self.CORNER, self.SIDE_X, self.SIDE_Y, self.OWN):
            self.swap(c, m).start()

    def join(self, c, m):
        self.swap(c, m).wait_recv()
        self.add(c, m, self.pin.at[c])

    def corner(self, i):
        m = self.plane(i)
        self.join(self.CORNER, m)
        even = lax.rem(m, 2) == 0
        pl.when(even)(lambda: self.hop(0, m, True).start())
        pl.when(~even)(lambda: self.hop(0, m, False).start())

    def sides(self, i):
        m = self.plane(i)
        even = lax.rem(m, 2) == 0
        self.join(self.SIDE_X, m)
        self.join(self.SIDE_Y, m)
        pl.when(even)(lambda: self.hop(1, m).start())
        pl.when(~even)(lambda: self.hop(2, m).start())

    def relay(self, i):
        m = self.plane(i)
        even = lax.rem(m, 2) == 0
        self.hop(0, m).wait_recv()

        @pl.when(even)
        def _():
            self.add(self.SIDE_Y, m, self.din)
            self.hop(2, m).start()

        @pl.when(~even)
        def _():
            self.add(self.SIDE_X, m, self.din)
            self.hop(1, m).start()

    def line(self, i):
        p = self.p
        m = self.plane(i)
        self.join(self.OWN, m)
        self.hop(1, m).wait_recv()
        self.hop(2, m).wait_recv()
        self.add(self.OWN, m, self.xin, self.yin)

        @pl.when(m > p.z)
        def _():
            @pl.when(p.low)
            def _():
                self.climbed(m, True).wait_recv()
                self.add(self.OWN, m, self.zin)

            self.climb(m, True).start()

        @pl.when(m < p.z)
        def _():
            @pl.when(p.high)
            def _():
                self.climbed(m, False).wait_recv()
                self.add(self.OWN, m, self.zin)

            self.climb(m, False).start()

    def result(self):
        p = self.p
        self.out[...] = self.unit(self.OWN, p.z)[...].astype(F32)

        @pl.when(p.low)
        def _():
            self.climbed(p.z, True).wait_recv()
            self.out[...] += self.zin[p.z].astype(F32)

        @pl.when(p.high)
        def _():
            self.climbed(p.z, False).wait_recv()
            self.out[...] += self.zin[LINE].astype(F32)

    def part(self, kind, i):
        if kind == 4:
            return self.result
        return functools.partial((self.corner, self.sides, self.relay, self.line)[kind], i)

    def settle(self):
        @pl.loop(0, LINE)
        def _(m):
            for c in range(4):
                self.swap(c, m).wait_send()
            for kind in range(3):
                self.hop(kind, m).wait_send()
            pl.when(m != self.p.z)(lambda: self.climb(m, True).wait_send())


class DirectCollect(Collect):
    def throw(self, m):
        p = self.p
        return self.remote(
            self.unit(self.OWN, m),
            self.zin.at[p.z],
            self.sems.at[3, m],
            self.sems.at[7, p.z],
            (p.s, m),
        )

    def line(self, i):
        m = self.plane(i)
        self.join(self.OWN, m)
        self.hop(1, m).wait_recv()
        self.hop(2, m).wait_recv()
        self.add(self.OWN, m, self.xin, self.yin)
        pl.when(m != self.p.z)(lambda: self.throw(m).start())

    def result(self):
        p = self.p
        self.out[...] = self.unit(self.OWN, p.z)[...].astype(F32)
        for m in range(LINE):

            @pl.when(m != p.z)
            def _():
                zin = self.zin.at[m]
                self.remote(
                    zin, zin, self.sems.at[3, m], self.sems.at[7, m], (p.partner, p.z)
                ).wait_recv()
                self.out[...] += self.zin[m].astype(F32)


BUFFERS = ((4, LINE), (LINE,), (LINE,), (LINE,), (LINE + 1,))


def project(rows, weights, bias, local):
    return (dot(rows, weights[:, : 3 * local]) + bias[:, : 3 * local]).astype(BF)


def attend(query, keys, values, head, store, between):
    rows, local = query.shape
    half = rows // 2
    query_t = query.T * BF(1.0 / math.sqrt(head))
    value_t = values.T
    line = lax.broadcasted_iota(jnp.int32, (local, rows), 0)
    heads = []
    for h in range(local // head):
        own = (line >= h * head) & (line < (h + 1) * head)
        masked = jnp.where(own, query_t, BF(0.0))
        value_h = value_t[h * head : (h + 1) * head, :]
        parts = []
        for b in range(2):
            span = NB + (b + 1) * half
            scores = dot(keys[:span, :], masked[:, b * half : (b + 1) * half])
            key_at = lax.broadcasted_iota(jnp.int32, (half, half), 0)
            row_at = lax.broadcasted_iota(jnp.int32, (half, half), 1)
            edge = jnp.where(key_at <= row_at, scores[span - half :, :], -1e30)
            scores = jnp.concatenate([scores[: span - half, :], edge], axis=0)
            scores = jnp.exp(scores - jnp.max(scores, axis=0, keepdims=True))
            probs = (scores * (1.0 / jnp.sum(scores, axis=0, keepdims=True))).astype(BF)
            store(h, slice(0, span), slice(b * half, (b + 1) * half), probs)
            parts.append(dot(value_h[:, :span], probs))
        heads.append(jnp.concatenate(parts, axis=1).astype(BF))
        between(h)
    return jnp.concatenate(heads, axis=0)


def gelu_parts(pre):
    square = pre * pre
    inner = jnp.tanh(GELU_SCALE * (pre + GELU_CUBIC * pre * square))
    half_up = 0.5 * (1.0 + inner)
    slope = GELU_SCALE * (1.0 + 3.0 * GELU_CUBIC * square)
    return (pre * half_up).astype(BF), half_up + 0.5 * pre * (1.0 - inner * inner) * slope


def forward_kernel(
    tokens_ref,
    past_ref,
    pos_ref,
    counts_ref,
    stack_ref,
    b_qv_ref,
    b_up_ref,
    w_qkv_ref,
    w_out_ref,
    up_ref,
    down_ref,
    wa_ref,
    wu_ref,
    wd_ref,
    out_ref,
    res_ref,
    hmt_ref,
    h2t_ref,
    prob_ref,
    key_ref,
    val_ref,
    query_ref,
    att_ref,
    act_ref,
    slope_ref,
    vec_ref,
    inv_ref,
    coef_ref,
    meta_ref,
    hm_ref,
    h2_ref,
    room_ref,
    attn_ref,
    tok_ref,
    acc_ref,
    mom_ref,
    sampled_ref,
    all_sampled_ref,
    basis_ref,
    all_meta_ref,
    all_room_ref,
    coef_part_ref,
    all_coef_ref,
    wide_ref,
    past_vmem,
    flat_send,
    flat_recv,
    flat_local,
    send,
    recv,
    own_sem,
    line_send,
    line_recv,
    line_own,
    load_sem,
    *,
    items,
    head,
):
    step = pl.program_id(0)
    rows, width = tok_ref.shape
    local = query_ref.shape[2]
    place = Place()
    flat = [
        Spread(
            place, src, dst, flat_send.at[i], flat_recv.at[i], flat_local.at[i], line=False
        )
        for i, (src, dst) in enumerate(
            ((meta_ref, all_meta_ref), (sampled_ref, all_sampled_ref))
        )
    ]
    wide = [
        Spread(place, src, dst, send.at[i], recv.at[i], own_sem.at[i])
        for i, (src, dst) in enumerate(
            ((room_ref, all_room_ref), (attn_ref, wa_ref), (up_ref, wu_ref), (down_ref, wd_ref))
        )
    ]
    room, attn, up, down = wide
    line = Line(place, coef_part_ref, all_coef_ref, line_send, line_recv, line_own)

    attn_at = SOLVE_STEPS
    mlp_at = attn_at + LINE
    last = mlp_at + LINE - 1
    plan = {
        slot: [wide[i].part(kind, d) for i, kind, d in steps] for slot, steps in FORWARD_PLAN
    }

    def transfers(at, position):
        if plan.get((at, position)):

            @pl.when(step == at)
            def _():
                for one in plan[(at, position)]:
                    one()

    def load(ref, m, slot, which):
        return pltpu.make_async_copy(ref.at[m], wide_ref.at[slot, which], load_sem.at[slot, which])

    @pl.when(step == 0)
    def _():
        bring_tok = pltpu.make_async_copy(
            tokens_ref.at[pl.ds(place.z * rows, rows), :], tok_ref, load_sem.at[0, 0]
        )
        bring_past = pltpu.make_async_copy(past_ref, past_vmem, load_sem.at[0, 1])
        bring_tok.start()
        bring_past.start()
        greet(place)
        meta_ref[...] = meta_rows(
            pos_ref[...], counts_ref, place.s * items, PLANE * items, past_ref.shape[2]
        )
        bring_past.wait()
        sampled_ref[...] = pick_samples(past_vmem[...], meta_ref[...], items)
        for part in flat:
            part.first()
        room_ref[...] = small_rows(
            stack_ref[...].astype(F32),
            b_qv_ref[...].astype(F32),
            b_up_ref[...].astype(F32),
            place.s,
            width,
            head,
        )
        for i in range(3):
            attn_ref[:, i * local : (i + 1) * local] = w_qkv_ref[i]
        row, lane = iotas((w_out_ref.shape[1], w_out_ref.shape[1]))
        unit = (row == lane).astype(F32).astype(BF)
        attn_ref[:, 3 * local :] = dot_nt(unit, w_out_ref[...]).astype(BF)
        bring_tok.wait()
        acc_ref[...] = jnp.zeros_like(acc_ref)
        clear_moments(inv_ref, mom_ref)

    transfers(0, 0)

    meta, samples = flat

    @pl.when(step == 1)
    def _():
        for kind in (2, 3):
            meta.part(kind, 0)()
        samples.part(2, 0)()
        meta.own.wait()
        meta.close(0)

    transfers(1, 0)

    @pl.when(step == 1)
    def _():
        def owner(s, carry):
            rows = owner_basis(all_meta_ref[0, pl.ds(s * 8, 8), :], items)
            basis_ref[s] = rows
            inv_ref[...] += dot_tn(rows, rows, HIGHEST)
            return carry

        lax.fori_loop(0, PLANE, owner, 0)
        samples.part(3, 0)()
        samples.own.wait()
        samples.close(0)

    transfers(1, 1)

    @pl.when(step == 1)
    def _():
        def owner(s, carry):
            count = sampled_ref.shape[0]
            rows = all_sampled_ref[0, pl.ds(s * count, count), :]
            mom_ref[...] += dot_tn(basis_ref[s], rows.astype(F32), HIGHEST)
            return carry

        lax.fori_loop(0, PLANE, owner, 0)

    transfers(1, 2)

    inverse_end = 2 + NB // PIVOTS

    @pl.when((step >= 2) & (step < inverse_end))
    def _():
        invert_step(inv_ref)

    for at in range(2, inverse_end):
        transfers(at, 0)

    @pl.when(step == inverse_end)
    def _():
        coef_part_ref[...] = coefficients(inv_ref, mom_ref).astype(BF)
        line.first()

    transfers(inverse_end, 0)

    @pl.when(step == inverse_end)
    def _():
        room.own.wait()
        for m in range(LINE):
            room.close(m)
            total = all_room_ref[m, 0:16, :].astype(F32)
            for s in range(1, PLANE):
                total = total + all_room_ref[m, s * 16 : (s + 1) * 16, :].astype(F32)
            vec_ref[m] = total
        gain, bias = vec_ref[0, 0:1, :], vec_ref[0, 1:2, :]
        normed, _ = norm_parts(tok_ref[...].astype(F32))
        hm_ref[NB:, :] = (normed * gain + bias).astype(BF)
        hmt_ref[:, NB:] = hm_ref[NB:, :].T
        line.step(1)

    transfers(inverse_end, 1)

    @pl.when(step == inverse_end)
    def _():
        attn.own.wait()
        attn.close(0)
        load(wa_ref, 0, 0, 0).start()
        line.step(2)

    transfers(inverse_end, 2)

    @pl.when(step == inverse_end)
    def _():
        line.step(3)
        line.own.wait()
        gain, bias = vec_ref[0, 0:1, :], vec_ref[0, 1:2, :]
        for m in range(LINE):
            coef_ref[:, m * local : (m + 1) * local] = all_coef_ref[m]
        normed, _ = norm_parts(coef_ref[...].astype(F32))
        hm_ref[0:NB, :] = (normed * gain + bias).astype(BF)
        hmt_ref[:, 0:NB] = hm_ref[0:NB, :].T

    @pl.when((step >= attn_at) & (step < mlp_at))
    def _():
        m = step - attn_at
        slot = lax.rem(m, 2)
        load(wa_ref, m, slot, 0).wait()

        @pl.when(m < LINE - 1)
        def _():
            attn.close(m + 1)
            load(wa_ref, m + 1, 1 - slot, 0).start()

        weights = wide_ref[slot, 0]
        projected = project(hm_ref[...], weights, vec_ref[m, 6:7, :], local)
        query = projected[NB:, :local]
        keys = projected[:, local : 2 * local]
        values = projected[:, 2 * local :]
        query_ref[0] = query
        key_ref[0] = keys
        val_ref[0] = values

        def store(h, lines, columns, probs):
            prob_ref[0, h, lines, columns] = probs

        def between(h):
            for at in range(attn_at, mlp_at):
                transfers(at, h)

        attended = attend(query, keys, values, head, store, between)
        att_ref[0] = attended
        acc_ref[...] += dot_nt(attended.T, wide_ref[slot, 0, :, 3 * local :])

    transfers(mlp_at, 0)

    @pl.when(step == mlp_at)
    def _():
        for part in (up, down):
            part.own.wait()
            part.close(0)
        load(wu_ref, 0, 0, 0).start()
        load(wd_ref, 0, 0, 1).start()
        residual = tok_ref[...].astype(F32) + acc_ref[...] + vec_ref[0, 4:5, :]
        res_ref[...] = residual
        normed, _ = norm_parts(residual)
        h2_ref[...] = (normed * vec_ref[0, 2:3, :] + vec_ref[0, 3:4, :]).astype(BF)
        h2t_ref[...] = h2_ref[...].T
        acc_ref[...] = jnp.zeros_like(acc_ref)

    @pl.when(step >= mlp_at)
    def _():
        m = step - mlp_at
        slot = lax.rem(m, 2)
        load(wu_ref, m, slot, 0).wait()
        load(wd_ref, m, slot, 1).wait()

        @pl.when(m < LINE - 1)
        def _():
            up.close(m + 1)
            down.close(m + 1)
            load(wu_ref, m + 1, 1 - slot, 0).start()
            load(wd_ref, m + 1, 1 - slot, 1).start()

        pre = dot(h2_ref[...], wide_ref[slot, 0]) + vec_ref[m, 7:8, :]
        act, slope = gelu_parts(pre)
        act_ref[0] = act
        slope_ref[0] = slope.astype(BF)
        acc_ref[...] += dot_nt(act, wide_ref[slot, 1])

    @pl.when(step == last)
    def _():
        out_ref[...] = (res_ref[...] + acc_ref[...] + vec_ref[0, 5:6, :]).astype(BF)
        for part in flat + wide:
            part.settle()
        line.finish_sends()


SOLVE_STEPS = 3 + NB // PIVOTS


FORWARD_PLAN = (
    (
        (0, 0),
        ((0, 0, 0),),
    ),
    (
        (1, 0),
        ((1, 0, 0), (0, 1, 1), (0, 1, -1),),
    ),
    (
        (1, 1),
        ((0, 1, -2), (0, 1, 2), (1, 1, -1), (1, 1, 1),),
    ),
    (
        (1, 2),
        ((0, 1, -3), (0, 1, 3), (3, 0, 0),),
    ),
    (
        (2, 0),
        ((1, 1, 2), (1, 1, -2),),
    ),
    (
        (4, 0),
        ((0, 2, -3), (0, 2, 3), (1, 2, 0), (0, 2, -1), (0, 2, 1),),
    ),
    (
        (5, 0),
        ((0, 2, 0), (0, 2, -2), (0, 2, 2), (1, 1, -3), (1, 1, 3), (2, 0, 0),),
    ),
    (
        (7, 0),
        ((1, 2, -2), (1, 2, 2), (1, 2, 1), (1, 2, -1),),
    ),
    (
        (8, 0),
        ((3, 1, 1), (3, 1, -1),),
    ),
    (
        (9, 0),
        ((0, 3, 3), (0, 3, -3),),
    ),
    (
        (10, 0),
        ((0, 3, 1), (0, 3, -1), (1, 2, 3), (1, 2, -3), (0, 3, 0), (0, 3, 2), (0, 3, -2), (3, 1, -2), (3, 1, 2),),
    ),
    (
        (10, 1),
        ((3, 1, 3), (3, 1, -3), (1, 3, 0), (1, 3, 1), (1, 3, -2), (1, 3, 3), (1, 3, -1), (1, 3, 2), (1, 3, -3),),
    ),
    (
        (10, 2),
        ((2, 1, -1), (2, 1, 1),),
    ),
    (
        (11, 0),
        ((2, 1, -2), (2, 1, 2),),
    ),
    (
        (11, 1),
        ((2, 1, 3), (2, 1, -3), (3, 2, 0),),
    ),
    (
        (12, 0),
        ((2, 2, 1), (2, 2, -1), (2, 2, 0),),
    ),
    (
        (12, 1),
        ((2, 2, -3), (2, 2, 3), (3, 2, -2), (3, 2, 2),),
    ),
    (
        (13, 0),
        ((3, 2, -1), (3, 2, 1), (2, 2, 2), (2, 2, -2),),
    ),
    (
        (13, 1),
        ((2, 3, -1), (2, 3, 1), (3, 2, 3), (3, 2, -3), (2, 3, 0),),
    ),
    (
        (13, 2),
        ((3, 3, 0), (2, 3, 3), (2, 3, -3),),
    ),
    (
        (14, 1),
        ((3, 3, 1), (3, 3, -1), (3, 3, 2), (3, 3, -2), (2, 3, -2), (2, 3, 2), (3, 3, 3), (3, 3, -3),),
    ),
)


def forward_pass(tokens, past, positions, counts, stack, b_qv, b_up, w_qkv, w_out, up, down, head):
    width = tokens.shape[1]
    rows = tokens.shape[0] // LINE
    items = past.shape[0]
    local = width // LINE
    hidden = up.shape[1]
    heads = local // head
    keyed = NB + rows
    slots = positions.shape[1]
    samples = items * slots
    part = up.shape[0]
    attn_at = SOLVE_STEPS
    mlp_at = attn_at + LINE
    first = lambda i: jnp.clip(i - attn_at, 0, LINE - 1)
    second = lambda i: jnp.clip(i - mlp_at, 0, LINE - 1)
    whole = lambda shape: pl.BlockSpec(shape, lambda i: (0,) * len(shape))
    anywhere = pl.BlockSpec(memory_space=pl.ANY)
    vmem = pl.BlockSpec(memory_space=pltpu.VMEM)
    dma = pltpu.SemaphoreType.DMA
    shape = jax.ShapeDtypeStruct
    return pl.pallas_call(
        functools.partial(forward_kernel, items=items, head=head),
        grid=(mlp_at + LINE,),
        in_specs=[anywhere, anywhere, vmem, pl.BlockSpec(memory_space=pltpu.SMEM)]
        + [vmem] * 5
        + [anywhere, anywhere],
        out_specs=[
            anywhere,
            anywhere,
            anywhere,
            whole((rows, width)),
            whole((rows, width)),
            whole((width, keyed)),
            whole((width, rows)),
            pl.BlockSpec((1, heads, keyed, rows), lambda i: (first(i), 0, 0, 0)),
            pl.BlockSpec((1, keyed, local), lambda i: (first(i), 0, 0)),
            pl.BlockSpec((1, keyed, local), lambda i: (first(i), 0, 0)),
            pl.BlockSpec((1, rows, local), lambda i: (first(i), 0, 0)),
            pl.BlockSpec((1, local, rows), lambda i: (first(i), 0, 0)),
            pl.BlockSpec((1, rows, hidden), lambda i: (second(i), 0, 0)),
            pl.BlockSpec((1, rows, hidden), lambda i: (second(i), 0, 0)),
            whole((LINE, 16, width)),
            whole((NB, NB)),
            whole((NB, width)),
            whole((8, slots)),
        ],
        out_shape=[
            shape((LINE, width, width), BF),
            shape((LINE, width, hidden), BF),
            shape((LINE, width, hidden), BF),
            shape((rows, width), BF),
            shape((rows, width), F32),
            shape((width, keyed), BF),
            shape((width, rows), BF),
            shape((LINE, heads, keyed, rows), BF),
            shape((LINE, keyed, local), BF),
            shape((LINE, keyed, local), BF),
            shape((LINE, rows, local), BF),
            shape((LINE, local, rows), BF),
            shape((LINE, rows, hidden), BF),
            shape((LINE, rows, hidden), BF),
            shape((LINE, 16, width), F32),
            shape((NB, NB), F32),
            shape((NB, width), BF),
            shape((8, slots), F32),
        ],
        scratch_shapes=[
            pltpu.VMEM((keyed, width), BF),
            pltpu.VMEM((rows, width), BF),
            pltpu.VMEM((16, width), BF),
            pltpu.VMEM((part, width), BF),
            pltpu.VMEM((rows, width), BF),
            pltpu.VMEM((rows, width), F32),
            pltpu.VMEM((NB, local), F32),
            pltpu.VMEM((samples, local), BF),
            pltpu.VMEM((1, PLANE * samples, local), BF),
            pltpu.VMEM((PLANE, samples, NB), F32),
            pltpu.VMEM((1, PLANE * 8, slots), F32),
            pltpu.VMEM((LINE, PLANE * 16, width), BF),
            pltpu.VMEM((NB, local), BF),
            pltpu.VMEM((LINE, NB, local), BF),
            pltpu.VMEM((2, 2, width, width), BF),
            pltpu.VMEM(past.shape, BF),
            dma((2, 5, 4)),
            dma((2, PLANE)),
            dma((2,)),
            dma((4, 5, LINE * 4)),
            dma((4, LINE * PLANE)),
            dma((4,)),
            dma((2, LINE)),
            dma((LINE,)),
            dma(()),
            dma((2, 2)),
        ],
        compiler_params=pltpu.CompilerParams(
            collective_id=1, has_side_effects=True, vmem_limit_bytes=BIG_VMEM
        ),
        name="forward_pass",
    )(tokens, past, positions, counts, stack, b_qv, b_up, w_qkv, w_out, up, down)


def plain_forward_kernel(
    tok_ref,
    coef_ref,
    vec_ref,
    wa_ref,
    wu_ref,
    wd_ref,
    out_ref,
    res_ref,
    hm_ref,
    h2_ref,
    prob_ref,
    key_ref,
    val_ref,
    query_ref,
    att_ref,
    act_ref,
    slope_ref,
    acc_ref,
    *,
    groups,
    head,
):
    step = pl.program_id(0)
    rows, width = tok_ref.shape
    local = query_ref.shape[2]

    @pl.when(step == 0)
    def _():
        gain, bias = vec_ref[0, 0:1, :], vec_ref[0, 1:2, :]
        normed, _ = norm_parts(coef_ref[...].astype(F32))
        hm_ref[0:NB, :] = (normed * gain + bias).astype(BF)
        normed, _ = norm_parts(tok_ref[...].astype(F32))
        hm_ref[NB:, :] = (normed * gain + bias).astype(BF)
        acc_ref[...] = jnp.zeros_like(acc_ref)

    @pl.when(step < groups)
    def _():
        weights = wa_ref[0]
        projected = project(hm_ref[...], weights, vec_ref[step, 6:7, :], local)
        query = projected[NB:, :local]
        keys = projected[:, local : 2 * local]
        values = projected[:, 2 * local :]
        query_ref[0] = query
        key_ref[0] = keys
        val_ref[0] = values

        def store(h, lines, columns, probs):
            prob_ref[0, h, lines, columns] = probs

        attended = attend(query, keys, values, head, store, lambda h: None)
        att_ref[0] = attended
        acc_ref[...] += dot_nt(attended.T, weights[:, 3 * local :])

    @pl.when(step == groups)
    def _():
        residual = tok_ref[...].astype(F32) + acc_ref[...] + vec_ref[0, 4:5, :]
        res_ref[...] = residual
        normed, _ = norm_parts(residual)
        h2_ref[...] = (normed * vec_ref[0, 2:3, :] + vec_ref[0, 3:4, :]).astype(BF)
        acc_ref[...] = jnp.zeros_like(acc_ref)

    @pl.when(step >= groups)
    def _():
        pre = dot(h2_ref[...], wu_ref[0]) + vec_ref[step - groups, 7:8, :]
        act, slope = gelu_parts(pre)
        act_ref[0] = act
        slope_ref[0] = slope.astype(BF)
        acc_ref[...] += dot_nt(act, wd_ref[0])

    @pl.when(step == 2 * groups - 1)
    def _():
        out_ref[...] = (res_ref[...] + acc_ref[...] + vec_ref[0, 5:6, :]).astype(BF)


def plain_forward(tok, coef, vec, wide, head):
    rows, width = tok.shape
    groups = wide[0].shape[0]
    local = width // groups
    hidden = wide[1].shape[2]
    heads = local // head
    keyed = NB + rows
    first = lambda i: jnp.minimum(i, groups - 1)
    second = lambda i: jnp.maximum(i - groups, 0)
    whole = lambda shape: pl.BlockSpec(shape, lambda i: (0,) * len(shape))
    shape = jax.ShapeDtypeStruct
    return pl.pallas_call(
        functools.partial(plain_forward_kernel, groups=groups, head=head),
        grid=(2 * groups,),
        in_specs=[
            whole((rows, width)),
            whole((NB, width)),
            whole((groups, 16, width)),
            pl.BlockSpec((1, width, width), lambda i: (first(i), 0, 0)),
            pl.BlockSpec((1, width, hidden), lambda i: (second(i), 0, 0)),
            pl.BlockSpec((1, width, hidden), lambda i: (second(i), 0, 0)),
        ],
        out_specs=[
            whole((rows, width)),
            whole((rows, width)),
            whole((keyed, width)),
            whole((rows, width)),
            pl.BlockSpec((1, heads, keyed, rows), lambda i: (first(i), 0, 0, 0)),
            pl.BlockSpec((1, keyed, local), lambda i: (first(i), 0, 0)),
            pl.BlockSpec((1, keyed, local), lambda i: (first(i), 0, 0)),
            pl.BlockSpec((1, rows, local), lambda i: (first(i), 0, 0)),
            pl.BlockSpec((1, local, rows), lambda i: (first(i), 0, 0)),
            pl.BlockSpec((1, rows, hidden), lambda i: (second(i), 0, 0)),
            pl.BlockSpec((1, rows, hidden), lambda i: (second(i), 0, 0)),
        ],
        out_shape=[
            shape((rows, width), BF),
            shape((rows, width), F32),
            shape((keyed, width), BF),
            shape((rows, width), BF),
            shape((groups, heads, keyed, rows), BF),
            shape((groups, keyed, local), BF),
            shape((groups, keyed, local), BF),
            shape((groups, rows, local), BF),
            shape((groups, local, rows), BF),
            shape((groups, rows, hidden), BF),
            shape((groups, rows, hidden), BF),
        ],
        scratch_shapes=[pltpu.VMEM((rows, width), F32)],
        compiler_params=pltpu.CompilerParams(vmem_limit_bytes=BIG_VMEM),
        name="plain_forward",
    )(tok, coef, vec, *wide)


def attend_back(g_att, att_t, keys, values, query, probs_of, head, between):
    rows, local = g_att.shape
    half = rows // 2
    low = NB + rows - half
    g_att_t = g_att.T
    product = g_att_t.astype(F32) * att_t.astype(F32)
    key_t = keys.T
    scale = 1.0 / math.sqrt(head)
    line = lax.broadcasted_iota(jnp.int32, (local, rows), 0)
    lane = lax.broadcasted_iota(jnp.int32, (rows, local), 1)
    key_grad = [jnp.zeros((low, local), F32), jnp.zeros((half, local), F32)]
    val_grad = [jnp.zeros((low, local), F32), jnp.zeros((half, local), F32)]
    query_grads = []
    for h in range(local // head):
        own_t = (line >= h * head) & (line < (h + 1) * head)
        own = (lane >= h * head) & (lane < (h + 1) * head)
        grad_t = jnp.where(own_t, g_att_t, BF(0.0))
        grad_h = jnp.where(own, g_att, BF(0.0))
        query_h = jnp.where(own, query, BF(0.0))
        inner = jnp.sum(product[h * head : (h + 1) * head, :], axis=0, keepdims=True)
        key_h = key_t[h * head : (h + 1) * head, :]
        parts = []
        for b in range(2):
            span = NB + (b + 1) * half
            cols = slice(b * half, (b + 1) * half)
            probs = probs_of(h, slice(0, span), cols)
            dprob = dot(values[:span, :], grad_t[:, cols])
            dscore = (probs.astype(F32) * (dprob - inner[:, cols])).astype(BF)
            parts.append(dot(key_h[:, :span], dscore))
            val_part = dot(probs, grad_h[cols, :])
            key_part = dot(dscore, query_h[cols, :])
            val_grad[0] = val_grad[0] + val_part[:low, :]
            key_grad[0] = key_grad[0] + key_part[:low, :]
            if b == 1:
                val_grad[1] = val_grad[1] + val_part[low:, :]
                key_grad[1] = key_grad[1] + key_part[low:, :]
        query_grads.append(jnp.concatenate(parts, axis=1))
        between(h)
    query_grad = (jnp.concatenate(query_grads, axis=0) * scale).astype(BF).T
    key_grad = jnp.concatenate(key_grad, axis=0) * scale
    return query_grad, key_grad, jnp.concatenate(val_grad, axis=0)


def backward_kernel(
    tokens_ref,
    cots_ref,
    fwd_out_ref,
    res_ref,
    wa_ref,
    wu_ref,
    wd_ref,
    vec_ref,
    hmt_ref,
    h2t_ref,
    coef_ref,
    inv_ref,
    meta_ref,
    prob_ref,
    key_ref,
    val_ref,
    query_ref,
    att_ref,
    act_ref,
    slope_ref,
    outs_ref,
    tgs_ref,
    past_ref,
    vectors_ref,
    bias_ref,
    bias_up_ref,
    qkv_out_ref,
    wo_out_ref,
    up_out_ref,
    down_out_ref,
    *scratch,
    head,
):
    (
        tok_ref,
        cot_ref,
        cott_ref,
        gres_ref,
        acc_ref,
        proj_ref,
        gv_ref,
        ggv_ref,
        gmem_ref,
        wide_ref,
        side_ref,
        attn_ref,
        mlp_ref,
        gv_mem_ref,
        side_out_ref,
        attn_out_ref,
        mlp_out_ref,
    ) = scratch[:17]
    buffers = scratch[17:32]
    block_sems, sems, lsend, lrecv, lown, gsend, grecv, gown, load_sem = scratch[32:]
    step = pl.program_id(0)
    rows, width = tok_ref.shape
    local = query_ref.shape[2]
    items = past_ref.shape[0]
    place = Place()
    side, attn, mlp = [
        kind(place, grads, out, buffers[i::3], (block_sems.at[i], sems.at[i]))
        for i, (kind, grads, out) in enumerate(
            (
                (DirectCollect, side_ref, side_out_ref),
                (Collect, attn_ref, attn_out_ref),
                (Collect, mlp_ref, mlp_out_ref),
            )
        )
    ]
    outs, tgs = [
        [
            Line(
                place,
                src.at[pl.ds(h * (rows // count), rows // count), :],
                dst.at[:, pl.ds(h * (rows // count), rows // count), :],
                lsend.at[first + h],
                lrecv.at[first + h],
                lown.at[first + h],
            )
            for h in range(count)
        ]
        for src, dst, first, count in (
            (fwd_out_ref, outs_ref, 0, OUT_PIECES),
            (cot_ref, tgs_ref, OUT_PIECES, GRAD_PIECES),
        )
    ]
    mem = DirectSpread(place, side_out_ref.at[0, 0:8, :], gmem_ref, gsend, grecv, gown)
    mine = pl.ds(place.z * rows, rows)

    def load(ref, m, slot, which):
        return pltpu.make_async_copy(ref.at[m], wide_ref.at[slot, which], load_sem.at[slot, which])

    def bring(i, src, dst):
        return pltpu.make_async_copy(src, dst, load_sem.at[2, i])

    bring_cot = bring(0, cots_ref.at[mine, :], cot_ref)
    bring_tok = bring(1, tokens_ref.at[mine, :], tok_ref)
    bring_res = pltpu.make_async_copy(res_ref, gres_ref, load_sem.at[3, 0])

    def past():
        mem.own.wait()
        for m in range(LINE):
            mem.close(m)
        gmem = jnp.concatenate([gmem_ref[m] for m in range(LINE)], axis=0)
        give_past(gmem, coef_ref, vec_ref, inv_ref, meta_ref, past_ref, gv_mem_ref)
        own = side_out_ref[0, 8:16, :]
        own = jnp.concatenate([own[0:2] + gv_mem_ref[0:2, :], own[2:8]], axis=0)
        vectors, biases, bias_up = small_pieces(
            own, place.s, vectors_ref.shape[1], bias_ref.shape[2], head, bias_ref.shape[0]
        )
        vectors_ref[...] = vectors
        for h, bias in enumerate(biases):
            bias_ref[h] = bias
        bias_up_ref[...] = bias_up

    def give_attn():
        attn.result()
        for i in range(3):
            qkv_out_ref[i] = attn_out_ref[0, :, i * local : (i + 1) * local]
        row, lane = iotas((attn_out_ref.shape[1], attn_out_ref.shape[1]))
        unit = (row == lane).astype(F32)
        wo_out_ref[...] = dot_tn(attn_out_ref[0, :, 3 * local :], unit, HIGHEST)

    def give_mlp():
        mlp.result()
        up_out_ref[...] = mlp_out_ref[0]
        down_out_ref[...] = mlp_out_ref[1]

    def move(what, kind, i):
        if what == 1 and kind == 4:
            return [give_attn]
        if what == 2 and kind == 4:
            return [give_mlp]
        if what < 3:
            return [(side, attn, mlp)[what].part(kind, i)]
        if what == 3:
            return mem.steps(kind) if kind else [mem.first]
        if what == 4:
            return [past]
        line = (outs + tgs)[what - 5]
        return [functools.partial(line.step, i) if kind else line.first]

    plan = [[one for what in moves for one in move(*what)] for moves in BACKWARD_PLAN]

    def transfers(slot, condition=None):
        def go():
            for one in plan[slot]:
                one()

        if plan[slot]:
            when((condition,), go)

    @pl.when(step == 0)
    def _():
        bring_cot.start()
        bring_tok.start()
        bring_res.start()
        load(wu_ref, 0, 0, 0).start()
        load(wd_ref, 0, 0, 1).start()
        greet(place, whole_line=True)
        for line in outs:
            line.first()
        acc_ref[...] = jnp.zeros_like(acc_ref)
        gv_ref[...] = jnp.zeros_like(gv_ref)
        bring_cot.wait()
        bring_tok.wait()
        bring_res.wait()
        cott_ref[...] = cot_ref[...].T

    @pl.when(step < LINE)
    def _():
        m = step
        slot = lax.rem(m, 2)
        load(wu_ref, m, slot, 0).wait()
        load(wd_ref, m, slot, 1).wait()

        @pl.when(m < LINE - 1)
        def _():
            load(wu_ref, m + 1, 1 - slot, 0).start()
            load(wd_ref, m + 1, 1 - slot, 1).start()

        @pl.when(m == LINE - 1)
        def _():
            load(wa_ref, 0, 0, 0).start()

        upstream = cot_ref[...]
        grad = (dot(upstream, wide_ref[slot, 1]) * slope_ref[0].astype(F32)).astype(BF)
        mlp_ref[m, 1] = dot(cott_ref[...], act_ref[0]).astype(BF)
        mlp_ref[m, 0] = dot(h2t_ref[...], grad).astype(BF)
        mlp.begin(m)
        for at in range(LINE):
            transfers(at, step == at)
        ggv_ref[m, 1:2, :] = col_sum(grad.astype(F32))
        acc_ref[NB:, :] += dot_nt(grad, wide_ref[slot, 0])

    @pl.when(step == LINE)
    def _():
        transfers(LINE)
        upstream = cot_ref[...].astype(F32)
        normed, inverse = norm_parts(gres_ref[...])
        grad = acc_ref[NB:, :]
        g_res = upstream + norm_back(grad, normed, inverse, vec_ref[0, 2:3, :])
        gres_ref[...] = g_res
        g_attn = g_res.astype(BF)
        gv_ref[2:3, :] = col_sum(grad * normed)
        gv_ref[3:4, :] = col_sum(grad)
        gv_ref[4:5, :] = col_sum(g_attn.astype(F32))
        gv_ref[5:6, :] = col_sum(upstream)
        cott_ref[...] = g_attn.T
        acc_ref[...] = jnp.zeros_like(acc_ref)
        proj_ref[0:NB, :] = jnp.zeros((NB, proj_ref.shape[1]), BF)
        transfers(LINE + 1)

    @pl.when(step >= LINE)
    def _():
        m = step - LINE
        slot = lax.rem(m, 2)
        load(wa_ref, m, slot, 0).wait()

        @pl.when(m < LINE - 1)
        def _():
            load(wa_ref, m + 1, 1 - slot, 0).start()

        def between(h):
            for at in range(LINE):
                transfers(LINE + 2 + 4 * at + h, m == at)

        def probs_of(h, lines, columns):
            return prob_ref[0, h, lines, columns]

        g_attn = gres_ref[...].astype(BF)
        g_att = dot(g_attn, wide_ref[slot, 0, :, 3 * local :]).astype(BF)
        att_t = att_ref[0]
        query_grad, key_grad, val_grad = attend_back(
            g_att, att_t, key_ref[0], val_ref[0], query_ref[0], probs_of, head, between
        )
        proj_ref[NB:, 0:local] = query_grad
        proj_ref[:, local : 2 * local] = key_grad.astype(BF)
        proj_ref[:, 2 * local :] = val_grad.astype(BF)
        proj = proj_ref[...]
        ggv_ref[m, 0:1, 0 : 3 * local] = col_sum(proj.astype(F32))
        ggv_ref[m, 0:1, 3 * local :] = jnp.zeros((1, width - 3 * local), F32)
        attn_ref[m, 0, :, 0 : 3 * local] = dot(hmt_ref[...], proj).astype(BF)
        attn_ref[m, 0, :, 3 * local :] = dot_nt(cott_ref[...], att_t).astype(BF)
        attn.begin(m)
        acc_ref[...] += dot_nt(proj, wide_ref[slot, 0, :, : 3 * local])
        between(3)

    @pl.when(step == 2 * LINE - 1)
    def _():
        grad = acc_ref[NB:, :]
        normed, inverse = norm_parts(tok_ref[...].astype(F32))
        back = norm_back(grad, normed, inverse, vec_ref[0, 0:1, :])
        cot_ref[...] = (gres_ref[...] + back).astype(BF)
        tgs[0].first()
        gv_ref[0:1, :] = col_sum(grad * normed)
        gv_ref[1:2, :] = col_sum(grad)
        transfers(5 * LINE + 2)
        for m in range(LINE):
            below = jnp.concatenate([gv_ref[0:6, :], ggv_ref[m, 0:2, :]], axis=0)
            for s in range(PLANE):
                top = (m * PLANE + s) * 8
                side_ref[m, 0, s * 16 : s * 16 + 8, :] = acc_ref[top : top + 8, :]
                side_ref[m, 0, s * 16 + 8 : (s + 1) * 16, :] = below
            side.begin(m)
        transfers(5 * LINE + 3)
        mem.settle()
        for part in (side, attn, mlp):
            part.settle()
        for line in outs + tgs:
            line.finish()


OUT_PIECES, GRAD_PIECES = 2, 4

BACKWARD_PLAN = (
    (),
    (),
    (),
    (),
    ((5, 1, 1),),
    (),
    ((2, 0, 1),),
    ((6, 1, 1),),
    (),
    ((2, 0, 0),),
    ((2, 1, 0),),
    (),
    ((2, 0, 3),),
    ((5, 1, 2),),
    (),
    ((2, 2, 0),),
    ((1, 0, 1),),
    ((2, 0, 2), (6, 1, 2),),
    (),
    (),
    ((1, 0, 0),),
    (),
    ((8, 0, 0), (1, 0, 3), (1, 0, 2), (9, 0, 0), (10, 0, 0),),
    ((0, 0, 0), (0, 0, 1), (0, 0, 2), (0, 0, 3), (0, 1, 2), (1, 1, 2), (0, 1, 3), (1, 2, 2), (0, 2, 3), (0, 1, 1), (0, 2, 1), (0, 2, 2), (0, 1, 0), (0, 2, 0), (8, 1, 1), (1, 1, 1), (1, 2, 1), (0, 3, 1), (1, 1, 0), (1, 2, 0), (2, 1, 1), (2, 2, 1), (0, 3, 3), (0, 3, 2), (2, 1, 3), (2, 2, 3), (0, 3, 0), (2, 1, 2), (2, 2, 2), (7, 1, 1), (0, 4, 0), (3, 0, 0), (6, 1, 3), (10, 1, 1), (9, 1, 1), (5, 1, 3), (8, 1, 2), (1, 1, 3), (1, 2, 3), (2, 3, 0), (1, 3, 2), (3, 1, 0), (10, 1, 2), (1, 3, 0), (2, 3, 1), (7, 1, 2), (9, 1, 2), (2, 3, 3), (3, 2, 0), (3, 3, 0), (1, 3, 3), (2, 3, 2), (1, 3, 1), (4, 0, 0), (7, 1, 3), (8, 1, 3), (9, 1, 3), (10, 1, 3), (2, 4, 0), (1, 4, 0),),
)


def backward_pass(tokens, cots, out, meta, vec, inverse, coef, saved, wide, items, past_shape, head):
    res, hmt, h2t, prob, keys, vals, query, att, act, slope = saved
    rows, width = out.shape
    local = width // LINE
    hidden = wide[1].shape[2]
    heads = local // head
    keyed = NB + rows
    first = lambda i: jnp.minimum(i, LINE - 1)
    second = lambda i: jnp.maximum(i - LINE, 0)
    anywhere = pl.BlockSpec(memory_space=pl.ANY)
    vmem = pl.BlockSpec(memory_space=pltpu.VMEM)
    dma = pltpu.SemaphoreType.DMA
    shape = jax.ShapeDtypeStruct
    part = width // PLANE
    blocks = ((1, 16, width), (1, part, width), (2, part, width))
    kinds = (F32, BF, BF)
    pieces = OUT_PIECES + GRAD_PIECES
    return pl.pallas_call(
        functools.partial(backward_kernel, head=head),
        grid=(2 * LINE,),
        in_specs=[anywhere] * 7
        + [vmem] * 6
        + [
            pl.BlockSpec((1, heads, keyed, rows), lambda i: (second(i), 0, 0, 0)),
            pl.BlockSpec((1, keyed, local), lambda i: (second(i), 0, 0)),
            pl.BlockSpec((1, keyed, local), lambda i: (second(i), 0, 0)),
            pl.BlockSpec((1, rows, local), lambda i: (second(i), 0, 0)),
            pl.BlockSpec((1, local, rows), lambda i: (second(i), 0, 0)),
            pl.BlockSpec((1, rows, hidden), lambda i: (first(i), 0, 0)),
            pl.BlockSpec((1, rows, hidden), lambda i: (first(i), 0, 0)),
        ],
        out_specs=[anywhere, anywhere] + [vmem] * 8,
        out_shape=[
            shape((LINE, rows, width), BF),
            shape((LINE, rows, width), BF),
            shape(past_shape, F32),
            shape((8, part), F32),
            shape((local // head, 2, head // PLANE), F32),
            shape((head // PLANE, hidden // head), F32),
            shape((3, part, local), F32),
            shape((local, part), F32),
            shape((part, hidden), F32),
            shape((part, hidden), F32),
        ],
        scratch_shapes=[
            pltpu.VMEM((rows, width), BF),
            pltpu.VMEM((rows, width), BF),
            pltpu.VMEM((width, rows), BF),
            pltpu.VMEM((rows, width), F32),
            pltpu.VMEM((keyed, width), F32),
            pltpu.VMEM((keyed, 3 * local), BF),
            pltpu.VMEM((8, width), F32),
            pltpu.VMEM((LINE, 8, hidden), F32),
            pltpu.VMEM((LINE, PLANE * 8, width), F32),
            pltpu.VMEM((2, 2, width, width), BF),
        ]
        + [pltpu.VMEM((LINE, b[0], PLANE * b[1], b[2]), t) for b, t in zip(blocks, kinds)]
        + [pltpu.VMEM((8, width), F32)]
        + [pltpu.VMEM(b, F32) for b in blocks]
        + [pltpu.VMEM(lead + b, t) for lead in BUFFERS for b, t in zip(blocks, kinds)]
        + [
            dma((3, 2, 4, LINE)),
            dma((3, 9, LINE)),
            dma((pieces, 2, LINE)),
            dma((pieces, LINE)),
            dma((pieces,)),
            dma((5, LINE * 4)),
            dma((LINE * PLANE,)),
            dma(()),
            dma((4, 2)),
        ],
        compiler_params=pltpu.CompilerParams(
            collective_id=2, has_side_effects=True, vmem_limit_bytes=MAX_VMEM
        ),
        name="backward_pass",
    )(
        tokens,
        cots,
        out,
        res,
        *wide,
        vec,
        hmt,
        h2t,
        coef,
        inverse,
        meta,
        prob,
        keys,
        vals,
        query,
        att,
        act,
        slope,
    )


def plain_backward_kernel(
    tok_ref,
    cot_ref,
    res_ref,
    vec_ref,
    hm_ref,
    h2_ref,
    prob_ref,
    key_ref,
    val_ref,
    query_ref,
    att_ref,
    act_ref,
    slope_ref,
    wa_ref,
    wu_ref,
    wd_ref,
    tg_ref,
    gmem_ref,
    gup_ref,
    gdown_ref,
    gatt_ref,
    gv_ref,
    ggv_ref,
    acc_ref,
    hmt_ref,
    h2t_ref,
    cott_ref,
    gres_ref,
    proj_ref,
    *,
    groups,
    head,
):
    step = pl.program_id(0)
    rows, width = tok_ref.shape
    local = query_ref.shape[2]

    @pl.when(step == 0)
    def _():
        acc_ref[...] = jnp.zeros_like(acc_ref)
        h2t_ref[...] = h2_ref[...].T
        cott_ref[...] = cot_ref[...].T
        gv_ref[...] = jnp.zeros_like(gv_ref)

    @pl.when(step < groups)
    def _():
        upstream = cot_ref[...]
        grad = (dot(upstream, wd_ref[0]) * slope_ref[0].astype(F32)).astype(BF)
        gdown_ref[0] = dot(cott_ref[...], act_ref[0]).astype(BF)
        gup_ref[0] = dot(h2t_ref[...], grad).astype(BF)
        ggv_ref[0] = jnp.zeros_like(ggv_ref[0])
        ggv_ref[0, 0:1, :] = col_sum(grad.astype(F32))
        acc_ref[NB:, :] += dot_nt(grad, wu_ref[0])

    @pl.when(step == groups)
    def _():
        upstream = cot_ref[...].astype(F32)
        normed, inverse = norm_parts(res_ref[...])
        grad = acc_ref[NB:, :]
        g_res = upstream + norm_back(grad, normed, inverse, vec_ref[2:3, :])
        gres_ref[...] = g_res
        g_attn = g_res.astype(BF)
        gv_ref[2:3, :] = col_sum(grad * normed)
        gv_ref[3:4, :] = col_sum(grad)
        gv_ref[4:5, :] = col_sum(g_attn.astype(F32))
        gv_ref[5:6, :] = col_sum(upstream)
        cott_ref[...] = g_attn.T
        hmt_ref[...] = hm_ref[...].T
        acc_ref[...] = jnp.zeros_like(acc_ref)
        proj_ref[0:NB, :] = jnp.zeros((NB, proj_ref.shape[1]), BF)

    @pl.when(step >= groups)
    def _():
        weights = wa_ref[0]
        g_attn = gres_ref[...].astype(BF)
        g_att = dot(g_attn, weights[:, 3 * local :]).astype(BF)
        att_t = att_ref[0]
        query_grad, key_grad, val_grad = attend_back(
            g_att,
            att_t,
            key_ref[0],
            val_ref[0],
            query_ref[0],
            lambda h, lines, columns: prob_ref[0, h, lines, columns],
            head,
            lambda h: None,
        )
        key_grad, val_grad = key_grad.astype(BF), val_grad.astype(BF)
        proj_ref[NB:, 0:local] = query_grad
        proj_ref[:, local : 2 * local] = key_grad
        proj_ref[:, 2 * local :] = val_grad
        proj = proj_ref[...]
        ggv_ref[0] = jnp.zeros_like(ggv_ref[0])
        ggv_ref[0, 0:1, 0 : 3 * local] = col_sum(proj.astype(F32))
        gatt_ref[0, :, 0 : 3 * local] = dot(hmt_ref[...], proj).astype(BF)
        gatt_ref[0, :, 3 * local :] = dot_nt(cott_ref[...], att_t).astype(BF)
        acc_ref[...] += dot_nt(proj, weights[:, : 3 * local])

    @pl.when(step == 2 * groups - 1)
    def _():
        gmem_ref[...] = acc_ref[0:NB, :]
        grad = acc_ref[NB:, :]
        normed, inverse = norm_parts(tok_ref[...].astype(F32))
        part = norm_back(grad, normed, inverse, vec_ref[0:1, :])
        tg_ref[...] = (gres_ref[...] + part).astype(BF)
        gv_ref[0:1, :] = col_sum(grad * normed)
        gv_ref[1:2, :] = col_sum(grad)


def plain_backward(tok, cot, vec, saved, wide, head):
    res, hm, h2, prob, keys, vals, query, att, act, slope = saved
    rows, width = tok.shape
    groups = wide[0].shape[0]
    local = width // groups
    hidden = wide[1].shape[2]
    heads = local // head
    keyed = NB + rows
    first = lambda i: jnp.minimum(i, groups - 1)
    second = lambda i: jnp.maximum(i - groups, 0)
    whole = lambda shape: pl.BlockSpec(shape, lambda i: (0,) * len(shape))
    return pl.pallas_call(
        functools.partial(plain_backward_kernel, groups=groups, head=head),
        grid=(2 * groups,),
        in_specs=[
            whole((rows, width)),
            whole((rows, width)),
            whole((rows, width)),
            whole((16, width)),
            whole((keyed, width)),
            whole((rows, width)),
            pl.BlockSpec((1, heads, keyed, rows), lambda i: (second(i), 0, 0, 0)),
            pl.BlockSpec((1, keyed, local), lambda i: (second(i), 0, 0)),
            pl.BlockSpec((1, keyed, local), lambda i: (second(i), 0, 0)),
            pl.BlockSpec((1, rows, local), lambda i: (second(i), 0, 0)),
            pl.BlockSpec((1, local, rows), lambda i: (second(i), 0, 0)),
            pl.BlockSpec((1, rows, hidden), lambda i: (first(i), 0, 0)),
            pl.BlockSpec((1, rows, hidden), lambda i: (first(i), 0, 0)),
            pl.BlockSpec((1, width, width), lambda i: (second(i), 0, 0)),
            pl.BlockSpec((1, width, hidden), lambda i: (first(i), 0, 0)),
            pl.BlockSpec((1, width, hidden), lambda i: (first(i), 0, 0)),
        ],
        out_specs=[
            whole((rows, width)),
            whole((NB, width)),
            pl.BlockSpec((1, width, hidden), lambda i: (first(i), 0, 0)),
            pl.BlockSpec((1, width, hidden), lambda i: (first(i), 0, 0)),
            pl.BlockSpec((1, width, width), lambda i: (second(i), 0, 0)),
            whole((8, width)),
            pl.BlockSpec((1, 8, hidden), lambda i: (i, 0, 0)),
        ],
        out_shape=[
            jax.ShapeDtypeStruct((rows, width), BF),
            jax.ShapeDtypeStruct((NB, width), F32),
            jax.ShapeDtypeStruct((groups, width, hidden), BF),
            jax.ShapeDtypeStruct((groups, width, hidden), BF),
            jax.ShapeDtypeStruct((groups, width, width), BF),
            jax.ShapeDtypeStruct((8, width), F32),
            jax.ShapeDtypeStruct((2 * groups, 8, hidden), F32),
        ],
        scratch_shapes=[
            pltpu.VMEM((keyed, width), F32),
            pltpu.VMEM((width, keyed), BF),
            pltpu.VMEM((width, rows), BF),
            pltpu.VMEM((width, rows), BF),
            pltpu.VMEM((rows, width), F32),
            pltpu.VMEM((keyed, 3 * local), BF),
        ],
        compiler_params=pltpu.CompilerParams(vmem_limit_bytes=BIG_VMEM),
        name="plain_backward",
    )(
        tok, cot, res, vec, hm, h2, prob, keys, vals, query, att, act, slope, *wide
    )


def hand_over_kernel(*refs, count, rows):
    srcs, dsts, held = refs[:count], refs[count : 2 * count], refs[2 * count : 3 * count]
    sems = refs[3 * count]
    moves = []
    for i, (src, dst, mid) in enumerate(zip(srcs, dsts, held)):
        if i < rows:
            n = src.shape[1]
            for m in range(LINE):
                moves.append((src.at[m], mid.at[m], dst.at[pl.ds(m * n, n), :]))
        else:
            moves.append((src, mid, dst))
    copies = [
        (
            pltpu.make_async_copy(src, mid, sems.at[0, i]),
            pltpu.make_async_copy(mid, dst, sems.at[1, i]),
        )
        for i, (src, mid, dst) in enumerate(moves)
    ]
    for bring, _ in copies:
        bring.start()
    for bring, give in copies:
        bring.wait()
        give.start()
    for _, give in copies:
        give.wait()


def hand_over(rows, others):
    arrays = rows + others
    anywhere = pl.BlockSpec(memory_space=pl.ANY)
    moves = len(rows) * LINE + len(others)
    return pl.pallas_call(
        functools.partial(hand_over_kernel, count=len(arrays), rows=len(rows)),
        in_specs=[anywhere] * len(arrays),
        out_specs=[anywhere] * len(arrays),
        out_shape=[
            jax.ShapeDtypeStruct((a.shape[0] * a.shape[1], a.shape[2]), a.dtype) for a in rows
        ]
        + [jax.ShapeDtypeStruct(a.shape, a.dtype) for a in others],
        scratch_shapes=[pltpu.VMEM(a.shape, a.dtype) for a in arrays]
        + [pltpu.SemaphoreType.DMA((2, moves))],
        compiler_params=pltpu.CompilerParams(vmem_limit_bytes=16 * 1024 * 1024),
        name="hand_over",
    )(*arrays)


def local(
    tokens,
    cotangent,
    past_state,
    positions,
    counts,
    ln1_gain,
    ln1_bias,
    w_qkv,
    b_qv,
    w_out,
    b_out,
    ln2_gain,
    ln2_bias,
    w_up,
    b_up,
    w_down,
    b_down,
):
    seq, mp = lax.axis_size("seq"), lax.axis_size("mp")
    seq_index, mp_index = lax.axis_index("seq"), lax.axis_index("mp")
    item_count, seg_len, local_width = past_state.shape
    slots = positions.shape[1]
    total = item_count * seq
    width = tokens.shape[1]
    part = width // seq
    heads_local, piece = b_qv.shape[1], b_qv.shape[2]
    head = piece * seq
    hidden = w_up.shape[1]
    rows = tokens.shape[0] // mp
    direct = seq == PLANE and mp == LINE and part % 16 == 0 and hidden == width

    past_t = past_state.transpose(0, 2, 1)

    vectors = jnp.stack([ln1_gain, ln1_bias, ln2_gain, ln2_bias, b_out, b_down])
    if direct:
        results = forward_pass(
            tokens,
            past_t,
            positions,
            counts,
            vectors,
            b_qv.transpose(1, 0, 2),
            b_up.T,
            w_qkv,
            w_out,
            w_up,
            w_down.T,
            head,
        )
        wide, forward, (vec, inverse, coef, meta) = results[:3], results[3:14], results[14:]
        block_out, block_grad, *others = backward_pass(
            tokens,
            cotangent,
            forward[0],
            meta,
            vec,
            inverse,
            coef,
            forward[1:],
            wide,
            item_count,
            past_t.shape,
            head,
        )
        vec_own = others.pop(1)
        (block_out, block_grad, past_grad, bias, bias_up, qkv_grad, out_grad, *mlp) = hand_over(
            [block_out, block_grad], others
        )
        qv, up, (up_grad, down_grad) = bias.transpose(1, 0, 2), bias_up.T, mlp
    else:
        items = (seq_index * item_count + jnp.arange(item_count)).astype(F32)
        spots = positions.astype(F32)
        places = (items[:, None] + (spots + 0.5) / seg_len) / total
        used = (jnp.arange(slots)[None, :] < counts[:, None]).astype(F32)
        meta = jnp.concatenate([places, used, spots, jnp.zeros((8 - 3 * item_count, slots), F32)])

        here = (jnp.arange(seq) == seq_index).astype(BF)
        vectors = (vectors[:, None, :] * here[None, :, None]).reshape(6, width)
        bias_qv = (b_qv[:, :, None, :] * here[None, None, :, None]).reshape(2, local_width)
        bias_qv = jnp.concatenate([bias_qv, jnp.zeros((2, local_width), BF)], axis=1)
        bias_up = (b_up[:, None, :] * here[None, :, None]).reshape(1, hidden)
        room = jnp.concatenate(
            [vectors, bias_qv.reshape(1, width), bias_up, jnp.zeros((8, width), BF)]
        )
        attn = jnp.concatenate([w_qkv[0], w_qkv[1], w_qkv[2], w_out.T], axis=1)
        sampled = sample_rows(past_t, meta)
        all_sampled = lax.all_gather(sampled, "seq", axis=0)
        all_meta = lax.all_gather(meta, "seq", axis=0)
        coef_part, inverse = solve_memory(all_sampled, all_meta, item_count)
        coef = lax.all_gather(coef_part, "mp", axis=0).transpose(1, 0, 2).reshape(NB, width)
        wide = [
            lax.all_gather(lax.all_gather(shard, "seq", axis=0, tiled=True), "mp", axis=0)
            for shard in (attn, w_up, w_down.T)
        ]
        vec = lax.psum(room.astype(F32), "seq")
        vec = lax.all_gather(vec, "mp", axis=0)
        tok = lax.dynamic_slice_in_dim(tokens, mp_index * rows, rows, 0)
        cot = lax.dynamic_slice_in_dim(cotangent, mp_index * rows, rows, 0)
        forward = plain_forward(tok, coef, vec, wide, head)
        block_out = lax.all_gather(forward[0], "mp", axis=0, tiled=True)
        tok_grad, gmem, g_up, g_down, g_attn, gv, ggv = plain_backward(
            tok, cot, vec[0], forward[1:], wide, head
        )
        tail = jnp.concatenate(
            [jnp.broadcast_to(gv[None, :6], (mp, 6, width)), ggv[mp:, :1], ggv[:mp, :1]], axis=1
        )
        block_grad = lax.all_gather(tok_grad, "mp", axis=0, tiled=True)
        gmem, tail = lax.psum((gmem, tail), ("seq", "mp"))
        own = lax.dynamic_index_in_dim(tail, mp_index, 0, keepdims=False)
        attn, up_grad, down_grad = (
            lax.psum_scatter(
                lax.psum_scatter(g, "mp", scatter_dimension=0, tiled=False),
                "seq",
                scatter_dimension=0,
                tiled=True,
            ).astype(F32)
            for g in (g_attn, g_up, g_down)
        )
        past_grad, gv_mem = past_grads(
            gmem, coef, vec, inverse, meta, item_count, seg_len, local_width
        )
        own = own + jnp.concatenate([gv_mem[:2], jnp.zeros((6, width), F32)])
        vec_own = lax.dynamic_slice_in_dim(own[:6], seq_index * part, part, 1)
        qv = jnp.stack([own[6, :local_width], own[6, 2 * local_width : 3 * local_width]])
        qv = qv.reshape(2, heads_local, head)
        qv = lax.dynamic_slice_in_dim(qv, seq_index * piece, piece, 2)
        up = lax.dynamic_slice_in_dim(own[7].reshape(-1, head), seq_index * piece, piece, 1)
        qkv_grad = jnp.stack([attn[:, i * local_width : (i + 1) * local_width] for i in range(3)])
        out_grad = attn[:, 3 * local_width :].T
    return (
        block_out,
        block_grad,
        past_grad.transpose(0, 2, 1),
        vec_own[0],
        vec_own[1],
        qkv_grad,
        qv,
        out_grad,
        vec_own[4],
        vec_own[2],
        vec_own[3],
        up_grad,
        up,
        down_grad.T,
        vec_own[5],
    )


def solution(mesh):
    row = P("seq", None)
    placed = (
        row,
        row,
        P("seq", None, "mp"),
        row,
        P("seq"),
        P("seq"),
        P("seq"),
        P(None, "seq", "mp"),
        P(None, "mp", "seq"),
        P("mp", "seq"),
        P("seq"),
        P("seq"),
        P("seq"),
        P("seq", "mp"),
        P("mp", "seq"),
        P("mp", "seq"),
        P("seq"),
    )
    return jax.shard_map(
        local,
        mesh=mesh,
        in_specs=placed,
        out_specs=(row, row, placed[2]) + placed[5:],
        check_vma=False,
    )
```
